32 devices in a mesh: dp: 8 (over y, x, core), tp: 4 (over z).
Axes of the slice: x: 2, y: 2, z: 4, core: 2. Of those that a mesh axis runs over, the one named last changes fastest.
Arguments:
- x_in: float32 [2048, 8, 2048], P('tp', 'dp'), may hold values from -6 to 6
- target: float32 [2048, 8, 2048], P('tp', 'dp'), may hold values from -6 to 6
- seg_ids: int32 [8, 2048], P('dp'), may hold values from 0 to 11, never falling along the last dimension, each value on 1 to 1024 neighbouring positions
- valid: int32 [8, 2048], P('dp', 'tp'), may hold values 0 or 1
- pre_gain: float32 [2048], replicated, may hold values from 0.5 to 1.5
- w_z: bfloat16 [2048, 4096], P('dp', 'tp'), may hold values from -0.125 to 0.125
- w_x: bfloat16 [2048, 4096], P('dp', 'tp'), may hold values from -0.125 to 0.125
- w_bc: bfloat16 [2048, 256], P('dp', 'tp'), may hold values from -0.125 to 0.125
- w_dt: bfloat16 [2048, 64], P('dp', 'tp'), may hold values from -0.125 to 0.125
- conv_x_w: float32 [4096, 4], P('tp'), may hold values from -3 to 3
- conv_x_b: float32 [4096], P('tp'), may hold values from -3 to 3
- conv_bc_w: float32 [256, 4], P('tp'), may hold values from -3 to 3
- conv_bc_b: float32 [256], P('tp'), may hold values from -3 to 3
- dt_bias: float32 [64], P('tp'), may hold values from -9 to -3
- a_log: float32 [64], P('tp'), may hold values from 0 to 2.77
- d_skip: float32 [64], P('tp'), may hold values from 0.5 to 2
- norm_gain: float32 [4096], P('tp'), may hold values from 0.5 to 1.5
- w_out: bfloat16 [4096, 2048], P('tp', 'dp'), may hold values from -0.09375 to 0.09375
Outputs:
- layer_out: float32 [2048, 8, 2048], P('tp', 'dp')
- loss: float32 [], replicated
- grad_x: float32 [2048, 8, 2048], P('tp', 'dp')
- grad_pre_gain: float32 [2048], replicated
- grad_w_z: float32 [2048, 4096], P('dp', 'tp')
- grad_w_x: float32 [2048, 4096], P('dp', 'tp')
- grad_w_bc: float32 [2048, 256], P('dp', 'tp')
- grad_w_dt: float32 [2048, 64], P('dp', 'tp')
- grad_conv_x_w: float32 [4096, 4], P('tp')
- grad_conv_x_b: float32 [4096], P('tp')
- grad_conv_bc_w: float32 [256, 4], P('tp')
- grad_conv_bc_b: float32 [256], P('tp')
- grad_dt_bias: float32 [64], P('tp')
- grad_a_log: float32 [64], P('tp')
- grad_d_skip: float32 [64], P('tp')
- grad_norm_gain: float32 [4096], P('tp')
- grad_w_out: float32 [4096, 2048], P('tp', 'dp')
The draws below stay inside these ranges and needn't reach their ends.
Inputs may be any that keep to these rules, and one draw needn't show every extreme that they name: `seg_ids`: within each sequence the ids never fall; each id of the range names one run of positions, at most half of 2048 long.
All inputs are finite; a program needn't handle non-finite values. No bound on the sum of `valid` on one device may be relied on, other than what follows from the above.
Results may differ from the reference program's by a relative error of at most 0.011.
Values may be sent and summed in bfloat16 or wider, within the bound.
A program may use at most 320 MiB of HBM per device.

```python
import math
import jax
import jax.numpy as jnp
import numpy as np
from jax import lax

D = 2048
DI = 4096
H = 64
N = 128
KC = 4
CH = 256
SEQ_LEN = 2048
SEQ_DP = 1
NSEQ = 8


def touch_ends(entries, rng, low, largest):
    spot = [jax.random.randint(jax.random.fold_in(rng, axis), (), 0, length) for axis, length in enumerate(entries.shape)]
    main_axis = entries.shape.index(max(entries.shape))
    neighbour = spot[:main_axis] + [(spot[main_axis] + 1) % entries.shape[main_axis]] + spot[main_axis + 1:]
    return entries.at[tuple(spot)].set(low).at[tuple(neighbour)].set(largest)


def with_spikes(array, own_key, source, target, shards_of, factor):
    def block_of(dim):
        return (jnp.arange(array.shape[dim]) // (array.shape[dim] // shards_of)).reshape((-1,) + (1,) * (array.ndim - 1 - dim))

    one_side = jax.random.permutation(own_key, shards_of)[block_of(target)]
    far = (block_of(target) + shards_of // 2) % shards_of
    return jnp.where((block_of(source) == one_side) | (block_of(source) == far), factor * array, array)


def block_scale(rng, dims, cuts, least, high):
    factor_of = 1.0
    for dim, blocks in cuts:
        draws = jax.random.uniform(jax.random.fold_in(jax.random.fold_in(rng, 6), dim), (blocks,), jnp.float32, least / len(cuts), high / len(cuts))
        factor_of = factor_of * jnp.repeat(jnp.exp(draws), dims[dim] // blocks).reshape((-1,) + (1,) * (len(dims) - 1 - dim))
    return factor_of


def profile(amount, total, most, lean):
    weights = [(1 << 20) // math.isqrt(grade ** lean) + 1 for grade in range(2, amount + 1)]
    spare, counts = total - most - (amount - 1), [1] * (amount - 1)
    while spare > 0:
        movable = [i for i in range(amount - 1) if counts[i] < most]
        whole, left = sum([weights[i] for i in movable]), spare
        for i in movable:
            extra = min(most - counts[i], max(1, left * weights[i] // whole), spare)
            counts[i] = counts[i] + extra
            spare = spare - extra
    return np.array([most] + counts)


def ragged(own_key, amount, total, reach, slope):
    if amount == 2:
        one = jax.random.randint(own_key, (), max(1, total - reach), min(reach, total - 1) + 1)
        return jnp.stack([one, total - one])
    tallies = jnp.asarray(profile(amount, total, reach, slope), jnp.int32)
    pairs = (amount - 1) // 2
    giver, sink = tallies[1:1 + 2 * pairs:2], tallies[2:2 + 2 * pairs:2]
    room = jnp.minimum(giver - 1, reach - sink)
    shifted = jax.random.randint(jax.random.fold_in(own_key, 1), (pairs,), 0, 1 << 20) % (room + 1)
    tallies = tallies.at[1:1 + 2 * pairs:2].set(giver - shifted).at[2:2 + 2 * pairs:2].set(sink + shifted)
    return tallies[jax.random.permutation(jax.random.fold_in(own_key, 2), amount)]


def scatter_about(rng, dims, scale, limit, shards=(), held_as=jnp.bfloat16):
    factor_of = block_scale(rng, dims, shards, -0.22, 0.18) if shards else 1.0
    values = jax.random.normal(rng, dims, jnp.float32) * scale * factor_of
    return jnp.minimum(jnp.maximum(values, -limit), limit).astype(held_as)


def heavy_noise(rng, shape, width, most, shards, heavy, kind=jnp.bfloat16):
    result = width * jax.random.normal(rng, shape, jnp.float32)
    if shards:
        result = result * block_scale(rng, shape, shards, -0.22, 0.18)
    return jnp.clip(with_spikes(result, jax.random.fold_in(rng, 3), *heavy), -most, most).astype(kind)


def setup_inputs(seed: int = 0) -> dict:
    seeds = jax.random.split(jax.random.key(seed), 19)
    return {
        "x_in": heavy_noise(seeds[0], (SEQ_LEN, NSEQ, D), 1.0, 6.0, ((0, 4), (1, 8)), (1, 2, 8, 2.0), jnp.float32),
        "target": scatter_about(seeds[1], (SEQ_LEN, NSEQ, D), 1.0, 6.0, ((0, 4), (1, 8)), jnp.float32),
        "seg_ids": jax.vmap(lambda own: jnp.searchsorted(jnp.cumsum(ragged(own, 12, SEQ_LEN, SEQ_LEN // 2, 2)), jnp.arange(SEQ_LEN), side="right"))(jax.random.split(seeds[2], NSEQ)).reshape((NSEQ, SEQ_LEN)).astype(jnp.int32),
        "valid": touch_ends((jax.random.randint(seeds[3], (NSEQ, SEQ_LEN), 0, 8) < 7).astype(jnp.int32), jax.random.fold_in(seeds[3], 1), 0, 1),
        "pre_gain": jnp.clip(1.0 + 0.1 * jax.random.normal(seeds[4], (D,), jnp.float32), 0.5, 1.5),
        "w_z": scatter_about(seeds[5], (D, DI), D ** -0.5, 0.125, ((0, 8), (1, 4))),
        "w_x": scatter_about(seeds[6], (D, DI), D ** -0.5, 0.125, ((0, 8), (1, 4))),
        "w_bc": scatter_about(seeds[7], (D, 2 * N), D ** -0.5, 0.125, ((0, 8), (1, 4))),
        "w_dt": scatter_about(seeds[8], (D, H), D ** -0.5, 0.125, ((0, 8), (1, 4))),
        "conv_x_w": scatter_about(seeds[9], (DI, KC), 0.5, 3.0, ((0, 4),), jnp.float32),
        "conv_x_b": scatter_about(seeds[10], (DI,), 0.3, 3.0, ((0, 4),), jnp.float32),
        "conv_bc_w": scatter_about(seeds[11], (2 * N, KC), 0.5, 3.0, ((0, 4),), jnp.float32),
        "conv_bc_b": scatter_about(seeds[12], (2 * N,), 0.3, 3.0, ((0, 4),), jnp.float32),
        "dt_bias": jnp.clip(-9.0 + 6.0 * jax.random.uniform(seeds[13], (H,), jnp.float32) ** block_scale(seeds[13], (H,), ((0, 4),), -0.2, 0.2), -9.0, -3.0),
        "a_log": jnp.clip(2.77 * jax.random.uniform(seeds[14], (H,), jnp.float32) ** block_scale(seeds[14], (H,), ((0, 4),), -0.2, 0.2), 0.0, 2.77),
        "d_skip": jnp.clip(0.5 + 1.5 * jax.random.uniform(seeds[15], (H,), jnp.float32) ** block_scale(seeds[15], (H,), ((0, 4),), -0.2, 0.2), 0.5, 2.0),
        "norm_gain": jnp.clip(1.0 + 0.1 * jax.random.normal(seeds[16], (DI,), jnp.float32), 0.5, 1.5),
        "w_out": scatter_about(seeds[17], (DI, D), DI ** -0.5, 0.09375, ((0, 4), (1, 8))),
    }


epsilon = 1e-05
highest = lax.Precision.HIGHEST

@jax.custom_vjp
def low(v):
    return lax.optimization_barrier(v.astype(jnp.bfloat16)).astype(jnp.float32)

@jax.custom_vjp
def low_back(v):
    return v

def low_keep(v):
    return (low(v), None)

def low_pass(kept, grad):
    return (grad,)

def back_keep(v):
    return (v, None)

def back_low(kept, grad):
    return (low(grad),)
low.defvjp(low_keep, low_pass)
low_back.defvjp(back_keep, back_low)

def conv_causal(values, kernel, offsets, segment):
    width_k = kernel.shape[1]
    length = values.shape[0]
    padded = jnp.pad(values, ((width_k - 1, 0), (0, 0), (0, 0)))
    padded_seg = jnp.pad(segment, ((width_k - 1, 0), (0, 0)), constant_values=-1)
    summed = jnp.zeros(values.shape, values.dtype) + offsets
    for offset in range(width_k):
        matched = (padded_seg[offset:offset + length] == segment).astype(values.dtype)
        summed = summed + padded[offset:offset + length] * kernel[:, offset] * matched[:, :, None]
    return summed

def ssd_core(inner_x, step_dt, log_decay, b_rows, c_rows, segment):
    length, seq_count, head_count, head_dim = inner_x.shape
    blocks = length // CH
    x_blk = inner_x.reshape(blocks, CH, seq_count, head_count, head_dim)
    dt_blk = step_dt.reshape(blocks, CH, seq_count, head_count)
    cum_blk = jnp.cumsum(log_decay.reshape(blocks, CH, seq_count, head_count), axis=1)
    b_blk = b_rows.reshape(blocks, CH, seq_count, -1)
    c_blk = c_rows.reshape(blocks, CH, seq_count, -1)
    seg_blk = segment.reshape(blocks, CH, seq_count)
    last_seg = seg_blk[:, -1]
    prev_seg = jnp.concatenate([jnp.full((1, seq_count), -1, jnp.int32), last_seg[:-1].astype(jnp.int32)], axis=0)
    cum_t = jnp.transpose(cum_blk, (0, 2, 3, 1))
    dt_t = jnp.transpose(dt_blk, (0, 2, 3, 1))
    seg_t = jnp.transpose(seg_blk, (0, 2, 1))
    causal = jnp.arange(CH)[:, None] >= jnp.arange(CH)[None, :]
    same_doc = ((seg_t[..., :, None] == seg_t[..., None, :]) & causal)[:, :, None]
    log_gap = cum_t[..., :, None] - cum_t[..., None, :]
    decay_mat = jnp.where(same_doc, jnp.exp(jnp.where(same_doc, log_gap, 0.0)), 0.0)
    scores = jnp.einsum('cisn,cjsn->csij', c_blk, b_blk, precision=highest)
    mixing = decay_mat * scores[:, :, None] * dt_t[:, :, :, None, :]
    y_intra = jnp.einsum('cshij,cjshp->cishp', mixing, x_blk, precision=highest)
    end_mask = (seg_t == last_seg[:, :, None])[:, :, None]
    to_end = jnp.exp(cum_t[..., -1:] - cum_t) * end_mask * dt_t
    weighted_x = x_blk * jnp.transpose(to_end, (0, 3, 1, 2))[..., None]
    states = jnp.einsum('cjshp,cjsn->cshpn', weighted_x, b_blk, precision=highest)
    keep_flag = (last_seg == prev_seg).astype(states.dtype)
    carry_decay = jnp.exp(cum_t[..., -1]) * keep_flag[:, :, None]

    def advance(carried, pieces):
        state_now, factor = pieces
        return (state_now + factor[..., None, None] * carried, carried)
    _, entering = lax.scan(advance, jnp.zeros_like(states[0]), (states, carry_decay))
    start_mask = (seg_blk == prev_seg[:, None, :]).astype(states.dtype)
    y_inter = jnp.einsum('cisn,cshpn->cishp', c_blk, entering, precision=highest)
    y_inter = y_inter * (jnp.exp(cum_blk) * start_mask[..., None])[..., None]
    return (y_intra + y_inter).reshape(length, seq_count, head_count, head_dim)

def mixer_local(z_part, x_part, dt_raw, b_rows, c_rows, conv_x_w, conv_x_b, dt_bias, a_log, d_skip, segment):
    inner = jax.nn.silu(conv_causal(x_part, conv_x_w, conv_x_b, segment))
    length, seq_count, head_count = dt_raw.shape
    heads_x = inner.reshape(length, seq_count, head_count, -1)
    step_dt = jax.nn.softplus(dt_raw + dt_bias)
    log_decay = -jnp.exp(a_log) * step_dt
    y_ssd = jax.checkpoint(ssd_core)(heads_x, step_dt, log_decay, b_rows, c_rows, segment)
    full_y = y_ssd + d_skip[:, None] * heads_x
    return full_y.reshape(inner.shape) * jax.nn.silu(z_part)

def forward_group(params, x_grp, seg_grp):
    pre_gain, w_z, w_x, w_bc, w_dt, conv_x_w, conv_x_b, conv_bc_w, conv_bc_b, dt_bias, a_log, d_skip, norm_gain, w_out = params
    inv_rms = lax.rsqrt(lax.optimization_barrier(jnp.mean(x_grp * x_grp, axis=-1, keepdims=True)) + epsilon)
    normed = low(x_grp * inv_rms * pre_gain)

    def project(weight):
        return low_back(jnp.einsum('lsd,dc->lsc', normed, weight, precision=highest))
    z_part = project(w_z)
    x_part = project(w_x)
    bc_raw = project(w_bc)
    dt_raw = project(w_dt)
    bc_conv = low(jax.nn.silu(conv_causal(bc_raw, conv_bc_w, conv_bc_b, seg_grp)))
    n_state = bc_conv.shape[2] // 2
    gated = mixer_local(z_part, x_part, dt_raw, bc_conv[..., :n_state], bc_conv[..., n_state:], conv_x_w, conv_x_b, dt_bias, a_log, d_skip, seg_grp)
    gate_rms = lax.rsqrt(lax.optimization_barrier(jnp.mean(gated * gated, axis=-1, keepdims=True)) + epsilon)
    normed_out = low(gated * gate_rms * norm_gain)
    branch = low_back(jnp.einsum('lsk,kd->lsd', normed_out, w_out, precision=highest))
    return x_grp + branch

def reference(x_in, target, seg_ids, valid, pre_gain, w_z, w_x, w_bc, w_dt, conv_x_w, conv_x_b, conv_bc_w, conv_bc_b, dt_bias, a_log, d_skip, norm_gain, w_out):
    params = tuple((item.astype(jnp.float32) for item in (pre_gain, w_z, w_x, w_bc, w_dt, conv_x_w, conv_x_b, conv_bc_w, conv_bc_b, dt_bias, a_log, d_skip, norm_gain, w_out)))
    length, seq_total, model_dim = x_in.shape
    groups = seq_total // SEQ_DP
    x_groups = jnp.transpose(x_in.astype(jnp.float32).reshape(length, groups, SEQ_DP, model_dim), (1, 0, 2, 3))
    tgt_groups = jnp.transpose(target.astype(jnp.float32).reshape(length, groups, SEQ_DP, model_dim), (1, 0, 2, 3))
    seg_groups = jnp.transpose(seg_ids.reshape(groups, SEQ_DP, length), (0, 2, 1))
    mask_groups = jnp.transpose(valid.reshape(groups, SEQ_DP, length), (0, 2, 1)).astype(jnp.float32)[..., None]

    def run_all(weights, x_all):
        block_fn = jax.checkpoint(forward_group)

        def scan_step(carried, pieces):
            return (carried, block_fn(weights, pieces[0], pieces[1]))
        _, outs = lax.scan(scan_step, jnp.zeros((), jnp.float32), (x_all, seg_groups))
        return outs
    out_groups, pull_back = jax.vjp(run_all, params, x_groups)
    error = out_groups - tgt_groups
    d_out = error * mask_groups
    grad_params, grad_groups = pull_back(d_out)
    loss = jnp.sum(d_out * error) / (jnp.maximum(jnp.sum(mask_groups), 1.0) * D)
    layer_out = jnp.transpose(out_groups, (1, 0, 2, 3)).reshape(length, seq_total, model_dim)
    grad_x = jnp.transpose(grad_groups, (1, 0, 2, 3)).reshape(length, seq_total, model_dim)
    grad_pre, grad_wz, grad_wx, grad_wbc, grad_wdt, grad_cxw, grad_cxb, grad_cbw, grad_cbb, grad_dtb, grad_alog, grad_dskip, grad_gain, grad_wout = grad_params
    return (layer_out, loss, grad_x, grad_pre, grad_wz, grad_wx, grad_wbc, grad_wdt, grad_cxw, grad_cxb, grad_cbw, grad_cbb, grad_dtb, grad_alog, grad_dskip, grad_gain, grad_wout)
```

```python
from functools import partial

import jax
import jax.numpy as jnp
from jax import lax
from jax.experimental import pallas as pl
from jax.experimental.pallas import tpu as pltpu
from jax.sharding import PartitionSpec as P

T = 128
TB = 256
EPS = 1e-05
LOG2E = 1.4426950408889634
F32 = jnp.float32
BF16 = jnp.bfloat16
ZT = YT = F32
XT = CT = BF16
HIGHEST = lax.Precision.HIGHEST


def dot(a, b, precision=None):
    return jnp.dot(a, b, preferred_element_type=F32, precision=precision)


def dot_nt(a, b):
    return lax.dot_general(a, b, (((1,), (1,)), ((), ())), preferred_element_type=F32)


def lanes(column_of, index, rows=T):
    return jnp.broadcast_to(column_of[:, index : index + 1], (rows, 128))


def iota(shape, axis):
    return lax.broadcasted_iota(jnp.int32, shape, axis)


def step_sizes(raw, hp_ref):
    shifted = raw + hp_ref[0:1, :]
    dt = jnp.maximum(shifted, 0.0) + jnp.log1p(jnp.exp(-jnp.abs(shifted)))
    la = dt * hp_ref[1:2, :]
    inclusive = (iota((T, T), 0) >= iota((T, T), 1)).astype(F32)
    cum = dot(inclusive, la * LOG2E, HIGHEST)
    return shifted, dt, la, cum


def split_pair(value):
    first = iota((T, 128), 1) < 64
    zero = jnp.zeros_like(value)
    return jnp.concatenate([jnp.where(first, value, zero), jnp.where(first, zero, value)], axis=0)


def fwd_kernel(
    nb_ref, wz_ref, wx_ref, wbd_ref, tok_ref, segr_ref, chp_ref, bcp_ref, hp_ref,
    z_out, xs_out, xcv_out, y_out, u_out, bcr_out, bcv_out, dtr_out, bcc_out, st_out, sq_out,
    zbuf, xbuf, bcbuf, state,
):
    channels = wz_ref.shape[1]
    pairs = channels // 128

    @pl.when(pl.program_id(0) == 0)
    def _():
        state[...] = jnp.zeros_like(state)
        xbuf[0:8, :] = jnp.zeros((8, channels), F32)
        bcbuf[0:8, :] = jnp.zeros((8, 256), F32)

    nb = nb_ref[...]
    for n in range(channels // 256):
        cols = slice(n * 256, n * 256 + 256)
        zbuf[:, cols] = dot(nb, wz_ref[:, cols])
        xbuf[8 : 8 + TB, cols] = dot(nb, wx_ref[:, cols])
    bd = dot(nb, wbd_ref[...])
    bcbuf[8 : 8 + TB, :] = bd[:, :256]
    dtr_out[...] = bd[:, 256:]
    bcr_out[...] = bd[:, :256].astype(BF16)
    first = iota((T, 128), 1) < 64
    for c in range(TB // T):
        r0 = c * T
        rows = slice(r0, r0 + T)
        tok = tok_ref[rows, :]
        masks = [lanes(tok, d) for d in range(3)]
        seg_col, start_b, end_b = lanes(tok, 3), lanes(tok, 4), lanes(tok, 5)
        parts = []
        for half in range(2):
            cols = slice(half * 128, half * 128 + 128)
            acc = bcbuf[8 + r0 : 8 + r0 + T, cols] * bcp_ref[3:4, cols] + bcp_ref[4:5, cols]
            for d in (1, 2, 3):
                acc = acc + bcbuf[8 + r0 - d : 8 + r0 - d + T, cols] * bcp_ref[3 - d : 4 - d, cols] * masks[d - 1]
            bcv_out[rows, cols] = acc.astype(BF16)
            hv = 0.5 * acc
            parts.append((hv + hv * jnp.tanh(hv)).astype(BF16))
            bcc_out[rows, cols] = parts[-1]
        bm, cm = parts
        bt = bm.T
        _, dt, la, cum = step_sizes(dtr_out[rows, :], hp_ref)
        cum_t = cum.T
        scores = dot_nt(cm, bm)
        keep = (seg_col == segr_ref[c, 0:1, :]) & (iota((T, T), 0) >= iota((T, T), 1))
        qm = jnp.where(keep, scores, 0.0)
        sq = jnp.zeros((T, 128), F32)
        st_out[c, :, :] = state[...].astype(BF16)
        for j in range(pairs):
            cols = slice(j * 128, j * 128 + 128)
            acc = xbuf[8 + r0 : 8 + r0 + T, cols] * chp_ref[3:4, cols] + chp_ref[4:5, cols]
            xs_out[rows, cols] = xbuf[8 + r0 : 8 + r0 + T, cols].astype(XT)
            for d in (1, 2, 3):
                acc = acc + xbuf[8 + r0 - d : 8 + r0 - d + T, cols] * chp_ref[3 - d : 4 - d, cols] * masks[d - 1]
            xcv_out[rows, cols] = acc.astype(CT)
            hv = 0.5 * acc
            xc = hv + hv * jnp.tanh(hv)
            dt_e = jnp.where(first, lanes(dt, 2 * j), lanes(dt, 2 * j + 1))
            ca, cb = lanes(cum, 2 * j), lanes(cum, 2 * j + 1)
            cum_e = jnp.where(first, ca, cb)
            xdt = xc * dt_e
            ea = jnp.exp2(jnp.minimum(ca - cum_t[2 * j : 2 * j + 1, :], 0.0))
            eb = jnp.exp2(jnp.minimum(cb - cum_t[2 * j + 1 : 2 * j + 2, :], 0.0))
            mix = jnp.concatenate([(ea * qm).astype(BF16), (eb * qm).astype(BF16)], axis=1)
            y = dot(mix, split_pair(xdt.astype(BF16)))
            into = jnp.exp2(cum_e) * start_b
            last = cum_e[T - 1 : T, :]
            to_end = jnp.exp2(last - cum_e) * end_b
            y = y + into * dot(cm, st_out[c, :, cols])
            state[:, cols] = state[:, cols] * into[T - 1 : T, :] + dot(bt, (xdt * to_end).astype(BF16))
            y = y + chp_ref[5:6, cols] * xc
            y_out[rows, cols] = y.astype(YT)
            zz = zbuf[rows, cols]
            z_out[rows, cols] = zz.astype(ZT)
            hz = 0.5 * zz
            g = y * (hz + hz * jnp.tanh(hz))
            sq = sq + g * g
            u_out[rows, cols] = (g * chp_ref[6:7, cols]).astype(BF16)
        sq_out[rows, :] = sq
    xbuf[0:8, :] = xbuf[TB : TB + 8, :]
    bcbuf[0:8, :] = bcbuf[TB : TB + 8, :]


def row_sums(value):
    return jnp.sum(value.reshape(value.shape[0] // 8, 8, value.shape[1]), axis=0)


def bwd_kernel(
    db_ref, wo_ref, rk_ref, tok_ref, segr_ref, chp_ref, bcp_ref, hp_ref,
    z_ref, xs_ref, xcv_ref, y_ref, bcr_ref, bcv_ref, dtr_ref, bcc_ref, st_ref,
    dproj_out, yn_out, accc_out, accb_out, acch_out,
    dyn, dbuf, dbcbuf, dstate, dstate_b, dyec, xte, cs_rows, fold, pick,
):
    channels = wo_ref.shape[1]
    pairs = channels // 128

    @pl.when(pl.program_id(0) == 0)
    def _():
        dstate[...] = jnp.zeros_like(dstate)
        dbuf[...] = jnp.zeros_like(dbuf)
        dbcbuf[...] = jnp.zeros_like(dbcbuf)
        accc_out[...] = jnp.zeros_like(accc_out)
        accb_out[...] = jnp.zeros_like(accb_out)
        acch_out[...] = jnp.zeros_like(acch_out)
        cs_rows[...] = jnp.zeros_like(cs_rows)
        for j in range(pairs):
            half = (iota((128, 128), 0) >= 64).astype(jnp.int32)
            fold[j, :, :] = (iota((128, 128), 1) == 2 * j + half).astype(F32).astype(BF16)
            part = (iota((256, 128), 0) >= 128).astype(jnp.int32)
            pick[j, :, :] = (iota((256, 128), 1) == 2 * j + part).astype(F32).astype(BF16)

    db = db_ref[...]
    for n in range(channels // 256):
        cols = slice(n * 256, n * 256 + 256)
        dyn[:, cols] = dot(db, wo_ref[:, cols])
    first = iota((T, 128), 1) < 64
    for c in reversed(range(TB // T)):
        r0 = c * T
        rows = slice(r0, r0 + T)
        tok = tok_ref[rows, :]
        seg_col, start_b, end_b = lanes(tok, 3), lanes(tok, 4), lanes(tok, 5)
        ahead = [lanes(tok, 6 + d) for d in range(3)]
        rg_b, kc_b = lanes(rk_ref[rows, :], 0), lanes(rk_ref[rows, :], 1)
        bm, cm = bcc_ref[rows, 0:128], bcc_ref[rows, 128:256]
        ct = cm.T
        shifted, dt, la, cum = step_sizes(dtr_ref[rows, :], hp_ref)
        cum_t = cum.T
        scores, scores_t = dot_nt(cm, bm), dot_nt(bm, cm)
        same = seg_col == segr_ref[c, 0:1, :]
        below = iota((T, T), 0) >= iota((T, T), 1)
        strict = iota((T, T), 0) > iota((T, T), 1)
        above = iota((T, T), 0) <= iota((T, T), 1)
        qs = jnp.where(same & strict, scores, 0.0)
        qt = jnp.where(same & above, scores_t, 0.0)
        dstate_b[...] = dstate[...].astype(BF16)
        dq = jnp.zeros((T, T), F32)
        rsum = jnp.zeros((T, 128), F32)
        ddt = jnp.zeros((T, 128), F32)
        xsum = jnp.zeros((T, 128), F32)
        ksum = jnp.zeros((16, 128), F32)
        for j in range(pairs):
            cols = slice(j * 128, j * 128 + 128)
            zz = z_ref[rows, cols].astype(F32)
            y = y_ref[rows, cols].astype(F32)
            sz = 0.5 + 0.5 * jnp.tanh(0.5 * zz)
            silu_z = zz * sz
            dsz = sz + silu_z * (1.0 - sz)
            g = y * silu_z
            gr = g * rg_b
            gain = chp_ref[6:7, cols]
            dynp = dyn[rows, cols]
            yn_out[rows, cols] = (gr * gain).astype(BF16)
            accc_out[5, :, cols] += row_sums(dynp * gr)
            dg = rg_b * dynp * gain - g * kc_b
            dy = dg * silu_z
            dproj_out[rows, cols] = (dg * y * dsz).astype(BF16)
            xcv = xcv_ref[rows, cols].astype(F32)
            sx = 0.5 + 0.5 * jnp.tanh(0.5 * xcv)
            xc = xcv * sx
            dsx = sx + xc * (1.0 - sx)
            accc_out[6, :, cols] += row_sums(dy * xc)
            dt_e = jnp.where(first, lanes(dt, 2 * j), lanes(dt, 2 * j + 1))
            ca, cb = lanes(cum, 2 * j), lanes(cum, 2 * j + 1)
            cum_e = jnp.where(first, ca, cb)
            into = jnp.exp2(cum_e) * start_b
            to_end = jnp.exp2(cum_e[T - 1 : T, :] - cum_e) * end_b
            decay = into[T - 1 : T, :]
            xdt = xc * dt_e
            dy_b = dy.astype(BF16)
            ga = ca - cum_t[2 * j : 2 * j + 1, :]
            gb = cb - cum_t[2 * j + 1 : 2 * j + 2, :]
            grad = dot_nt(dy_b, split_pair(xdt.astype(BF16)))
            gea = grad[:, :128] * jnp.exp2(jnp.minimum(ga, 0.0))
            geb = grad[:, 128:] * jnp.exp2(jnp.minimum(gb, 0.0))
            dq = dq + gea + geb
            pp = jnp.concatenate([(gea * qs).astype(BF16), (geb * qs).astype(BF16)], axis=1)
            rsum = rsum + dot(pp, pick[j, :, :])
            csum = dot(jnp.ones((8, T), BF16), pp)
            cs_rows[2 * j : 2 * j + 1, :] = csum[0:1, :128]
            cs_rows[2 * j + 1 : 2 * j + 2, :] = csum[0:1, 128:]
            eta = (jnp.exp2(jnp.minimum(-ga, 0.0)) * qt).astype(BF16)
            etb = (jnp.exp2(jnp.minimum(-gb, 0.0)) * qt).astype(BF16)
            dxdt = dot(jnp.concatenate([eta, etb], axis=1), split_pair(dy_b))
            dx_state = to_end * dot(bm, dstate_b[:, cols])
            dxdt = dxdt + dx_state
            y_in = into * dot(cm, st_ref[c, :, cols])
            dyec_p = (dy * into).astype(BF16)
            dyec[:, cols] = dyec_p
            xte[:, cols] = (xdt * to_end).astype(BF16)
            ddt = ddt + dot((xc * dxdt).astype(BF16), fold[j, :, :])
            rsum = rsum + dot((dy * y_in).astype(BF16), fold[j, :, :])
            xsum = xsum + dot((xdt * dx_state).astype(BF16), fold[j, :, :])
            old = dstate[:, cols]
            kpart = row_sums(old * st_ref[c, :, cols].astype(F32)) * decay
            khigh = kpart.astype(BF16)
            klow = (kpart - khigh.astype(F32)).astype(BF16)
            ksum = ksum + dot(jnp.concatenate([khigh, klow], axis=0), fold[j, :, :])
            dstate[:, cols] = old * decay + dot(ct, dyec_p)
            dxcv = (dxdt * dt_e + chp_ref[5:6, cols] * dy) * dsx
            dbuf[0:T, cols] = dxcv
            xs = xs_ref[rows, cols].astype(F32)
            dxs = dxcv * chp_ref[3:4, cols]
            accc_out[4, :, cols] += row_sums(dxcv)
            accc_out[3, :, cols] += row_sums(dxcv * xs)
            for d in (1, 2, 3):
                moved = dbuf[d : d + T, cols] * ahead[d - 1]
                dxs = dxs + moved * chp_ref[3 - d : 4 - d, cols]
                accc_out[3 - d, :, cols] += row_sums(moved * xs)
            dproj_out[rows, channels + j * 128 : channels + j * 128 + 128] = dxs.astype(BF16)
        dbuf[T : T + 8, :] = dbuf[0:8, :]
        dqm = jnp.where(same & below, dq, 0.0)
        dc = dot(dqm.astype(BF16), bm) + dot_nt(dyec[...], st_ref[c, :, :])
        db_rows = dot(dqm.T.astype(BF16), cm) + dot_nt(xte[...], dstate_b[...])
        for half, grad_half in enumerate((db_rows, dc)):
            cols = slice(half * 128, half * 128 + 128)
            raw = bcv_ref[rows, cols].astype(F32)
            sb = 0.5 + 0.5 * jnp.tanh(0.5 * raw)
            dcv = grad_half * (sb + raw * sb * (1.0 - sb))
            dbcbuf[0:T, cols] = dcv
            xs = bcr_ref[rows, cols].astype(F32)
            dxs = dcv * bcp_ref[3:4, cols]
            accb_out[4, :, cols] += row_sums(dcv)
            accb_out[3, :, cols] += row_sums(dcv * xs)
            for d in (1, 2, 3):
                moved = dbcbuf[d : d + T, cols] * ahead[d - 1]
                dxs = dxs + moved * bcp_ref[3 - d : 4 - d, cols]
                accb_out[3 - d, :, cols] += row_sums(moved * xs)
            dproj_out[rows, 2 * channels + half * 128 : 2 * channels + half * 128 + 128] = dxs.astype(BF16)
        dbcbuf[T : T + 8, :] = dbcbuf[0:8, :]
        after = (iota((T, T), 0) <= iota((T, T), 1)).astype(F32)
        before = (iota((T, T), 0) > iota((T, T), 1)).astype(F32)
        dla = dot(after, rsum - cs_rows[...].T, HIGHEST) + dot(before, xsum, HIGHEST)
        dla = dla + jnp.sum(ksum, axis=0, keepdims=True)
        ddtr = (ddt + dla * hp_ref[1:2, :]) * (0.5 + 0.5 * jnp.tanh(0.5 * shifted))
        acch_out[0, :, :] += row_sums(ddtr)
        acch_out[1, :, :] += row_sums(dla * la)
        dproj_out[rows, 2 * channels + 256 : 2 * channels + 384] = ddtr.astype(BF16)


def forward(normed, wz, wx, wbd, tok, segr, chp, bcp, hp):
    length, width = normed.shape
    channels = wz.shape[1]
    grid = length // TB
    once = dict(pipeline_mode=pl.Buffered(1))

    def block(cols):
        return pl.BlockSpec((TB, cols), lambda i: (i, 0))

    def whole(array):
        return pl.BlockSpec(array.shape, lambda i: (0,) * array.ndim, **once)

    chunk3 = pl.BlockSpec((TB // T, 8, 128), lambda i: (i, 0, 0))
    outs = [
        (channels, ZT), (channels, XT), (channels, CT), (channels, YT), (channels, BF16),
        (256, BF16), (256, BF16), (128, F32), (256, BF16), None, (128, F32),
    ]
    out_shape, out_specs = [], []
    for item in outs:
        if item is None:
            out_shape.append(jax.ShapeDtypeStruct((length // T, 128, channels), BF16))
            out_specs.append(pl.BlockSpec((TB // T, 128, channels), lambda i: (i, 0, 0)))
        else:
            out_shape.append(jax.ShapeDtypeStruct((length, item[0]), item[1]))
            out_specs.append(block(item[0]))
    return pl.pallas_call(
        fwd_kernel,
        grid=(grid,),
        in_specs=[block(width), whole(wz), whole(wx), whole(wbd), block(128), chunk3, whole(chp), whole(bcp), whole(hp)],
        out_specs=out_specs,
        out_shape=out_shape,
        scratch_shapes=[
            pltpu.VMEM((TB, channels), F32),
            pltpu.VMEM((TB + 8, channels), F32),
            pltpu.VMEM((TB + 8, 256), F32),
            pltpu.VMEM((128, channels), F32),
        ],
        compiler_params=pltpu.CompilerParams(vmem_limit_bytes=56 << 20),
        name="ssd_forward",
    )(normed, wz, wx, wbd, tok, segr, chp, bcp, hp)


def backward(db, wo, rk, tok, segr, chp, bcp, hp, z, xs, xcv, y, bcr, bcv, dtr, bcc, st):
    length, width = db.shape
    channels = wo.shape[1]
    pairs = channels // 128
    grid = length // TB
    once = dict(pipeline_mode=pl.Buffered(1))

    def block(cols):
        return pl.BlockSpec((TB, cols), lambda i: (grid - 1 - i, 0))

    def whole(shape):
        return pl.BlockSpec(shape, lambda i: (0,) * len(shape), **once)

    chunk3 = pl.BlockSpec((TB // T, 8, 128), lambda i: (grid - 1 - i, 0, 0))
    states = pl.BlockSpec((TB // T, 128, channels), lambda i: (grid - 1 - i, 0, 0))
    total = 2 * channels + 384
    return pl.pallas_call(
        bwd_kernel,
        grid=(grid,),
        in_specs=[
            block(width), whole(wo.shape), block(128), block(128), chunk3,
            whole(chp.shape), whole(bcp.shape), whole(hp.shape),
            block(channels), block(channels), block(channels), block(channels),
            block(256), block(256), block(128), block(256), states,
        ],
        out_specs=[
            block(total), block(channels),
            pl.BlockSpec((7, 8, channels), lambda i: (0, 0, 0)),
            pl.BlockSpec((5, 8, 256), lambda i: (0, 0, 0)),
            pl.BlockSpec((2, 8, 128), lambda i: (0, 0, 0)),
        ],
        out_shape=[
            jax.ShapeDtypeStruct((length, total), BF16),
            jax.ShapeDtypeStruct((length, channels), BF16),
            jax.ShapeDtypeStruct((7, 8, channels), F32),
            jax.ShapeDtypeStruct((5, 8, 256), F32),
            jax.ShapeDtypeStruct((2, 8, 128), F32),
        ],
        scratch_shapes=[
            pltpu.VMEM((TB, channels), F32),
            pltpu.VMEM((T + 8, channels), F32),
            pltpu.VMEM((T + 8, 256), F32),
            pltpu.VMEM((128, channels), F32),
            pltpu.VMEM((128, channels), BF16),
            pltpu.VMEM((T, channels), BF16),
            pltpu.VMEM((T, channels), BF16),
            pltpu.VMEM((128, 128), F32),
            pltpu.VMEM((pairs, 128, 128), BF16),
            pltpu.VMEM((pairs, 256, 128), BF16),
        ],
        compiler_params=pltpu.CompilerParams(vmem_limit_bytes=56 << 20),
        name="ssd_backward",
    )(db, wo, rk, tok, segr, chp, bcp, hp, z, xs, xcv, y, bcr, bcv, dtr, bcc, st)


MESH_ID = pl.DeviceIdType.MESH


def meet_neighbours(n):
    me = lax.axis_index("tp")
    barrier = pltpu.get_barrier_semaphore()

    @pl.when(me > 0)
    def _():
        pl.semaphore_signal(barrier, inc=1, device_id={"tp": me - 1}, device_id_type=MESH_ID)

    @pl.when(me < n - 1)
    def _():
        pl.semaphore_signal(barrier, inc=1, device_id={"tp": me + 1}, device_id_type=MESH_ID)

    at_end = (me == 0) | (me == n - 1)

    @pl.when(at_end)
    def _():
        pl.semaphore_wait(barrier, 1)

    @pl.when(jnp.logical_not(at_end))
    def _():
        pl.semaphore_wait(barrier, 2)

    return me


def gather_kernel(n, pieces, x_ref, out_ref, local_sem, send_sem, recv_sem):
    rows = x_ref.shape[0]
    piece = rows // pieces
    me = meet_neighbours(n)
    keep = pltpu.make_async_copy(x_ref, out_ref.at[pl.ds(pl.multiple_of(me * rows, rows), rows)], local_sem)
    keep.start()

    def place(owner, p):
        return out_ref.at[pl.ds(pl.multiple_of(owner * rows + p * piece, piece), piece)]

    def outgoing(way, step, p):
        owner = me - step if way == 0 else me + step
        source = x_ref.at[pl.ds(p * piece, piece)] if step == 0 else place(owner, p)
        return pltpu.make_async_remote_copy(
            src_ref=source,
            dst_ref=place(owner, p),
            send_sem=send_sem.at[way, step, p],
            recv_sem=recv_sem.at[way, step, p],
            device_id={"tp": me + 1 if way == 0 else me - 1},
            device_id_type=MESH_ID,
        )

    def incoming(way, step, p):
        owner = me - 1 - step if way == 0 else me + 1 + step
        return pltpu.make_async_remote_copy(
            src_ref=place(owner, p),
            dst_ref=place(owner, p),
            send_sem=send_sem.at[way, step, p],
            recv_sem=recv_sem.at[way, step, p],
            device_id={"tp": me - 1 if way == 0 else me + 1},
            device_id_type=MESH_ID,
        )

    def sends(way, step):
        if way == 0:
            return (me - step >= 0) & (me < n - 1)
        return (me + step <= n - 1) & (me > 0)

    def receives(way, step):
        return me - 1 - step >= 0 if way == 0 else me + 1 + step <= n - 1

    for step in range(n):
        for p in range(pieces):
            for way in (0, 1):
                if step > 0:

                    @pl.when(receives(way, step - 1))
                    def _():
                        incoming(way, step - 1, p).wait_recv()

                if step < n - 1:

                    @pl.when(sends(way, step))
                    def _():
                        outgoing(way, step, p).start()

    for step in range(n - 1):
        for p in range(pieces):
            for way in (0, 1):

                @pl.when(sends(way, step))
                def _():
                    outgoing(way, step, p).wait_send()

    keep.wait()


def gather_rows(x, n, collective_id):
    rows, width = x.shape
    pieces = 4
    return pl.pallas_call(
        partial(gather_kernel, n, pieces),
        out_shape=jax.ShapeDtypeStruct((n * rows, width), x.dtype),
        in_specs=[pl.BlockSpec(memory_space=pl.ANY)],
        out_specs=pl.BlockSpec(memory_space=pl.ANY),
        scratch_shapes=[
            pltpu.SemaphoreType.DMA,
            pltpu.SemaphoreType.DMA((2, n - 1, pieces)),
            pltpu.SemaphoreType.DMA((2, n - 1, pieces)),
        ],
        compiler_params=pltpu.CompilerParams(collective_id=collective_id, has_side_effects=True),
        cost_estimate=pl.CostEstimate(flops=0, bytes_accessed=400 << 20, transcendentals=0),
        name="gather_rows",
    )(x)


def scatter_kernel(n, parts, *refs):
    a_ref, right_refs = refs[0], refs[1 : 1 + parts]
    out_ref, slots, send_sem, recv_sem = refs[1 + parts :]
    rows, width = out_ref.shape
    piece = slots.shape[2]
    pieces = rows // piece
    me = meet_neighbours(n)

    def link(way, shard, p):
        return pltpu.make_async_remote_copy(
            src_ref=slots.at[way, shard * pieces + p],
            dst_ref=slots.at[way, shard * pieces + p],
            send_sem=send_sem.at[way, shard * pieces + p],
            recv_sem=recv_sem.at[way, shard * pieces + p],
            device_id={"tp": me + 1 if way == 0 else me - 1},
            device_id_type=MESH_ID,
        )

    def own(start, cols):
        total, at = None, 0
        for w_ref in right_refs:
            depth = w_ref.shape[1]
            term = dot_nt(a_ref[pl.ds(start, piece), at : at + depth], w_ref[cols, :])
            total = term if total is None else total + term
            at += depth
        return total

    def pass_on(way, shard, p, first):
        start = shard * rows + p * piece

        def tile(i, carry):
            cols = pl.ds(pl.multiple_of(i * 256, 256), 256)
            value = own(start, cols)
            if not first:
                value = value + slots[way, shard * pieces + p, :, cols].astype(F32)
            slots[way, shard * pieces + p, :, cols] = value.astype(BF16)
            return carry

        lax.fori_loop(0, width // 256, tile, 0)
        link(way, shard, p).start()

    for k in range(n - 1):
        for p in range(pieces):
            for way, shard in ((0, n - 1 - k), (1, k)):
                inside = (me < shard) if way == 0 else (me > shard)
                at_end = (me == 0) if way == 0 else (me == n - 1)

                @pl.when(inside & at_end)
                def _():
                    pass_on(way, shard, p, True)

                @pl.when(inside & jnp.logical_not(at_end))
                def _():
                    link(way, shard, p).wait_recv()
                    pass_on(way, shard, p, False)

    for p in range(pieces):
        start = pl.multiple_of(me * rows + p * piece, piece)

        def tile(i, carry):
            cols = pl.ds(pl.multiple_of(i * 256, 256), 256)
            out_ref[p * piece : (p + 1) * piece, cols] = own(start, cols)
            return carry

        lax.fori_loop(0, width // 256, tile, 0)
        for way in (0, 1):

            @pl.when((me > 0) if way == 0 else (me < n - 1))
            def _():
                link(way, me, p).wait_recv()
                out_ref[p * piece : (p + 1) * piece, :] += slots[way, me * pieces + p].astype(F32)

    for k in range(n - 1):
        for p in range(pieces):
            for way, shard in ((0, n - 1 - k), (1, k)):

                @pl.when((me < shard) if way == 0 else (me > shard))
                def _():
                    link(way, shard, p).wait_send()


def scatter_product(left, rights, n, collective_id):
    length = left.shape[0]
    width = rights[0].shape[0]
    rows = length // n
    piece = 128
    parts = len(rights)
    depth = sum(w.shape[1] for w in rights)
    vmem = pl.BlockSpec(memory_space=pltpu.VMEM)
    return pl.pallas_call(
        partial(scatter_kernel, n, parts),
        out_shape=jax.ShapeDtypeStruct((rows, width), F32),
        in_specs=[vmem] * (1 + parts),
        out_specs=vmem,
        scratch_shapes=[
            pltpu.VMEM((2, length // piece, piece, width), BF16),
            pltpu.SemaphoreType.DMA((2, length // piece)),
            pltpu.SemaphoreType.DMA((2, length // piece)),
        ],
        compiler_params=pltpu.CompilerParams(
            collective_id=collective_id, has_side_effects=True, vmem_limit_bytes=60 << 20
        ),
        cost_estimate=pl.CostEstimate(flops=2 * length * width * depth, bytes_accessed=400 << 20, transcendentals=0),
        name="scatter_product",
    )(left, *rights)


def token_table(seg):
    length = seg.shape[0]
    segf = seg.astype(F32)
    columns = []
    for d in (1, 2, 3):
        behind = jnp.concatenate([jnp.full((d,), -1, seg.dtype), seg[:-d]])
        columns.append((behind == seg).astype(F32))
    blocks = seg.reshape(length // T, T)
    last = blocks[:, -1]
    prev = jnp.concatenate([jnp.full((1,), -1, seg.dtype), last[:-1]])
    columns.append(segf)
    columns.append((blocks == prev[:, None]).astype(F32).reshape(length))
    columns.append((blocks == last[:, None]).astype(F32).reshape(length))
    for d in (1, 2, 3):
        ahead = jnp.concatenate([seg[d:], jnp.full((d,), -1, seg.dtype)])
        columns.append((ahead == seg).astype(F32))
    stacked = jnp.stack(columns, axis=1)
    tok = jnp.pad(stacked, ((0, 0), (0, 128 - stacked.shape[1])))
    segr = jnp.broadcast_to(segf.reshape(length // T, 1, T), (length // T, 8, T))
    return tok, segr


def local(
    x_in, target, seg_ids, valid, pre_gain, w_z, w_x, w_bc, w_dt, conv_x_w, conv_x_b,
    conv_bc_w, conv_bc_b, dt_bias, a_log, d_skip, norm_gain, w_out,
):
    rows, _, width = x_in.shape
    channels = w_z.shape[1]
    heads = w_dt.shape[1]
    head_dim = channels // heads
    tp = lax.axis_size("tp")
    inner = channels * tp
    bc_local = w_bc.shape[1]
    x2 = x_in.reshape(rows, width)
    t2 = target.reshape(rows, width)
    inv_rms = lax.rsqrt(jnp.mean(x2 * x2, axis=-1, keepdims=True) + EPS)
    normed = (x2 * inv_rms * pre_gain).astype(BF16)
    w_bc_all = lax.all_gather(w_bc, "tp", axis=1, tiled=True)
    w_bd = jnp.concatenate([w_bc_all, jnp.pad(w_dt, ((0, 0), (0, 128 - heads)))], axis=1)
    wbd = lax.all_gather(w_bd, "dp", axis=0, tiled=True)
    wx = lax.all_gather(w_x, "dp", axis=0, tiled=True)
    wz = lax.all_gather(w_z, "dp", axis=0, tiled=True)
    wo = lax.all_gather(w_out.T, "dp", axis=0, tiled=True)
    normed_all = gather_rows(normed, tp, 0)

    tok, segr = token_table(seg_ids.reshape(-1))
    repeat = lambda v: jnp.repeat(v, head_dim)
    chp = jnp.concatenate(
        [conv_x_w.T, jnp.stack([conv_x_b, repeat(d_skip), norm_gain, jnp.zeros_like(conv_x_b)])], axis=0
    )
    bc_w = lax.all_gather(jnp.concatenate([conv_bc_w.T, conv_bc_b[None]], axis=0), "tp", axis=1, tiled=True)
    bcp = jnp.pad(bc_w, ((0, 3), (0, 0)))
    decay_rate = -jnp.exp(a_log)
    hp = jnp.stack([
        jnp.pad(dt_bias, (0, 128 - heads), constant_values=-9.0),
        jnp.pad(decay_rate, (0, 128 - heads)),
    ])
    hp = jnp.pad(hp, ((0, 6), (0, 0)))

    z, xs, xcv, y, u, bcr, bcv, dtr, bcc, st, sq = forward(normed_all, wz, wx, wbd, tok, segr, chp, bcp, hp)
    sq_all = lax.psum(jnp.sum(sq, axis=-1), "tp")
    rg = lax.rsqrt(sq_all / inner + EPS)
    branch = scatter_product(u, (wo,), tp, 1)
    rg_own = lax.dynamic_slice_in_dim(rg, lax.axis_index("tp") * rows, rows)[:, None]
    branch = branch * rg_own
    layer_out = x2 + branch
    error = layer_out - t2
    mask = valid.reshape(rows, 1).astype(F32)
    d_out = error * mask
    loss_part = jnp.sum(d_out * error)
    count_part = jnp.sum(mask)
    d_branch = d_out.astype(BF16)
    kc_own = jnp.sum(d_branch.astype(F32) * branch, axis=-1) * (rg_own[:, 0] * rg_own[:, 0] / inner)
    db_all = gather_rows(d_branch, tp, 2)
    kc = lax.all_gather(kc_own, "tp", axis=0, tiled=True)
    rk = jnp.pad(jnp.stack([rg, kc], axis=1), ((0, 0), (0, 126)))
    dproj, yn, accc, accb, acch = backward(
        db_all, wo, rk, tok, segr, chp, bcp, hp, z, xs, xcv, y, bcr, bcv, dtr, bcc, st
    )

    def dot_tn(a, b):
        return lax.dot_general(a, b, (((0,), (0,)), ((), ())), preferred_element_type=F32)

    g_out = dot_tn(db_all, yn).astype(BF16)
    g_cat = dot_tn(normed_all, dproj).astype(BF16)
    g_out, g_cat, dproj = lax.optimization_barrier((g_out, g_cat, dproj))
    g_out = lax.psum_scatter(g_out, "dp", scatter_dimension=0, tiled=True).astype(F32)
    g_cat = lax.psum_scatter(g_cat, "dp", scatter_dimension=0, tiled=True).astype(F32)
    d_normed = scatter_product(dproj, (wz, wx, wbd), tp, 3)
    grad_wz, grad_wx = g_cat[:, :channels], g_cat[:, channels : 2 * channels]
    grad_wdt = g_cat[:, 2 * channels + 256 : 2 * channels + 256 + heads]
    grad_wbc = lax.psum_scatter(g_cat[:, 2 * channels : 2 * channels + 256], "tp", scatter_dimension=1, tiled=True)
    accc = lax.psum(jnp.sum(accc, axis=1), "dp")
    acch = lax.psum(jnp.sum(acch, axis=1), "dp")
    accb = lax.psum(jnp.sum(accb, axis=1), ("dp", "tp"))
    accb = lax.dynamic_slice_in_dim(accb, lax.axis_index("tp") * bc_local, bc_local, axis=1)
    gain_part = jnp.sum(d_normed * x2 * inv_rms, axis=0)
    weighted_in = d_normed * pre_gain
    grad_x = d_out + inv_rms * weighted_in - x2 * inv_rms**3 * jnp.mean(weighted_in * x2, axis=-1, keepdims=True)
    loss_sum, count_sum, grad_pre = lax.psum((loss_part, count_part, gain_part), ("dp", "tp"))
    loss = loss_sum / (jnp.maximum(count_sum, 1.0) * width)
    return (
        layer_out.reshape(x_in.shape),
        loss,
        grad_x.reshape(x_in.shape),
        grad_pre,
        grad_wz,
        grad_wx,
        grad_wbc,
        grad_wdt,
        accc[0:4].T,
        accc[4],
        accb[0:4].T,
        accb[4],
        acch[0, :heads],
        acch[1, :heads],
        jnp.sum(accc[6].reshape(heads, head_dim), axis=1),
        accc[5],
        g_out.T,
    )


def solution(mesh):
    tok, col, head = P("tp", "dp", None), P("dp", "tp"), P("tp")
    in_specs = (
        tok, tok, P("dp", None), col, P(), col, col, col, col,
        P("tp", None), head, P("tp", None), head, head, head, head, head, P("tp", "dp"),
    )
    out_specs = (
        tok, P(), tok, P(), col, col, col, col,
        P("tp", None), head, P("tp", None), head, head, head, head, head, P("tp", "dp"),
    )
    return jax.shard_map(local, mesh=mesh, in_specs=in_specs, out_specs=out_specs, check_vma=False)
```

```python
from functools import partial

import jax
import jax.numpy as jnp
from jax import lax
from jax.experimental import pallas as pl
from jax.experimental.pallas import tpu as pltpu
from jax.sharding import PartitionSpec as P

T = 128
TB = 256
EPS = 1e-05
LOG2E = 1.4426950408889634
F32 = jnp.float32
BF16 = jnp.bfloat16
ZT = YT = F32
XT = CT = BF16
HIGHEST = lax.Precision.HIGHEST


def dot(a, b, precision=None):
    return jnp.dot(a, b, preferred_element_type=F32, precision=precision)


def dot_nt(a, b):
    return lax.dot_general(a, b, (((1,), (1,)), ((), ())), preferred_element_type=F32)


def lanes(column_of, index, rows=T):
    return jnp.broadcast_to(column_of[:, index : index + 1], (rows, 128))


def iota(shape, axis):
    return lax.broadcasted_iota(jnp.int32, shape, axis)


def step_sizes(raw, hp_ref):
    shifted = raw + hp_ref[0:1, :]
    dt = jnp.maximum(shifted, 0.0) + jnp.log1p(jnp.exp(-jnp.abs(shifted)))
    la = dt * hp_ref[1:2, :]
    inclusive = (iota((T, T), 0) >= iota((T, T), 1)).astype(F32)
    cum = dot(inclusive, la * LOG2E, HIGHEST)
    return shifted, dt, la, cum


def split_pair(value):
    first = iota((T, 128), 1) < 64
    zero = jnp.zeros_like(value)
    return jnp.concatenate([jnp.where(first, value, zero), jnp.where(first, zero, value)], axis=0)


def fwd_kernel(
    nb_ref, wz_ref, wx_ref, wbd_ref, tok_ref, segr_ref, chp_ref, bcp_ref, hp_ref,
    z_out, xs_out, xcv_out, y_out, u_out, bcr_out, bcv_out, dtr_out, bcc_out, st_out, sq_out,
    zbuf, xbuf, bcbuf, state,
):
    channels = wz_ref.shape[1]
    pairs = channels // 128

    @pl.when(pl.program_id(0) == 0)
    def _():
        state[...] = jnp.zeros_like(state)
        xbuf[0:8, :] = jnp.zeros((8, channels), F32)
        bcbuf[0:8, :] = jnp.zeros((8, 256), F32)

    nb = nb_ref[...]
    for n in range(channels // 256):
        cols = slice(n * 256, n * 256 + 256)
        zbuf[:, cols] = dot(nb, wz_ref[:, cols])
        xbuf[8 : 8 + TB, cols] = dot(nb, wx_ref[:, cols])
    bd = dot(nb, wbd_ref[...])
    bcbuf[8 : 8 + TB, :] = bd[:, :256]
    dtr_out[...] = bd[:, 256:]
    bcr_out[...] = bd[:, :256].astype(BF16)
    first = iota((T, 128), 1) < 64
    for c in range(TB // T):
        r0 = c * T
        rows = slice(r0, r0 + T)
        tok = tok_ref[rows, :]
        masks = [lanes(tok, d) for d in range(3)]
        seg_col, start_b, end_b = lanes(tok, 3), lanes(tok, 4), lanes(tok, 5)
        parts = []
        for half in range(2):
            cols = slice(half * 128, half * 128 + 128)
            acc = bcbuf[8 + r0 : 8 + r0 + T, cols] * bcp_ref[3:4, cols] + bcp_ref[4:5, cols]
            for d in (1, 2, 3):
                acc = acc + bcbuf[8 + r0 - d : 8 + r0 - d + T, cols] * bcp_ref[3 - d : 4 - d, cols] * masks[d - 1]
            bcv_out[rows, cols] = acc.astype(BF16)
            hv = 0.5 * acc
            parts.append((hv + hv * jnp.tanh(hv)).astype(BF16))
            bcc_out[rows, cols] = parts[-1]
        bm, cm = parts
        bt = bm.T
        _, dt, la, cum = step_sizes(dtr_out[rows, :], hp_ref)
        cum_t = cum.T
        scores = dot_nt(cm, bm)
        keep = (seg_col == segr_ref[c, 0:1, :]) & (iota((T, T), 0) >= iota((T, T), 1))
        qm = jnp.where(keep, scores, 0.0)
        sq = jnp.zeros((T, 128), F32)
        st_out[c, :, :] = state[...].astype(BF16)
        for j in range(pairs):
            cols = slice(j * 128, j * 128 + 128)
            acc = xbuf[8 + r0 : 8 + r0 + T, cols] * chp_ref[3:4, cols] + chp_ref[4:5, cols]
            xs_out[rows, cols] = xbuf[8 + r0 : 8 + r0 + T, cols].astype(XT)
            for d in (1, 2, 3):
                acc = acc + xbuf[8 + r0 - d : 8 + r0 - d + T, cols] * chp_ref[3 - d : 4 - d, cols] * masks[d - 1]
            xcv_out[rows, cols] = acc.astype(CT)
            hv = 0.5 * acc
            xc = hv + hv * jnp.tanh(hv)
            dt_e = jnp.where(first, lanes(dt, 2 * j), lanes(dt, 2 * j + 1))
            ca, cb = lanes(cum, 2 * j), lanes(cum, 2 * j + 1)
            cum_e = jnp.where(first, ca, cb)
            xdt = xc * dt_e
            ea = jnp.exp2(jnp.minimum(ca - cum_t[2 * j : 2 * j + 1, :], 0.0))
            eb = jnp.exp2(jnp.minimum(cb - cum_t[2 * j + 1 : 2 * j + 2, :], 0.0))
            mix = jnp.concatenate([(ea * qm).astype(BF16), (eb * qm).astype(BF16)], axis=1)
            y = dot(mix, split_pair(xdt.astype(BF16)))
            into = jnp.exp2(cum_e) * start_b
            last = cum_e[T - 1 : T, :]
            to_end = jnp.exp2(last - cum_e) * end_b
            y = y + into * dot(cm, st_out[c, :, cols])
            state[:, cols] = state[:, cols] * into[T - 1 : T, :] + dot(bt, (xdt * to_end).astype(BF16))
            y = y + chp_ref[5:6, cols] * xc
            y_out[rows, cols] = y.astype(YT)
            zz = zbuf[rows, cols]
            z_out[rows, cols] = zz.astype(ZT)
            hz = 0.5 * zz
            g = y * (hz + hz * jnp.tanh(hz))
            sq = sq + g * g
            u_out[rows, cols] = (g * chp_ref[6:7, cols]).astype(BF16)
        sq_out[c, :, :] = lax.dot_general(
            jnp.ones((8, 128), F32), sq, (((1,), (1,)), ((), ())), preferred_element_type=F32, precision=HIGHEST
        )
    xbuf[0:8, :] = xbuf[TB : TB + 8, :]
    bcbuf[0:8, :] = bcbuf[TB : TB + 8, :]


def eye():
    return iota((T, T), 0) == iota((T, T), 1)


def column(row):
    return jnp.sum(jnp.where(eye(), jnp.broadcast_to(row, (T, T)), 0.0), axis=1, keepdims=True)


def row(col):
    return jnp.sum(jnp.where(eye(), jnp.broadcast_to(col, (T, T)), 0.0), axis=0, keepdims=True)


def row_sums(value):
    return jnp.sum(value.reshape(value.shape[0] // 8, 8, value.shape[1]), axis=0)


def bwd_kernel(
    db_ref, wo_ref, rk_ref, tok_ref, segr_ref, chp_ref, bcp_ref, hp_ref,
    z_ref, xs_ref, xcv_ref, y_ref, bcr_ref, bcv_ref, dtr_ref, bcc_ref, st_ref,
    dproj_out, yn_out, accc_out, accb_out, acch_out,
    dyn, dbuf, dbcbuf, dstate, dstate_b, dyec, xte, cs_rows, fold, pick,
):
    channels = wo_ref.shape[1]
    pairs = channels // 128

    @pl.when(pl.program_id(0) == 0)
    def _():
        dstate[...] = jnp.zeros_like(dstate)
        dbuf[...] = jnp.zeros_like(dbuf)
        dbcbuf[...] = jnp.zeros_like(dbcbuf)
        accc_out[...] = jnp.zeros_like(accc_out)
        accb_out[...] = jnp.zeros_like(accb_out)
        acch_out[...] = jnp.zeros_like(acch_out)
        cs_rows[...] = jnp.zeros_like(cs_rows)
        for j in range(pairs):
            half = (iota((128, 128), 0) >= 64).astype(jnp.int32)
            fold[j, :, :] = (iota((128, 128), 1) == 2 * j + half).astype(F32).astype(BF16)
            part = (iota((256, 128), 0) >= 128).astype(jnp.int32)
            pick[j, :, :] = (iota((256, 128), 1) == 2 * j + part).astype(F32).astype(BF16)

    db = db_ref[...]
    for n in range(channels // 256):
        cols = slice(n * 256, n * 256 + 256)
        dyn[:, cols] = dot(db, wo_ref[:, cols])
    first = iota((T, 128), 1) < 64
    for c in reversed(range(TB // T)):
        r0 = c * T
        rows = slice(r0, r0 + T)
        tok = tok_ref[rows, :]
        seg_col, start_b, end_b = lanes(tok, 3), lanes(tok, 4), lanes(tok, 5)
        ahead = [lanes(tok, 6 + d) for d in range(3)]
        rg_b = jnp.broadcast_to(column(rk_ref[c, 0:1, :]), (T, 128))
        kc_b = jnp.broadcast_to(column(rk_ref[c, 1:2, :]), (T, 128))
        bm, cm = bcc_ref[rows, 0:128], bcc_ref[rows, 128:256]
        ct = cm.T
        shifted, dt, la, cum = step_sizes(dtr_ref[rows, :], hp_ref)
        cum_t = cum.T
        scores, scores_t = dot_nt(cm, bm), dot_nt(bm, cm)
        same = seg_col == segr_ref[c, 0:1, :]
        below = iota((T, T), 0) >= iota((T, T), 1)
        strict = iota((T, T), 0) > iota((T, T), 1)
        above = iota((T, T), 0) <= iota((T, T), 1)
        qs = jnp.where(same & strict, scores, 0.0)
        qt = jnp.where(same & above, scores_t, 0.0)
        dstate_b[...] = dstate[...].astype(BF16)
        dq = jnp.zeros((T, T), F32)
        rsum = jnp.zeros((T, 128), F32)
        ddt = jnp.zeros((T, 128), F32)
        xsum = jnp.zeros((T, 128), F32)
        ksum = jnp.zeros((16, 128), F32)
        for j in range(pairs):
            cols = slice(j * 128, j * 128 + 128)
            zz = z_ref[rows, cols].astype(F32)
            y = y_ref[rows, cols].astype(F32)
            sz = 0.5 + 0.5 * jnp.tanh(0.5 * zz)
            silu_z = zz * sz
            dsz = sz + silu_z * (1.0 - sz)
            g = y * silu_z
            gr = g * rg_b
            gain = chp_ref[6:7, cols]
            dynp = dyn[rows, cols]
            yn_out[rows, cols] = (gr * gain).astype(BF16)
            accc_out[5, :, cols] += row_sums(dynp * gr)
            dg = rg_b * dynp * gain - g * kc_b
            dy = dg * silu_z
            dproj_out[rows, cols] = (dg * y * dsz).astype(BF16)
            xcv = xcv_ref[rows, cols].astype(F32)
            sx = 0.5 + 0.5 * jnp.tanh(0.5 * xcv)
            xc = xcv * sx
            dsx = sx + xc * (1.0 - sx)
            accc_out[6, :, cols] += row_sums(dy * xc)
            dt_e = jnp.where(first, lanes(dt, 2 * j), lanes(dt, 2 * j + 1))
            ca, cb = lanes(cum, 2 * j), lanes(cum, 2 * j + 1)
            cum_e = jnp.where(first, ca, cb)
            into = jnp.exp2(cum_e) * start_b
            to_end = jnp.exp2(cum_e[T - 1 : T, :] - cum_e) * end_b
            decay = into[T - 1 : T, :]
            xdt = xc * dt_e
            dy_b = dy.astype(BF16)
            ga = ca - cum_t[2 * j : 2 * j + 1, :]
            gb = cb - cum_t[2 * j + 1 : 2 * j + 2, :]
            grad = dot_nt(dy_b, split_pair(xdt.astype(BF16)))
            gea = grad[:, :128] * jnp.exp2(jnp.minimum(ga, 0.0))
            geb = grad[:, 128:] * jnp.exp2(jnp.minimum(gb, 0.0))
            dq = dq + gea + geb
            pp = jnp.concatenate([(gea * qs).astype(BF16), (geb * qs).astype(BF16)], axis=1)
            rsum = rsum + dot(pp, pick[j, :, :])
            csum = dot(jnp.ones((8, T), BF16), pp)
            cs_rows[2 * j : 2 * j + 1, :] = csum[0:1, :128]
            cs_rows[2 * j + 1 : 2 * j + 2, :] = csum[0:1, 128:]
            eta = (jnp.exp2(jnp.minimum(-ga, 0.0)) * qt).astype(BF16)
            etb = (jnp.exp2(jnp.minimum(-gb, 0.0)) * qt).astype(BF16)
            dxdt = dot(jnp.concatenate([eta, etb], axis=1), split_pair(dy_b))
            dx_state = to_end * dot(bm, dstate_b[:, cols])
            dxdt = dxdt + dx_state
            y_in = into * dot(cm, st_ref[c, :, cols])
            dyec_p = (dy * into).astype(BF16)
            dyec[:, cols] = dyec_p
            xte[:, cols] = (xdt * to_end).astype(BF16)
            ddt = ddt + dot((xc * dxdt).astype(BF16), fold[j, :, :])
            rsum = rsum + dot((dy * y_in).astype(BF16), fold[j, :, :])
            xsum = xsum + dot((xdt * dx_state).astype(BF16), fold[j, :, :])
            old = dstate[:, cols]
            kpart = row_sums(old * st_ref[c, :, cols].astype(F32)) * decay
            khigh = kpart.astype(BF16)
            klow = (kpart - khigh.astype(F32)).astype(BF16)
            ksum = ksum + dot(jnp.concatenate([khigh, klow], axis=0), fold[j, :, :])
            dstate[:, cols] = old * decay + dot(ct, dyec_p)
            dxcv = (dxdt * dt_e + chp_ref[5:6, cols] * dy) * dsx
            dbuf[0:T, cols] = dxcv
            xs = xs_ref[rows, cols].astype(F32)
            dxs = dxcv * chp_ref[3:4, cols]
            accc_out[4, :, cols] += row_sums(dxcv)
            accc_out[3, :, cols] += row_sums(dxcv * xs)
            for d in (1, 2, 3):
                moved = dbuf[d : d + T, cols] * ahead[d - 1]
                dxs = dxs + moved * chp_ref[3 - d : 4 - d, cols]
                accc_out[3 - d, :, cols] += row_sums(moved * xs)
            dproj_out[rows, channels + j * 128 : channels + j * 128 + 128] = dxs.astype(BF16)
        dbuf[T : T + 8, :] = dbuf[0:8, :]
        dqm = jnp.where(same & below, dq, 0.0)
        dc = dot(dqm.astype(BF16), bm) + dot_nt(dyec[...], st_ref[c, :, :])
        db_rows = dot(dqm.T.astype(BF16), cm) + dot_nt(xte[...], dstate_b[...])
        for half, grad_half in enumerate((db_rows, dc)):
            cols = slice(half * 128, half * 128 + 128)
            raw = bcv_ref[rows, cols].astype(F32)
            sb = 0.5 + 0.5 * jnp.tanh(0.5 * raw)
            dcv = grad_half * (sb + raw * sb * (1.0 - sb))
            dbcbuf[0:T, cols] = dcv
            xs = bcr_ref[rows, cols].astype(F32)
            dxs = dcv * bcp_ref[3:4, cols]
            accb_out[4, :, cols] += row_sums(dcv)
            accb_out[3, :, cols] += row_sums(dcv * xs)
            for d in (1, 2, 3):
                moved = dbcbuf[d : d + T, cols] * ahead[d - 1]
                dxs = dxs + moved * bcp_ref[3 - d : 4 - d, cols]
                accb_out[3 - d, :, cols] += row_sums(moved * xs)
            dproj_out[rows, 2 * channels + half * 128 : 2 * channels + half * 128 + 128] = dxs.astype(BF16)
        dbcbuf[T : T + 8, :] = dbcbuf[0:8, :]
        after = (iota((T, T), 0) <= iota((T, T), 1)).astype(F32)
        before = (iota((T, T), 0) > iota((T, T), 1)).astype(F32)
        dla = dot(after, rsum - cs_rows[...].T, HIGHEST) + dot(before, xsum, HIGHEST)
        dla = dla + jnp.sum(ksum, axis=0, keepdims=True)
        ddtr = (ddt + dla * hp_ref[1:2, :]) * (0.5 + 0.5 * jnp.tanh(0.5 * shifted))
        acch_out[0, :, :] += row_sums(ddtr)
        acch_out[1, :, :] += row_sums(dla * la)
        dproj_out[rows, 2 * channels + 256 : 2 * channels + 384] = ddtr.astype(BF16)


def forward(normed, wz, wx, wbd, tok, segr, chp, bcp, hp):
    length, width = normed.shape
    channels = wz.shape[1]
    grid = length // TB
    once = dict(pipeline_mode=pl.Buffered(1))

    def block(cols):
        return pl.BlockSpec((TB, cols), lambda i: (i, 0))

    def whole(array):
        return pl.BlockSpec(array.shape, lambda i: (0,) * array.ndim, **once)

    chunk3 = pl.BlockSpec((TB // T, 8, 128), lambda i: (i, 0, 0))
    outs = [
        (channels, ZT), (channels, XT), (channels, CT), (channels, YT), (channels, BF16),
        (256, BF16), (256, BF16), (128, F32), (256, BF16), None, "rows",
    ]
    out_shape, out_specs = [], []
    for item in outs:
        if item is None:
            out_shape.append(jax.ShapeDtypeStruct((length // T, 128, channels), BF16))
            out_specs.append(pl.BlockSpec((TB // T, 128, channels), lambda i: (i, 0, 0)))
        elif item == "rows":
            out_shape.append(jax.ShapeDtypeStruct((length // T, 8, 128), F32))
            out_specs.append(chunk3)
        else:
            out_shape.append(jax.ShapeDtypeStruct((length, item[0]), item[1]))
            out_specs.append(block(item[0]))
    return pl.pallas_call(
        fwd_kernel,
        grid=(grid,),
        in_specs=[block(width), whole(wz), whole(wx), whole(wbd), block(128), chunk3, whole(chp), whole(bcp), whole(hp)],
        out_specs=out_specs,
        out_shape=out_shape,
        scratch_shapes=[
            pltpu.VMEM((TB, channels), F32),
            pltpu.VMEM((TB + 8, channels), F32),
            pltpu.VMEM((TB + 8, 256), F32),
            pltpu.VMEM((128, channels), F32),
        ],
        compiler_params=pltpu.CompilerParams(vmem_limit_bytes=56 << 20),
        name="ssd_forward",
    )(normed, wz, wx, wbd, tok, segr, chp, bcp, hp)


def backward(db, wo, rk, tok, segr, chp, bcp, hp, z, xs, xcv, y, bcr, bcv, dtr, bcc, st):
    length, width = db.shape
    channels = wo.shape[1]
    pairs = channels // 128
    grid = length // TB
    once = dict(pipeline_mode=pl.Buffered(1))

    def block(cols):
        return pl.BlockSpec((TB, cols), lambda i: (grid - 1 - i, 0))

    def whole(shape):
        return pl.BlockSpec(shape, lambda i: (0,) * len(shape), **once)

    chunk3 = pl.BlockSpec((TB // T, 8, 128), lambda i: (grid - 1 - i, 0, 0))
    states = pl.BlockSpec((TB // T, 128, channels), lambda i: (grid - 1 - i, 0, 0))
    total = 2 * channels + 384
    return pl.pallas_call(
        bwd_kernel,
        grid=(grid,),
        in_specs=[
            block(width), whole(wo.shape), chunk3, block(128), chunk3,
            whole(chp.shape), whole(bcp.shape), whole(hp.shape),
            block(channels), block(channels), block(channels), block(channels),
            block(256), block(256), block(128), block(256), states,
        ],
        out_specs=[
            block(total), block(channels),
            pl.BlockSpec((7, 8, channels), lambda i: (0, 0, 0)),
            pl.BlockSpec((5, 8, 256), lambda i: (0, 0, 0)),
            pl.BlockSpec((2, 8, 128), lambda i: (0, 0, 0)),
        ],
        out_shape=[
            jax.ShapeDtypeStruct((length, total), BF16),
            jax.ShapeDtypeStruct((length, channels), BF16),
            jax.ShapeDtypeStruct((7, 8, channels), F32),
            jax.ShapeDtypeStruct((5, 8, 256), F32),
            jax.ShapeDtypeStruct((2, 8, 128), F32),
        ],
        scratch_shapes=[
            pltpu.VMEM((TB, channels), F32),
            pltpu.VMEM((T + 8, channels), F32),
            pltpu.VMEM((T + 8, 256), F32),
            pltpu.VMEM((128, channels), F32),
            pltpu.VMEM((128, channels), BF16),
            pltpu.VMEM((T, channels), BF16),
            pltpu.VMEM((T, channels), BF16),
            pltpu.VMEM((128, 128), F32),
            pltpu.VMEM((pairs, 128, 128), BF16),
            pltpu.VMEM((pairs, 256, 128), BF16),
        ],
        compiler_params=pltpu.CompilerParams(vmem_limit_bytes=56 << 20),
        name="ssd_backward",
    )(db, wo, rk, tok, segr, chp, bcp, hp, z, xs, xcv, y, bcr, bcv, dtr, bcc, st)


MESH_ID = pl.DeviceIdType.MESH


def meet(n, axis):
    me = lax.axis_index(axis)
    barrier = pltpu.get_barrier_semaphore()
    for peer in range(n):

        @pl.when(me != peer)
        def _():
            pl.semaphore_signal(barrier, inc=1, device_id={axis: peer}, device_id_type=MESH_ID)

    pl.semaphore_wait(barrier, n - 1)
    return me


def to_peer(source, target, send_sem, recv_sem, axis, peer):
    return pltpu.make_async_remote_copy(
        src_ref=source, dst_ref=target, send_sem=send_sem, recv_sem=recv_sem,
        device_id={axis: peer}, device_id_type=MESH_ID,
    )


def share_kernel(n, count, *refs):
    ins, outs = refs[:count], refs[count : 2 * count]
    send_sem, recv_sem = refs[2 * count :]
    me = meet(n, "tp")
    for i in range(count):
        for peer in range(n):

            @pl.when(me != peer)
            def _():
                to_peer(ins[i], outs[i].at[me], send_sem.at[i, peer], recv_sem.at[i, me], "tp", peer).start()

        outs[i][pl.ds(me, 1)] = ins[i][...][None]
    for i in range(count):
        for peer in range(n):

            @pl.when(me != peer)
            def _():
                to_peer(ins[i], outs[i].at[peer], send_sem.at[i, peer], recv_sem.at[i, peer], "tp", peer).wait_recv()
                to_peer(ins[i], outs[i].at[me], send_sem.at[i, peer], recv_sem.at[i, me], "tp", peer).wait_send()


def share(arrays, n, collective_id):
    vmem = pl.BlockSpec(memory_space=pltpu.VMEM)
    count = len(arrays)
    return pl.pallas_call(
        partial(share_kernel, n, count),
        out_shape=[jax.ShapeDtypeStruct((n,) + a.shape, a.dtype) for a in arrays],
        in_specs=[vmem] * count,
        out_specs=[vmem] * count,
        scratch_shapes=[pltpu.SemaphoreType.DMA((count, n)), pltpu.SemaphoreType.DMA((count, n))],
        compiler_params=pltpu.CompilerParams(collective_id=collective_id, has_side_effects=True),
        name="share",
    )(*arrays)


def finish_kernel(dp, tp, mine, both, cols, mine_out, both_out, cols_out, got, got_both, got_cols, sems):
    me_dp, me_tp = lax.axis_index("dp"), lax.axis_index("tp")
    barrier = pltpu.get_barrier_semaphore()
    for peer in range(dp):

        @pl.when(me_dp != peer)
        def _():
            pl.semaphore_signal(barrier, inc=1, device_id={"dp": peer}, device_id_type=MESH_ID)

    for peer in range(tp):

        @pl.when(me_tp != peer)
        def _():
            pl.semaphore_signal(barrier, inc=1, device_id={"tp": peer}, device_id_type=MESH_ID)

    pl.semaphore_wait(barrier, dp - 1 + tp - 1)
    first = mine.shape[0]
    got[pl.ds(me_dp, 1), 0:first, :] = mine[...][None]
    got[pl.ds(me_dp, 1), first:, :] = both[...][None]

    def over_dp(peer, slot):
        return to_peer(got.at[me_dp], got.at[slot], sems.at[0, peer], sems.at[1, slot], "dp", peer)

    def over_tp(peer, slot):
        return to_peer(got_both.at[me_tp], got_both.at[slot], sems.at[2, peer], sems.at[3, slot], "tp", peer)

    def over_cols(peer, slot):
        return to_peer(cols.at[peer], got_cols.at[slot], sems.at[4, peer], sems.at[5, slot], "tp", peer)

    for peer in range(dp):

        @pl.when(me_dp != peer)
        def _():
            over_dp(peer, me_dp).start()

    for peer in range(tp):

        @pl.when(me_tp != peer)
        def _():
            over_cols(peer, me_tp).start()

    got_cols[pl.ds(me_tp, 1)] = cols[pl.ds(me_tp, 1)]
    for peer in range(dp):

        @pl.when(me_dp != peer)
        def _():
            over_dp(peer, peer).wait_recv()

    total = got[0]
    for peer in range(1, dp):
        total = total + got[peer]
    mine_out[...] = total[:first]
    got_both[pl.ds(me_tp, 1)] = total[first:][None]
    for peer in range(tp):

        @pl.when(me_tp != peer)
        def _():
            over_tp(peer, me_tp).start()

    for peer in range(tp):

        @pl.when(me_tp != peer)
        def _():
            over_cols(peer, peer).wait_recv()
            over_tp(peer, peer).wait_recv()

    total, columns = got_both[0], got_cols[0]
    for peer in range(1, tp):
        total, columns = total + got_both[peer], columns + got_cols[peer]
    both_out[...] = total
    cols_out[...] = columns
    for peer in range(dp):

        @pl.when(me_dp != peer)
        def _():
            over_dp(peer, me_dp).wait_send()

    for peer in range(tp):

        @pl.when(me_tp != peer)
        def _():
            over_cols(peer, me_tp).wait_send()
            over_tp(peer, me_tp).wait_send()


def finish(mine, both, cols, dp, tp, collective_id):
    vmem = pl.BlockSpec(memory_space=pltpu.VMEM)
    rows = mine.shape[0] + both.shape[0]
    return pl.pallas_call(
        partial(finish_kernel, dp, tp),
        out_shape=[
            jax.ShapeDtypeStruct(mine.shape, F32),
            jax.ShapeDtypeStruct(both.shape, F32),
            jax.ShapeDtypeStruct(cols.shape[1:], F32),
        ],
        in_specs=[vmem] * 3,
        out_specs=[vmem] * 3,
        scratch_shapes=[
            pltpu.VMEM((dp, rows, 128), F32),
            pltpu.VMEM((tp,) + both.shape, F32),
            pltpu.VMEM(cols.shape, F32),
            pltpu.SemaphoreType.DMA((6, max(dp, tp))),
        ],
        compiler_params=pltpu.CompilerParams(collective_id=collective_id, has_side_effects=True),
        name="finish",
    )(mine, both, cols)


def gather_kernel(n, pieces, extra, *refs):
    if extra:
        x_ref, e_ref, out_ref, eo_ref, local_sem, send_sem, recv_sem, es_sem, er_sem = refs
    else:
        x_ref, out_ref, local_sem, send_sem, recv_sem = refs
    rows = x_ref.shape[0]
    piece = rows // pieces
    me = meet(n, "tp")

    def place(owner, p):
        return out_ref.at[pl.ds(pl.multiple_of(owner * rows + p * piece, piece), piece)]

    def outgoing(way, step, p):
        owner = me - step if way == 0 else me + step
        source = x_ref.at[pl.ds(p * piece, piece)] if step == 0 else place(owner, p)
        peer = me + 1 if way == 0 else me - 1
        return to_peer(source, place(owner, p), send_sem.at[way, step, p], recv_sem.at[way, step, p], "tp", peer)

    def incoming(way, step, p):
        owner = me - 1 - step if way == 0 else me + 1 + step
        peer = me - 1 if way == 0 else me + 1
        return to_peer(place(owner, p), place(owner, p), send_sem.at[way, step, p], recv_sem.at[way, step, p], "tp", peer)

    def sends(way, step):
        if way == 0:
            return (me - step >= 0) & (me < n - 1)
        return (me + step <= n - 1) & (me > 0)

    def receives(way, step):
        return me - 1 - step >= 0 if way == 0 else me + 1 + step <= n - 1

    keep = pltpu.make_async_copy(x_ref, out_ref.at[pl.ds(pl.multiple_of(me * rows, rows), rows)], local_sem.at[0])
    if extra:
        count = e_ref.shape[0]

        def extra_to(peer, owner):
            there = eo_ref.at[pl.ds(owner * count, count)]
            return to_peer(e_ref, there, es_sem.at[peer], er_sem.at[owner], "tp", peer)

        keep_extra = pltpu.make_async_copy(e_ref, eo_ref.at[pl.ds(me * count, count)], local_sem.at[1])
        keep_extra.start()
        for peer in range(n):

            @pl.when(me != peer)
            def _():
                extra_to(peer, me).start()

    for step in range(n):
        for p in range(pieces):
            for way in (0, 1):
                if step > 0:

                    @pl.when(receives(way, step - 1))
                    def _():
                        incoming(way, step - 1, p).wait_recv()

                if step < n - 1:

                    @pl.when(sends(way, step))
                    def _():
                        outgoing(way, step, p).start()

        if step == 0:
            keep.start()

    for step in range(n - 1):
        for p in range(pieces):
            for way in (0, 1):

                @pl.when(sends(way, step))
                def _():
                    outgoing(way, step, p).wait_send()

    keep.wait()
    if extra:
        keep_extra.wait()
        for peer in range(n):

            @pl.when(me != peer)
            def _():
                extra_to(peer, me).wait_send()
                extra_to(peer, peer).wait_recv()


def gather_rows(x, n, collective_id, extra=None):
    rows, width = x.shape
    pieces = 4
    anywhere = pl.BlockSpec(memory_space=pl.ANY)
    out_shape = [jax.ShapeDtypeStruct((n * rows, width), x.dtype)]
    scratch = [
        pltpu.SemaphoreType.DMA((2,)),
        pltpu.SemaphoreType.DMA((2, n - 1, pieces)),
        pltpu.SemaphoreType.DMA((2, n - 1, pieces)),
    ]
    operands = [x]
    if extra is not None:
        operands.append(extra)
        out_shape.append(jax.ShapeDtypeStruct((n * extra.shape[0],) + extra.shape[1:], extra.dtype))
        scratch += [pltpu.SemaphoreType.DMA((n,)), pltpu.SemaphoreType.DMA((n,))]
    return pl.pallas_call(
        partial(gather_kernel, n, pieces, extra is not None),
        out_shape=out_shape,
        in_specs=[anywhere] * len(operands),
        out_specs=[anywhere] * len(operands),
        scratch_shapes=scratch,
        compiler_params=pltpu.CompilerParams(collective_id=collective_id, has_side_effects=True),
        cost_estimate=pl.CostEstimate(flops=0, bytes_accessed=400 << 20, transcendentals=0),
        name="gather_rows",
    )(*operands)


def scatter_body(n, me, a_ref, right_refs, acc, part, slots, send_sem, recv_sem):
    rows, width = acc.shape
    group = part.shape[0]
    piece = slots.shape[2]
    pieces = rows // piece
    groups = rows // group
    subs = group // piece

    def link(way, index):
        peer = me + 1 if way == 0 else me - 1
        return to_peer(
            slots.at[way, index], slots.at[way, index], send_sem.at[way, index], recv_sem.at[way, index], "tp", peer
        )

    def own(start, target, base):
        def tile(i, carry):
            cols = pl.ds(pl.multiple_of(i * 256, 256), 256)
            total, at = None, 0
            for w_ref in right_refs:
                depth = w_ref.shape[1]
                term = dot_nt(a_ref[pl.ds(start, group), at : at + depth], w_ref[cols, :])
                total = term if total is None else total + term
                at += depth
            target[pl.ds(base, group), cols] = total
            return carry

        lax.fori_loop(0, width // 256, tile, 0)

    def pass_on(way, q, at_end):
        shard = n - 1 - q // groups if way == 0 else q // groups
        start = pl.multiple_of(shard * rows + (q % groups) * group, group)
        own(start, part, 0)
        for sub in range(subs):
            index = shard * pieces + (q % groups) * subs + sub
            here = slice(sub * piece, (sub + 1) * piece)

            @pl.when(at_end)
            def _():
                slots[way, index] = part[here, :].astype(BF16)

            @pl.when(jnp.logical_not(at_end))
            def _():
                link(way, index).wait_recv()
                slots[way, index] = (part[here, :] + slots[way, index].astype(F32)).astype(BF16)

            link(way, index).start()

    def turn(t, carry):
        for way in (0, 1):
            hops = me if way == 0 else n - 1 - me
            q = t - hops

            @pl.when((q >= 0) & (q < (n - 1 - hops) * groups))
            def _():
                pass_on(way, q, hops == 0)

        late = t - (n - 1)

        @pl.when((late >= 0) & (late < groups))
        def _():
            base = pl.multiple_of(late * group, group)
            own(pl.multiple_of(me * rows + late * group, group), acc, base)

        return carry

    lax.fori_loop(0, (n - 1) * groups + n - 1, turn, 0)

    def arrived(p):
        for way in (0, 1):

            @pl.when((me > 0) if way == 0 else (me < n - 1))
            def _():
                link(way, me * pieces + p).wait_recv()
                here = pl.ds(pl.multiple_of(p * piece, piece), piece)
                acc[here, :] += slots[way, me * pieces + p].astype(F32)

    def drain():
        def done(index, carry):
            shard = index // pieces
            for way in (0, 1):

                @pl.when((me < shard) if way == 0 else (me > shard))
                def _():
                    link(way, index).wait_send()

            return carry

        lax.fori_loop(0, n * pieces, done, 0)

    return arrived, drain


def branch_kernel(
    n, inner, a_ref, w_ref, sq_ref, x_ref, t_ref, v_ref,
    lo_out, do_out, db_out, rk_out, loss_out,
    acc, part, slots, sqs, send_sem, recv_sem, qs_sem, qr_sem,
):
    me = meet(n, "tp")
    rows, width = acc.shape
    pieces = rows // T
    tiles = width // 128

    def squares_to(peer, slot):
        return to_peer(sq_ref.at[pl.ds(peer * pieces, pieces)], sqs.at[slot], qs_sem.at[peer], qr_sem.at[slot], "tp", peer)

    for peer in range(n):

        @pl.when(me != peer)
        def _():
            squares_to(peer, me).start()

    sqs[pl.ds(me, 1)] = sq_ref[pl.ds(me * pieces, pieces)][None]
    arrived, drain = scatter_body(n, me, a_ref, (w_ref,), acc, part, slots, send_sem, recv_sem)
    for peer in range(n):

        @pl.when(me != peer)
        def _():
            squares_to(peer, peer).wait_recv()

    loss_out[...] = jnp.zeros_like(loss_out)

    def last(p, carry):
        arrived(p)
        total = sqs[0, p]
        for peer in range(1, n):
            total = total + sqs[peer, p]
        rg_row = lax.rsqrt(total / inner + EPS)
        rg_b = jnp.broadcast_to(column(rg_row[0:1, :]), (T, 128))
        mask_b = jnp.broadcast_to(column(v_ref[p, 0:1, :]), (T, 128))
        here = pl.ds(pl.multiple_of(p * T, T), T)
        dots = jnp.zeros((T, 128), F32)
        lost = jnp.zeros((T, 128), F32)
        for c in range(tiles):
            cols = slice(c * 128, c * 128 + 128)
            view = pl.ds(p * (T * tiles) + c, T, stride=tiles)
            branch = acc[here, cols] * rg_b
            lo = x_ref[view, :] + branch
            lo_out[view, :] = lo
            error = lo - t_ref[view, :]
            d_out = error * mask_b
            do_out[here, cols] = d_out
            d_branch = d_out.astype(BF16)
            db_out[here, cols] = d_branch
            lost = lost + d_out * error
            dots = dots + d_branch.astype(F32) * branch
        loss_out[0:8, :] += row_sums(lost)
        loss_out[8:9, :] += v_ref[p, 0:1, :]
        coefficient = jnp.sum(dots, axis=1, keepdims=True)
        rk_out[p, 0:1, :] = rg_row[0:1, :]
        rk_out[p, 1:2, :] = row(coefficient) * rg_row[0:1, :] * rg_row[0:1, :] / inner
        rk_out[p, 2:8, :] = jnp.zeros((6, 128), F32)
        return carry

    lax.fori_loop(0, pieces, last, 0)
    drain()
    for peer in range(n):

        @pl.when(me != peer)
        def _():
            squares_to(peer, me).wait_send()


def scatter_scratch(length, rows, width):
    return [
        pltpu.VMEM((rows, width), F32),
        pltpu.VMEM((min(rows, 256), width), F32),
        pltpu.VMEM((2, length // T, T, width), BF16),
    ], [
        pltpu.SemaphoreType.DMA((2, length // T)),
        pltpu.SemaphoreType.DMA((2, length // T)),
    ]


def branch_stage(u, wo, sq, x_view, t_view, v_rows, n, inner, collective_id):
    length, width = u.shape[0], wo.shape[0]
    rows = length // n
    vmem = pl.BlockSpec(memory_space=pltpu.VMEM)
    buffers, sems = scatter_scratch(length, rows, width)
    return pl.pallas_call(
        partial(branch_kernel, n, inner),
        out_shape=[
            jax.ShapeDtypeStruct(x_view.shape, F32),
            jax.ShapeDtypeStruct((rows, width), F32),
            jax.ShapeDtypeStruct((rows, width), BF16),
            jax.ShapeDtypeStruct((rows // T, 8, 128), F32),
            jax.ShapeDtypeStruct((16, 128), F32),
        ],
        in_specs=[vmem] * 6,
        out_specs=[vmem] * 5,
        scratch_shapes=buffers
        + [pltpu.VMEM((n, rows // T, 8, 128), F32)]
        + sems
        + [pltpu.SemaphoreType.DMA((n,)), pltpu.SemaphoreType.DMA((n,))],
        compiler_params=pltpu.CompilerParams(
            collective_id=collective_id, has_side_effects=True, vmem_limit_bytes=60 << 20
        ),
        cost_estimate=pl.CostEstimate(
            flops=2 * length * width * u.shape[1], bytes_accessed=400 << 20, transcendentals=0
        ),
        name="branch_stage",
    )(u, wo, sq, x_view, t_view, v_rows)


def input_kernel(
    n, parts, a_ref, *refs,
):
    right_refs = refs[:parts]
    x_ref, do_ref, pg_ref, gx_out, gp_out, acc, part, slots, send_sem, recv_sem = refs[parts:]
    me = meet(n, "tp")
    rows, width = acc.shape
    tiles = width // 128
    arrived, drain = scatter_body(n, me, a_ref, right_refs, acc, part, slots, send_sem, recv_sem)
    gp_out[...] = jnp.zeros_like(gp_out)

    def last(p, carry):
        arrived(p)
        here = pl.ds(pl.multiple_of(p * T, T), T)
        squares = jnp.zeros((T, 128), F32)
        dots = jnp.zeros((T, 128), F32)
        for c in range(tiles):
            cols = slice(c * 128, c * 128 + 128)
            xt = x_ref[pl.ds(p * (T * tiles) + c, T, stride=tiles), :]
            squares = squares + xt * xt
            dots = dots + acc[here, cols] * pg_ref[0:1, cols] * xt
        inv = lax.rsqrt(jnp.sum(squares, axis=1, keepdims=True) / width + EPS)
        inv_b = jnp.broadcast_to(inv, (T, 128))
        mean = jnp.sum(dots, axis=1, keepdims=True) / width
        back_b = jnp.broadcast_to(inv * inv * inv * mean, (T, 128))
        for c in range(tiles):
            cols = slice(c * 128, c * 128 + 128)
            view = pl.ds(p * (T * tiles) + c, T, stride=tiles)
            xt = x_ref[view, :]
            scaled = acc[here, cols] * inv_b
            gx_out[view, :] = do_ref[here, cols] + scaled * pg_ref[0:1, cols] - xt * back_b
            gp_out[:, cols] += row_sums(scaled * xt)
        return carry

    lax.fori_loop(0, rows // T, last, 0)
    drain()


def input_stage(dproj, weights, x_view, d_out, pg, n, collective_id):
    length, width = dproj.shape[0], weights[0].shape[0]
    rows = length // n
    vmem = pl.BlockSpec(memory_space=pltpu.VMEM)
    buffers, sems = scatter_scratch(length, rows, width)
    return pl.pallas_call(
        partial(input_kernel, n, len(weights)),
        out_shape=[jax.ShapeDtypeStruct(x_view.shape, F32), jax.ShapeDtypeStruct((8, width), F32)],
        in_specs=[vmem] * (4 + len(weights)),
        out_specs=[vmem] * 2,
        scratch_shapes=buffers + sems,
        compiler_params=pltpu.CompilerParams(
            collective_id=collective_id, has_side_effects=True, vmem_limit_bytes=62 << 20
        ),
        cost_estimate=pl.CostEstimate(
            flops=2 * length * width * dproj.shape[1], bytes_accessed=400 << 20, transcendentals=0
        ),
        name="input_stage",
    )(dproj, *weights, x_view, d_out, pg)


def token_table(seg):
    length = seg.shape[0]
    segf = seg.astype(F32)
    columns = []
    for d in (1, 2, 3):
        behind = jnp.concatenate([jnp.full((d,), -1, seg.dtype), seg[:-d]])
        columns.append((behind == seg).astype(F32))
    blocks = seg.reshape(length // T, T)
    last = blocks[:, -1]
    prev = jnp.concatenate([jnp.full((1,), -1, seg.dtype), last[:-1]])
    columns.append(segf)
    columns.append((blocks == prev[:, None]).astype(F32).reshape(length))
    columns.append((blocks == last[:, None]).astype(F32).reshape(length))
    for d in (1, 2, 3):
        ahead = jnp.concatenate([seg[d:], jnp.full((d,), -1, seg.dtype)])
        columns.append((ahead == seg).astype(F32))
    stacked = jnp.stack(columns, axis=1)
    tok = jnp.pad(stacked, ((0, 0), (0, 128 - stacked.shape[1])))
    segr = jnp.broadcast_to(segf.reshape(length // T, 1, T), (length // T, 8, T))
    return tok, segr


def local(
    x_in, target, seg_ids, valid, pre_gain, w_z, w_x, w_bc, w_dt, conv_x_w, conv_x_b,
    conv_bc_w, conv_bc_b, dt_bias, a_log, d_skip, norm_gain, w_out,
):
    rows, _, width = x_in.shape
    channels = w_z.shape[1]
    heads = w_dt.shape[1]
    head_dim = channels // heads
    tp = lax.axis_size("tp")
    inner = channels * tp
    bc_local = w_bc.shape[1]
    dp = lax.axis_size("dp")
    x2 = x_in.reshape(rows, width)
    x_view = x_in.reshape(rows * width // 128, 128)
    t_view = target.reshape(rows * width // 128, 128)
    inv_rms = lax.rsqrt(jnp.mean(x2 * x2, axis=-1, keepdims=True) + EPS)
    normed = (x2 * inv_rms * pre_gain).astype(BF16)
    bc_params = jnp.pad(jnp.concatenate([conv_bc_w.T, conv_bc_b[None]], axis=0), ((0, 3), (0, 0)))
    w_bc_all, bc_params = share((w_bc.T, bc_params), tp, 4)
    w_bc_all = w_bc_all.reshape(tp * bc_local, -1).T
    bcp = jnp.transpose(bc_params, (1, 0, 2)).reshape(8, tp * bc_local)
    w_bd = jnp.concatenate([w_bc_all, jnp.pad(w_dt, ((0, 0), (0, 128 - heads)))], axis=1)
    wbd = lax.all_gather(w_bd, "dp", axis=0, tiled=True)
    wx = lax.all_gather(w_x, "dp", axis=0, tiled=True)
    wz = lax.all_gather(w_z, "dp", axis=0, tiled=True)
    wo = lax.all_gather(w_out.T, "dp", axis=0, tiled=True)
    normed_all = gather_rows(normed, tp, 0)[0]

    tok, segr = token_table(seg_ids.reshape(-1))
    repeat = lambda v: jnp.repeat(v, head_dim)
    chp = jnp.concatenate(
        [conv_x_w.T, jnp.stack([conv_x_b, repeat(d_skip), norm_gain, jnp.zeros_like(conv_x_b)])], axis=0
    )
    decay_rate = -jnp.exp(a_log)
    hp = jnp.stack([
        jnp.pad(dt_bias, (0, 128 - heads), constant_values=-9.0),
        jnp.pad(decay_rate, (0, 128 - heads)),
    ])
    hp = jnp.pad(hp, ((0, 6), (0, 0)))

    z, xs, xcv, y, u, bcr, bcv, dtr, bcc, st, sq = forward(normed_all, wz, wx, wbd, tok, segr, chp, bcp, hp)
    v_rows = jnp.broadcast_to(valid.reshape(rows // T, 1, T).astype(F32), (rows // T, 8, T))
    lo_view, d_out, d_branch, rk_own, lost = branch_stage(u, wo, sq, x_view, t_view, v_rows, tp, inner, 1)
    db_all, rk = gather_rows(d_branch, tp, 2, rk_own)
    dproj, yn, accc, accb, acch = backward(
        db_all, wo, rk, tok, segr, chp, bcp, hp, z, xs, xcv, y, bcr, bcv, dtr, bcc, st
    )

    def dot_tn(a, b):
        return lax.dot_general(a, b, (((0,), (0,)), ((), ())), preferred_element_type=F32)

    g_out = dot_tn(db_all, yn).astype(BF16)
    g_cat = dot_tn(normed_all, dproj).astype(BF16)
    g_out, g_cat, dproj = lax.optimization_barrier((g_out, g_cat, dproj))
    g_out = lax.psum_scatter(g_out, "dp", scatter_dimension=0, tiled=True).astype(F32)
    g_cat = lax.psum_scatter(g_cat, "dp", scatter_dimension=0, tiled=True).astype(F32)
    pg = jnp.broadcast_to(pre_gain[None], (8, width))
    gx_view, gain_part = input_stage(dproj, (wz, wx, wbd), x_view, d_out, pg, tp, 3)
    grad_wz, grad_wx = g_cat[:, :channels], g_cat[:, channels : 2 * channels]
    grad_wdt = g_cat[:, 2 * channels + 256 : 2 * channels + 256 + heads]
    cols = g_cat[:, 2 * channels : 2 * channels + 256].T.reshape(tp, bc_local, -1)
    per_channel = 7 * channels // 128
    mine = jnp.concatenate([jnp.sum(accc, axis=1).reshape(per_channel, 128), jnp.sum(acch, axis=1)], axis=0)
    mine = jnp.pad(mine, ((0, -mine.shape[0] % 8), (0, 0)))
    lost_rows = jnp.stack([jnp.sum(lost[0:8], axis=0), lost[8]])
    both = jnp.concatenate(
        [jnp.sum(gain_part, axis=0).reshape(width // 128, 128), jnp.sum(accb, axis=1).reshape(10, 128), lost_rows], axis=0
    )
    both = jnp.pad(both, ((0, -both.shape[0] % 8), (0, 0)))
    mine, both, cols = finish(mine, both, cols, dp, tp, 5)
    accc = mine[:per_channel].reshape(7, channels)
    acch = mine[per_channel : per_channel + 2]
    grad_pre = both[: width // 128].reshape(width)
    accb = both[width // 128 : width // 128 + 10].reshape(5, 256)
    accb = lax.dynamic_slice_in_dim(accb, lax.axis_index("tp") * bc_local, bc_local, axis=1)
    sums = jnp.sum(both[width // 128 + 10 : width // 128 + 12], axis=1)
    loss = sums[0] / (jnp.maximum(sums[1], 1.0) * width)
    grad_wbc = cols.T
    return (
        lo_view.reshape(x_in.shape),
        loss,
        gx_view.reshape(x_in.shape),
        grad_pre,
        grad_wz,
        grad_wx,
        grad_wbc,
        grad_wdt,
        accc[0:4].T,
        accc[4],
        accb[0:4].T,
        accb[4],
        acch[0, :heads],
        acch[1, :heads],
        jnp.sum(accc[6].reshape(heads, head_dim), axis=1),
        accc[5],
        g_out.T,
    )


def solution(mesh):
    tok, col, head = P("tp", "dp", None), P("dp", "tp"), P("tp")
    in_specs = (
        tok, tok, P("dp", None), col, P(), col, col, col, col,
        P("tp", None), head, P("tp", None), head, head, head, head, head, P("tp", "dp"),
    )
    out_specs = (
        tok, P(), tok, P(), col, col, col, col,
        P("tp", None), head, P("tp", None), head, head, head, head, head, P("tp", "dp"),
    )
    return jax.shard_map(local, mesh=mesh, in_specs=in_specs, out_specs=out_specs, check_vma=False)
```

```python
from functools import partial

import jax
import jax.numpy as jnp
from jax import lax
from jax.experimental import pallas as pl
from jax.experimental.pallas import tpu as pltpu
from jax.sharding import PartitionSpec as P

T = 128
TB = 256
EPS = 1e-05
LOG2E = 1.4426950408889634
F32 = jnp.float32
BF16 = jnp.bfloat16
ZT = YT = F32
XT = CT = BF16
HIGHEST = lax.Precision.HIGHEST


def dot(a, b, precision=None):
    return jnp.dot(a, b, preferred_element_type=F32, precision=precision)


def dot_nt(a, b):
    return lax.dot_general(a, b, (((1,), (1,)), ((), ())), preferred_element_type=F32)


def lanes(column_of, index, rows=T):
    return jnp.broadcast_to(column_of[:, index : index + 1], (rows, 128))


def iota(shape, axis):
    return lax.broadcasted_iota(jnp.int32, shape, axis)


def step_sizes(raw, hp_ref):
    shifted = raw + hp_ref[0:1, :]
    dt = jnp.maximum(shifted, 0.0) + jnp.log1p(jnp.exp(-jnp.abs(shifted)))
    la = dt * hp_ref[1:2, :]
    inclusive = (iota((T, T), 0) >= iota((T, T), 1)).astype(F32)
    cum = dot(inclusive, la * LOG2E, HIGHEST)
    return shifted, dt, la, cum


def split_pair(value):
    first = iota((T, 128), 1) < 64
    zero = jnp.zeros_like(value)
    return jnp.concatenate([jnp.where(first, value, zero), jnp.where(first, zero, value)], axis=0)


def eye():
    return iota((T, T), 0) == iota((T, T), 1)


def column(row):
    return jnp.sum(jnp.where(eye(), jnp.broadcast_to(row, (T, T)), 0.0), axis=1, keepdims=True)


def row(col):
    return jnp.sum(jnp.where(eye(), jnp.broadcast_to(col, (T, T)), 0.0), axis=0, keepdims=True)


def row_sums(value):
    return jnp.sum(value.reshape(value.shape[0] // 8, 8, value.shape[1]), axis=0)


def bwd_kernel(
    db_ref, wo_ref, rk_ref, tok_ref, segr_ref, chp_ref, bcp_ref, hp_ref,
    z_ref, xs_ref, xcv_ref, y_ref, bcr_ref, bcv_ref, dtr_ref, bcc_ref, st_ref,
    dproj_out, yn_out, accc_out, accb_out, acch_out,
    dyn, dbuf, dbcbuf, dstate, dstate_b, dyec, xte, cs_rows, fold, pick,
):
    channels = wo_ref.shape[1]
    pairs = channels // 128

    @pl.when(pl.program_id(0) == 0)
    def _():
        dstate[...] = jnp.zeros_like(dstate)
        dbuf[...] = jnp.zeros_like(dbuf)
        dbcbuf[...] = jnp.zeros_like(dbcbuf)
        accc_out[...] = jnp.zeros_like(accc_out)
        accb_out[...] = jnp.zeros_like(accb_out)
        acch_out[...] = jnp.zeros_like(acch_out)
        cs_rows[...] = jnp.zeros_like(cs_rows)
        for j in range(pairs):
            half = (iota((128, 128), 0) >= 64).astype(jnp.int32)
            fold[j, :, :] = (iota((128, 128), 1) == 2 * j + half).astype(F32).astype(BF16)
            part = (iota((256, 128), 0) >= 128).astype(jnp.int32)
            pick[j, :, :] = (iota((256, 128), 1) == 2 * j + part).astype(F32).astype(BF16)

    db = db_ref[...]
    for n in range(channels // 256):
        cols = slice(n * 256, n * 256 + 256)
        dyn[:, cols] = dot(db, wo_ref[:, cols])
    first = iota((T, 128), 1) < 64
    for c in reversed(range(TB // T)):
        r0 = c * T
        rows = slice(r0, r0 + T)
        tok = tok_ref[rows, :]
        seg_col, start_b, end_b = lanes(tok, 3), lanes(tok, 4), lanes(tok, 5)
        ahead = [lanes(tok, 6 + d) for d in range(3)]
        rg_b = jnp.broadcast_to(column(rk_ref[c, 0:1, :]), (T, 128))
        kc_b = jnp.broadcast_to(column(rk_ref[c, 1:2, :]), (T, 128))
        bm, cm = bcc_ref[rows, 0:128], bcc_ref[rows, 128:256]
        ct = cm.T
        shifted, dt, la, cum = step_sizes(dtr_ref[rows, :], hp_ref)
        cum_t = cum.T
        scores, scores_t = dot_nt(cm, bm), dot_nt(bm, cm)
        same = seg_col == segr_ref[c, 0:1, :]
        below = iota((T, T), 0) >= iota((T, T), 1)
        strict = iota((T, T), 0) > iota((T, T), 1)
        above = iota((T, T), 0) <= iota((T, T), 1)
        qs = jnp.where(same & strict, scores, 0.0)
        qt = jnp.where(same & above, scores_t, 0.0)
        dstate_b[...] = dstate[...].astype(BF16)
        dq = jnp.zeros((T, T), F32)
        rsum = jnp.zeros((T, 128), F32)
        ddt = jnp.zeros((T, 128), F32)
        xsum = jnp.zeros((T, 128), F32)
        ksum = jnp.zeros((16, 128), F32)
        for j in range(pairs):
            cols = slice(j * 128, j * 128 + 128)
            zz = z_ref[rows, cols].astype(F32)
            y = y_ref[rows, cols].astype(F32)
            sz = 0.5 + 0.5 * jnp.tanh(0.5 * zz)
            silu_z = zz * sz
            dsz = sz + silu_z * (1.0 - sz)
            g = y * silu_z
            gr = g * rg_b
            gain = chp_ref[6:7, cols]
            dynp = dyn[rows, cols]
            yn_out[rows, cols] = (gr * gain).astype(BF16)
            accc_out[5, :, cols] += row_sums(dynp * gr)
            dg = rg_b * dynp * gain - g * kc_b
            dy = dg * silu_z
            dproj_out[rows, cols] = (dg * y * dsz).astype(BF16)
            xcv = xcv_ref[rows, cols].astype(F32)
            sx = 0.5 + 0.5 * jnp.tanh(0.5 * xcv)
            xc = xcv * sx
            dsx = sx + xc * (1.0 - sx)
            accc_out[6, :, cols] += row_sums(dy * xc)
            dt_e = jnp.where(first, lanes(dt, 2 * j), lanes(dt, 2 * j + 1))
            ca, cb = lanes(cum, 2 * j), lanes(cum, 2 * j + 1)
            cum_e = jnp.where(first, ca, cb)
            into = jnp.exp2(cum_e) * start_b
            to_end = jnp.exp2(cum_e[T - 1 : T, :] - cum_e) * end_b
            decay = into[T - 1 : T, :]
            xdt = xc * dt_e
            dy_b = dy.astype(BF16)
            ga = ca - cum_t[2 * j : 2 * j + 1, :]
            gb = cb - cum_t[2 * j + 1 : 2 * j + 2, :]
            grad = dot_nt(dy_b, split_pair(xdt.astype(BF16)))
            gea = grad[:, :128] * jnp.exp2(jnp.minimum(ga, 0.0))
            geb = grad[:, 128:] * jnp.exp2(jnp.minimum(gb, 0.0))
            dq = dq + gea + geb
            pp = jnp.concatenate([(gea * qs).astype(BF16), (geb * qs).astype(BF16)], axis=1)
            rsum = rsum + dot(pp, pick[j, :, :])
            csum = dot(jnp.ones((8, T), BF16), pp)
            cs_rows[2 * j : 2 * j + 1, :] = csum[0:1, :128]
            cs_rows[2 * j + 1 : 2 * j + 2, :] = csum[0:1, 128:]
            eta = (jnp.exp2(jnp.minimum(-ga, 0.0)) * qt).astype(BF16)
            etb = (jnp.exp2(jnp.minimum(-gb, 0.0)) * qt).astype(BF16)
            dxdt = dot(jnp.concatenate([eta, etb], axis=1), split_pair(dy_b))
            dx_state = to_end * dot(bm, dstate_b[:, cols])
            dxdt = dxdt + dx_state
            y_in = into * dot(cm, st_ref[c, :, cols])
            dyec_p = (dy * into).astype(BF16)
            dyec[:, cols] = dyec_p
            xte[:, cols] = (xdt * to_end).astype(BF16)
            ddt = ddt + dot((xc * dxdt).astype(BF16), fold[j, :, :])
            rsum = rsum + dot((dy * y_in).astype(BF16), fold[j, :, :])
            xsum = xsum + dot((xdt * dx_state).astype(BF16), fold[j, :, :])
            old = dstate[:, cols]
            kpart = row_sums(old * st_ref[c, :, cols].astype(F32)) * decay
            khigh = kpart.astype(BF16)
            klow = (kpart - khigh.astype(F32)).astype(BF16)
            ksum = ksum + dot(jnp.concatenate([khigh, klow], axis=0), fold[j, :, :])
            dstate[:, cols] = old * decay + dot(ct, dyec_p)
            dxcv = (dxdt * dt_e + chp_ref[5:6, cols] * dy) * dsx
            dbuf[0:T, cols] = dxcv
            xs = xs_ref[rows, cols].astype(F32)
            dxs = dxcv * chp_ref[3:4, cols]
            accc_out[4, :, cols] += row_sums(dxcv)
            accc_out[3, :, cols] += row_sums(dxcv * xs)
            for d in (1, 2, 3):
                moved = dbuf[d : d + T, cols] * ahead[d - 1]
                dxs = dxs + moved * chp_ref[3 - d : 4 - d, cols]
                accc_out[3 - d, :, cols] += row_sums(moved * xs)
            dproj_out[rows, channels + j * 128 : channels + j * 128 + 128] = dxs.astype(BF16)
        dbuf[T : T + 8, :] = dbuf[0:8, :]
        dqm = jnp.where(same & below, dq, 0.0)
        dc = dot(dqm.astype(BF16), bm) + dot_nt(dyec[...], st_ref[c, :, :])
        db_rows = dot(dqm.T.astype(BF16), cm) + dot_nt(xte[...], dstate_b[...])
        for half, grad_half in enumerate((db_rows, dc)):
            cols = slice(half * 128, half * 128 + 128)
            raw = bcv_ref[rows, cols].astype(F32)
            sb = 0.5 + 0.5 * jnp.tanh(0.5 * raw)
            dcv = grad_half * (sb + raw * sb * (1.0 - sb))
            dbcbuf[0:T, cols] = dcv
            xs = bcr_ref[rows, cols].astype(F32)
            dxs = dcv * bcp_ref[3:4, cols]
            accb_out[4, :, cols] += row_sums(dcv)
            accb_out[3, :, cols] += row_sums(dcv * xs)
            for d in (1, 2, 3):
                moved = dbcbuf[d : d + T, cols] * ahead[d - 1]
                dxs = dxs + moved * bcp_ref[3 - d : 4 - d, cols]
                accb_out[3 - d, :, cols] += row_sums(moved * xs)
            dproj_out[rows, 2 * channels + half * 128 : 2 * channels + half * 128 + 128] = dxs.astype(BF16)
        dbcbuf[T : T + 8, :] = dbcbuf[0:8, :]
        after = (iota((T, T), 0) <= iota((T, T), 1)).astype(F32)
        before = (iota((T, T), 0) > iota((T, T), 1)).astype(F32)
        dla = dot(after, rsum - cs_rows[...].T, HIGHEST) + dot(before, xsum, HIGHEST)
        dla = dla + jnp.sum(ksum, axis=0, keepdims=True)
        ddtr = (ddt + dla * hp_ref[1:2, :]) * (0.5 + 0.5 * jnp.tanh(0.5 * shifted))
        acch_out[0, :, :] += row_sums(ddtr)
        acch_out[1, :, :] += row_sums(dla * la)
        dproj_out[rows, 2 * channels + 256 : 2 * channels + 384] = ddtr.astype(BF16)


def backward(db, wo, rk, tok, segr, chp, bcp, hp, z, xs, xcv, y, bcr, bcv, dtr, bcc, st):
    length, width = db.shape
    channels = wo.shape[1]
    pairs = channels // 128
    grid = length // TB
    once = dict(pipeline_mode=pl.Buffered(1))

    def block(cols):
        return pl.BlockSpec((TB, cols), lambda i: (grid - 1 - i, 0))

    def whole(shape):
        return pl.BlockSpec(shape, lambda i: (0,) * len(shape), **once)

    chunk3 = pl.BlockSpec((TB // T, 8, 128), lambda i: (grid - 1 - i, 0, 0))
    states = pl.BlockSpec((TB // T, 128, channels), lambda i: (grid - 1 - i, 0, 0))
    total = 2 * channels + 384
    return pl.pallas_call(
        bwd_kernel,
        grid=(grid,),
        in_specs=[
            block(width), whole(wo.shape), chunk3, block(128), chunk3,
            whole(chp.shape), whole(bcp.shape), whole(hp.shape),
            block(channels), block(channels), block(channels), block(channels),
            block(256), block(256), block(128), block(256), states,
        ],
        out_specs=[
            block(total), block(channels),
            pl.BlockSpec((7, 8, channels), lambda i: (0, 0, 0)),
            pl.BlockSpec((5, 8, 256), lambda i: (0, 0, 0)),
            pl.BlockSpec((2, 8, 128), lambda i: (0, 0, 0)),
        ],
        out_shape=[
            jax.ShapeDtypeStruct((length, total), BF16),
            jax.ShapeDtypeStruct((length, channels), BF16),
            jax.ShapeDtypeStruct((7, 8, channels), F32),
            jax.ShapeDtypeStruct((5, 8, 256), F32),
            jax.ShapeDtypeStruct((2, 8, 128), F32),
        ],
        scratch_shapes=[
            pltpu.VMEM((TB, channels), F32),
            pltpu.VMEM((T + 8, channels), F32),
            pltpu.VMEM((T + 8, 256), F32),
            pltpu.VMEM((128, channels), F32),
            pltpu.VMEM((128, channels), BF16),
            pltpu.VMEM((T, channels), BF16),
            pltpu.VMEM((T, channels), BF16),
            pltpu.VMEM((128, 128), F32),
            pltpu.VMEM((pairs, 128, 128), BF16),
            pltpu.VMEM((pairs, 256, 128), BF16),
        ],
        compiler_params=pltpu.CompilerParams(vmem_limit_bytes=56 << 20),
        name="ssd_backward",
    )(db, wo, rk, tok, segr, chp, bcp, hp, z, xs, xcv, y, bcr, bcv, dtr, bcc, st)


MESH_ID = pl.DeviceIdType.MESH


def meet(n, axis):
    me = lax.axis_index(axis)
    barrier = pltpu.get_barrier_semaphore()
    for peer in range(n):

        @pl.when(me != peer)
        def _():
            pl.semaphore_signal(barrier, inc=1, device_id={axis: peer}, device_id_type=MESH_ID)

    pl.semaphore_wait(barrier, n - 1)
    return me


def to_peer(source, target, send_sem, recv_sem, axis, peer):
    return pltpu.make_async_remote_copy(
        src_ref=source, dst_ref=target, send_sem=send_sem, recv_sem=recv_sem,
        device_id={axis: peer}, device_id_type=MESH_ID,
    )


def share_kernel(n, count, *refs):
    ins, outs = refs[:count], refs[count : 2 * count]
    send_sem, recv_sem = refs[2 * count :]
    me = meet(n, "tp")
    for i in range(count):
        for peer in range(n):

            @pl.when(me != peer)
            def _():
                to_peer(ins[i], outs[i].at[me], send_sem.at[i, peer], recv_sem.at[i, me], "tp", peer).start()

        outs[i][pl.ds(me, 1)] = ins[i][...][None]
    for i in range(count):
        for peer in range(n):

            @pl.when(me != peer)
            def _():
                to_peer(ins[i], outs[i].at[peer], send_sem.at[i, peer], recv_sem.at[i, peer], "tp", peer).wait_recv()
                to_peer(ins[i], outs[i].at[me], send_sem.at[i, peer], recv_sem.at[i, me], "tp", peer).wait_send()


def share(arrays, n, collective_id):
    vmem = pl.BlockSpec(memory_space=pltpu.VMEM)
    count = len(arrays)
    return pl.pallas_call(
        partial(share_kernel, n, count),
        out_shape=[jax.ShapeDtypeStruct((n,) + a.shape, a.dtype) for a in arrays],
        in_specs=[vmem] * count,
        out_specs=[vmem] * count,
        scratch_shapes=[pltpu.SemaphoreType.DMA((count, n)), pltpu.SemaphoreType.DMA((count, n))],
        compiler_params=pltpu.CompilerParams(collective_id=collective_id, has_side_effects=True),
        name="share",
    )(*arrays)


def finish_kernel(dp, tp, mine, both, cols, mine_out, both_out, cols_out, got, got_both, got_cols, sems):
    me_dp, me_tp = lax.axis_index("dp"), lax.axis_index("tp")
    barrier = pltpu.get_barrier_semaphore()
    for peer in range(dp):

        @pl.when(me_dp != peer)
        def _():
            pl.semaphore_signal(barrier, inc=1, device_id={"dp": peer}, device_id_type=MESH_ID)

    for peer in range(tp):

        @pl.when(me_tp != peer)
        def _():
            pl.semaphore_signal(barrier, inc=1, device_id={"tp": peer}, device_id_type=MESH_ID)

    pl.semaphore_wait(barrier, dp - 1 + tp - 1)
    first = mine.shape[0]
    got[pl.ds(me_dp, 1), 0:first, :] = mine[...][None]
    got[pl.ds(me_dp, 1), first:, :] = both[...][None]

    def over_dp(peer, slot):
        return to_peer(got.at[me_dp], got.at[slot], sems.at[0, peer], sems.at[1, slot], "dp", peer)

    def over_tp(peer, slot):
        return to_peer(got_both.at[me_tp], got_both.at[slot], sems.at[2, peer], sems.at[3, slot], "tp", peer)

    def over_cols(peer, slot):
        return to_peer(cols.at[peer], got_cols.at[slot], sems.at[4, peer], sems.at[5, slot], "tp", peer)

    for peer in range(dp):

        @pl.when(me_dp != peer)
        def _():
            over_dp(peer, me_dp).start()

    for peer in range(tp):

        @pl.when(me_tp != peer)
        def _():
            over_cols(peer, me_tp).start()

    got_cols[pl.ds(me_tp, 1)] = cols[pl.ds(me_tp, 1)]
    for peer in range(dp):

        @pl.when(me_dp != peer)
        def _():
            over_dp(peer, peer).wait_recv()

    total = got[0]
    for peer in range(1, dp):
        total = total + got[peer]
    mine_out[...] = total[:first]
    got_both[pl.ds(me_tp, 1)] = total[first:][None]
    for peer in range(tp):

        @pl.when(me_tp != peer)
        def _():
            over_tp(peer, me_tp).start()

    for peer in range(tp):

        @pl.when(me_tp != peer)
        def _():
            over_cols(peer, peer).wait_recv()
            over_tp(peer, peer).wait_recv()

    total, columns = got_both[0], got_cols[0]
    for peer in range(1, tp):
        total, columns = total + got_both[peer], columns + got_cols[peer]
    both_out[...] = total
    cols_out[...] = columns
    for peer in range(dp):

        @pl.when(me_dp != peer)
        def _():
            over_dp(peer, me_dp).wait_send()

    for peer in range(tp):

        @pl.when(me_tp != peer)
        def _():
            over_cols(peer, me_tp).wait_send()
            over_tp(peer, me_tp).wait_send()


def finish(mine, both, cols, dp, tp, collective_id):
    vmem = pl.BlockSpec(memory_space=pltpu.VMEM)
    rows = mine.shape[0] + both.shape[0]
    return pl.pallas_call(
        partial(finish_kernel, dp, tp),
        out_shape=[
            jax.ShapeDtypeStruct(mine.shape, F32),
            jax.ShapeDtypeStruct(both.shape, F32),
            jax.ShapeDtypeStruct(cols.shape[1:], F32),
        ],
        in_specs=[vmem] * 3,
        out_specs=[vmem] * 3,
        scratch_shapes=[
            pltpu.VMEM((dp, rows, 128), F32),
            pltpu.VMEM((tp,) + both.shape, F32),
            pltpu.VMEM(cols.shape, F32),
            pltpu.SemaphoreType.DMA((6, max(dp, tp))),
        ],
        compiler_params=pltpu.CompilerParams(collective_id=collective_id, has_side_effects=True),
        name="finish",
    )(mine, both, cols)


def gather_kernel(n, pieces, extra, *refs):
    if extra:
        x_ref, e_ref, out_ref, eo_ref, local_sem, send_sem, recv_sem, es_sem, er_sem = refs
    else:
        x_ref, out_ref, local_sem, send_sem, recv_sem = refs
    rows = x_ref.shape[0]
    piece = rows // pieces
    me = meet(n, "tp")

    def place(owner, p):
        return out_ref.at[pl.ds(pl.multiple_of(owner * rows + p * piece, piece), piece)]

    def outgoing(way, step, p):
        owner = me - step if way == 0 else me + step
        source = x_ref.at[pl.ds(p * piece, piece)] if step == 0 else place(owner, p)
        peer = me + 1 if way == 0 else me - 1
        return to_peer(source, place(owner, p), send_sem.at[way, step, p], recv_sem.at[way, step, p], "tp", peer)

    def incoming(way, step, p):
        owner = me - 1 - step if way == 0 else me + 1 + step
        peer = me - 1 if way == 0 else me + 1
        return to_peer(place(owner, p), place(owner, p), send_sem.at[way, step, p], recv_sem.at[way, step, p], "tp", peer)

    def sends(way, step):
        if way == 0:
            return (me - step >= 0) & (me < n - 1)
        return (me + step <= n - 1) & (me > 0)

    def receives(way, step):
        return me - 1 - step >= 0 if way == 0 else me + 1 + step <= n - 1

    keep = pltpu.make_async_copy(x_ref, out_ref.at[pl.ds(pl.multiple_of(me * rows, rows), rows)], local_sem.at[0])
    if extra:
        count = e_ref.shape[0]

        def extra_to(peer, owner):
            there = eo_ref.at[pl.ds(owner * count, count)]
            return to_peer(e_ref, there, es_sem.at[peer], er_sem.at[owner], "tp", peer)

        keep_extra = pltpu.make_async_copy(e_ref, eo_ref.at[pl.ds(me * count, count)], local_sem.at[1])
        keep_extra.start()
        for peer in range(n):

            @pl.when(me != peer)
            def _():
                extra_to(peer, me).start()

    for step in range(n):
        for p in range(pieces):
            for way in (0, 1):
                if step > 0:

                    @pl.when(receives(way, step - 1))
                    def _():
                        incoming(way, step - 1, p).wait_recv()

                if step < n - 1:

                    @pl.when(sends(way, step))
                    def _():
                        outgoing(way, step, p).start()

        if step == 0:
            keep.start()

    for step in range(n - 1):
        for p in range(pieces):
            for way in (0, 1):

                @pl.when(sends(way, step))
                def _():
                    outgoing(way, step, p).wait_send()

    keep.wait()
    if extra:
        keep_extra.wait()
        for peer in range(n):

            @pl.when(me != peer)
            def _():
                extra_to(peer, me).wait_send()
                extra_to(peer, peer).wait_recv()


def gather_rows(x, n, collective_id, extra=None):
    rows, width = x.shape
    pieces = 4
    anywhere = pl.BlockSpec(memory_space=pl.ANY)
    out_shape = [jax.ShapeDtypeStruct((n * rows, width), x.dtype)]
    scratch = [
        pltpu.SemaphoreType.DMA((2,)),
        pltpu.SemaphoreType.DMA((2, n - 1, pieces)),
        pltpu.SemaphoreType.DMA((2, n - 1, pieces)),
    ]
    operands = [x]
    if extra is not None:
        operands.append(extra)
        out_shape.append(jax.ShapeDtypeStruct((n * extra.shape[0],) + extra.shape[1:], extra.dtype))
        scratch += [pltpu.SemaphoreType.DMA((n,)), pltpu.SemaphoreType.DMA((n,))]
    return pl.pallas_call(
        partial(gather_kernel, n, pieces, extra is not None),
        out_shape=out_shape,
        in_specs=[anywhere] * len(operands),
        out_specs=[anywhere] * len(operands),
        scratch_shapes=scratch,
        compiler_params=pltpu.CompilerParams(collective_id=collective_id, has_side_effects=True),
        cost_estimate=pl.CostEstimate(flops=0, bytes_accessed=400 << 20, transcendentals=0),
        name="gather_rows",
    )(*operands)


def scatter_body(n, me, a_ref, right_refs, acc, part, slots, send_sem, recv_sem):
    rows, width = acc.shape
    group = part.shape[0]
    piece = slots.shape[2]
    pieces = rows // piece
    groups = rows // group
    subs = group // piece

    def link(way, index):
        peer = me + 1 if way == 0 else me - 1
        return to_peer(
            slots.at[way, index], slots.at[way, index], send_sem.at[way, index], recv_sem.at[way, index], "tp", peer
        )

    def own(start, target, base):
        def tile(i, carry):
            cols = pl.ds(pl.multiple_of(i * 256, 256), 256)
            total, at = None, 0
            for w_ref in right_refs:
                depth = w_ref.shape[1]
                term = dot_nt(a_ref[pl.ds(start, group), at : at + depth], w_ref[cols, :])
                total = term if total is None else total + term
                at += depth
            target[pl.ds(base, group), cols] = total
            return carry

        lax.fori_loop(0, width // 256, tile, 0)

    def pass_on(way, q, at_end):
        shard = n - 1 - q // groups if way == 0 else q // groups
        start = pl.multiple_of(shard * rows + (q % groups) * group, group)
        own(start, part, 0)
        for sub in range(subs):
            index = shard * pieces + (q % groups) * subs + sub
            here = slice(sub * piece, (sub + 1) * piece)

            @pl.when(at_end)
            def _():
                slots[way, index] = part[here, :].astype(BF16)

            @pl.when(jnp.logical_not(at_end))
            def _():
                link(way, index).wait_recv()
                slots[way, index] = (part[here, :] + slots[way, index].astype(F32)).astype(BF16)

            link(way, index).start()

    def turn(t, carry):
        for way in (0, 1):
            hops = me if way == 0 else n - 1 - me
            q = t - hops

            @pl.when((q >= 0) & (q < (n - 1 - hops) * groups))
            def _():
                pass_on(way, q, hops == 0)

        late = t - (n - 1)

        @pl.when((late >= 0) & (late < groups))
        def _():
            base = pl.multiple_of(late * group, group)
            own(pl.multiple_of(me * rows + late * group, group), acc, base)

        return carry

    lax.fori_loop(0, (n - 1) * groups + n - 1, turn, 0)

    def arrived(p):
        for way in (0, 1):

            @pl.when((me > 0) if way == 0 else (me < n - 1))
            def _():
                link(way, me * pieces + p).wait_recv()
                here = pl.ds(pl.multiple_of(p * piece, piece), piece)
                acc[here, :] += slots[way, me * pieces + p].astype(F32)

    def drain():
        def done(index, carry):
            shard = index // pieces
            for way in (0, 1):

                @pl.when((me < shard) if way == 0 else (me > shard))
                def _():
                    link(way, index).wait_send()

            return carry

        lax.fori_loop(0, n * pieces, done, 0)

    return arrived, drain


def forward_block(
    t, nb, wc, tok_ref, segr_ref, chp_ref, bcp_ref, hp_ref,
    zbuf, xs_out, xcv_out, y_out, u_all, bcr_out, bcv_out, dtr_out, bcc_out, st_out, sq_all,
    xbuf, bcbuf, state,
):
    channels = zbuf.shape[1]
    pairs = channels // 128
    start = pl.multiple_of(t * TB, TB)
    nb_rows = pl.ds(start, TB)
    for n in range(channels // 256):
        cols = slice(n * 256, n * 256 + 256)
        zbuf[:, cols] = dot(nb[nb_rows, :], wc[:, cols])
        xbuf[8 : 8 + TB, cols] = dot(nb[nb_rows, :], wc[:, channels + n * 256 : channels + n * 256 + 256])
    bd = dot(nb[nb_rows, :], wc[:, 2 * channels :])
    bcbuf[8 : 8 + TB, :] = bd[:, :256]
    dtr_out[...] = bd[:, 256:]
    bcr_out[...] = bd[:, :256].astype(BF16)
    first = iota((T, 128), 1) < 64
    for c in range(TB // T):
        r0 = c * T
        rows = slice(r0, r0 + T)
        chunk = t * (TB // T) + c
        at = pl.ds(pl.multiple_of(start + r0, T), T)
        tok = tok_ref[at, :]
        masks = [lanes(tok, d) for d in range(3)]
        seg_col, start_b, end_b = lanes(tok, 3), lanes(tok, 4), lanes(tok, 5)
        parts = []
        for half in range(2):
            cols = slice(half * 128, half * 128 + 128)
            acc = bcbuf[8 + r0 : 8 + r0 + T, cols] * bcp_ref[3:4, cols] + bcp_ref[4:5, cols]
            for d in (1, 2, 3):
                acc = acc + bcbuf[8 + r0 - d : 8 + r0 - d + T, cols] * bcp_ref[3 - d : 4 - d, cols] * masks[d - 1]
            bcv_out[rows, cols] = acc.astype(BF16)
            hv = 0.5 * acc
            parts.append((hv + hv * jnp.tanh(hv)).astype(BF16))
            bcc_out[rows, cols] = parts[-1]
        bm, cm = parts
        bt = bm.T
        _, dt, la, cum = step_sizes(dtr_out[rows, :], hp_ref)
        cum_t = cum.T
        scores = dot_nt(cm, bm)
        keep = (seg_col == segr_ref[chunk, 0:1, :]) & (iota((T, T), 0) >= iota((T, T), 1))
        qm = jnp.where(keep, scores, 0.0)
        sq = jnp.zeros((T, 128), F32)
        st_out[c, :, :] = state[...].astype(BF16)
        for j in range(pairs):
            cols = slice(j * 128, j * 128 + 128)
            acc = xbuf[8 + r0 : 8 + r0 + T, cols] * chp_ref[3:4, cols] + chp_ref[4:5, cols]
            xs_out[rows, cols] = xbuf[8 + r0 : 8 + r0 + T, cols].astype(BF16)
            for d in (1, 2, 3):
                acc = acc + xbuf[8 + r0 - d : 8 + r0 - d + T, cols] * chp_ref[3 - d : 4 - d, cols] * masks[d - 1]
            xcv_out[rows, cols] = acc.astype(BF16)
            hv = 0.5 * acc
            xc = hv + hv * jnp.tanh(hv)
            dt_e = jnp.where(first, lanes(dt, 2 * j), lanes(dt, 2 * j + 1))
            ca, cb = lanes(cum, 2 * j), lanes(cum, 2 * j + 1)
            cum_e = jnp.where(first, ca, cb)
            xdt = xc * dt_e
            ea = jnp.exp2(jnp.minimum(ca - cum_t[2 * j : 2 * j + 1, :], 0.0))
            eb = jnp.exp2(jnp.minimum(cb - cum_t[2 * j + 1 : 2 * j + 2, :], 0.0))
            mix = jnp.concatenate([(ea * qm).astype(BF16), (eb * qm).astype(BF16)], axis=1)
            y = dot(mix, split_pair(xdt.astype(BF16)))
            into = jnp.exp2(cum_e) * start_b
            last = cum_e[T - 1 : T, :]
            to_end = jnp.exp2(last - cum_e) * end_b
            y = y + into * dot(cm, st_out[c, :, cols])
            state[:, cols] = state[:, cols] * into[T - 1 : T, :] + dot(bt, (xdt * to_end).astype(BF16))
            y = y + chp_ref[5:6, cols] * xc
            y_out[rows, cols] = y
            hz = 0.5 * zbuf[rows, cols]
            g = y * (hz + hz * jnp.tanh(hz))
            sq = sq + g * g
            u_all[at, cols] = (g * chp_ref[6:7, cols]).astype(BF16)
        sq_all[chunk, :, :] = lax.dot_general(
            jnp.ones((8, 128), F32), sq, (((1,), (1,)), ((), ())), preferred_element_type=F32, precision=HIGHEST
        )
    xbuf[0:8, :] = xbuf[TB : TB + 8, :]
    bcbuf[0:8, :] = bcbuf[TB : TB + 8, :]


def front_kernel(
    n, dp, inner,
    x_ref, t_ref, wcs_ref, wos_ref, pg_ref, tok_ref, segr_ref, chp_ref, bcp_ref, hp_ref, v_ref,
    z_out, xs_out, xcv_out, y_out, bcr_out, bcv_out, dtr_out, bcc_out, st_out,
    nb_out, wc_out, wo_out, lo_out, do_out, db_out, rk_out, loss_out,
    nb, wc, wo, u_all, slots, acc, part,
    zbuf, xsb, xcvb, yb, bcrb, bcvb, dtrb, bccb, stb,
    xbuf, bcbuf, state, sq_all, sqs, xst, tst, lost_buf, dob, dbb,
    load_sem, keep_sem, save_sem, w_send, w_pass, w_recv, ag_send, ag_recv, rs_send, rs_recv, q_send, q_recv,
):
    me, me_dp = lax.axis_index("tp"), lax.axis_index("dp")
    rows, width = acc.shape
    pieces = rows // T
    tiles = width // 128
    gps = rows // TB
    subs = TB // T
    blocks = n * gps
    share_rows = wcs_ref.shape[0]
    barrier = pltpu.get_barrier_semaphore()
    for peer in range(dp):

        @pl.when(me_dp != peer)
        def _():
            pl.semaphore_signal(barrier, inc=1, device_id={"dp": peer}, device_id_type=MESH_ID)

    for peer in range(n):

        @pl.when(me != peer)
        def _():
            pl.semaphore_signal(barrier, inc=1, device_id={"tp": peer}, device_id_type=MESH_ID)

    def load(source, target, slot, p):
        view = source.at[pl.ds(pl.multiple_of(p * (T * tiles), T * tiles), T * tiles)]
        return pltpu.make_async_copy(view, target.at[slot], load_sem.at[0 if target is xst else 1, slot])

    load(x_ref, xst, 0, 0).start()

    def shard_rows(owner):
        return pl.ds(pl.multiple_of(owner * share_rows, share_rows), share_rows)

    full = (wc, wo)
    local = (wcs_ref, wos_ref)
    for i in range(2):
        pltpu.make_async_copy(local[i], full[i].at[shard_rows(me_dp)], keep_sem.at[i]).start()
    state[...] = jnp.zeros_like(state)
    xbuf[0:8, :] = jnp.zeros((8, xbuf.shape[1]), F32)
    bcbuf[0:8, :] = jnp.zeros((8, 256), F32)
    pl.semaphore_wait(barrier, dp - 1 + n - 1)

    core = me_dp % 2
    chip = me_dp // 2
    sibling = me_dp + 1 - 2 * core

    def give(i, peer):
        return to_peer(local[i], full[i].at[shard_rows(me_dp)], w_send.at[i, peer], w_recv.at[i, me_dp], "dp", peer)

    def passed(i, owner):
        there = full[i].at[shard_rows(owner)]
        return to_peer(there, there, w_pass.at[i, owner], w_recv.at[i, owner], "dp", sibling)

    def give_all(i):
        for k in range(dp // 2):

            @pl.when(chip != k)
            def _():
                give(i, 2 * k + core).start()

        give(i, sibling).start()

    def pass_all(i):
        for k in range(dp // 2):

            @pl.when(chip != k)
            def _():
                passed(i, 2 * k + core).wait_recv()
                passed(i, 2 * k + core).start()

    def wait_all(i):
        pltpu.make_async_copy(local[i], full[i].at[shard_rows(me_dp)], keep_sem.at[i]).wait()
        passed(i, sibling).wait_recv()
        for k in range(dp // 2):

            @pl.when(chip != k)
            def _():
                passed(i, 2 * k + 1 - core).wait_recv()

    give_all(0)
    give_all(1)

    def ag(way, index):
        here = nb.at[pl.ds(pl.multiple_of(index * T, T), T)]
        peer = me + 1 if way == 0 else me - 1
        return to_peer(here, here, ag_send.at[way, index], ag_recv.at[way, index], "tp", peer)

    for p in range(pieces):
        load(x_ref, xst, p % 2, p).wait()
        if p + 1 < pieces:
            load(x_ref, xst, (p + 1) % 2, p + 1).start()
        squares = jnp.zeros((T, 128), F32)
        for c in range(tiles):
            xt = xst[p % 2, pl.ds(c, T, stride=tiles), :]
            squares = squares + xt * xt
        inv = lax.rsqrt(jnp.sum(squares, axis=1, keepdims=True) / width + EPS)
        inv_b = jnp.broadcast_to(inv, (T, 128))
        index = me * pieces + p
        here = pl.ds(pl.multiple_of(index * T, T), T)
        for c in range(tiles):
            cols = slice(c * 128, c * 128 + 128)
            xt = xst[p % 2, pl.ds(c, T, stride=tiles), :]
            nb[here, cols] = (xt * inv_b * pg_ref[0:1, cols]).astype(BF16)
        o = p // subs

        @pl.when((me < n - 1) & ((me == 0) | (me > o)))
        def _():
            ag(0, index).start()

        @pl.when(me > 0)
        def _():
            ag(1, index).start()

    def relay(k):
        for sub in range(subs):
            low = k * subs + sub

            @pl.when(k < me * gps)
            def _():
                ag(0, low).wait_recv()

                @pl.when(me < n - 1)
                def _():
                    ag(0, low).start()

            high = ((me + 1) * gps + k) * subs + sub

            @pl.when((me + 1) * gps + k < blocks)
            def _():
                ag(1, high).wait_recv()

                @pl.when(me > 0)
                def _():
                    ag(1, high).start()

        @pl.when((k == me * gps - 1) & (me < n - 1))
        def _():
            for o in range(gps):

                @pl.when(me <= o)
                def _():
                    for sub in range(subs):
                        ag(0, (me * gps + o) * subs + sub).start()

    early = min(2, blocks - gps)
    for k in range(early):
        relay(k)
    pass_all(0)
    wait_all(0)

    saves = (
        (zbuf, z_out), (xsb, xs_out), (xcvb, xcv_out), (yb, y_out),
        (bcrb, bcr_out), (bcvb, bcv_out), (dtrb, dtr_out), (bccb, bcc_out),
    )

    def save(i, t):
        if i == len(saves):
            there = st_out.at[pl.ds(pl.multiple_of(t * subs, subs), subs)]
            return pltpu.make_async_copy(stb, there, save_sem.at[i])
        there = saves[i][1].at[pl.ds(pl.multiple_of(t * TB, TB), TB)]
        return pltpu.make_async_copy(saves[i][0], there, save_sem.at[i])

    def link(way, shard, p):
        source = shard * pieces + p
        if way == 0:
            target, peer = source, me + 1
        else:
            gap = jnp.minimum(me - 1 - shard, 1)
            target, peer = (shard + (n - shard) * (1 - gap)) * pieces + p, me - 1
        return to_peer(slots.at[source], slots.at[target], rs_send.at[way, source], rs_recv.at[way, target], "tp", peer)

    def landed(way, slot):
        peer = me - 1 if way == 0 else me + 1
        return to_peer(slots.at[slot], slots.at[slot], rs_send.at[way, slot], rs_recv.at[way, slot], "tp", peer)

    def own(block, target, base):
        def tile(i, carry):
            cols = pl.ds(pl.multiple_of(i * 256, 256), 256)
            target[pl.ds(base, TB), cols] = dot_nt(u_all[pl.ds(pl.multiple_of(block * TB, TB), TB), :], wo[cols, :])
            return carry

        lax.fori_loop(0, width // 256, tile, 0)

    def pass_on(way, block, at_end):
        shard = block // gps
        own(block, part, 0)
        for sub in range(subs):
            p = (block % gps) * subs + sub
            slot = shard * pieces + p
            here = slice(sub * T, sub * T + T)

            @pl.when(at_end)
            def _():
                slots[slot] = part[here, :].astype(BF16)

            @pl.when(jnp.logical_not(at_end))
            def _():
                landed(way, slot).wait_recv()
                slots[slot] = (part[here, :] + slots[slot].astype(F32)).astype(BF16)

            link(way, shard, p).start()

    def squares_to(peer, slot):
        return to_peer(sq_all.at[pl.ds(peer * pieces, pieces)], sqs.at[slot], q_send.at[peer], q_recv.at[slot], "tp", peer)

    def turn(t, carry):
        @pl.when(t < blocks)
        def _():
            @pl.when((t >= early) & (t < blocks - gps))
            def _():
                relay(t)

            @pl.when(t > 0)
            def _():
                for i in range(len(saves) + 1):
                    save(i, t - 1).wait()

            forward_block(
                t, nb, wc, tok_ref, segr_ref, chp_ref, bcp_ref, hp_ref,
                zbuf, xsb, xcvb, yb, u_all, bcrb, bcvb, dtrb, bccb, stb, sq_all,
                xbuf, bcbuf, state,
            )
            for i in range(len(saves) + 1):
                save(i, t).start()

        @pl.when(t == 0)
        def _():
            pass_all(1)
            wait_all(1)

        @pl.when(t == blocks - 1)
        def _():
            for peer in range(n):

                @pl.when(me != peer)
                def _():
                    squares_to(peer, me).start()

        left = t - (n - 1 - me)

        @pl.when((left >= 0) & (left < me * gps))
        def _():
            pass_on(1, left, me == n - 1)

        right = t - me

        @pl.when((right >= (me + 1) * gps) & (right < blocks))
        def _():
            pass_on(0, right, me == 0)

        mine = t - 1 - me * gps

        @pl.when((mine >= 0) & (mine < gps))
        def _():
            own(t - 1, acc, pl.multiple_of(mine * TB, TB))

        return carry

    lax.fori_loop(0, blocks + n - 1, turn, 0)
    kept = (
        pltpu.make_async_copy(nb, nb_out, keep_sem.at[2]),
        pltpu.make_async_copy(wc, wc_out, keep_sem.at[3]),
        pltpu.make_async_copy(wo, wo_out, keep_sem.at[4]),
    )
    for copy in kept:
        copy.start()
    load(x_ref, xst, 0, 0).start()
    load(t_ref, tst, 0, 0).start()
    sqs[pl.ds(me, 1)] = sq_all[pl.ds(me * pieces, pieces)][None]
    for peer in range(n):

        @pl.when(me != peer)
        def _():
            squares_to(peer, peer).wait_recv()

    loss_out[...] = jnp.zeros_like(loss_out)

    def store(i, p):
        if i == 0:
            there = lo_out.at[pl.ds(pl.multiple_of(p * (T * tiles), T * tiles), T * tiles)]
            return pltpu.make_async_copy(lost_buf, there, save_sem.at[0])
        source, target = ((dob, do_out), (dbb, db_out))[i - 1]
        return pltpu.make_async_copy(source, target.at[pl.ds(pl.multiple_of(p * T, T), T)], save_sem.at[i])

    for i in range(len(saves) + 1):
        save(i, blocks - 1).wait()
    for p in range(pieces):
        load(x_ref, xst, p % 2, p).wait()
        load(t_ref, tst, p % 2, p).wait()
        if p + 1 < pieces:
            load(x_ref, xst, (p + 1) % 2, p + 1).start()
            load(t_ref, tst, (p + 1) % 2, p + 1).start()
        here = slice(p * T, p * T + T)

        @pl.when(me > 0)
        def _():
            landed(0, me * pieces + p).wait_recv()
            acc[here, :] += slots[me * pieces + p].astype(F32)

        @pl.when(me < n - 1)
        def _():
            landed(1, n * pieces + p).wait_recv()
            acc[here, :] += slots[n * pieces + p].astype(F32)

        if p > 0:
            for i in range(3):
                store(i, p - 1).wait()
        total = sqs[0, p]
        for peer in range(1, n):
            total = total + sqs[peer, p]
        rg_row = lax.rsqrt(total / inner + EPS)
        rg_b = jnp.broadcast_to(column(rg_row[0:1, :]), (T, 128))
        mask_b = jnp.broadcast_to(column(v_ref[p, 0:1, :]), (T, 128))
        dots = jnp.zeros((T, 128), F32)
        lost = jnp.zeros((T, 128), F32)
        for c in range(tiles):
            cols = slice(c * 128, c * 128 + 128)
            view = pl.ds(c, T, stride=tiles)
            branch = acc[here, cols] * rg_b
            lo = xst[p % 2, view, :] + branch
            lost_buf[view, :] = lo
            error = lo - tst[p % 2, view, :]
            d_out = error * mask_b
            dob[:, cols] = d_out
            d_branch = d_out.astype(BF16)
            dbb[:, cols] = d_branch
            lost = lost + d_out * error
            dots = dots + d_branch.astype(F32) * branch
        loss_out[0:8, :] += row_sums(lost)
        loss_out[8:9, :] += v_ref[p, 0:1, :]
        coefficient = jnp.sum(dots, axis=1, keepdims=True)
        rk_out[p, 0:1, :] = rg_row[0:1, :]
        rk_out[p, 1:2, :] = row(coefficient) * rg_row[0:1, :] * rg_row[0:1, :] / inner
        rk_out[p, 2:8, :] = jnp.zeros((6, 128), F32)
        for i in range(3):
            store(i, p).start()

    for i in range(3):
        store(i, pieces - 1).wait()
    for copy in kept:
        copy.wait()

    def drain(index, carry):
        block = index // subs
        shard = index // pieces

        @pl.when((me < n - 1) & (block < (me + 1) * gps))
        def _():
            ag(0, index).wait_send()

        @pl.when((me > 0) & (block >= me * gps))
        def _():
            ag(1, index).wait_send()

        @pl.when(me < shard)
        def _():
            link(0, shard, index % pieces).wait_send()

        @pl.when(me > shard)
        def _():
            link(1, shard, index % pieces).wait_send()

        return carry

    lax.fori_loop(0, n * pieces, drain, 0)
    for i in range(2):
        give(i, sibling).wait_send()
        for k in range(dp // 2):

            @pl.when(chip != k)
            def _():
                give(i, 2 * k + core).wait_send()
                passed(i, 2 * k + core).wait_send()

    for peer in range(n):

        @pl.when(me != peer)
        def _():
            squares_to(peer, me).wait_send()


def front_stage(x_view, t_view, wcs, wos, pg, tok, segr, chp, bcp, hp, v_rows, n, dp, inner, collective_id):
    width = pg.shape[1]
    rows = x_view.shape[0] * 128 // width
    length = n * rows
    channels = wos.shape[1]
    total = wcs.shape[1]
    vmem = pl.BlockSpec(memory_space=pltpu.VMEM)
    anywhere = pl.BlockSpec(memory_space=pl.ANY)
    tile_rows = T * width // 128
    shape = jax.ShapeDtypeStruct
    saved = [
        shape((length, channels), F32), shape((length, channels), BF16), shape((length, channels), BF16),
        shape((length, channels), F32), shape((length, 256), BF16), shape((length, 256), BF16),
        shape((length, 128), F32), shape((length, 256), BF16),
        shape((length // T, 128, channels), BF16),
    ]
    buffers = [pltpu.VMEM((TB,) + item.shape[1:], item.dtype) for item in saved[:-1]]
    buffers.append(pltpu.VMEM((TB // T, 128, channels), BF16))
    dma = pltpu.SemaphoreType.DMA
    return pl.pallas_call(
        partial(front_kernel, n, dp, inner),
        out_shape=saved + [
            shape((length, width), BF16), shape((width, total), BF16), shape((width, channels), BF16),
            shape(x_view.shape, F32), shape((rows, width), F32), shape((rows, width), BF16),
            shape((rows // T, 8, 128), F32), shape((16, 128), F32),
        ],
        in_specs=[anywhere] * 4 + [vmem] * 7,
        out_specs=[anywhere] * 15 + [vmem] * 2,
        scratch_shapes=[
            pltpu.VMEM((length, width), BF16),
            pltpu.VMEM((width, total), BF16),
            pltpu.VMEM((width, channels), BF16),
            pltpu.VMEM((length, channels), BF16),
            pltpu.VMEM(((n + 1) * rows // T, T, width), BF16),
            pltpu.VMEM((rows, width), F32),
            pltpu.VMEM((TB, width), F32),
        ] + buffers + [
            pltpu.VMEM((TB + 8, channels), F32),
            pltpu.VMEM((TB + 8, 256), F32),
            pltpu.VMEM((128, channels), F32),
            pltpu.VMEM((length // T, 8, 128), F32),
            pltpu.VMEM((n, rows // T, 8, 128), F32),
            pltpu.VMEM((2, tile_rows, 128), F32),
            pltpu.VMEM((2, tile_rows, 128), F32),
            pltpu.VMEM((tile_rows, 128), F32),
            pltpu.VMEM((T, width), F32),
            pltpu.VMEM((T, width), BF16),
            dma((2, 2)), dma((5,)), dma((9,)),
            dma((2, dp)), dma((2, dp)), dma((2, dp)),
            dma((2, length // T)), dma((2, length // T)),
            dma((2, (n + 1) * rows // T)), dma((2, (n + 1) * rows // T)),
            dma((n,)), dma((n,)),
        ],
        compiler_params=pltpu.CompilerParams(
            collective_id=collective_id, has_side_effects=True, vmem_limit_bytes=63 << 20
        ),
        name="front_stage",
    )(x_view, t_view, wcs, wos, pg, tok, segr, chp, bcp, hp, v_rows)


def scatter_scratch(length, rows, width):
    return [
        pltpu.VMEM((rows, width), F32),
        pltpu.VMEM((min(rows, 256), width), F32),
        pltpu.VMEM((2, length // T, T, width), BF16),
    ], [
        pltpu.SemaphoreType.DMA((2, length // T)),
        pltpu.SemaphoreType.DMA((2, length // T)),
    ]


def input_kernel(
    n, parts, a_ref, *refs,
):
    right_refs = refs[:parts]
    x_ref, do_ref, pg_ref, gx_out, gp_out, acc, part, slots, send_sem, recv_sem = refs[parts:]
    me = meet(n, "tp")
    rows, width = acc.shape
    tiles = width // 128
    arrived, drain = scatter_body(n, me, a_ref, right_refs, acc, part, slots, send_sem, recv_sem)
    gp_out[...] = jnp.zeros_like(gp_out)

    def last(p, carry):
        arrived(p)
        here = pl.ds(pl.multiple_of(p * T, T), T)
        squares = jnp.zeros((T, 128), F32)
        dots = jnp.zeros((T, 128), F32)
        for c in range(tiles):
            cols = slice(c * 128, c * 128 + 128)
            xt = x_ref[pl.ds(p * (T * tiles) + c, T, stride=tiles), :]
            squares = squares + xt * xt
            dots = dots + acc[here, cols] * pg_ref[0:1, cols] * xt
        inv = lax.rsqrt(jnp.sum(squares, axis=1, keepdims=True) / width + EPS)
        inv_b = jnp.broadcast_to(inv, (T, 128))
        mean = jnp.sum(dots, axis=1, keepdims=True) / width
        back_b = jnp.broadcast_to(inv * inv * inv * mean, (T, 128))
        for c in range(tiles):
            cols = slice(c * 128, c * 128 + 128)
            view = pl.ds(p * (T * tiles) + c, T, stride=tiles)
            xt = x_ref[view, :]
            scaled = acc[here, cols] * inv_b
            gx_out[view, :] = do_ref[here, cols] + scaled * pg_ref[0:1, cols] - xt * back_b
            gp_out[:, cols] += row_sums(scaled * xt)
        return carry

    lax.fori_loop(0, rows // T, last, 0)
    drain()


def input_stage(dproj, weights, x_view, d_out, pg, n, collective_id):
    length, width = dproj.shape[0], weights[0].shape[0]
    rows = length // n
    vmem = pl.BlockSpec(memory_space=pltpu.VMEM)
    buffers, sems = scatter_scratch(length, rows, width)
    return pl.pallas_call(
        partial(input_kernel, n, len(weights)),
        out_shape=[jax.ShapeDtypeStruct(x_view.shape, F32), jax.ShapeDtypeStruct((8, width), F32)],
        in_specs=[vmem] * (4 + len(weights)),
        out_specs=[vmem] * 2,
        scratch_shapes=buffers + sems,
        compiler_params=pltpu.CompilerParams(
            collective_id=collective_id, has_side_effects=True, vmem_limit_bytes=62 << 20
        ),
        cost_estimate=pl.CostEstimate(
            flops=2 * length * width * dproj.shape[1], bytes_accessed=400 << 20, transcendentals=0
        ),
        name="input_stage",
    )(dproj, *weights, x_view, d_out, pg)


def token_table(seg):
    length = seg.shape[0]
    segf = seg.astype(F32)
    columns = []
    for d in (1, 2, 3):
        behind = jnp.concatenate([jnp.full((d,), -1, seg.dtype), seg[:-d]])
        columns.append((behind == seg).astype(F32))
    blocks = seg.reshape(length // T, T)
    last = blocks[:, -1]
    prev = jnp.concatenate([jnp.full((1,), -1, seg.dtype), last[:-1]])
    columns.append(segf)
    columns.append((blocks == prev[:, None]).astype(F32).reshape(length))
    columns.append((blocks == last[:, None]).astype(F32).reshape(length))
    for d in (1, 2, 3):
        ahead = jnp.concatenate([seg[d:], jnp.full((d,), -1, seg.dtype)])
        columns.append((ahead == seg).astype(F32))
    stacked = jnp.stack(columns, axis=1)
    tok = jnp.pad(stacked, ((0, 0), (0, 128 - stacked.shape[1])))
    segr = jnp.broadcast_to(segf.reshape(length // T, 1, T), (length // T, 8, T))
    return tok, segr


def local(
    x_in, target, seg_ids, valid, pre_gain, w_z, w_x, w_bc, w_dt, conv_x_w, conv_x_b,
    conv_bc_w, conv_bc_b, dt_bias, a_log, d_skip, norm_gain, w_out,
):
    rows, _, width = x_in.shape
    channels = w_z.shape[1]
    heads = w_dt.shape[1]
    head_dim = channels // heads
    tp = lax.axis_size("tp")
    inner = channels * tp
    bc_local = w_bc.shape[1]
    dp = lax.axis_size("dp")
    x_view = x_in.reshape(rows * width // 128, 128)
    t_view = target.reshape(rows * width // 128, 128)
    bc_params = jnp.pad(jnp.concatenate([conv_bc_w.T, conv_bc_b[None]], axis=0), ((0, 3), (0, 0)))
    w_bc_all, bc_params = share((w_bc.T, bc_params), tp, 4)
    w_bc_all = w_bc_all.reshape(tp * bc_local, -1).T
    bcp = jnp.transpose(bc_params, (1, 0, 2)).reshape(8, tp * bc_local)
    wcs = jnp.concatenate([w_z, w_x, w_bc_all, jnp.pad(w_dt, ((0, 0), (0, 128 - heads)))], axis=1)
    tok, segr = token_table(seg_ids.reshape(-1))
    repeat = lambda v: jnp.repeat(v, head_dim)
    chp = jnp.concatenate(
        [conv_x_w.T, jnp.stack([conv_x_b, repeat(d_skip), norm_gain, jnp.zeros_like(conv_x_b)])], axis=0
    )
    decay_rate = -jnp.exp(a_log)
    hp = jnp.stack([
        jnp.pad(dt_bias, (0, 128 - heads), constant_values=-9.0),
        jnp.pad(decay_rate, (0, 128 - heads)),
    ])
    hp = jnp.pad(hp, ((0, 6), (0, 0)))

    v_rows = jnp.broadcast_to(valid.reshape(rows // T, 1, T).astype(F32), (rows // T, 8, T))
    pg = jnp.broadcast_to(pre_gain[None], (8, width))
    (
        z, xs, xcv, y, bcr, bcv, dtr, bcc, st,
        normed_all, wc, wo, lo_view, d_out, d_branch, rk_own, lost,
    ) = front_stage(x_view, t_view, wcs, w_out.T, pg, tok, segr, chp, bcp, hp, v_rows, tp, dp, inner, 1)
    db_all, rk = gather_rows(d_branch, tp, 2, rk_own)
    dproj, yn, accc, accb, acch = backward(
        db_all, wo, rk, tok, segr, chp, bcp, hp, z, xs, xcv, y, bcr, bcv, dtr, bcc, st
    )

    def dot_tn(a, b):
        return lax.dot_general(a, b, (((0,), (0,)), ((), ())), preferred_element_type=F32)

    g_out = dot_tn(db_all, yn).astype(BF16)
    g_cat = dot_tn(normed_all, dproj).astype(BF16)
    g_out, g_cat, dproj = lax.optimization_barrier((g_out, g_cat, dproj))
    g_out = lax.psum_scatter(g_out, "dp", scatter_dimension=0, tiled=True).astype(F32)
    g_cat = lax.psum_scatter(g_cat, "dp", scatter_dimension=0, tiled=True).astype(F32)
    gx_view, gain_part = input_stage(dproj, (wc,), x_view, d_out, pg, tp, 3)
    grad_wz, grad_wx = g_cat[:, :channels], g_cat[:, channels : 2 * channels]
    grad_wdt = g_cat[:, 2 * channels + 256 : 2 * channels + 256 + heads]
    cols = g_cat[:, 2 * channels : 2 * channels + 256].T.reshape(tp, bc_local, -1)
    per_channel = 7 * channels // 128
    mine = jnp.concatenate([jnp.sum(accc, axis=1).reshape(per_channel, 128), jnp.sum(acch, axis=1)], axis=0)
    mine = jnp.pad(mine, ((0, -mine.shape[0] % 8), (0, 0)))
    lost_rows = jnp.stack([jnp.sum(lost[0:8], axis=0), lost[8]])
    both = jnp.concatenate(
        [jnp.sum(gain_part, axis=0).reshape(width // 128, 128), jnp.sum(accb, axis=1).reshape(10, 128), lost_rows], axis=0
    )
    both = jnp.pad(both, ((0, -both.shape[0] % 8), (0, 0)))
    mine, both, cols = finish(mine, both, cols, dp, tp, 5)
    accc = mine[:per_channel].reshape(7, channels)
    acch = mine[per_channel : per_channel + 2]
    grad_pre = both[: width // 128].reshape(width)
    accb = both[width // 128 : width // 128 + 10].reshape(5, 256)
    accb = lax.dynamic_slice_in_dim(accb, lax.axis_index("tp") * bc_local, bc_local, axis=1)
    sums = jnp.sum(both[width // 128 + 10 : width // 128 + 12], axis=1)
    loss = sums[0] / (jnp.maximum(sums[1], 1.0) * width)
    grad_wbc = cols.T
    return (
        lo_view.reshape(x_in.shape),
        loss,
        gx_view.reshape(x_in.shape),
        grad_pre,
        grad_wz,
        grad_wx,
        grad_wbc,
        grad_wdt,
        accc[0:4].T,
        accc[4],
        accb[0:4].T,
        accb[4],
        acch[0, :heads],
        acch[1, :heads],
        jnp.sum(accc[6].reshape(heads, head_dim), axis=1),
        accc[5],
        g_out.T,
    )


def solution(mesh):
    tok, col, head = P("tp", "dp", None), P("dp", "tp"), P("tp")
    in_specs = (
        tok, tok, P("dp", None), col, P(), col, col, col, col,
        P("tp", None), head, P("tp", None), head, head, head, head, head, P("tp", "dp"),
    )
    out_specs = (
        tok, P(), tok, P(), col, col, col, col,
        P("tp", None), head, P("tp", None), head, head, head, head, head, P("tp", "dp"),
    )
    return jax.shard_map(local, mesh=mesh, in_specs=in_specs, out_specs=out_specs, check_vma=False)
```

```python
from functools import partial

import jax
import jax.numpy as jnp
from jax import lax
from jax.experimental import pallas as pl
from jax.experimental.pallas import tpu as pltpu
from jax.sharding import PartitionSpec as P

T = 128
TB = 256
EPS = 1e-05
LOG2E = 1.4426950408889634
F32 = jnp.float32
BF16 = jnp.bfloat16
ZT = YT = F32
XT = CT = BF16
HIGHEST = lax.Precision.HIGHEST


def dot(a, b, precision=None):
    return jnp.dot(a, b, preferred_element_type=F32, precision=precision)


def dot_nt(a, b):
    return lax.dot_general(a, b, (((1,), (1,)), ((), ())), preferred_element_type=F32)


def lanes(column_of, index, rows=T):
    return jnp.broadcast_to(column_of[:, index : index + 1], (rows, 128))


def iota(shape, axis):
    return lax.broadcasted_iota(jnp.int32, shape, axis)


def step_sizes(raw, hp_ref):
    shifted = raw + hp_ref[0:1, :]
    dt = jnp.maximum(shifted, 0.0) + jnp.log1p(jnp.exp(-jnp.abs(shifted)))
    la = dt * hp_ref[1:2, :]
    inclusive = (iota((T, T), 0) >= iota((T, T), 1)).astype(F32)
    cum = dot(inclusive, la * LOG2E, HIGHEST)
    return shifted, dt, la, cum


def split_pair(value):
    first = iota((T, 128), 1) < 64
    zero = jnp.zeros_like(value)
    return jnp.concatenate([jnp.where(first, value, zero), jnp.where(first, zero, value)], axis=0)


def eye():
    return iota((T, T), 0) == iota((T, T), 1)


def column(row):
    return jnp.sum(jnp.where(eye(), jnp.broadcast_to(row, (T, T)), 0.0), axis=1, keepdims=True)


def row(col):
    return jnp.sum(jnp.where(eye(), jnp.broadcast_to(col, (T, T)), 0.0), axis=0, keepdims=True)


def document_columns(seg_ref, segc, segf):
    length = segc.shape[0] - 16
    segf[...] = seg_ref[...].astype(F32)
    segc[0:8, :] = jnp.full((8, 128), -1.0, F32)
    segc[length + 8 : length + 16, :] = jnp.full((8, 128), -1.0, F32)

    def chunk(i, carry):
        here = pl.ds(pl.multiple_of(i * T + 8, 8), T)
        segc[here, :] = jnp.broadcast_to(column(segf[pl.ds(i, 1), :]), (T, 128))
        return carry

    lax.fori_loop(0, length // T, chunk, 0)


def row_sums(value):
    return jnp.sum(value.reshape(value.shape[0] // 8, 8, value.shape[1]), axis=0)


def backward_block(
    t, block, dball, wo_ref, rk_all, segc, segf, chp_ref, bcp_ref, hp_ref,
    z_ref, xs_ref, xcv_ref, y_ref, bcr_ref, bcv_ref, dtr_ref, bcc_ref, st_ref,
    dproj_out, yn_out, accc_out, accb_out, acch_out,
    dyn, dbuf, dbcbuf, dstate, dstate_b, dyec, xte, cs_rows, fold, pick,
):
    channels = wo_ref.shape[0]
    pairs = channels // 128
    start = pl.multiple_of(block * TB, TB)
    for n in range(channels // 256):
        cols = slice(n * 256, n * 256 + 256)
        dyn[:, cols] = dot_nt(dball[pl.ds(start, TB), :], wo_ref[cols, :])
    first = iota((T, 128), 1) < 64
    for c in reversed(range(TB // T)):
        r0 = c * T
        rows = slice(r0, r0 + T)
        chunk = block * (TB // T) + c
        near = segc[pl.ds(pl.multiple_of(start + r0, T), T + 16), :]
        seg_col = near[8 : T + 8, :]
        ahead = [(near[8 + d : 8 + d + T, :] == seg_col).astype(F32) for d in (1, 2, 3)]
        start_b = (seg_col == near[7:8, :]).astype(F32)
        end_b = (seg_col == near[T + 7 : T + 8, :]).astype(F32)
        rg_b = jnp.broadcast_to(column(rk_all[chunk, 0:1, :]), (T, 128))
        kc_b = jnp.broadcast_to(column(rk_all[chunk, 1:2, :]), (T, 128))
        bm, cm = bcc_ref[rows, 0:128], bcc_ref[rows, 128:256]
        ct = cm.T
        shifted, dt, la, cum = step_sizes(dtr_ref[rows, :], hp_ref)
        cum_t = cum.T
        scores, scores_t = dot_nt(cm, bm), dot_nt(bm, cm)
        same = seg_col == segf[pl.ds(chunk, 1), :]
        below = iota((T, T), 0) >= iota((T, T), 1)
        strict = iota((T, T), 0) > iota((T, T), 1)
        above = iota((T, T), 0) <= iota((T, T), 1)
        qs = jnp.where(same & strict, scores, 0.0)
        qt = jnp.where(same & above, scores_t, 0.0)
        dstate_b[...] = dstate[...].astype(BF16)
        dq = jnp.zeros((T, T), F32)
        rsum = jnp.zeros((T, 128), F32)
        ddt = jnp.zeros((T, 128), F32)
        xsum = jnp.zeros((T, 128), F32)
        ksum = jnp.zeros((16, 128), F32)
        for j in range(pairs):
            cols = slice(j * 128, j * 128 + 128)
            zz = z_ref[rows, cols].astype(F32)
            y = y_ref[rows, cols].astype(F32)
            sz = 0.5 + 0.5 * jnp.tanh(0.5 * zz)
            silu_z = zz * sz
            dsz = sz + silu_z * (1.0 - sz)
            g = y * silu_z
            gr = g * rg_b
            gain = chp_ref[6:7, cols]
            dynp = dyn[rows, cols]
            yn_out[rows, cols] = (gr * gain).astype(BF16)
            accc_out[5, :, cols] += row_sums(dynp * gr)
            dg = rg_b * dynp * gain - g * kc_b
            dy = dg * silu_z
            dproj_out[rows, cols] = (dg * y * dsz).astype(BF16)
            xcv = xcv_ref[rows, cols].astype(F32)
            sx = 0.5 + 0.5 * jnp.tanh(0.5 * xcv)
            xc = xcv * sx
            dsx = sx + xc * (1.0 - sx)
            accc_out[6, :, cols] += row_sums(dy * xc)
            dt_e = jnp.where(first, lanes(dt, 2 * j), lanes(dt, 2 * j + 1))
            ca, cb = lanes(cum, 2 * j), lanes(cum, 2 * j + 1)
            cum_e = jnp.where(first, ca, cb)
            into = jnp.exp2(cum_e) * start_b
            to_end = jnp.exp2(cum_e[T - 1 : T, :] - cum_e) * end_b
            decay = into[T - 1 : T, :]
            xdt = xc * dt_e
            dy_b = dy.astype(BF16)
            ga = ca - cum_t[2 * j : 2 * j + 1, :]
            gb = cb - cum_t[2 * j + 1 : 2 * j + 2, :]
            grad = dot_nt(dy_b, split_pair(xdt.astype(BF16)))
            gea = grad[:, :128] * jnp.exp2(jnp.minimum(ga, 0.0))
            geb = grad[:, 128:] * jnp.exp2(jnp.minimum(gb, 0.0))
            dq = dq + gea + geb
            pp = jnp.concatenate([(gea * qs).astype(BF16), (geb * qs).astype(BF16)], axis=1)
            rsum = rsum + dot(pp, pick[j, :, :])
            csum = dot(jnp.ones((8, T), BF16), pp)
            cs_rows[2 * j : 2 * j + 1, :] = csum[0:1, :128]
            cs_rows[2 * j + 1 : 2 * j + 2, :] = csum[0:1, 128:]
            eta = (jnp.exp2(jnp.minimum(-ga, 0.0)) * qt).astype(BF16)
            etb = (jnp.exp2(jnp.minimum(-gb, 0.0)) * qt).astype(BF16)
            dxdt = dot(jnp.concatenate([eta, etb], axis=1), split_pair(dy_b))
            dx_state = to_end * dot(bm, dstate_b[:, cols])
            dxdt = dxdt + dx_state
            y_in = into * dot(cm, st_ref[c, :, cols])
            dyec_p = (dy * into).astype(BF16)
            dyec[:, cols] = dyec_p
            xte[:, cols] = (xdt * to_end).astype(BF16)
            ddt = ddt + dot((xc * dxdt).astype(BF16), fold[j, :, :])
            rsum = rsum + dot((dy * y_in).astype(BF16), fold[j, :, :])
            xsum = xsum + dot((xdt * dx_state).astype(BF16), fold[j, :, :])
            old = dstate[:, cols]
            kpart = row_sums(old * st_ref[c, :, cols].astype(F32)) * decay
            khigh = kpart.astype(BF16)
            klow = (kpart - khigh.astype(F32)).astype(BF16)
            ksum = ksum + dot(jnp.concatenate([khigh, klow], axis=0), fold[j, :, :])
            dstate[:, cols] = old * decay + dot(ct, dyec_p)
            dxcv = (dxdt * dt_e + chp_ref[5:6, cols] * dy) * dsx
            dbuf[0:T, cols] = dxcv
            xs = xs_ref[rows, cols].astype(F32)
            dxs = dxcv * chp_ref[3:4, cols]
            accc_out[4, :, cols] += row_sums(dxcv)
            accc_out[3, :, cols] += row_sums(dxcv * xs)
            for d in (1, 2, 3):
                moved = dbuf[d : d + T, cols] * ahead[d - 1]
                dxs = dxs + moved * chp_ref[3 - d : 4 - d, cols]
                accc_out[3 - d, :, cols] += row_sums(moved * xs)
            dproj_out[rows, channels + j * 128 : channels + j * 128 + 128] = dxs.astype(BF16)
        dbuf[T : T + 8, :] = dbuf[0:8, :]
        dqm = jnp.where(same & below, dq, 0.0)
        dc = dot(dqm.astype(BF16), bm) + dot_nt(dyec[...], st_ref[c, :, :])
        db_rows = dot(dqm.T.astype(BF16), cm) + dot_nt(xte[...], dstate_b[...])
        for half, grad_half in enumerate((db_rows, dc)):
            cols = slice(half * 128, half * 128 + 128)
            raw = bcv_ref[rows, cols].astype(F32)
            sb = 0.5 + 0.5 * jnp.tanh(0.5 * raw)
            dcv = grad_half * (sb + raw * sb * (1.0 - sb))
            dbcbuf[0:T, cols] = dcv
            xs = bcr_ref[rows, cols].astype(F32)
            dxs = dcv * bcp_ref[3:4, cols]
            accb_out[4, :, cols] += row_sums(dcv)
            accb_out[3, :, cols] += row_sums(dcv * xs)
            for d in (1, 2, 3):
                moved = dbcbuf[d : d + T, cols] * ahead[d - 1]
                dxs = dxs + moved * bcp_ref[3 - d : 4 - d, cols]
                accb_out[3 - d, :, cols] += row_sums(moved * xs)
            dproj_out[rows, 2 * channels + half * 128 : 2 * channels + half * 128 + 128] = dxs.astype(BF16)
        dbcbuf[T : T + 8, :] = dbcbuf[0:8, :]
        after = (iota((T, T), 0) <= iota((T, T), 1)).astype(F32)
        before = (iota((T, T), 0) > iota((T, T), 1)).astype(F32)
        dla = dot(after, rsum - cs_rows[...].T, HIGHEST) + dot(before, xsum, HIGHEST)
        dla = dla + jnp.sum(ksum, axis=0, keepdims=True)
        ddtr = (ddt + dla * hp_ref[1:2, :]) * (0.5 + 0.5 * jnp.tanh(0.5 * shifted))
        acch_out[0, :, :] += row_sums(ddtr)
        acch_out[1, :, :] += row_sums(dla * la)
        dproj_out[rows, 2 * channels + 256 : 2 * channels + 384] = ddtr.astype(BF16)


MESH_ID = pl.DeviceIdType.MESH


def meet(n, axis):
    me = lax.axis_index(axis)
    barrier = pltpu.get_barrier_semaphore()
    for peer in range(n):

        @pl.when(me != peer)
        def _():
            pl.semaphore_signal(barrier, inc=1, device_id={axis: peer}, device_id_type=MESH_ID)

    pl.semaphore_wait(barrier, n - 1)
    return me


def to_peer(source, target, send_sem, recv_sem, axis, peer):
    return pltpu.make_async_remote_copy(
        src_ref=source, dst_ref=target, send_sem=send_sem, recv_sem=recv_sem,
        device_id={axis: peer}, device_id_type=MESH_ID,
    )


def copy_kernel(first, second, first_out, second_out):
    first_out[...] = first[...]
    second_out[...] = second[...]


def plain_copies(first, second):
    block = pl.BlockSpec((first.shape[0] // 8, 128), lambda i: (i, 0))
    same = jax.ShapeDtypeStruct(first.shape, first.dtype)
    return pl.pallas_call(
        copy_kernel, grid=(8,), in_specs=[block] * 2, out_specs=[block] * 2, out_shape=[same] * 2, name="plain_copies"
    )(first, second)


def finish_kernel(dp, tp, mine, both, cols, mine_out, both_out, cols_out, got, got_both, got_cols, sems):
    me_dp, me_tp = lax.axis_index("dp"), lax.axis_index("tp")
    barrier = pltpu.get_barrier_semaphore()
    for peer in range(dp):

        @pl.when(me_dp != peer)
        def _():
            pl.semaphore_signal(barrier, inc=1, device_id={"dp": peer}, device_id_type=MESH_ID)

    for peer in range(tp):

        @pl.when(me_tp != peer)
        def _():
            pl.semaphore_signal(barrier, inc=1, device_id={"tp": peer}, device_id_type=MESH_ID)

    pl.semaphore_wait(barrier, dp - 1 + tp - 1)
    first = mine.shape[0]
    got[pl.ds(me_dp, 1), 0:first, :] = mine[...][None]
    got[pl.ds(me_dp, 1), first:, :] = both[...][None]

    def over_dp(peer, slot):
        return to_peer(got.at[me_dp], got.at[slot], sems.at[0, peer], sems.at[1, slot], "dp", peer)

    def over_tp(peer, slot):
        return to_peer(got_both.at[me_tp], got_both.at[slot], sems.at[2, peer], sems.at[3, slot], "tp", peer)

    def over_cols(peer, slot):
        return to_peer(cols.at[peer], got_cols.at[slot], sems.at[4, peer], sems.at[5, slot], "tp", peer)

    for peer in range(dp):

        @pl.when(me_dp != peer)
        def _():
            over_dp(peer, me_dp).start()

    for peer in range(tp):

        @pl.when(me_tp != peer)
        def _():
            over_cols(peer, me_tp).start()

    got_cols[pl.ds(me_tp, 1)] = cols[pl.ds(me_tp, 1)]
    for peer in range(dp):

        @pl.when(me_dp != peer)
        def _():
            over_dp(peer, peer).wait_recv()

    total = got[0]
    for peer in range(1, dp):
        total = total + got[peer]
    mine_out[...] = total[:first]
    got_both[pl.ds(me_tp, 1)] = total[first:][None]
    for peer in range(tp):

        @pl.when(me_tp != peer)
        def _():
            over_tp(peer, me_tp).start()

    for peer in range(tp):

        @pl.when(me_tp != peer)
        def _():
            over_cols(peer, peer).wait_recv()
            over_tp(peer, peer).wait_recv()

    total, columns = got_both[0], got_cols[0]
    for peer in range(1, tp):
        total, columns = total + got_both[peer], columns + got_cols[peer]
    both_out[...] = total
    cols_out[...] = columns
    for peer in range(dp):

        @pl.when(me_dp != peer)
        def _():
            over_dp(peer, me_dp).wait_send()

    for peer in range(tp):

        @pl.when(me_tp != peer)
        def _():
            over_cols(peer, me_tp).wait_send()
            over_tp(peer, me_tp).wait_send()


def finish(mine, both, cols, dp, tp, collective_id):
    vmem = pl.BlockSpec(memory_space=pltpu.VMEM)
    rows = mine.shape[0] + both.shape[0]
    return pl.pallas_call(
        partial(finish_kernel, dp, tp),
        out_shape=[
            jax.ShapeDtypeStruct(mine.shape, F32),
            jax.ShapeDtypeStruct(both.shape, F32),
            jax.ShapeDtypeStruct(cols.shape[1:], F32),
        ],
        in_specs=[vmem] * 3,
        out_specs=[vmem] * 3,
        scratch_shapes=[
            pltpu.VMEM((dp, rows, 128), F32),
            pltpu.VMEM((tp,) + both.shape, F32),
            pltpu.VMEM(cols.shape, F32),
            pltpu.SemaphoreType.DMA((6, max(dp, tp))),
        ],
        compiler_params=pltpu.CompilerParams(collective_id=collective_id, has_side_effects=True),
        name="finish",
    )(mine, both, cols)


def back_kernel(
    n, db_ref, rk_ref, seg_ref, chp_ref, bcp_ref, hp_ref, wo_any,
    z_any, xs_any, xcv_any, y_any, bcr_any, bcv_any, dtr_any, bcc_any, st_any,
    dproj_any, yn_any, dball_any, accc_out, accb_out, acch_out,
    dball, rk_all, wo, zb, xsb, xcvb, yb, bcrb, bcvb, dtrb, bccb, stb, dprojb, ynb,
    dyn, dbuf, dbcbuf, dstate, dstate_b, dyec, xte, cs_rows, fold, pick, segc, segf,
    keep_sem, load_sem, save_sem, ag_send, ag_recv, r_send, r_recv,
):
    rows = db_ref.shape[0]
    pieces = rows // T
    gps = rows // TB
    subs = TB // T
    blocks = n * gps
    pairs = wo.shape[0] // 128
    sources = (z_any, xs_any, xcv_any, y_any, bcr_any, bcv_any, dtr_any, bcc_any, st_any)
    held = (zb, xsb, xcvb, yb, bcrb, bcvb, dtrb, bccb, stb)

    def load(i, t):
        block = blocks - 1 - t
        step = subs if i == len(held) - 1 else TB
        there = sources[i].at[pl.ds(pl.multiple_of(block * step, step), step)]
        return pltpu.make_async_copy(there, held[i].at[t % 2], load_sem.at[i, t % 2])

    fetch = pltpu.make_async_copy(wo_any, wo, keep_sem.at[0])
    fetch.start()
    own_rows = pl.ds(pl.multiple_of(lax.axis_index("tp") * rows, rows), rows)
    keep = pltpu.make_async_copy(db_ref, dball.at[own_rows], keep_sem.at[1])
    keep.start()
    for i in range(len(held)):
        load(i, 0).start()
    me = meet(n, "tp")

    def rk_to(peer, owner):
        return to_peer(rk_ref, rk_all.at[pl.ds(owner * pieces, pieces)], r_send.at[peer], r_recv.at[owner], "tp", peer)

    for peer in range(n):

        @pl.when(me != peer)
        def _():
            rk_to(peer, me).start()

    rk_all[pl.ds(me * pieces, pieces)] = rk_ref[...]

    def ag(way, index):
        here = dball.at[pl.ds(pl.multiple_of(index * T, T), T)]
        peer = me + 1 if way == 0 else me - 1
        return to_peer(here, here, ag_send.at[way, index], ag_recv.at[way, index], "tp", peer)

    keep.wait()
    mirror = n - 1 - me
    for o in range(gps):
        for sub in range(subs):
            index = ((me + 1) * gps - 1 - o) * subs + sub

            @pl.when(me < n - 1)
            def _():
                ag(0, index).start()

            @pl.when((me > 0) & ((mirror == 0) | (mirror > o)))
            def _():
                ag(1, index).start()

    def relay(k):
        for sub in range(subs):
            high = (blocks - 1 - k) * subs + sub

            @pl.when(k < mirror * gps)
            def _():
                ag(1, high).wait_recv()

                @pl.when(me > 0)
                def _():
                    ag(1, high).start()

            low = (me * gps - 1 - k) * subs + sub

            @pl.when(me * gps - 1 - k >= 0)
            def _():
                ag(0, low).wait_recv()

                @pl.when(me < n - 1)
                def _():
                    ag(0, low).start()

        @pl.when((k == mirror * gps - 1) & (me > 0))
        def _():
            for o in range(gps):

                @pl.when(mirror <= o)
                def _():
                    for sub in range(subs):
                        ag(1, ((me + 1) * gps - 1 - o) * subs + sub).start()

    document_columns(seg_ref, segc, segf)
    dstate[...] = jnp.zeros_like(dstate)
    dbuf[...] = jnp.zeros_like(dbuf)
    dbcbuf[...] = jnp.zeros_like(dbcbuf)
    accc_out[...] = jnp.zeros_like(accc_out)
    accb_out[...] = jnp.zeros_like(accb_out)
    acch_out[...] = jnp.zeros_like(acch_out)
    cs_rows[...] = jnp.zeros_like(cs_rows)
    for j in range(pairs):
        half = (iota((128, 128), 0) >= 64).astype(jnp.int32)
        fold[j, :, :] = (iota((128, 128), 1) == 2 * j + half).astype(F32).astype(BF16)
        part = (iota((256, 128), 0) >= 128).astype(jnp.int32)
        pick[j, :, :] = (iota((256, 128), 1) == 2 * j + part).astype(F32).astype(BF16)
    for peer in range(n):

        @pl.when(me != peer)
        def _():
            rk_to(peer, peer).wait_recv()

    fetch.wait()
    relay(0)

    def save(i, t):
        block = blocks - 1 - t
        source, target = ((dprojb, dproj_any), (ynb, yn_any))[i]
        return pltpu.make_async_copy(source, target.at[pl.ds(pl.multiple_of(block * TB, TB), TB)], save_sem.at[i])

    def turn(t, carry):
        @pl.when(t + 1 < blocks)
        def _():
            for i in range(len(held)):
                load(i, t + 1).start()

        for i in range(len(held)):
            load(i, t).wait()

        @pl.when(t > 0)
        def _():
            for i in range(2):
                save(i, t - 1).wait()

        slot = t % 2
        backward_block(
            t, blocks - 1 - t, dball, wo, rk_all, segc, segf, chp_ref, bcp_ref, hp_ref,
            zb.at[slot], xsb.at[slot], xcvb.at[slot], yb.at[slot], bcrb.at[slot], bcvb.at[slot],
            dtrb.at[slot], bccb.at[slot], stb.at[slot],
            dprojb, ynb, accc_out, accb_out, acch_out,
            dyn, dbuf, dbcbuf, dstate, dstate_b, dyec, xte, cs_rows, fold, pick,
        )
        for i in range(2):
            save(i, t).start()

        @pl.when(t + 1 < blocks - gps)
        def _():
            relay(t + 1)

        return carry

    lax.fori_loop(0, blocks, turn, 0)
    keep_all = pltpu.make_async_copy(dball, dball_any, keep_sem.at[2])
    keep_all.start()
    for i in range(2):
        save(i, blocks - 1).wait()

    def drain(index, carry):
        block = index // subs

        @pl.when((me < n - 1) & (block < (me + 1) * gps))
        def _():
            ag(0, index).wait_send()

        @pl.when((me > 0) & (block >= me * gps))
        def _():
            ag(1, index).wait_send()

        return carry

    lax.fori_loop(0, n * pieces, drain, 0)
    for peer in range(n):

        @pl.when(me != peer)
        def _():
            rk_to(peer, me).wait_send()

    keep_all.wait()


def back_stage(db, rk, seg, chp, bcp, hp, wo, saved, n, collective_id):
    rows, width = db.shape
    length = n * rows
    channels = wo.shape[0]
    pairs = channels // 128
    total = 2 * channels + 384
    shape = jax.ShapeDtypeStruct
    vmem = pl.BlockSpec(memory_space=pltpu.VMEM)
    anywhere = pl.BlockSpec(memory_space=pl.ANY)
    dma = pltpu.SemaphoreType.DMA
    held = [pltpu.VMEM((2, TB) + item.shape[1:], item.dtype) for item in saved[:-1]]
    held.append(pltpu.VMEM((2, TB // T, 128, channels), BF16))
    return pl.pallas_call(
        partial(back_kernel, n),
        out_shape=[
            shape((length, total), BF16), shape((length, channels), BF16), shape((length, width), BF16),
            shape((7, 8, channels), F32), shape((5, 8, 256), F32), shape((2, 8, 128), F32),
        ],
        in_specs=[anywhere] + [vmem] * 5 + [anywhere] * 10,
        out_specs=[anywhere] * 3 + [vmem] * 3,
        scratch_shapes=[
            pltpu.VMEM((length, width), BF16),
            pltpu.VMEM((length // T, 8, 128), F32),
            pltpu.VMEM(wo.shape, BF16),
        ] + held + [
            pltpu.VMEM((TB, total), BF16),
            pltpu.VMEM((TB, channels), BF16),
            pltpu.VMEM((TB, channels), F32),
            pltpu.VMEM((T + 8, channels), F32),
            pltpu.VMEM((T + 8, 256), F32),
            pltpu.VMEM((128, channels), F32),
            pltpu.VMEM((128, channels), BF16),
            pltpu.VMEM((T, channels), BF16),
            pltpu.VMEM((T, channels), BF16),
            pltpu.VMEM((128, 128), F32),
            pltpu.VMEM((pairs, 128, 128), BF16),
            pltpu.VMEM((pairs, 256, 128), BF16),
            pltpu.VMEM((length + 16, 128), F32),
            pltpu.VMEM((length // T, 128), F32),
            dma((3,)), dma((9, 2)), dma((2,)),
            dma((2, length // T)), dma((2, length // T)), dma((n,)), dma((n,)),
        ],
        compiler_params=pltpu.CompilerParams(
            collective_id=collective_id, has_side_effects=True, vmem_limit_bytes=60 << 20
        ),
        name="back_stage",
    )(db, rk, seg, chp, bcp, hp, wo, *saved)


def scatter_body(n, me, a_ref, right_refs, acc, part, slots, send_sem, recv_sem):
    rows, width = acc.shape
    group = part.shape[0]
    piece = slots.shape[2]
    pieces = rows // piece
    groups = rows // group
    subs = group // piece

    def link(way, index):
        peer = me + 1 if way == 0 else me - 1
        return to_peer(
            slots.at[way, index], slots.at[way, index], send_sem.at[way, index], recv_sem.at[way, index], "tp", peer
        )

    def own(start, target, base):
        def tile(i, carry):
            cols = pl.ds(pl.multiple_of(i * 256, 256), 256)
            total, at = None, 0
            for w_ref in right_refs:
                depth = w_ref.shape[1]
                term = dot_nt(a_ref[pl.ds(start, group), at : at + depth], w_ref[cols, :])
                total = term if total is None else total + term
                at += depth
            target[pl.ds(base, group), cols] = total
            return carry

        lax.fori_loop(0, width // 256, tile, 0)

    def pass_on(way, q, at_end):
        shard = n - 1 - q // groups if way == 0 else q // groups
        start = pl.multiple_of(shard * rows + (q % groups) * group, group)
        own(start, part, 0)
        for sub in range(subs):
            index = shard * pieces + (q % groups) * subs + sub
            here = slice(sub * piece, (sub + 1) * piece)

            @pl.when(at_end)
            def _():
                slots[way, index] = part[here, :].astype(BF16)

            @pl.when(jnp.logical_not(at_end))
            def _():
                link(way, index).wait_recv()
                slots[way, index] = (part[here, :] + slots[way, index].astype(F32)).astype(BF16)

            link(way, index).start()

    def turn(t, carry):
        for way in (0, 1):
            hops = me if way == 0 else n - 1 - me
            q = t - hops

            @pl.when((q >= 0) & (q < (n - 1 - hops) * groups))
            def _():
                pass_on(way, q, hops == 0)

        late = t - (n - 1)

        @pl.when((late >= 0) & (late < groups))
        def _():
            base = pl.multiple_of(late * group, group)
            own(pl.multiple_of(me * rows + late * group, group), acc, base)

        return carry

    lax.fori_loop(0, (n - 1) * groups + n - 1, turn, 0)

    def arrived(p):
        for way in (0, 1):

            @pl.when((me > 0) if way == 0 else (me < n - 1))
            def _():
                link(way, me * pieces + p).wait_recv()
                here = pl.ds(pl.multiple_of(p * piece, piece), piece)
                acc[here, :] += slots[way, me * pieces + p].astype(F32)

    def drain():
        def done(index, carry):
            shard = index // pieces
            for way in (0, 1):

                @pl.when((me < shard) if way == 0 else (me > shard))
                def _():
                    link(way, index).wait_send()

            return carry

        lax.fori_loop(0, n * pieces, done, 0)

    return arrived, drain


def forward_block(
    t, nb, wc, segc, segf, chp_ref, bcp_ref, hp_ref,
    zbuf, xs_out, xcv_out, y_out, u_all, bcr_out, bcv_out, dtr_out, bcc_out, st_out, sq_all,
    xbuf, bcbuf, state,
):
    channels = zbuf.shape[1]
    pairs = channels // 128
    start = pl.multiple_of(t * TB, TB)
    nb_rows = pl.ds(start, TB)
    for n in range(channels // 256):
        cols = slice(n * 256, n * 256 + 256)
        zbuf[:, cols] = dot(nb[nb_rows, :], wc[:, cols])
        xbuf[8 : 8 + TB, cols] = dot(nb[nb_rows, :], wc[:, channels + n * 256 : channels + n * 256 + 256])
    bd = dot(nb[nb_rows, :], wc[:, 2 * channels :])
    bcbuf[8 : 8 + TB, :] = bd[:, :256]
    dtr_out[...] = bd[:, 256:]
    bcr_out[...] = bd[:, :256].astype(BF16)
    first = iota((T, 128), 1) < 64
    for c in range(TB // T):
        r0 = c * T
        rows = slice(r0, r0 + T)
        chunk = t * (TB // T) + c
        at = pl.ds(pl.multiple_of(start + r0, T), T)
        near = segc[pl.ds(pl.multiple_of(start + r0, T), T + 8), :]
        seg_col = near[8:, :]
        masks = [(near[8 - d : 8 - d + T, :] == seg_col).astype(F32) for d in (1, 2, 3)]
        start_b = (seg_col == near[7:8, :]).astype(F32)
        end_b = (seg_col == near[T + 7 : T + 8, :]).astype(F32)
        parts = []
        for half in range(2):
            cols = slice(half * 128, half * 128 + 128)
            acc = bcbuf[8 + r0 : 8 + r0 + T, cols] * bcp_ref[3:4, cols] + bcp_ref[4:5, cols]
            for d in (1, 2, 3):
                acc = acc + bcbuf[8 + r0 - d : 8 + r0 - d + T, cols] * bcp_ref[3 - d : 4 - d, cols] * masks[d - 1]
            bcv_out[rows, cols] = acc.astype(BF16)
            hv = 0.5 * acc
            parts.append((hv + hv * jnp.tanh(hv)).astype(BF16))
            bcc_out[rows, cols] = parts[-1]
        bm, cm = parts
        bt = bm.T
        _, dt, la, cum = step_sizes(dtr_out[rows, :], hp_ref)
        cum_t = cum.T
        scores = dot_nt(cm, bm)
        keep = (seg_col == segf[pl.ds(chunk, 1), :]) & (iota((T, T), 0) >= iota((T, T), 1))
        qm = jnp.where(keep, scores, 0.0)
        sq = jnp.zeros((T, 128), F32)
        st_out[c, :, :] = state[...].astype(BF16)
        for j in range(pairs):
            cols = slice(j * 128, j * 128 + 128)
            acc = xbuf[8 + r0 : 8 + r0 + T, cols] * chp_ref[3:4, cols] + chp_ref[4:5, cols]
            xs_out[rows, cols] = xbuf[8 + r0 : 8 + r0 + T, cols].astype(BF16)
            for d in (1, 2, 3):
                acc = acc + xbuf[8 + r0 - d : 8 + r0 - d + T, cols] * chp_ref[3 - d : 4 - d, cols] * masks[d - 1]
            xcv_out[rows, cols] = acc.astype(BF16)
            hv = 0.5 * acc
            xc = hv + hv * jnp.tanh(hv)
            dt_e = jnp.where(first, lanes(dt, 2 * j), lanes(dt, 2 * j + 1))
            ca, cb = lanes(cum, 2 * j), lanes(cum, 2 * j + 1)
            cum_e = jnp.where(first, ca, cb)
            xdt = xc * dt_e
            ea = jnp.exp2(jnp.minimum(ca - cum_t[2 * j : 2 * j + 1, :], 0.0))
            eb = jnp.exp2(jnp.minimum(cb - cum_t[2 * j + 1 : 2 * j + 2, :], 0.0))
            mix = jnp.concatenate([(ea * qm).astype(BF16), (eb * qm).astype(BF16)], axis=1)
            y = dot(mix, split_pair(xdt.astype(BF16)))
            into = jnp.exp2(cum_e) * start_b
            last = cum_e[T - 1 : T, :]
            to_end = jnp.exp2(last - cum_e) * end_b
            y = y + into * dot(cm, st_out[c, :, cols])
            state[:, cols] = state[:, cols] * into[T - 1 : T, :] + dot(bt, (xdt * to_end).astype(BF16))
            y = y + chp_ref[5:6, cols] * xc
            y_out[rows, cols] = y
            hz = 0.5 * zbuf[rows, cols]
            g = y * (hz + hz * jnp.tanh(hz))
            sq = sq + g * g
            u_all[at, cols] = (g * chp_ref[6:7, cols]).astype(BF16)
        sq_all[chunk, :, :] = lax.dot_general(
            jnp.ones((8, 128), F32), sq, (((1,), (1,)), ((), ())), preferred_element_type=F32, precision=HIGHEST
        )
    xbuf[0:8, :] = xbuf[TB : TB + 8, :]
    bcbuf[0:8, :] = bcbuf[TB : TB + 8, :]


def front_kernel(
    n, dp, inner,
    x_ref, t_ref, wz_ref, wx_ref, wos_ref, bct_ref, dtt_ref, bp_ref, pg_ref, seg_ref, cw_ref, cb_ref, gain_ref, hp_ref, v_ref,
    z_out, xs_out, xcv_out, y_out, bcr_out, bcv_out, dtr_out, bcc_out, st_out,
    nb_out, wc_out, wo_out, lo_out, do_out, db_out, rk_out, loss_out, chp_out, bcp_out, hp_out,
    nb, wc, wo, u_all, slots, acc, part,
    zbuf, xsb, xcvb, yb, bcrb, bcvb, dtrb, bccb, stb,
    xbuf, bcbuf, state, sq_all, sqs, xst, tst, lost_buf, dob, dbb,
    segc, segf, bc_all, bp_all, wbd,
    load_sem, keep_sem, save_sem, s_send, s_recv, w_send, w_pass, w_recv, ag_send, ag_recv, rs_send, rs_recv, q_send, q_recv,
):
    me, me_dp = lax.axis_index("tp"), lax.axis_index("dp")
    rows, width = acc.shape
    pieces = rows // T
    tiles = width // 128
    gps = rows // TB
    subs = TB // T
    blocks = n * gps
    share_rows = wz_ref.shape[0]
    channels = wz_ref.shape[1]
    pairs = channels // 128
    barrier = pltpu.get_barrier_semaphore()
    for peer in range(dp):

        @pl.when(me_dp != peer)
        def _():
            pl.semaphore_signal(barrier, inc=1, device_id={"dp": peer}, device_id_type=MESH_ID)

    for peer in range(n):

        @pl.when(me != peer)
        def _():
            pl.semaphore_signal(barrier, inc=1, device_id={"tp": peer}, device_id_type=MESH_ID)

    def load(source, target, slot, p):
        view = source.at[pl.ds(pl.multiple_of(p * (T * tiles), T * tiles), T * tiles)]
        return pltpu.make_async_copy(view, target.at[slot], load_sem.at[0 if target is xst else 1, slot])

    load(x_ref, xst, 0, 0).start()

    def place(i, owner):
        at = pl.ds(pl.multiple_of(owner * share_rows, share_rows), share_rows)
        if i == 0:
            return wc.at[at, 0:channels]
        if i == 1:
            return wc.at[at, channels : 2 * channels]
        if i == 2:
            return wc.at[at, 2 * channels : 2 * channels + 384]
        return wo.at[:, at]

    local = (wz_ref, wx_ref, wbd, wos_ref)

    def keep_own(i):
        return pltpu.make_async_copy(local[i], place(i, me_dp), keep_sem.at[3 + i])

    for i in (0, 1, 3):
        keep_own(i).start()
    state[...] = jnp.zeros_like(state)
    xbuf[0:8, :] = jnp.zeros((8, xbuf.shape[1]), F32)
    bcbuf[0:8, :] = jnp.zeros((8, 256), F32)
    pl.semaphore_wait(barrier, dp - 1 + n - 1)

    core = me_dp % 2
    chip = me_dp // 2
    sibling = me_dp + 1 - 2 * core

    def give(i, peer):
        return to_peer(local[i], place(i, me_dp), w_send.at[i, peer], w_recv.at[i, me_dp], "dp", peer)

    def passed(i, owner):
        there = place(i, owner)
        return to_peer(there, there, w_pass.at[i, owner], w_recv.at[i, owner], "dp", sibling)

    def give_all(i):
        for k in range(dp // 2):

            @pl.when(chip != k)
            def _():
                give(i, 2 * k + core).start()

        give(i, sibling).start()

    def pass_all(i):
        for k in range(dp // 2):

            @pl.when(chip != k)
            def _():
                passed(i, 2 * k + core).wait_recv()
                passed(i, 2 * k + core).start()

    def wait_all(i):
        keep_own(i).wait()
        passed(i, sibling).wait_recv()
        for k in range(dp // 2):

            @pl.when(chip != k)
            def _():
                passed(i, 2 * k + 1 - core).wait_recv()

    def swap(i, peer, slot):
        source, target = ((bct_ref, bc_all), (bp_ref, bp_all))[i]
        return to_peer(source, target.at[slot], s_send.at[i, peer], s_recv.at[i, slot], "tp", peer)

    for peer in range(n):

        @pl.when(me != peer)
        def _():
            swap(0, peer, me).start()
            swap(1, peer, me).start()

    bc_all[pl.ds(me, 1)] = bct_ref[...][None]
    bp_all[pl.ds(me, 1)] = bp_ref[...][None]
    give_all(1)
    give_all(0)

    def ag(way, index):
        here = nb.at[pl.ds(pl.multiple_of(index * T, T), T)]
        peer = me + 1 if way == 0 else me - 1
        return to_peer(here, here, ag_send.at[way, index], ag_recv.at[way, index], "tp", peer)

    for p in range(pieces):
        load(x_ref, xst, p % 2, p).wait()
        if p + 1 < pieces:
            load(x_ref, xst, (p + 1) % 2, p + 1).start()
        squares = jnp.zeros((T, 128), F32)
        for c in range(tiles):
            xt = xst[p % 2, pl.ds(c, T, stride=tiles), :]
            squares = squares + xt * xt
        inv = lax.rsqrt(jnp.sum(squares, axis=1, keepdims=True) / width + EPS)
        inv_b = jnp.broadcast_to(inv, (T, 128))
        index = me * pieces + p
        here = pl.ds(pl.multiple_of(index * T, T), T)
        for c in range(tiles):
            cols = slice(c * 128, c * 128 + 128)
            xt = xst[p % 2, pl.ds(c, T, stride=tiles), :]
            nb[here, cols] = (xt * inv_b * pg_ref[0:1, cols]).astype(BF16)
        o = p // subs

        @pl.when((me < n - 1) & ((me == 0) | (me > o)))
        def _():
            ag(0, index).start()

        @pl.when(me > 0)
        def _():
            ag(1, index).start()

    for peer in range(n):

        @pl.when(me != peer)
        def _():
            swap(0, peer, peer).wait_recv()
            swap(1, peer, peer).wait_recv()

    columns = bc_all.shape[0] * bc_all.shape[1]
    wbd[:, 0:256] = bc_all[...].reshape(columns, share_rows).T
    wbd[:, 256:384] = dtt_ref[...].T
    keep_own(2).start()
    give_all(2)
    bcp_out[...] = bp_all[...].reshape(columns, 128).T[0:8, :]
    hp_out[...] = hp_ref[...]
    hp_out[1:2, :] = -jnp.exp(hp_ref[1:2, :])
    chp_out[0:4, :] = cw_ref[...]
    chp_out[4:5, :] = cb_ref[...]
    chp_out[6:7, :] = gain_ref[...]
    chp_out[7:8, :] = gain_ref[...]
    half = iota((1, 128), 1) < 64
    for j in range(pairs):
        low, high = hp_ref[2:3, 2 * j : 2 * j + 1], hp_ref[2:3, 2 * j + 1 : 2 * j + 2]
        chp_out[5:6, j * 128 : j * 128 + 128] = jnp.where(
            half, jnp.broadcast_to(low, (1, 128)), jnp.broadcast_to(high, (1, 128))
        )
    document_columns(seg_ref, segc, segf)

    def relay(k):
        for sub in range(subs):
            low = k * subs + sub

            @pl.when(k < me * gps)
            def _():
                ag(0, low).wait_recv()

                @pl.when(me < n - 1)
                def _():
                    ag(0, low).start()

            high = ((me + 1) * gps + k) * subs + sub

            @pl.when((me + 1) * gps + k < blocks)
            def _():
                ag(1, high).wait_recv()

                @pl.when(me > 0)
                def _():
                    ag(1, high).start()

        @pl.when((k == me * gps - 1) & (me < n - 1))
        def _():
            for o in range(gps):

                @pl.when(me <= o)
                def _():
                    for sub in range(subs):
                        ag(0, (me * gps + o) * subs + sub).start()

    early = min(2, blocks - gps)
    for k in range(early):
        relay(k)
    for i in (1, 0, 2):
        pass_all(i)
    give_all(3)
    for i in range(3):
        wait_all(i)

    saves = (
        (zbuf, z_out), (xsb, xs_out), (xcvb, xcv_out), (yb, y_out),
        (bcrb, bcr_out), (bcvb, bcv_out), (dtrb, dtr_out), (bccb, bcc_out),
    )

    def save(i, t):
        if i == len(saves):
            there = st_out.at[pl.ds(pl.multiple_of(t * subs, subs), subs)]
            return pltpu.make_async_copy(stb, there, save_sem.at[i])
        there = saves[i][1].at[pl.ds(pl.multiple_of(t * TB, TB), TB)]
        return pltpu.make_async_copy(saves[i][0], there, save_sem.at[i])

    def link(way, shard, p):
        source = shard * pieces + p
        if way == 0:
            target, peer = source, me + 1
        else:
            gap = jnp.minimum(me - 1 - shard, 1)
            target, peer = (shard + (n - shard) * (1 - gap)) * pieces + p, me - 1
        return to_peer(slots.at[source], slots.at[target], rs_send.at[way, source], rs_recv.at[way, target], "tp", peer)

    def landed(way, slot):
        peer = me - 1 if way == 0 else me + 1
        return to_peer(slots.at[slot], slots.at[slot], rs_send.at[way, slot], rs_recv.at[way, slot], "tp", peer)

    def own(block, target, base):
        def tile(i, carry):
            cols = pl.ds(pl.multiple_of(i * 256, 256), 256)
            target[pl.ds(base, TB), cols] = dot(u_all[pl.ds(pl.multiple_of(block * TB, TB), TB), :], wo[:, cols])
            return carry

        lax.fori_loop(0, width // 256, tile, 0)

    def pass_on(way, block, at_end):
        shard = block // gps
        own(block, part, 0)
        for sub in range(subs):
            p = (block % gps) * subs + sub
            slot = shard * pieces + p
            here = slice(sub * T, sub * T + T)

            @pl.when(at_end)
            def _():
                slots[slot] = part[here, :].astype(BF16)

            @pl.when(jnp.logical_not(at_end))
            def _():
                landed(way, slot).wait_recv()
                slots[slot] = (part[here, :] + slots[slot].astype(F32)).astype(BF16)

            link(way, shard, p).start()

    def squares_to(peer, slot):
        return to_peer(sq_all.at[pl.ds(peer * pieces, pieces)], sqs.at[slot], q_send.at[peer], q_recv.at[slot], "tp", peer)

    kept = (
        pltpu.make_async_copy(nb, nb_out, keep_sem.at[0]),
        pltpu.make_async_copy(wc, wc_out, keep_sem.at[1]),
        pltpu.make_async_copy(wo, wo_out, keep_sem.at[2]),
    )

    def turn(t, carry):
        @pl.when(t < blocks)
        def _():
            @pl.when(t > 0)
            def _():
                for i in range(len(saves) + 1):
                    save(i, t - 1).wait()

            forward_block(
                t, nb, wc, segc, segf, chp_out, bcp_out, hp_out,
                zbuf, xsb, xcvb, yb, u_all, bcrb, bcvb, dtrb, bccb, stb, sq_all,
                xbuf, bcbuf, state,
            )
            for i in range(len(saves) + 1):
                save(i, t).start()

            @pl.when((t + 1 >= early) & (t + 1 < blocks - gps))
            def _():
                relay(t + 1)

        @pl.when(t == 0)
        def _():
            pass_all(3)
            wait_all(3)
            for copy in kept[1:]:
                copy.start()

        @pl.when(t == blocks - 1)
        def _():
            kept[0].start()
            for peer in range(n):

                @pl.when(me != peer)
                def _():
                    squares_to(peer, me).start()

        left = t - (n - 1 - me)

        @pl.when((left >= 0) & (left < me * gps))
        def _():
            pass_on(1, left, me == n - 1)

        right = t - me

        @pl.when((right >= (me + 1) * gps) & (right < blocks))
        def _():
            pass_on(0, right, me == 0)

        mine = t - 1 - me * gps

        @pl.when((mine >= 0) & (mine < gps))
        def _():
            own(t - 1, acc, pl.multiple_of(mine * TB, TB))

        return carry

    lax.fori_loop(0, blocks + n - 1, turn, 0)
    load(x_ref, xst, 0, 0).start()
    load(t_ref, tst, 0, 0).start()
    sqs[pl.ds(me, 1)] = sq_all[pl.ds(me * pieces, pieces)][None]
    for peer in range(n):

        @pl.when(me != peer)
        def _():
            squares_to(peer, peer).wait_recv()

    loss_out[...] = jnp.zeros_like(loss_out)

    def store(i, p):
        if i == 0:
            there = lo_out.at[pl.ds(pl.multiple_of(p * (T * tiles), T * tiles), T * tiles)]
            return pltpu.make_async_copy(lost_buf, there, save_sem.at[0])
        source, target = ((dob, do_out), (dbb, db_out))[i - 1]
        return pltpu.make_async_copy(source, target.at[pl.ds(pl.multiple_of(p * T, T), T)], save_sem.at[i])

    for i in range(len(saves) + 1):
        save(i, blocks - 1).wait()
    for p in range(pieces):
        load(x_ref, xst, p % 2, p).wait()
        load(t_ref, tst, p % 2, p).wait()
        if p + 1 < pieces:
            load(x_ref, xst, (p + 1) % 2, p + 1).start()
            load(t_ref, tst, (p + 1) % 2, p + 1).start()
        here = slice(p * T, p * T + T)

        @pl.when(me > 0)
        def _():
            landed(0, me * pieces + p).wait_recv()
            acc[here, :] += slots[me * pieces + p].astype(F32)

        @pl.when(me < n - 1)
        def _():
            landed(1, n * pieces + p).wait_recv()
            acc[here, :] += slots[n * pieces + p].astype(F32)

        if p > 0:
            for i in range(3):
                store(i, p - 1).wait()
        total = sqs[0, p]
        for peer in range(1, n):
            total = total + sqs[peer, p]
        rg_row = lax.rsqrt(total / inner + EPS)
        rg_b = jnp.broadcast_to(column(rg_row[0:1, :]), (T, 128))
        valid_row = v_ref[p : p + 1, :].astype(F32)
        mask_b = jnp.broadcast_to(column(valid_row), (T, 128))
        dots = jnp.zeros((T, 128), F32)
        lost = jnp.zeros((T, 128), F32)
        for c in range(tiles):
            cols = slice(c * 128, c * 128 + 128)
            view = pl.ds(c, T, stride=tiles)
            branch = acc[here, cols] * rg_b
            lo = xst[p % 2, view, :] + branch
            lost_buf[view, :] = lo
            error = lo - tst[p % 2, view, :]
            d_out = error * mask_b
            dob[:, cols] = d_out
            d_branch = d_out.astype(BF16)
            dbb[:, cols] = d_branch
            lost = lost + d_out * error
            dots = dots + d_branch.astype(F32) * branch
        loss_out[0:8, :] += row_sums(lost)
        loss_out[8:9, :] += valid_row
        coefficient = jnp.sum(dots, axis=1, keepdims=True)
        rk_out[p, 0:1, :] = rg_row[0:1, :]
        rk_out[p, 1:2, :] = row(coefficient) * rg_row[0:1, :] * rg_row[0:1, :] / inner
        rk_out[p, 2:8, :] = jnp.zeros((6, 128), F32)
        for i in range(3):
            store(i, p).start()

    for i in range(3):
        store(i, pieces - 1).wait()
    for copy in kept:
        copy.wait()

    def drain(index, carry):
        block = index // subs
        shard = index // pieces

        @pl.when((me < n - 1) & (block < (me + 1) * gps))
        def _():
            ag(0, index).wait_send()

        @pl.when((me > 0) & (block >= me * gps))
        def _():
            ag(1, index).wait_send()

        @pl.when(me < shard)
        def _():
            link(0, shard, index % pieces).wait_send()

        @pl.when(me > shard)
        def _():
            link(1, shard, index % pieces).wait_send()

        return carry

    lax.fori_loop(0, n * pieces, drain, 0)
    for i in range(4):
        give(i, sibling).wait_send()
        for k in range(dp // 2):

            @pl.when(chip != k)
            def _():
                give(i, 2 * k + core).wait_send()
                passed(i, 2 * k + core).wait_send()

    for peer in range(n):

        @pl.when(me != peer)
        def _():
            swap(0, peer, me).wait_send()
            swap(1, peer, me).wait_send()
            squares_to(peer, me).wait_send()


def front_stage(x_view, t_view, wz, wx, wos, bct, dtt, bp, pg, seg, cw, cb, gain, hp, v_rows, n, dp, inner, collective_id):
    width = pg.shape[1]
    rows = x_view.shape[0] * 128 // width
    length = n * rows
    share_rows, channels = wz.shape
    total = 2 * channels + 384
    vmem = pl.BlockSpec(memory_space=pltpu.VMEM)
    anywhere = pl.BlockSpec(memory_space=pl.ANY)
    tile_rows = T * width // 128
    shape = jax.ShapeDtypeStruct
    saved = [
        shape((length, channels), F32), shape((length, channels), BF16), shape((length, channels), BF16),
        shape((length, channels), F32), shape((length, 256), BF16), shape((length, 256), BF16),
        shape((length, 128), F32), shape((length, 256), BF16),
        shape((length // T, 128, channels), BF16),
    ]
    buffers = [pltpu.VMEM((TB,) + item.shape[1:], item.dtype) for item in saved[:-1]]
    buffers.append(pltpu.VMEM((TB // T, 128, channels), BF16))
    dma = pltpu.SemaphoreType.DMA
    return pl.pallas_call(
        partial(front_kernel, n, dp, inner),
        out_shape=saved + [
            shape((length, width), BF16), shape((width, total), BF16), shape((channels, width), BF16),
            shape(x_view.shape, F32), shape((rows, width), F32), shape((rows, width), BF16),
            shape((rows // T, 8, 128), F32), shape((16, 128), F32),
            shape((8, channels), F32), shape((8, 256), F32), shape((8, 128), F32),
        ],
        in_specs=[anywhere] * 5 + [vmem] * 10,
        out_specs=[anywhere] * 15 + [vmem] * 5,
        scratch_shapes=[
            pltpu.VMEM((length, width), BF16),
            pltpu.VMEM((width, total), BF16),
            pltpu.VMEM((channels, width), BF16),
            pltpu.VMEM((length, channels), BF16),
            pltpu.VMEM(((n + 1) * rows // T, T, width), BF16),
            pltpu.VMEM((rows, width), F32),
            pltpu.VMEM((TB, width), F32),
        ] + buffers + [
            pltpu.VMEM((TB + 8, channels), F32),
            pltpu.VMEM((TB + 8, 256), F32),
            pltpu.VMEM((128, channels), F32),
            pltpu.VMEM((length // T, 8, 128), F32),
            pltpu.VMEM((n, rows // T, 8, 128), F32),
            pltpu.VMEM((2, tile_rows, 128), F32),
            pltpu.VMEM((2, tile_rows, 128), F32),
            pltpu.VMEM((tile_rows, 128), F32),
            pltpu.VMEM((T, width), F32),
            pltpu.VMEM((T, width), BF16),
            pltpu.VMEM((length + 16, 128), F32),
            pltpu.VMEM((length // T, 128), F32),
            pltpu.VMEM((n,) + bct.shape, BF16),
            pltpu.VMEM((n,) + bp.shape, F32),
            pltpu.VMEM((share_rows, 384), BF16),
            dma((2, 2)), dma((7,)), dma((9,)), dma((2, n)), dma((2, n)),
            dma((4, dp)), dma((4, dp)), dma((4, dp)),
            dma((2, length // T)), dma((2, length // T)),
            dma((2, (n + 1) * rows // T)), dma((2, (n + 1) * rows // T)),
            dma((n,)), dma((n,)),
        ],
        compiler_params=pltpu.CompilerParams(
            collective_id=collective_id, has_side_effects=True, vmem_limit_bytes=63 << 20
        ),
        name="front_stage",
    )(x_view, t_view, wz, wx, wos, bct, dtt, bp, pg, seg, cw, cb, gain, hp, v_rows)


def scatter_scratch(length, rows, width):
    return [
        pltpu.VMEM((rows, width), F32),
        pltpu.VMEM((min(rows, 256), width), F32),
        pltpu.VMEM((2, length // T, T, width), BF16),
    ], [
        pltpu.SemaphoreType.DMA((2, length // T)),
        pltpu.SemaphoreType.DMA((2, length // T)),
    ]


def input_kernel(
    n, parts, a_ref, *refs,
):
    right_refs = refs[:parts]
    x_ref, do_ref, pg_ref, gx_out, gp_out, acc, part, slots, send_sem, recv_sem = refs[parts:]
    me = meet(n, "tp")
    rows, width = acc.shape
    tiles = width // 128
    arrived, drain = scatter_body(n, me, a_ref, right_refs, acc, part, slots, send_sem, recv_sem)
    gp_out[...] = jnp.zeros_like(gp_out)

    def last(p, carry):
        arrived(p)
        here = pl.ds(pl.multiple_of(p * T, T), T)
        squares = jnp.zeros((T, 128), F32)
        dots = jnp.zeros((T, 128), F32)
        for c in range(tiles):
            cols = slice(c * 128, c * 128 + 128)
            xt = x_ref[pl.ds(p * (T * tiles) + c, T, stride=tiles), :]
            squares = squares + xt * xt
            dots = dots + acc[here, cols] * pg_ref[0:1, cols] * xt
        inv = lax.rsqrt(jnp.sum(squares, axis=1, keepdims=True) / width + EPS)
        inv_b = jnp.broadcast_to(inv, (T, 128))
        mean = jnp.sum(dots, axis=1, keepdims=True) / width
        back_b = jnp.broadcast_to(inv * inv * inv * mean, (T, 128))
        for c in range(tiles):
            cols = slice(c * 128, c * 128 + 128)
            view = pl.ds(p * (T * tiles) + c, T, stride=tiles)
            xt = x_ref[view, :]
            scaled = acc[here, cols] * inv_b
            gx_out[view, :] = do_ref[here, cols] + scaled * pg_ref[0:1, cols] - xt * back_b
            gp_out[:, cols] += row_sums(scaled * xt)
        return carry

    lax.fori_loop(0, rows // T, last, 0)
    drain()


def input_stage(dproj, weights, x_view, d_out, pg, n, collective_id):
    length, width = dproj.shape[0], weights[0].shape[0]
    rows = length // n
    vmem = pl.BlockSpec(memory_space=pltpu.VMEM)
    buffers, sems = scatter_scratch(length, rows, width)
    return pl.pallas_call(
        partial(input_kernel, n, len(weights)),
        out_shape=[jax.ShapeDtypeStruct(x_view.shape, F32), jax.ShapeDtypeStruct((8, width), F32)],
        in_specs=[vmem] * (4 + len(weights)),
        out_specs=[vmem] * 2,
        scratch_shapes=buffers + sems,
        compiler_params=pltpu.CompilerParams(
            collective_id=collective_id, has_side_effects=True, vmem_limit_bytes=62 << 20
        ),
        cost_estimate=pl.CostEstimate(
            flops=2 * length * width * dproj.shape[1], bytes_accessed=400 << 20, transcendentals=0
        ),
        name="input_stage",
    )(dproj, *weights, x_view, d_out, pg)


def local(
    x_in, target, seg_ids, valid, pre_gain, w_z, w_x, w_bc, w_dt, conv_x_w, conv_x_b,
    conv_bc_w, conv_bc_b, dt_bias, a_log, d_skip, norm_gain, w_out,
):
    rows, _, width = x_in.shape
    channels = w_z.shape[1]
    heads = w_dt.shape[1]
    head_dim = channels // heads
    tp = lax.axis_size("tp")
    inner = channels * tp
    bc_local = w_bc.shape[1]
    dp = lax.axis_size("dp")
    x_view = x_in.reshape(rows * width // 128, 128)
    t_view = target.reshape(rows * width // 128, 128)
    seg = seg_ids.reshape(-1, 128)
    bp = jnp.pad(jnp.concatenate([conv_bc_w, conv_bc_b[:, None]], axis=1), ((0, 0), (0, 123)))
    dtt = jnp.pad(w_dt.T, ((0, 128 - heads), (0, 0)))
    hp = jnp.pad(jnp.stack([dt_bias, a_log, d_skip]), ((0, 5), (0, 128 - heads)), constant_values=-100.0)
    (
        z, xs, xcv, y, bcr, bcv, dtr, bcc, st,
        normed_all, wc, wo, lo_view, d_out, d_branch, rk_own, lost, chp, bcp, hp,
    ) = front_stage(
        x_view, t_view, w_z, w_x, w_out, w_bc.T, dtt, bp, pre_gain[None], seg, conv_x_w.T, conv_x_b[None],
        norm_gain[None], hp, valid.reshape(-1, 128), tp, dp, inner, 1,
    )
    saved = (z, xs, xcv, y, bcr, bcv, dtr, bcc, st)
    dproj, yn, db_all, accc, accb, acch = back_stage(d_branch, rk_own, seg, chp, bcp, hp, wo, saved, tp, 2)

    def dot_tn(a, b):
        return lax.dot_general(a, b, (((0,), (0,)), ((), ())), preferred_element_type=F32)

    g_out = dot_tn(db_all, yn).astype(BF16)
    g_cat = dot_tn(normed_all, dproj).astype(BF16)
    g_out, g_cat, dproj = lax.optimization_barrier((g_out, g_cat, dproj))
    g_out = lax.psum_scatter(g_out, "dp", scatter_dimension=0, tiled=True).astype(F32)
    g_cat = lax.psum_scatter(g_cat, "dp", scatter_dimension=0, tiled=True).astype(F32)
    pg = pre_gain[None]
    gx_view, gain_part = input_stage(dproj, (wc,), x_view, d_out, pg, tp, 3)
    lo_view, gx_view = plain_copies(lo_view, gx_view)
    grad_wz, grad_wx = g_cat[:, :channels], g_cat[:, channels : 2 * channels]
    grad_wdt = g_cat[:, 2 * channels + 256 : 2 * channels + 256 + heads]
    cols = g_cat[:, 2 * channels : 2 * channels + 256].T.reshape(tp, bc_local, -1)
    per_channel = 7 * channels // 128
    mine = jnp.concatenate([jnp.sum(accc, axis=1).reshape(per_channel, 128), jnp.sum(acch, axis=1)], axis=0)
    mine = jnp.pad(mine, ((0, -mine.shape[0] % 8), (0, 0)))
    lost_rows = jnp.stack([jnp.sum(lost[0:8], axis=0), lost[8]])
    both = jnp.concatenate(
        [jnp.sum(gain_part, axis=0).reshape(width // 128, 128), jnp.sum(accb, axis=1).reshape(10, 128), lost_rows], axis=0
    )
    both = jnp.pad(both, ((0, -both.shape[0] % 8), (0, 0)))
    mine, both, cols = finish(mine, both, cols, dp, tp, 5)
    accc = mine[:per_channel].reshape(7, channels)
    acch = mine[per_channel : per_channel + 2]
    grad_pre = both[: width // 128].reshape(width)
    accb = both[width // 128 : width // 128 + 10].reshape(5, 256)
    accb = lax.dynamic_slice_in_dim(accb, lax.axis_index("tp") * bc_local, bc_local, axis=1)
    sums = jnp.sum(both[width // 128 + 10 : width // 128 + 12], axis=1)
    loss = sums[0] / (jnp.maximum(sums[1], 1.0) * width)
    grad_wbc = cols.T
    return (
        lo_view.reshape(x_in.shape),
        loss,
        gx_view.reshape(x_in.shape),
        grad_pre,
        grad_wz,
        grad_wx,
        grad_wbc,
        grad_wdt,
        accc[0:4].T,
        accc[4],
        accb[0:4].T,
        accb[4],
        acch[0, :heads],
        acch[1, :heads],
        jnp.sum(accc[6].reshape(heads, head_dim), axis=1),
        accc[5],
        g_out.T,
    )


def solution(mesh):
    tok, col, head = P("tp", "dp", None), P("dp", "tp"), P("tp")
    in_specs = (
        tok, tok, P("dp", None), col, P(), col, col, col, col,
        P("tp", None), head, P("tp", None), head, head, head, head, head, P("tp", "dp"),
    )
    out_specs = (
        tok, P(), tok, P(), col, col, col, col,
        P("tp", None), head, P("tp", None), head, head, head, head, head, P("tp", "dp"),
    )
    return jax.shard_map(local, mesh=mesh, in_specs=in_specs, out_specs=out_specs, check_vma=False)
```

```python
from functools import partial

import jax
import jax.numpy as jnp
from jax import lax
from jax.experimental import pallas as pl
from jax.experimental.pallas import tpu as pltpu
from jax.sharding import PartitionSpec as P

T = 128
TB = 256
EPS = 1e-05
LOG2E = 1.4426950408889634
F32 = jnp.float32
BF16 = jnp.bfloat16
ZT = YT = F32
XT = CT = BF16
HIGHEST = lax.Precision.HIGHEST


def dot(a, b, precision=None):
    return jnp.dot(a, b, preferred_element_type=F32, precision=precision)


def dot_nt(a, b):
    return lax.dot_general(a, b, (((1,), (1,)), ((), ())), preferred_element_type=F32)


def lanes(column_of, index, rows=T):
    return jnp.broadcast_to(column_of[:, index : index + 1], (rows, 128))


def iota(shape, axis):
    return lax.broadcasted_iota(jnp.int32, shape, axis)


def step_sizes(raw, hp_ref):
    shifted = raw + hp_ref[0:1, :]
    dt = jnp.maximum(shifted, 0.0) + jnp.log1p(jnp.exp(-jnp.abs(shifted)))
    la = dt * hp_ref[1:2, :]
    inclusive = (iota((T, T), 0) >= iota((T, T), 1)).astype(F32)
    cum = dot(inclusive, la * LOG2E, HIGHEST)
    return shifted, dt, la, cum


def split_pair(value):
    first = iota((T, 128), 1) < 64
    zero = jnp.zeros_like(value)
    return jnp.concatenate([jnp.where(first, value, zero), jnp.where(first, zero, value)], axis=0)


def eye():
    return iota((T, T), 0) == iota((T, T), 1)


def column(row):
    return jnp.sum(jnp.where(eye(), jnp.broadcast_to(row, (T, T)), 0.0), axis=1, keepdims=True)


def row(col):
    return jnp.sum(jnp.where(eye(), jnp.broadcast_to(col, (T, T)), 0.0), axis=0, keepdims=True)


def document_columns(seg_ref, segc, segf):
    length = segc.shape[0] - 16
    segf[...] = seg_ref[...].astype(F32)
    segc[0:8, :] = jnp.full((8, 128), -1.0, F32)
    segc[length + 8 : length + 16, :] = jnp.full((8, 128), -1.0, F32)

    def chunk(i, carry):
        here = pl.ds(pl.multiple_of(i * T + 8, 8), T)
        segc[here, :] = jnp.broadcast_to(column(segf[pl.ds(i, 1), :]), (T, 128))
        return carry

    lax.fori_loop(0, length // T, chunk, 0)


def row_sums(value):
    return jnp.sum(value.reshape(value.shape[0] // 8, 8, value.shape[1]), axis=0)


def backward_block(
    t, block, dball, wo_ref, rk_all, segc, segf, chp_ref, bcp_ref, hp_ref,
    z_ref, xs_ref, xcv_ref, y_ref, bcr_ref, bcv_ref, dtr_ref, bcc_ref, st_ref,
    dproj_out, yn_out, accc_out, accb_out, acch_out,
    dyn, dbuf, dbcbuf, dstate, dstate_b, dyec, xte, cs_rows, fold, pick,
):
    channels = wo_ref.shape[0]
    pairs = channels // 128
    start = pl.multiple_of(block * TB, TB)
    for n in range(channels // 256):
        cols = slice(n * 256, n * 256 + 256)
        dyn[:, cols] = dot_nt(dball[pl.ds(start, TB), :], wo_ref[cols, :])
    first = iota((T, 128), 1) < 64
    for c in reversed(range(TB // T)):
        r0 = c * T
        rows = slice(r0, r0 + T)
        chunk = block * (TB // T) + c
        near = segc[pl.ds(pl.multiple_of(start + r0, T), T + 16), :]
        seg_col = near[8 : T + 8, :]
        ahead = [(near[8 + d : 8 + d + T, :] == seg_col).astype(F32) for d in (1, 2, 3)]
        start_b = (seg_col == near[7:8, :]).astype(F32)
        end_b = (seg_col == near[T + 7 : T + 8, :]).astype(F32)
        rg_b = jnp.broadcast_to(column(rk_all[chunk, 0:1, :]), (T, 128))
        kc_b = jnp.broadcast_to(column(rk_all[chunk, 1:2, :]), (T, 128))
        bm, cm = bcc_ref[rows, 0:128], bcc_ref[rows, 128:256]
        ct = cm.T
        shifted, dt, la, cum = step_sizes(dtr_ref[rows, :], hp_ref)
        cum_t = cum.T
        scores, scores_t = dot_nt(cm, bm), dot_nt(bm, cm)
        same = seg_col == segf[pl.ds(chunk, 1), :]
        below = iota((T, T), 0) >= iota((T, T), 1)
        strict = iota((T, T), 0) > iota((T, T), 1)
        above = iota((T, T), 0) <= iota((T, T), 1)
        qs = jnp.where(same & strict, scores, 0.0)
        qt = jnp.where(same & above, scores_t, 0.0)
        dstate_b[...] = dstate[...].astype(BF16)
        dq = jnp.zeros((T, T), F32)
        rsum = jnp.zeros((T, 128), F32)
        ddt = jnp.zeros((T, 128), F32)
        xsum = jnp.zeros((T, 128), F32)
        ksum = jnp.zeros((16, 128), F32)
        for j in range(pairs):
            cols = slice(j * 128, j * 128 + 128)
            zz = z_ref[rows, cols].astype(F32)
            y = y_ref[rows, cols].astype(F32)
            sz = 0.5 + 0.5 * jnp.tanh(0.5 * zz)
            silu_z = zz * sz
            dsz = sz + silu_z * (1.0 - sz)
            g = y * silu_z
            gr = g * rg_b
            gain = chp_ref[6:7, cols]
            dynp = dyn[rows, cols]
            yn_out[rows, cols] = (gr * gain).astype(BF16)
            accc_out[5, :, cols] += row_sums(dynp * gr)
            dg = rg_b * dynp * gain - g * kc_b
            dy = dg * silu_z
            dproj_out[rows, cols] = (dg * y * dsz).astype(BF16)
            xcv = xcv_ref[rows, cols].astype(F32)
            sx = 0.5 + 0.5 * jnp.tanh(0.5 * xcv)
            xc = xcv * sx
            dsx = sx + xc * (1.0 - sx)
            accc_out[6, :, cols] += row_sums(dy * xc)
            dt_e = jnp.where(first, lanes(dt, 2 * j), lanes(dt, 2 * j + 1))
            ca, cb = lanes(cum, 2 * j), lanes(cum, 2 * j + 1)
            cum_e = jnp.where(first, ca, cb)
            into = jnp.exp2(cum_e) * start_b
            to_end = jnp.exp2(cum_e[T - 1 : T, :] - cum_e) * end_b
            decay = into[T - 1 : T, :]
            xdt = xc * dt_e
            dy_b = dy.astype(BF16)
            ga = ca - cum_t[2 * j : 2 * j + 1, :]
            gb = cb - cum_t[2 * j + 1 : 2 * j + 2, :]
            grad = dot_nt(dy_b, split_pair(xdt.astype(BF16)))
            gea = grad[:, :128] * jnp.exp2(jnp.minimum(ga, 0.0))
            geb = grad[:, 128:] * jnp.exp2(jnp.minimum(gb, 0.0))
            dq = dq + gea + geb
            pp = jnp.concatenate([(gea * qs).astype(BF16), (geb * qs).astype(BF16)], axis=1)
            rsum = rsum + dot(pp, pick[j, :, :])
            csum = dot(jnp.ones((8, T), BF16), pp)
            cs_rows[2 * j : 2 * j + 1, :] = csum[0:1, :128]
            cs_rows[2 * j + 1 : 2 * j + 2, :] = csum[0:1, 128:]
            eta = (jnp.exp2(jnp.minimum(-ga, 0.0)) * qt).astype(BF16)
            etb = (jnp.exp2(jnp.minimum(-gb, 0.0)) * qt).astype(BF16)
            dxdt = dot(jnp.concatenate([eta, etb], axis=1), split_pair(dy_b))
            dx_state = to_end * dot(bm, dstate_b[:, cols])
            dxdt = dxdt + dx_state
            y_in = into * dot(cm, st_ref[c, :, cols])
            dyec_p = (dy * into).astype(BF16)
            dyec[:, cols] = dyec_p
            xte[:, cols] = (xdt * to_end).astype(BF16)
            ddt = ddt + dot((xc * dxdt).astype(BF16), fold[j, :, :])
            rsum = rsum + dot((dy * y_in).astype(BF16), fold[j, :, :])
            xsum = xsum + dot((xdt * dx_state).astype(BF16), fold[j, :, :])
            old = dstate[:, cols]
            kpart = row_sums(old * st_ref[c, :, cols].astype(F32)) * decay
            khigh = kpart.astype(BF16)
            klow = (kpart - khigh.astype(F32)).astype(BF16)
            ksum = ksum + dot(jnp.concatenate([khigh, klow], axis=0), fold[j, :, :])
            dstate[:, cols] = old * decay + dot(ct, dyec_p)
            dxcv = (dxdt * dt_e + chp_ref[5:6, cols] * dy) * dsx
            dbuf[0:T, cols] = dxcv
            xs = xs_ref[rows, cols].astype(F32)
            dxs = dxcv * chp_ref[3:4, cols]
            accc_out[4, :, cols] += row_sums(dxcv)
            accc_out[3, :, cols] += row_sums(dxcv * xs)
            for d in (1, 2, 3):
                moved = dbuf[d : d + T, cols] * ahead[d - 1]
                dxs = dxs + moved * chp_ref[3 - d : 4 - d, cols]
                accc_out[3 - d, :, cols] += row_sums(moved * xs)
            dproj_out[rows, channels + j * 128 : channels + j * 128 + 128] = dxs.astype(BF16)
        dbuf[T : T + 8, :] = dbuf[0:8, :]
        dqm = jnp.where(same & below, dq, 0.0)
        dc = dot(dqm.astype(BF16), bm) + dot_nt(dyec[...], st_ref[c, :, :])
        db_rows = dot(dqm.T.astype(BF16), cm) + dot_nt(xte[...], dstate_b[...])
        for half, grad_half in enumerate((db_rows, dc)):
            cols = slice(half * 128, half * 128 + 128)
            raw = bcv_ref[rows, cols].astype(F32)
            sb = 0.5 + 0.5 * jnp.tanh(0.5 * raw)
            dcv = grad_half * (sb + raw * sb * (1.0 - sb))
            dbcbuf[0:T, cols] = dcv
            xs = bcr_ref[rows, cols].astype(F32)
            dxs = dcv * bcp_ref[3:4, cols]
            accb_out[4, :, cols] += row_sums(dcv)
            accb_out[3, :, cols] += row_sums(dcv * xs)
            for d in (1, 2, 3):
                moved = dbcbuf[d : d + T, cols] * ahead[d - 1]
                dxs = dxs + moved * bcp_ref[3 - d : 4 - d, cols]
                accb_out[3 - d, :, cols] += row_sums(moved * xs)
            dproj_out[rows, 2 * channels + half * 128 : 2 * channels + half * 128 + 128] = dxs.astype(BF16)
        dbcbuf[T : T + 8, :] = dbcbuf[0:8, :]
        after = (iota((T, T), 0) <= iota((T, T), 1)).astype(F32)
        before = (iota((T, T), 0) > iota((T, T), 1)).astype(F32)
        dla = dot(after, rsum - cs_rows[...].T, HIGHEST) + dot(before, xsum, HIGHEST)
        dla = dla + jnp.sum(ksum, axis=0, keepdims=True)
        ddtr = (ddt + dla * hp_ref[1:2, :]) * (0.5 + 0.5 * jnp.tanh(0.5 * shifted))
        acch_out[0, :, :] += row_sums(ddtr)
        acch_out[1, :, :] += row_sums(dla * la)
        dproj_out[rows, 2 * channels + 256 : 2 * channels + 384] = ddtr.astype(BF16)


MESH_ID = pl.DeviceIdType.MESH


def meet(n, axis):
    me = lax.axis_index(axis)
    barrier = pltpu.get_barrier_semaphore()
    for peer in range(n):

        @pl.when(me != peer)
        def _():
            pl.semaphore_signal(barrier, inc=1, device_id={axis: peer}, device_id_type=MESH_ID)

    pl.semaphore_wait(barrier, n - 1)
    return me


def to_peer(source, target, send_sem, recv_sem, axis, peer):
    return pltpu.make_async_remote_copy(
        src_ref=source, dst_ref=target, send_sem=send_sem, recv_sem=recv_sem,
        device_id={axis: peer}, device_id_type=MESH_ID,
    )


def finish_kernel(
    dp, tp, ac_ref, ah_ref, ab_ref, gp_ref, lost_ref, gc_ref,
    mine_out, both_out, cols_out, got, got_both, cols, got_cols, sems,
):
    me_dp, me_tp = lax.axis_index("dp"), lax.axis_index("tp")
    barrier = pltpu.get_barrier_semaphore()
    for peer in range(dp):

        @pl.when(me_dp != peer)
        def _():
            pl.semaphore_signal(barrier, inc=1, device_id={"dp": peer}, device_id_type=MESH_ID)

    for peer in range(tp):

        @pl.when(me_tp != peer)
        def _():
            pl.semaphore_signal(barrier, inc=1, device_id={"tp": peer}, device_id_type=MESH_ID)

    channels = ac_ref.shape[2]
    per = channels // 128
    first = mine_out.shape[0]
    top = gp_ref.shape[1] // 128
    got[me_dp] = jnp.zeros_like(got[0])

    def put(line, value):
        got[pl.ds(me_dp, 1), line : line + 1, :] = value[None]

    for k in range(7):
        sums = jnp.sum(ac_ref[k], axis=0, keepdims=True)
        for c in range(per):
            put(k * per + c, sums[:, c * 128 : c * 128 + 128])
    for k in range(2):
        put(7 * per + k, jnp.sum(ah_ref[k], axis=0, keepdims=True))
    sums = jnp.sum(gp_ref[...], axis=0, keepdims=True)
    for c in range(top):
        put(first + c, sums[:, c * 128 : c * 128 + 128])
    for k in range(5):
        sums = jnp.sum(ab_ref[k], axis=0, keepdims=True)
        for c in range(2):
            put(first + top + 2 * k + c, sums[:, c * 128 : c * 128 + 128])
    put(first + top + 10, jnp.sum(lost_ref[0:8, :], axis=0, keepdims=True))
    put(first + top + 11, lost_ref[8:9, :])
    turned = gc_ref[:, 2 * channels : 2 * channels + 256].astype(F32).T
    cols[...] = turned.reshape(cols.shape)
    pl.semaphore_wait(barrier, dp - 1 + tp - 1)

    def over_dp(peer, slot):
        return to_peer(got.at[me_dp], got.at[slot], sems.at[0, peer], sems.at[1, slot], "dp", peer)

    def over_tp(peer, slot):
        return to_peer(got_both.at[me_tp], got_both.at[slot], sems.at[2, peer], sems.at[3, slot], "tp", peer)

    def over_cols(peer, slot):
        return to_peer(cols.at[peer], got_cols.at[slot], sems.at[4, peer], sems.at[5, slot], "tp", peer)

    for peer in range(dp):

        @pl.when(me_dp != peer)
        def _():
            over_dp(peer, me_dp).start()

    for peer in range(tp):

        @pl.when(me_tp != peer)
        def _():
            over_cols(peer, me_tp).start()

    got_cols[pl.ds(me_tp, 1)] = cols[pl.ds(me_tp, 1)]
    for peer in range(dp):

        @pl.when(me_dp != peer)
        def _():
            over_dp(peer, peer).wait_recv()

    total = got[0]
    for peer in range(1, dp):
        total = total + got[peer]
    mine_out[...] = total[:first]
    got_both[pl.ds(me_tp, 1)] = total[first:][None]
    for peer in range(tp):

        @pl.when(me_tp != peer)
        def _():
            over_tp(peer, me_tp).start()

    for peer in range(tp):

        @pl.when(me_tp != peer)
        def _():
            over_cols(peer, peer).wait_recv()
            over_tp(peer, peer).wait_recv()

    total, columns = got_both[0], got_cols[0]
    for peer in range(1, tp):
        total, columns = total + got_both[peer], columns + got_cols[peer]
    both_out[...] = total
    cols_out[...] = columns
    for peer in range(dp):

        @pl.when(me_dp != peer)
        def _():
            over_dp(peer, me_dp).wait_send()

    for peer in range(tp):

        @pl.when(me_tp != peer)
        def _():
            over_cols(peer, me_tp).wait_send()
            over_tp(peer, me_tp).wait_send()


def finish(accc, acch, accb, gain_part, lost, g_cat, dp, tp, collective_id):
    vmem = pl.BlockSpec(memory_space=pltpu.VMEM)
    first = -(-(7 * accc.shape[2] // 128 + 2) // 8) * 8
    second = -(-(gain_part.shape[1] // 128 + 12) // 8) * 8
    cols = (tp, 256 // tp, g_cat.shape[0])
    shape = jax.ShapeDtypeStruct
    return pl.pallas_call(
        partial(finish_kernel, dp, tp),
        out_shape=[shape((first, 128), F32), shape((second, 128), F32), shape(cols[1:], F32)],
        in_specs=[vmem] * 6,
        out_specs=[vmem] * 3,
        scratch_shapes=[
            pltpu.VMEM((dp, first + second, 128), F32),
            pltpu.VMEM((tp, second, 128), F32),
            pltpu.VMEM(cols, F32),
            pltpu.VMEM(cols, F32),
            pltpu.SemaphoreType.DMA((6, max(dp, tp))),
        ],
        compiler_params=pltpu.CompilerParams(collective_id=collective_id, has_side_effects=True),
        name="finish",
    )(accc, acch, accb, gain_part, lost, g_cat)


def back_kernel(
    n, db_ref, rk_ref, seg_ref, chp_ref, bcp_ref, hp_ref, wo_any,
    z_any, xs_any, xcv_any, y_any, bcr_any, bcv_any, dtr_any, bcc_any, st_any,
    dproj_any, yn_any, dball_any, accc_out, accb_out, acch_out,
    dball, rk_all, wo, zb, xsb, xcvb, yb, bcrb, bcvb, dtrb, bccb, stb, dprojb, ynb,
    dyn, dbuf, dbcbuf, dstate, dstate_b, dyec, xte, cs_rows, fold, pick, segc, segf,
    keep_sem, load_sem, save_sem, ag_send, ag_recv, r_send, r_recv,
):
    rows = db_ref.shape[0]
    pieces = rows // T
    gps = rows // TB
    subs = TB // T
    blocks = n * gps
    pairs = wo.shape[0] // 128
    sources = (z_any, xs_any, xcv_any, y_any, bcr_any, bcv_any, dtr_any, bcc_any, st_any)
    held = (zb, xsb, xcvb, yb, bcrb, bcvb, dtrb, bccb, stb)

    def load(i, t):
        block = blocks - 1 - t
        step = subs if i == len(held) - 1 else TB
        there = sources[i].at[pl.ds(pl.multiple_of(block * step, step), step)]
        return pltpu.make_async_copy(there, held[i].at[t % 2], load_sem.at[i, t % 2])

    fetch = pltpu.make_async_copy(wo_any, wo, keep_sem.at[0])
    fetch.start()
    own_rows = pl.ds(pl.multiple_of(lax.axis_index("tp") * rows, rows), rows)
    keep = pltpu.make_async_copy(db_ref, dball.at[own_rows], keep_sem.at[1])
    keep.start()
    for i in range(len(held)):
        load(i, 0).start()
    me = meet(n, "tp")

    def rk_to(peer, owner):
        return to_peer(rk_ref, rk_all.at[pl.ds(owner * pieces, pieces)], r_send.at[peer], r_recv.at[owner], "tp", peer)

    for peer in range(n):

        @pl.when(me != peer)
        def _():
            rk_to(peer, me).start()

    rk_all[pl.ds(me * pieces, pieces)] = rk_ref[...]

    def ag(way, index):
        here = dball.at[pl.ds(pl.multiple_of(index * T, T), T)]
        peer = me + 1 if way == 0 else me - 1
        return to_peer(here, here, ag_send.at[way, index], ag_recv.at[way, index], "tp", peer)

    keep.wait()
    mirror = n - 1 - me
    for p in range(pieces):
        index = ((me + 1) * gps - 1 - p // subs) * subs + p % subs

        @pl.when(me < n - 1)
        def _():
            ag(0, index).start()

        @pl.when((me > 0) & ((mirror == 0) | (mirror > p)))
        def _():
            ag(1, index).start()

    def relay(k):
        for sub in range(subs):
            high = (blocks - 1 - k) * subs + sub

            @pl.when(k < mirror * gps)
            def _():
                ag(1, high).wait_recv()

                @pl.when(me > 0)
                def _():
                    ag(1, high).start()

            low = (me * gps - 1 - k) * subs + sub

            @pl.when(me * gps - 1 - k >= 0)
            def _():
                ag(0, low).wait_recv()

                @pl.when(me < n - 1)
                def _():
                    ag(0, low).start()

        @pl.when((k == mirror * gps - 1) & (me > 0))
        def _():
            for p in range(pieces):

                @pl.when(mirror <= p)
                def _():
                    ag(1, ((me + 1) * gps - 1 - p // subs) * subs + p % subs).start()

    document_columns(seg_ref, segc, segf)
    dstate[...] = jnp.zeros_like(dstate)
    dbuf[...] = jnp.zeros_like(dbuf)
    dbcbuf[...] = jnp.zeros_like(dbcbuf)
    accc_out[...] = jnp.zeros_like(accc_out)
    accb_out[...] = jnp.zeros_like(accb_out)
    acch_out[...] = jnp.zeros_like(acch_out)
    cs_rows[...] = jnp.zeros_like(cs_rows)
    for j in range(pairs):
        half = (iota((128, 128), 0) >= 64).astype(jnp.int32)
        fold[j, :, :] = (iota((128, 128), 1) == 2 * j + half).astype(F32).astype(BF16)
        part = (iota((256, 128), 0) >= 128).astype(jnp.int32)
        pick[j, :, :] = (iota((256, 128), 1) == 2 * j + part).astype(F32).astype(BF16)
    for peer in range(n):

        @pl.when(me != peer)
        def _():
            rk_to(peer, peer).wait_recv()

    fetch.wait()
    relay(0)

    def save(i, t):
        block = blocks - 1 - t
        source, target = ((dprojb, dproj_any), (ynb, yn_any))[i]
        return pltpu.make_async_copy(source, target.at[pl.ds(pl.multiple_of(block * TB, TB), TB)], save_sem.at[i])

    def turn(t, carry):
        @pl.when(t + 1 < blocks)
        def _():
            for i in range(len(held)):
                load(i, t + 1).start()

        for i in range(len(held)):
            load(i, t).wait()

        @pl.when(t > 0)
        def _():
            for i in range(2):
                save(i, t - 1).wait()

        slot = t % 2
        backward_block(
            t, blocks - 1 - t, dball, wo, rk_all, segc, segf, chp_ref, bcp_ref, hp_ref,
            zb.at[slot], xsb.at[slot], xcvb.at[slot], yb.at[slot], bcrb.at[slot], bcvb.at[slot],
            dtrb.at[slot], bccb.at[slot], stb.at[slot],
            dprojb, ynb, accc_out, accb_out, acch_out,
            dyn, dbuf, dbcbuf, dstate, dstate_b, dyec, xte, cs_rows, fold, pick,
        )
        for i in range(2):
            save(i, t).start()

        @pl.when(t + 1 < blocks - gps)
        def _():
            relay(t + 1)

        return carry

    lax.fori_loop(0, blocks, turn, 0)
    keep_all = pltpu.make_async_copy(dball, dball_any, keep_sem.at[2])
    keep_all.start()
    for i in range(2):
        save(i, blocks - 1).wait()

    def drain(index, carry):
        block = index // subs

        @pl.when((me < n - 1) & (block < (me + 1) * gps))
        def _():
            ag(0, index).wait_send()

        @pl.when((me > 0) & (block >= me * gps))
        def _():
            ag(1, index).wait_send()

        return carry

    lax.fori_loop(0, n * pieces, drain, 0)
    for peer in range(n):

        @pl.when(me != peer)
        def _():
            rk_to(peer, me).wait_send()

    keep_all.wait()


def back_stage(db, rk, seg, chp, bcp, hp, wo, saved, n, collective_id):
    rows, width = db.shape
    length = n * rows
    channels = wo.shape[0]
    pairs = channels // 128
    total = 2 * channels + 384
    shape = jax.ShapeDtypeStruct
    vmem = pl.BlockSpec(memory_space=pltpu.VMEM)
    anywhere = pl.BlockSpec(memory_space=pl.ANY)
    dma = pltpu.SemaphoreType.DMA
    held = [pltpu.VMEM((2, TB) + item.shape[1:], item.dtype) for item in saved[:-1]]
    held.append(pltpu.VMEM((2, TB // T, 128, channels), BF16))
    return pl.pallas_call(
        partial(back_kernel, n),
        out_shape=[
            shape((length, total), BF16), shape((length, channels), BF16), shape((length, width), BF16),
            shape((7, 8, channels), F32), shape((5, 8, 256), F32), shape((2, 8, 128), F32),
        ],
        in_specs=[anywhere] + [vmem] * 5 + [anywhere] * 10,
        out_specs=[anywhere] * 3 + [vmem] * 3,
        scratch_shapes=[
            pltpu.VMEM((length, width), BF16),
            pltpu.VMEM((length // T, 8, 128), F32),
            pltpu.VMEM(wo.shape, BF16),
        ] + held + [
            pltpu.VMEM((TB, total), BF16),
            pltpu.VMEM((TB, channels), BF16),
            pltpu.VMEM((TB, channels), F32),
            pltpu.VMEM((T + 8, channels), F32),
            pltpu.VMEM((T + 8, 256), F32),
            pltpu.VMEM((128, channels), F32),
            pltpu.VMEM((128, channels), BF16),
            pltpu.VMEM((T, channels), BF16),
            pltpu.VMEM((T, channels), BF16),
            pltpu.VMEM((128, 128), F32),
            pltpu.VMEM((pairs, 128, 128), BF16),
            pltpu.VMEM((pairs, 256, 128), BF16),
            pltpu.VMEM((length + 16, 128), F32),
            pltpu.VMEM((length // T, 128), F32),
            dma((3,)), dma((9, 2)), dma((2,)),
            dma((2, length // T)), dma((2, length // T)), dma((n,)), dma((n,)),
        ],
        compiler_params=pltpu.CompilerParams(
            collective_id=collective_id, has_side_effects=True, vmem_limit_bytes=60 << 20
        ),
        name="back_stage",
    )(db, rk, seg, chp, bcp, hp, wo, *saved)


def scatter_body(n, me, a_ref, right_refs, acc, part, slots, send_sem, recv_sem):
    rows, width = acc.shape
    group = part.shape[0]
    piece = slots.shape[2]
    pieces = rows // piece
    groups = rows // group
    subs = group // piece

    def link(way, index):
        peer = me + 1 if way == 0 else me - 1
        return to_peer(
            slots.at[way, index], slots.at[way, index], send_sem.at[way, index], recv_sem.at[way, index], "tp", peer
        )

    def own(start, target, base):
        def tile(i, carry):
            cols = pl.ds(pl.multiple_of(i * 256, 256), 256)
            total, at = None, 0
            for w_ref in right_refs:
                depth = w_ref.shape[1]
                term = dot_nt(a_ref[pl.ds(start, group), at : at + depth], w_ref[cols, :])
                total = term if total is None else total + term
                at += depth
            target[pl.ds(base, group), cols] = total
            return carry

        lax.fori_loop(0, width // 256, tile, 0)

    def pass_on(way, q, at_end):
        shard = n - 1 - q // groups if way == 0 else q // groups
        start = pl.multiple_of(shard * rows + (q % groups) * group, group)
        own(start, part, 0)
        for sub in range(subs):
            index = shard * pieces + (q % groups) * subs + sub
            here = slice(sub * piece, (sub + 1) * piece)

            @pl.when(at_end)
            def _():
                slots[way, index] = part[here, :].astype(BF16)

            @pl.when(jnp.logical_not(at_end))
            def _():
                link(way, index).wait_recv()
                slots[way, index] = (part[here, :] + slots[way, index].astype(F32)).astype(BF16)

            link(way, index).start()

    def turn(t, carry):
        for way in (0, 1):
            hops = me if way == 0 else n - 1 - me
            q = t - hops

            @pl.when((q >= 0) & (q < (n - 1 - hops) * groups))
            def _():
                pass_on(way, q, hops == 0)

        late = t - (n - 1)

        @pl.when((late >= 0) & (late < groups))
        def _():
            base = pl.multiple_of(late * group, group)
            own(pl.multiple_of(me * rows + late * group, group), acc, base)

        return carry

    lax.fori_loop(0, (n - 1) * groups + n - 1, turn, 0)

    def arrived(p):
        for way in (0, 1):

            @pl.when((me > 0) if way == 0 else (me < n - 1))
            def _():
                link(way, me * pieces + p).wait_recv()
                here = pl.ds(pl.multiple_of(p * piece, piece), piece)
                acc[here, :] += slots[way, me * pieces + p].astype(F32)

    def drain():
        def done(index, carry):
            shard = index // pieces
            for way in (0, 1):

                @pl.when((me < shard) if way == 0 else (me > shard))
                def _():
                    link(way, index).wait_send()

            return carry

        lax.fori_loop(0, n * pieces, done, 0)

    return arrived, drain


def forward_block(
    t, nb, wc, segc, segf, chp_ref, bcp_ref, hp_ref,
    zbuf, xs_out, xcv_out, y_out, u_all, bcr_out, bcv_out, dtr_out, bcc_out, st_out, sq_all,
    xbuf, bcbuf, state,
):
    channels = zbuf.shape[1]
    pairs = channels // 128
    start = pl.multiple_of(t * TB, TB)
    nb_rows = pl.ds(start, TB)
    for n in range(channels // 256):
        cols = slice(n * 256, n * 256 + 256)
        zbuf[:, cols] = dot(nb[nb_rows, :], wc[:, cols])
        xbuf[8 : 8 + TB, cols] = dot(nb[nb_rows, :], wc[:, channels + n * 256 : channels + n * 256 + 256])
    bd = dot(nb[nb_rows, :], wc[:, 2 * channels :])
    bcbuf[8 : 8 + TB, :] = bd[:, :256]
    dtr_out[...] = bd[:, 256:]
    bcr_out[...] = bd[:, :256].astype(BF16)
    first = iota((T, 128), 1) < 64
    for c in range(TB // T):
        r0 = c * T
        rows = slice(r0, r0 + T)
        chunk = t * (TB // T) + c
        at = pl.ds(pl.multiple_of(start + r0, T), T)
        near = segc[pl.ds(pl.multiple_of(start + r0, T), T + 8), :]
        seg_col = near[8:, :]
        masks = [(near[8 - d : 8 - d + T, :] == seg_col).astype(F32) for d in (1, 2, 3)]
        start_b = (seg_col == near[7:8, :]).astype(F32)
        end_b = (seg_col == near[T + 7 : T + 8, :]).astype(F32)
        parts = []
        for half in range(2):
            cols = slice(half * 128, half * 128 + 128)
            acc = bcbuf[8 + r0 : 8 + r0 + T, cols] * bcp_ref[3:4, cols] + bcp_ref[4:5, cols]
            for d in (1, 2, 3):
                acc = acc + bcbuf[8 + r0 - d : 8 + r0 - d + T, cols] * bcp_ref[3 - d : 4 - d, cols] * masks[d - 1]
            bcv_out[rows, cols] = acc.astype(BF16)
            hv = 0.5 * acc
            parts.append((hv + hv * jnp.tanh(hv)).astype(BF16))
            bcc_out[rows, cols] = parts[-1]
        bm, cm = parts
        bt = bm.T
        _, dt, la, cum = step_sizes(dtr_out[rows, :], hp_ref)
        cum_t = cum.T
        scores = dot_nt(cm, bm)
        keep = (seg_col == segf[pl.ds(chunk, 1), :]) & (iota((T, T), 0) >= iota((T, T), 1))
        qm = jnp.where(keep, scores, 0.0)
        sq = jnp.zeros((T, 128), F32)
        st_out[c, :, :] = state[...].astype(BF16)
        for j in range(pairs):
            cols = slice(j * 128, j * 128 + 128)
            acc = xbuf[8 + r0 : 8 + r0 + T, cols] * chp_ref[3:4, cols] + chp_ref[4:5, cols]
            xs_out[rows, cols] = xbuf[8 + r0 : 8 + r0 + T, cols].astype(BF16)
            for d in (1, 2, 3):
                acc = acc + xbuf[8 + r0 - d : 8 + r0 - d + T, cols] * chp_ref[3 - d : 4 - d, cols] * masks[d - 1]
            xcv_out[rows, cols] = acc.astype(BF16)
            hv = 0.5 * acc
            xc = hv + hv * jnp.tanh(hv)
            dt_e = jnp.where(first, lanes(dt, 2 * j), lanes(dt, 2 * j + 1))
            ca, cb = lanes(cum, 2 * j), lanes(cum, 2 * j + 1)
            cum_e = jnp.where(first, ca, cb)
            xdt = xc * dt_e
            ea = jnp.exp2(jnp.minimum(ca - cum_t[2 * j : 2 * j + 1, :], 0.0))
            eb = jnp.exp2(jnp.minimum(cb - cum_t[2 * j + 1 : 2 * j + 2, :], 0.0))
            mix = jnp.concatenate([(ea * qm).astype(BF16), (eb * qm).astype(BF16)], axis=1)
            y = dot(mix, split_pair(xdt.astype(BF16)))
            into = jnp.exp2(cum_e) * start_b
            last = cum_e[T - 1 : T, :]
            to_end = jnp.exp2(last - cum_e) * end_b
            y = y + into * dot(cm, st_out[c, :, cols])
            state[:, cols] = state[:, cols] * into[T - 1 : T, :] + dot(bt, (xdt * to_end).astype(BF16))
            y = y + chp_ref[5:6, cols] * xc
            y_out[rows, cols] = y
            hz = 0.5 * zbuf[rows, cols]
            g = y * (hz + hz * jnp.tanh(hz))
            sq = sq + g * g
            u_all[at, cols] = (g * chp_ref[6:7, cols]).astype(BF16)
        sq_all[chunk, :, :] = lax.dot_general(
            jnp.ones((8, 128), F32), sq, (((1,), (1,)), ((), ())), preferred_element_type=F32, precision=HIGHEST
        )
    xbuf[0:8, :] = xbuf[TB : TB + 8, :]
    bcbuf[0:8, :] = bcbuf[TB : TB + 8, :]


def front_kernel(
    n, dp, inner,
    x_ref, t_ref, wz_ref, wx_ref, wos_ref, bct_ref, dtt_ref, bp_ref, pg_ref, seg_ref, cw_ref, cb_ref, gain_ref, hp_ref, v_ref,
    z_out, xs_out, xcv_out, y_out, bcr_out, bcv_out, dtr_out, bcc_out, st_out,
    nb_out, wc_out, wo_out, er_out, db_out, rk_out, loss_out, chp_out, bcp_out, hp_out,
    nb, wc, wo, u_all, slots, acc, part,
    zbuf, xsb, xcvb, yb, bcrb, bcvb, dtrb, bccb, stb,
    xbuf, bcbuf, state, sq_all, sqs, xst, tst, erb, dbb,
    segc, segf, bc_all, bp_all, wbd,
    load_sem, keep_sem, save_sem, s_send, s_recv, w_send, w_hop, w_pass, w_recv, ag_send, ag_recv, rs_send, rs_recv, q_send, q_recv,
):
    me, me_dp = lax.axis_index("tp"), lax.axis_index("dp")
    rows, width = acc.shape
    pieces = rows // T
    tiles = width // 128
    gps = rows // TB
    subs = TB // T
    blocks = n * gps
    share_rows = wz_ref.shape[0]
    channels = wz_ref.shape[1]
    pairs = channels // 128
    barrier = pltpu.get_barrier_semaphore()
    for peer in range(dp):

        @pl.when(me_dp != peer)
        def _():
            pl.semaphore_signal(barrier, inc=1, device_id={"dp": peer}, device_id_type=MESH_ID)

    for peer in range(n):

        @pl.when(me != peer)
        def _():
            pl.semaphore_signal(barrier, inc=1, device_id={"tp": peer}, device_id_type=MESH_ID)

    def load(source, target, slot, p):
        view = source.at[pl.ds(pl.multiple_of(p * (T * tiles), T * tiles), T * tiles)]
        return pltpu.make_async_copy(view, target.at[slot], load_sem.at[0 if target is xst else 1, slot])

    load(x_ref, xst, 0, 0).start()

    def place(i, owner):
        at = pl.ds(pl.multiple_of(owner * share_rows, share_rows), share_rows)
        if i == 0:
            return wc.at[at, 0:channels]
        if i == 1:
            return wc.at[at, channels : 2 * channels]
        if i == 2:
            return wc.at[at, 2 * channels : 2 * channels + 384]
        return wo.at[:, at]

    local = (wz_ref, wx_ref, wbd, wos_ref)

    def keep_own(i):
        return pltpu.make_async_copy(local[i], place(i, me_dp), keep_sem.at[3 + i])

    for i in (0, 1, 3):
        keep_own(i).start()
    state[...] = jnp.zeros_like(state)
    xbuf[0:8, :] = jnp.zeros((8, xbuf.shape[1]), F32)
    bcbuf[0:8, :] = jnp.zeros((8, 256), F32)
    pl.semaphore_wait(barrier, dp - 1 + n - 1)

    core = me_dp % 2
    chip = me_dp // 2
    sibling = me_dp + 1 - 2 * core

    def give(i, peer):
        return to_peer(local[i], place(i, me_dp), w_send.at[i, peer], w_recv.at[i, me_dp], "dp", peer)

    def passed(i, owner):
        there = place(i, owner)
        return to_peer(there, there, w_pass.at[i, owner], w_recv.at[i, owner], "dp", sibling)

    square = dp == 8
    across = chip + 1 - 2 * (chip % 2)
    along = (chip + 2) % 4
    corner = 3 - chip

    def hop(i, owner, peer):
        there = place(i, owner)
        return to_peer(there, there, w_hop.at[i], w_recv.at[i, owner], "dp", peer)

    def onward(i):
        source, target = ((across, along), (along, across))[i]
        return hop(i, 2 * source + core, 2 * target + core)

    def give_all(i):
        if square and i < 2:
            give(i, 2 * across + core).start()
            give(i, 2 * along + core).start()
        else:
            for k in range(dp // 2):

                @pl.when(chip != k)
                def _():
                    give(i, 2 * k + core).start()

        give(i, sibling).start()

    def turn_corner(i):
        if square:
            owner = 2 * (across, along)[i] + core
            passed(i, owner).wait_recv()
            onward(i).start()
            passed(i, owner).start()

    def pass_all(i):
        if square and i < 2:
            for owner in (2 * (along, across)[i] + core, 2 * corner + core):
                passed(i, owner).wait_recv()
                passed(i, owner).start()
        else:
            for k in range(dp // 2):

                @pl.when(chip != k)
                def _():
                    passed(i, 2 * k + core).wait_recv()
                    passed(i, 2 * k + core).start()

    def wait_all(i):
        keep_own(i).wait()
        passed(i, sibling).wait_recv()
        for k in range(dp // 2):

            @pl.when(chip != k)
            def _():
                passed(i, 2 * k + 1 - core).wait_recv()

    def swap(i, peer, slot):
        source, target = ((bct_ref, bc_all), (bp_ref, bp_all))[i]
        return to_peer(source, target.at[slot], s_send.at[i, peer], s_recv.at[i, slot], "tp", peer)

    for peer in range(n):

        @pl.when(me != peer)
        def _():
            swap(0, peer, me).start()
            swap(1, peer, me).start()

    bc_all[pl.ds(me, 1)] = bct_ref[...][None]
    bp_all[pl.ds(me, 1)] = bp_ref[...][None]
    give_all(1)
    give_all(0)

    def ag(way, index):
        here = nb.at[pl.ds(pl.multiple_of(index * T, T), T)]
        peer = me + 1 if way == 0 else me - 1
        return to_peer(here, here, ag_send.at[way, index], ag_recv.at[way, index], "tp", peer)

    for p in range(pieces):
        load(x_ref, xst, p % 2, p).wait()
        if p + 1 < pieces:
            load(x_ref, xst, (p + 1) % 2, p + 1).start()
        squares = jnp.zeros((T, 128), F32)
        for c in range(tiles):
            xt = xst[p % 2, pl.ds(c, T, stride=tiles), :]
            squares = squares + xt * xt
        inv = lax.rsqrt(jnp.sum(squares, axis=1, keepdims=True) / width + EPS)
        inv_b = jnp.broadcast_to(inv, (T, 128))
        index = me * pieces + p
        here = pl.ds(pl.multiple_of(index * T, T), T)
        for c in range(tiles):
            cols = slice(c * 128, c * 128 + 128)
            xt = xst[p % 2, pl.ds(c, T, stride=tiles), :]
            nb[here, cols] = (xt * inv_b * pg_ref[0:1, cols]).astype(BF16)
        @pl.when((me < n - 1) & ((me == 0) | (me > p)))
        def _():
            ag(0, index).start()

        @pl.when(me > 0)
        def _():
            ag(1, index).start()

    for peer in range(n):

        @pl.when(me != peer)
        def _():
            swap(0, peer, peer).wait_recv()
            swap(1, peer, peer).wait_recv()

    columns = bc_all.shape[0] * bc_all.shape[1]
    wbd[:, 0:256] = bc_all[...].reshape(columns, share_rows).T
    wbd[:, 256:384] = dtt_ref[...].T
    keep_own(2).start()
    give_all(2)
    bcp_out[...] = bp_all[...].reshape(columns, 128).T[0:8, :]
    hp_out[...] = hp_ref[...]
    hp_out[1:2, :] = -jnp.exp(hp_ref[1:2, :])
    chp_out[0:4, :] = cw_ref[...]
    chp_out[4:5, :] = cb_ref[...]
    chp_out[6:7, :] = gain_ref[...]
    chp_out[7:8, :] = gain_ref[...]
    half = iota((1, 128), 1) < 64
    for j in range(pairs):
        low, high = hp_ref[2:3, 2 * j : 2 * j + 1], hp_ref[2:3, 2 * j + 1 : 2 * j + 2]
        chp_out[5:6, j * 128 : j * 128 + 128] = jnp.where(
            half, jnp.broadcast_to(low, (1, 128)), jnp.broadcast_to(high, (1, 128))
        )
    document_columns(seg_ref, segc, segf)

    def relay(k):
        for sub in range(subs):
            low = k * subs + sub

            @pl.when(k < me * gps)
            def _():
                ag(0, low).wait_recv()

                @pl.when(me < n - 1)
                def _():
                    ag(0, low).start()

            high = ((me + 1) * gps + k) * subs + sub

            @pl.when((me + 1) * gps + k < blocks)
            def _():
                ag(1, high).wait_recv()

                @pl.when(me > 0)
                def _():
                    ag(1, high).start()

        @pl.when((k == me * gps - 1) & (me < n - 1))
        def _():
            for p in range(pieces):

                @pl.when(me <= p)
                def _():
                    ag(0, me * pieces + p).start()

    turn_corner(1)
    turn_corner(0)
    early = min(2, blocks - gps)
    for k in range(early):
        relay(k)
    for i in (1, 0, 2):
        pass_all(i)
    give_all(3)
    for i in range(3):
        wait_all(i)

    saves = (
        (zbuf, z_out), (xsb, xs_out), (xcvb, xcv_out), (yb, y_out),
        (bcrb, bcr_out), (bcvb, bcv_out), (dtrb, dtr_out), (bccb, bcc_out),
    )

    def save(i, t):
        if i == len(saves):
            there = st_out.at[pl.ds(pl.multiple_of(t * subs, subs), subs)]
            return pltpu.make_async_copy(stb, there, save_sem.at[i])
        there = saves[i][1].at[pl.ds(pl.multiple_of(t * TB, TB), TB)]
        return pltpu.make_async_copy(saves[i][0], there, save_sem.at[i])

    def link(way, shard, p):
        source = shard * pieces + p
        if way == 0:
            target, peer = source, me + 1
        else:
            gap = jnp.minimum(me - 1 - shard, 1)
            target, peer = (shard + (n - shard) * (1 - gap)) * pieces + p, me - 1
        return to_peer(slots.at[source], slots.at[target], rs_send.at[way, source], rs_recv.at[way, target], "tp", peer)

    def landed(way, slot):
        peer = me - 1 if way == 0 else me + 1
        return to_peer(slots.at[slot], slots.at[slot], rs_send.at[way, slot], rs_recv.at[way, slot], "tp", peer)

    def own(block, target, base):
        def tile(i, carry):
            cols = pl.ds(pl.multiple_of(i * 256, 256), 256)
            target[pl.ds(base, TB), cols] = dot(u_all[pl.ds(pl.multiple_of(block * TB, TB), TB), :], wo[:, cols])
            return carry

        lax.fori_loop(0, width // 256, tile, 0)

    def pass_on(way, block, at_end):
        shard = block // gps
        own(block, part, 0)
        for sub in range(subs):
            p = (block % gps) * subs + sub
            slot = shard * pieces + p
            here = slice(sub * T, sub * T + T)

            @pl.when(at_end)
            def _():
                slots[slot] = part[here, :].astype(BF16)

            @pl.when(jnp.logical_not(at_end))
            def _():
                landed(way, slot).wait_recv()
                slots[slot] = (part[here, :] + slots[slot].astype(F32)).astype(BF16)

            link(way, shard, p).start()

    def squares_to(peer, slot):
        return to_peer(sq_all.at[pl.ds(peer * pieces, pieces)], sqs.at[slot], q_send.at[peer], q_recv.at[slot], "tp", peer)

    kept = (
        pltpu.make_async_copy(nb, nb_out, keep_sem.at[0]),
        pltpu.make_async_copy(wc, wc_out, keep_sem.at[1]),
        pltpu.make_async_copy(wo, wo_out, keep_sem.at[2]),
    )

    def turn(t, carry):
        @pl.when(t < blocks)
        def _():
            @pl.when(t > 0)
            def _():
                for i in range(len(saves) + 1):
                    save(i, t - 1).wait()

            forward_block(
                t, nb, wc, segc, segf, chp_out, bcp_out, hp_out,
                zbuf, xsb, xcvb, yb, u_all, bcrb, bcvb, dtrb, bccb, stb, sq_all,
                xbuf, bcbuf, state,
            )
            for i in range(len(saves) + 1):
                save(i, t).start()

            @pl.when((t + 1 >= early) & (t + 1 < blocks - gps))
            def _():
                relay(t + 1)

        @pl.when(t == jnp.minimum(n - 1 - me, gps))
        def _():
            pass_all(3)
            wait_all(3)
            for copy in kept[1:]:
                copy.start()

        @pl.when(t == blocks - 1)
        def _():
            kept[0].start()
            for peer in range(n):

                @pl.when(me != peer)
                def _():
                    squares_to(peer, me).start()

        left = t - (n - 1 - me)

        @pl.when((left >= 0) & (left < me * gps))
        def _():
            pass_on(1, left, me == n - 1)

        right = t - me

        @pl.when((right >= (me + 1) * gps) & (right < blocks))
        def _():
            pass_on(0, right, me == 0)

        mine = t - gps - me * gps

        @pl.when((mine >= 0) & (mine < gps))
        def _():
            own(t - gps, acc, pl.multiple_of(mine * TB, TB))

        return carry

    lax.fori_loop(0, blocks + n - 1, turn, 0)
    load(x_ref, xst, 0, 0).start()
    load(t_ref, tst, 0, 0).start()
    sqs[pl.ds(me, 1)] = sq_all[pl.ds(me * pieces, pieces)][None]
    for peer in range(n):

        @pl.when(me != peer)
        def _():
            squares_to(peer, peer).wait_recv()

    loss_out[...] = jnp.zeros_like(loss_out)

    def store(i, p):
        source, target = ((erb, er_out), (dbb, db_out))[i]
        return pltpu.make_async_copy(source, target.at[pl.ds(pl.multiple_of(p * T, T), T)], save_sem.at[i])

    for i in range(len(saves) + 1):
        save(i, blocks - 1).wait()
    for p in range(pieces):
        load(x_ref, xst, p % 2, p).wait()
        load(t_ref, tst, p % 2, p).wait()
        if p + 1 < pieces:
            load(x_ref, xst, (p + 1) % 2, p + 1).start()
            load(t_ref, tst, (p + 1) % 2, p + 1).start()
        here = slice(p * T, p * T + T)

        @pl.when(me > 0)
        def _():
            landed(0, me * pieces + p).wait_recv()
            acc[here, :] += slots[me * pieces + p].astype(F32)

        @pl.when(me < n - 1)
        def _():
            landed(1, n * pieces + p).wait_recv()
            acc[here, :] += slots[n * pieces + p].astype(F32)

        if p > 0:
            for i in range(2):
                store(i, p - 1).wait()
        total = sqs[0, p]
        for peer in range(1, n):
            total = total + sqs[peer, p]
        rg_row = lax.rsqrt(total / inner + EPS)
        rg_b = jnp.broadcast_to(column(rg_row[0:1, :]), (T, 128))
        valid_row = v_ref[p : p + 1, :].astype(F32)
        mask_b = jnp.broadcast_to(column(valid_row), (T, 128))
        dots = jnp.zeros((T, 128), F32)
        lost = jnp.zeros((T, 128), F32)
        for c in range(tiles):
            cols = slice(c * 128, c * 128 + 128)
            view = pl.ds(c, T, stride=tiles)
            branch = acc[here, cols] * rg_b
            error = xst[p % 2, view, :] + branch - tst[p % 2, view, :]
            d_out = error * mask_b
            erb[:, cols] = error
            d_branch = d_out.astype(BF16)
            dbb[:, cols] = d_branch
            lost = lost + d_out * error
            dots = dots + d_branch.astype(F32) * branch
        loss_out[0:8, :] += row_sums(lost)
        loss_out[8:9, :] += valid_row
        coefficient = jnp.sum(dots, axis=1, keepdims=True)
        rk_out[p, 0:1, :] = rg_row[0:1, :]
        rk_out[p, 1:2, :] = row(coefficient) * rg_row[0:1, :] * rg_row[0:1, :] / inner
        rk_out[p, 2:8, :] = jnp.zeros((6, 128), F32)
        for i in range(2):
            store(i, p).start()

    for i in range(2):
        store(i, pieces - 1).wait()
    for copy in kept:
        copy.wait()

    def drain(index, carry):
        block = index // subs
        shard = index // pieces

        @pl.when((me < n - 1) & (block < (me + 1) * gps))
        def _():
            ag(0, index).wait_send()

        @pl.when((me > 0) & (block >= me * gps))
        def _():
            ag(1, index).wait_send()

        @pl.when(me < shard)
        def _():
            link(0, shard, index % pieces).wait_send()

        @pl.when(me > shard)
        def _():
            link(1, shard, index % pieces).wait_send()

        return carry

    lax.fori_loop(0, n * pieces, drain, 0)
    for i in range(4):
        give(i, sibling).wait_send()
        if square and i < 2:
            onward(i).wait_send()
            give(i, 2 * across + core).wait_send()
            give(i, 2 * along + core).wait_send()
            for owner in (2 * across + core, 2 * along + core, 2 * corner + core):
                passed(i, owner).wait_send()
        else:
            for k in range(dp // 2):

                @pl.when(chip != k)
                def _():
                    give(i, 2 * k + core).wait_send()
                    passed(i, 2 * k + core).wait_send()

    for peer in range(n):

        @pl.when(me != peer)
        def _():
            swap(0, peer, me).wait_send()
            swap(1, peer, me).wait_send()
            squares_to(peer, me).wait_send()


def front_stage(x_view, t_view, wz, wx, wos, bct, dtt, bp, pg, seg, cw, cb, gain, hp, v_rows, n, dp, inner, collective_id):
    width = pg.shape[1]
    rows = x_view.shape[0] * 128 // width
    length = n * rows
    share_rows, channels = wz.shape
    total = 2 * channels + 384
    vmem = pl.BlockSpec(memory_space=pltpu.VMEM)
    anywhere = pl.BlockSpec(memory_space=pl.ANY)
    tile_rows = T * width // 128
    shape = jax.ShapeDtypeStruct
    saved = [
        shape((length, channels), F32), shape((length, channels), BF16), shape((length, channels), BF16),
        shape((length, channels), F32), shape((length, 256), BF16), shape((length, 256), BF16),
        shape((length, 128), F32), shape((length, 256), BF16),
        shape((length // T, 128, channels), BF16),
    ]
    buffers = [pltpu.VMEM((TB,) + item.shape[1:], item.dtype) for item in saved[:-1]]
    buffers.append(pltpu.VMEM((TB // T, 128, channels), BF16))
    dma = pltpu.SemaphoreType.DMA
    return pl.pallas_call(
        partial(front_kernel, n, dp, inner),
        out_shape=saved + [
            shape((length, width), BF16), shape((width, total), BF16), shape((channels, width), BF16),
            shape((rows, width), F32), shape((rows, width), BF16),
            shape((rows // T, 8, 128), F32), shape((16, 128), F32),
            shape((8, channels), F32), shape((8, 256), F32), shape((8, 128), F32),
        ],
        in_specs=[anywhere] * 5 + [vmem] * 10,
        out_specs=[anywhere] * 14 + [vmem] * 5,
        scratch_shapes=[
            pltpu.VMEM((length, width), BF16),
            pltpu.VMEM((width, total), BF16),
            pltpu.VMEM((channels, width), BF16),
            pltpu.VMEM((length, channels), BF16),
            pltpu.VMEM(((n + 1) * rows // T, T, width), BF16),
            pltpu.VMEM((rows, width), F32),
            pltpu.VMEM((TB, width), F32),
        ] + buffers + [
            pltpu.VMEM((TB + 8, channels), F32),
            pltpu.VMEM((TB + 8, 256), F32),
            pltpu.VMEM((128, channels), F32),
            pltpu.VMEM((length // T, 8, 128), F32),
            pltpu.VMEM((n, rows // T, 8, 128), F32),
            pltpu.VMEM((2, tile_rows, 128), F32),
            pltpu.VMEM((2, tile_rows, 128), F32),
            pltpu.VMEM((T, width), F32),
            pltpu.VMEM((T, width), BF16),
            pltpu.VMEM((length + 16, 128), F32),
            pltpu.VMEM((length // T, 128), F32),
            pltpu.VMEM((n,) + bct.shape, BF16),
            pltpu.VMEM((n,) + bp.shape, F32),
            pltpu.VMEM((share_rows, 384), BF16),
            dma((2, 2)), dma((7,)), dma((9,)), dma((2, n)), dma((2, n)),
            dma((4, dp)), dma((2,)), dma((4, dp)), dma((4, dp)),
            dma((2, length // T)), dma((2, length // T)),
            dma((2, (n + 1) * rows // T)), dma((2, (n + 1) * rows // T)),
            dma((n,)), dma((n,)),
        ],
        compiler_params=pltpu.CompilerParams(
            collective_id=collective_id, has_side_effects=True, vmem_limit_bytes=63 << 20
        ),
        name="front_stage",
    )(x_view, t_view, wz, wx, wos, bct, dtt, bp, pg, seg, cw, cb, gain, hp, v_rows)


def scatter_scratch(length, rows, width):
    return [
        pltpu.VMEM((rows, width), F32),
        pltpu.VMEM((min(rows, 256), width), F32),
        pltpu.VMEM((2, length // T, T, width), BF16),
    ], [
        pltpu.SemaphoreType.DMA((2, length // T)),
        pltpu.SemaphoreType.DMA((2, length // T)),
    ]


def input_kernel(n, a_any, w_any, acc, a_ref, w_ref, part, slots, load_sem, send_sem, recv_sem):
    loads = [
        pltpu.make_async_copy(source, target, load_sem.at[i])
        for i, (source, target) in enumerate(((w_any, w_ref), (a_any, a_ref)))
    ]
    for copy in loads:
        copy.start()
    me = meet(n, "tp")
    for copy in loads:
        copy.wait()
    arrived, drain = scatter_body(n, me, a_ref, (w_ref,), acc, part, slots, send_sem, recv_sem)

    def last(p, carry):
        arrived(p)
        return carry

    lax.fori_loop(0, acc.shape[0] // T, last, 0)
    drain()


def input_stage(dproj, weight, n, collective_id):
    length, width = dproj.shape[0], weight.shape[0]
    rows = length // n
    vmem = pl.BlockSpec(memory_space=pltpu.VMEM)
    anywhere = pl.BlockSpec(memory_space=pl.ANY)
    buffers, sems = scatter_scratch(length, rows, width)
    return pl.pallas_call(
        partial(input_kernel, n),
        out_shape=jax.ShapeDtypeStruct((rows, width), F32),
        in_specs=[anywhere] * 2,
        out_specs=vmem,
        scratch_shapes=[pltpu.VMEM(dproj.shape, BF16), pltpu.VMEM(weight.shape, BF16)]
        + buffers[1:] + [pltpu.SemaphoreType.DMA((2,))] + sems,
        compiler_params=pltpu.CompilerParams(
            collective_id=collective_id, has_side_effects=True, vmem_limit_bytes=60 << 20
        ),
        cost_estimate=pl.CostEstimate(
            flops=2 * length * width * dproj.shape[1], bytes_accessed=400 << 20, transcendentals=0
        ),
        name="input_stage",
    )(dproj, weight)


def output_kernel(dn_ref, er_ref, x_ref, t_ref, v_ref, pg_ref, lo_out, gx_out, gp_out):
    width = dn_ref.shape[1]
    tiles = width // 128

    @pl.when(pl.program_id(0) == 0)
    def _():
        gp_out[...] = jnp.zeros_like(gp_out)

    squares = jnp.zeros((T, 128), F32)
    dots = jnp.zeros((T, 128), F32)
    for c in range(tiles):
        cols = slice(c * 128, c * 128 + 128)
        xt = x_ref[pl.ds(c, T, stride=tiles), :]
        squares = squares + xt * xt
        dots = dots + dn_ref[:, cols] * pg_ref[0:1, cols] * xt
    inv = lax.rsqrt(jnp.sum(squares, axis=1, keepdims=True) / width + EPS)
    inv_b = jnp.broadcast_to(inv, (T, 128))
    mean = jnp.sum(dots, axis=1, keepdims=True) / width
    back_b = jnp.broadcast_to(inv * inv * inv * mean, (T, 128))
    mask_b = jnp.broadcast_to(column(v_ref[pl.ds(pl.program_id(0), 1), :].astype(F32)), (T, 128))
    for c in range(tiles):
        cols = slice(c * 128, c * 128 + 128)
        view = pl.ds(c, T, stride=tiles)
        xt = x_ref[view, :]
        scaled = dn_ref[:, cols] * inv_b
        error = er_ref[:, cols]
        lo_out[view, :] = error + t_ref[view, :]
        gx_out[view, :] = error * mask_b + scaled * pg_ref[0:1, cols] - xt * back_b
        gp_out[:, cols] += row_sums(scaled * xt)


def output_stage(dn, error, x_view, t_view, valid_rows, pg):
    rows, width = dn.shape
    block = pl.BlockSpec((T, width), lambda i: (i, 0))
    view = pl.BlockSpec((T * width // 128, 128), lambda i: (i, 0))
    whole = lambda shape: pl.BlockSpec(shape, lambda i: (0, 0))
    shape = jax.ShapeDtypeStruct
    return pl.pallas_call(
        output_kernel,
        grid=(rows // T,),
        in_specs=[block, block, view, view, whole(valid_rows.shape), whole(pg.shape)],
        out_specs=[view, view, whole((8, width))],
        out_shape=[shape(x_view.shape, F32), shape(x_view.shape, F32), shape((8, width), F32)],
        compiler_params=pltpu.CompilerParams(vmem_limit_bytes=40 << 20),
        name="output_stage",
    )(dn, error, x_view, t_view, valid_rows, pg)


def last_kernel(
    tp, mine, both, cols, gc_ref, go_ref,
    wz_out, wx_out, wdt_out, wbc_out, wo_out, cw_out, cb_out, gain_out, skip_out, dtb_out, alog_out,
    gp_out, bw_out, bb_out, loss_out,
):
    channels = wz_out.shape[1]
    heads = wdt_out.shape[0]
    width = gp_out.shape[1]
    wz_out[...] = gc_ref[:, 0:channels].astype(F32)
    wx_out[...] = gc_ref[:, channels : 2 * channels].astype(F32)
    wdt_out[...] = gc_ref[:, 2 * channels + 256 : 2 * channels + 384].astype(F32).T[0:heads, :]
    wbc_out[...] = cols[...]
    for c in range(channels // 128):
        here = slice(c * 128, c * 128 + 128)
        wo_out[here, :] = go_ref[:, here].astype(F32).T
    per = channels // 128
    for k in range(7):
        for c in range(per):
            here = slice(c * 128, c * 128 + 128)
            line = mine[k * per + c : k * per + c + 1, :]
            if k < 4:
                cw_out[k : k + 1, here] = line
            elif k == 4:
                cb_out[:, here] = line
            elif k == 5:
                gain_out[:, here] = line
    lane = iota((1, 128), 1)
    skip = jnp.zeros((1, 128), F32)
    for c in range(per):
        line = mine[6 * per + c : 6 * per + c + 1, :]
        low = jnp.sum(jnp.where(lane < 64, line, 0.0), axis=1, keepdims=True)
        high = jnp.sum(jnp.where(lane < 64, 0.0, line), axis=1, keepdims=True)
        skip = skip + jnp.where(lane == 2 * c, low, 0.0) + jnp.where(lane == 2 * c + 1, high, 0.0)
    skip_out[...] = skip[:, 0:heads]
    dtb_out[...] = mine[7 * per : 7 * per + 1, 0:heads]
    alog_out[...] = mine[7 * per + 1 : 7 * per + 2, 0:heads]
    top = width // 128
    for c in range(top):
        gp_out[:, c * 128 : c * 128 + 128] = both[c : c + 1, :]
    me = lax.axis_index("tp")
    local = bb_out.shape[1]
    for k in range(5):
        for peer in range(tp):
            at = peer * local
            line = both[top + 2 * k + at // 128 : top + 2 * k + at // 128 + 1, at % 128 : at % 128 + local]

            @pl.when(me == peer)
            def _():
                if k < 4:
                    bw_out[k : k + 1, :] = line
                else:
                    bb_out[...] = line

    lost = jnp.sum(both[top + 10 : top + 11, :], axis=1, keepdims=True)
    count = jnp.sum(both[top + 11 : top + 12, :], axis=1, keepdims=True)
    loss_out[...] = lost / (jnp.maximum(count, 1.0) * width)


def last_stage(mine, both, cols, g_cat, g_out, heads, width, tp):
    rows = g_cat.shape[0]
    channels = g_out.shape[1]
    local = cols.shape[0]
    vmem = pl.BlockSpec(memory_space=pltpu.VMEM)
    shapes = [
        (rows, channels), (rows, channels), (heads, rows), cols.shape, (channels, rows),
        (4, channels), (1, channels), (1, channels), (1, heads), (1, heads), (1, heads),
        (1, width), (4, local), (1, local), (1, 1),
    ]
    return pl.pallas_call(
        partial(last_kernel, tp),
        in_specs=[vmem] * 5,
        out_specs=[vmem] * len(shapes),
        out_shape=[jax.ShapeDtypeStruct(shape, F32) for shape in shapes],
        compiler_params=pltpu.CompilerParams(vmem_limit_bytes=40 << 20),
        name="last_stage",
    )(mine, both, cols, g_cat, g_out)


def local(
    x_in, target, seg_ids, valid, pre_gain, w_z, w_x, w_bc, w_dt, conv_x_w, conv_x_b,
    conv_bc_w, conv_bc_b, dt_bias, a_log, d_skip, norm_gain, w_out,
):
    rows, _, width = x_in.shape
    channels = w_z.shape[1]
    heads = w_dt.shape[1]
    tp = lax.axis_size("tp")
    inner = channels * tp
    bc_local = w_bc.shape[1]
    dp = lax.axis_size("dp")
    x_view = x_in.reshape(rows * width // 128, 128)
    t_view = target.reshape(rows * width // 128, 128)
    seg = seg_ids.reshape(-1, 128)
    bp = jnp.pad(jnp.concatenate([conv_bc_w, conv_bc_b[:, None]], axis=1), ((0, 0), (0, 123)))
    dtt = jnp.pad(w_dt.T, ((0, 128 - heads), (0, 0)))
    hp = jnp.pad(jnp.stack([dt_bias, a_log, d_skip]), ((0, 5), (0, 128 - heads)), constant_values=-100.0)
    (
        z, xs, xcv, y, bcr, bcv, dtr, bcc, st,
        normed_all, wc, wo, error, d_branch, rk_own, lost, chp, bcp, hp,
    ) = front_stage(
        x_view, t_view, w_z, w_x, w_out, w_bc.T, dtt, bp, pre_gain[None], seg, conv_x_w.T, conv_x_b[None],
        norm_gain[None], hp, valid.reshape(-1, 128), tp, dp, inner, 1,
    )
    saved = (z, xs, xcv, y, bcr, bcv, dtr, bcc, st)
    dproj, yn, db_all, accc, accb, acch = back_stage(d_branch, rk_own, seg, chp, bcp, hp, wo, saved, tp, 2)

    def dot_tn(a, b):
        return lax.dot_general(a, b, (((0,), (0,)), ((), ())), preferred_element_type=F32)

    g_out = dot_tn(db_all, yn).astype(BF16)
    g_cat = dot_tn(normed_all, dproj).astype(BF16)
    g_out, g_cat, dproj = lax.optimization_barrier((g_out, g_cat, dproj))
    g_out = lax.psum_scatter(g_out, "dp", scatter_dimension=0, tiled=True)
    g_cat = lax.psum_scatter(g_cat, "dp", scatter_dimension=0, tiled=True)
    d_normed = input_stage(dproj, wc, tp, 3)
    lo_view, gx_view, gain_part = output_stage(
        d_normed, error, x_view, t_view, valid.reshape(-1, 128), pre_gain[None]
    )
    mine, both, cols = finish(accc, acch, accb, gain_part, lost, g_cat, dp, tp, 5)
    (
        grad_wz, grad_wx, grad_wdt, grad_wbc, grad_wo, grad_cw, grad_cb, grad_gain, grad_skip, grad_dtb, grad_alog,
        grad_pre, grad_bw, grad_bb, loss,
    ) = last_stage(mine, both, cols, g_cat, g_out, heads, width, tp)
    return (
        lo_view.reshape(x_in.shape),
        loss.reshape(()),
        gx_view.reshape(x_in.shape),
        grad_pre.reshape(-1),
        grad_wz,
        grad_wx,
        grad_wbc.T,
        grad_wdt.T,
        grad_cw.T,
        grad_cb.reshape(-1),
        grad_bw.T,
        grad_bb.reshape(-1),
        grad_dtb.reshape(-1),
        grad_alog.reshape(-1),
        grad_skip.reshape(-1),
        grad_gain.reshape(-1),
        grad_wo,
    )


def solution(mesh):
    tok, col, head = P("tp", "dp", None), P("dp", "tp"), P("tp")
    in_specs = (
        tok, tok, P("dp", None), col, P(), col, col, col, col,
        P("tp", None), head, P("tp", None), head, head, head, head, head, P("tp", "dp"),
    )
    out_specs = (
        tok, P(), tok, P(), col, col, col, col,
        P("tp", None), head, P("tp", None), head, head, head, head, head, P("tp", "dp"),
    )
    return jax.shard_map(local, mesh=mesh, in_specs=in_specs, out_specs=out_specs, check_vma=False)
```

```python
from functools import partial

import jax
import jax.numpy as jnp
from jax import lax
from jax.experimental import pallas as pl
from jax.experimental.pallas import tpu as pltpu
from jax.sharding import PartitionSpec as P

T = 128
TB = 256
EPS = 1e-05
LEFT_LAG = 3
LOG2E = 1.4426950408889634
F32 = jnp.float32
BF16 = jnp.bfloat16
ZT = YT = F32
XT = CT = BF16
HIGHEST = lax.Precision.HIGHEST


def dot(a, b, precision=None):
    return jnp.dot(a, b, preferred_element_type=F32, precision=precision)


def dot_nt(a, b):
    return lax.dot_general(a, b, (((1,), (1,)), ((), ())), preferred_element_type=F32)


def lanes(column_of, index, rows=T):
    return jnp.broadcast_to(column_of[:, index : index + 1], (rows, 128))


def iota(shape, axis):
    return lax.broadcasted_iota(jnp.int32, shape, axis)


def step_sizes(raw, hp_ref):
    shifted = raw + hp_ref[0:1, :]
    dt = jnp.maximum(shifted, 0.0) + jnp.log1p(jnp.exp(-jnp.abs(shifted)))
    la = dt * hp_ref[1:2, :]
    inclusive = (iota((T, T), 0) >= iota((T, T), 1)).astype(F32)
    cum = dot(inclusive, la * LOG2E, HIGHEST)
    return shifted, dt, la, cum


def split_pair(value):
    first = iota((T, 128), 1) < 64
    zero = jnp.zeros_like(value)
    return jnp.concatenate([jnp.where(first, value, zero), jnp.where(first, zero, value)], axis=0)


def eye():
    return iota((T, T), 0) == iota((T, T), 1)


def column(row):
    return jnp.sum(jnp.where(eye(), jnp.broadcast_to(row, (T, T)), 0.0), axis=1, keepdims=True)


def row(col):
    return jnp.sum(jnp.where(eye(), jnp.broadcast_to(col, (T, T)), 0.0), axis=0, keepdims=True)


def document_columns(seg_ref, segc, segf):
    length = segc.shape[0] - 16
    segf[...] = seg_ref[...].astype(F32)
    segc[0:8, :] = jnp.full((8, 128), -1.0, F32)
    segc[length + 8 : length + 16, :] = jnp.full((8, 128), -1.0, F32)

    def chunk(i, carry):
        here = pl.ds(pl.multiple_of(i * T + 8, 8), T)
        segc[here, :] = jnp.broadcast_to(column(segf[pl.ds(i, 1), :]), (T, 128))
        return carry

    lax.fori_loop(0, length // T, chunk, 0)


def row_sums(value):
    return jnp.sum(value.reshape(value.shape[0] // 8, 8, value.shape[1]), axis=0)


def backward_block(
    t, block, dball, wo_ref, rk_all, segc, segf, chp_ref, bcp_ref, hp_ref,
    z_ref, xs_ref, xcv_ref, y_ref, bcr_ref, bcv_ref, dtr_ref, bcc_ref, st_ref,
    dproj_out, yn_out, accc_out, accb_out, acch_out,
    dyn, dbuf, dbcbuf, dstate, dstate_b, dyec, xte, cs_rows, fold, pick,
):
    channels = wo_ref.shape[0]
    pairs = channels // 128
    start = pl.multiple_of(block * TB, TB)
    for n in range(channels // 256):
        cols = slice(n * 256, n * 256 + 256)
        dyn[:, cols] = dot_nt(dball[pl.ds(start, TB), :], wo_ref[cols, :])
    first = iota((T, 128), 1) < 64
    for c in reversed(range(TB // T)):
        r0 = c * T
        rows = slice(r0, r0 + T)
        chunk = block * (TB // T) + c
        near = segc[pl.ds(pl.multiple_of(start + r0, T), T + 16), :]
        seg_col = near[8 : T + 8, :]
        ahead = [(near[8 + d : 8 + d + T, :] == seg_col).astype(F32) for d in (1, 2, 3)]
        start_b = (seg_col == near[7:8, :]).astype(F32)
        end_b = (seg_col == near[T + 7 : T + 8, :]).astype(F32)
        rg_b = jnp.broadcast_to(column(rk_all[chunk, 0:1, :]), (T, 128))
        kc_b = jnp.broadcast_to(column(rk_all[chunk, 1:2, :]), (T, 128))
        bm, cm = bcc_ref[rows, 0:128], bcc_ref[rows, 128:256]
        ct = cm.T
        shifted, dt, la, cum = step_sizes(dtr_ref[rows, :], hp_ref)
        cum_t = cum.T
        scores, scores_t = dot_nt(cm, bm), dot_nt(bm, cm)
        same = seg_col == segf[pl.ds(chunk, 1), :]
        below = iota((T, T), 0) >= iota((T, T), 1)
        strict = iota((T, T), 0) > iota((T, T), 1)
        above = iota((T, T), 0) <= iota((T, T), 1)
        qs = jnp.where(same & strict, scores, 0.0)
        qt = jnp.where(same & above, scores_t, 0.0)
        dstate_b[...] = dstate[...].astype(BF16)
        dq = jnp.zeros((T, T), F32)
        rsum = jnp.zeros((T, 128), F32)
        ddt = jnp.zeros((T, 128), F32)
        xsum = jnp.zeros((T, 128), F32)
        ksum = jnp.zeros((16, 128), F32)
        for j in range(pairs):
            cols = slice(j * 128, j * 128 + 128)
            zz = z_ref[rows, cols].astype(F32)
            y = y_ref[rows, cols].astype(F32)
            sz = 0.5 + 0.5 * jnp.tanh(0.5 * zz)
            silu_z = zz * sz
            dsz = sz + silu_z * (1.0 - sz)
            g = y * silu_z
            gr = g * rg_b
            gain = chp_ref[6:7, cols]
            dynp = dyn[rows, cols]
            yn_out[rows, cols] = (gr * gain).astype(BF16)
            accc_out[5, :, cols] += row_sums(dynp * gr)
            dg = rg_b * dynp * gain - g * kc_b
            dy = dg * silu_z
            dproj_out[rows, cols] = (dg * y * dsz).astype(BF16)
            xcv = xcv_ref[rows, cols].astype(F32)
            sx = 0.5 + 0.5 * jnp.tanh(0.5 * xcv)
            xc = xcv * sx
            dsx = sx + xc * (1.0 - sx)
            accc_out[6, :, cols] += row_sums(dy * xc)
            dt_e = jnp.where(first, lanes(dt, 2 * j), lanes(dt, 2 * j + 1))
            ca, cb = lanes(cum, 2 * j), lanes(cum, 2 * j + 1)
            cum_e = jnp.where(first, ca, cb)
            into = jnp.exp2(cum_e) * start_b
            to_end = jnp.exp2(cum_e[T - 1 : T, :] - cum_e) * end_b
            decay = into[T - 1 : T, :]
            xdt = xc * dt_e
            dy_b = dy.astype(BF16)
            ga = ca - cum_t[2 * j : 2 * j + 1, :]
            gb = cb - cum_t[2 * j + 1 : 2 * j + 2, :]
            grad = dot_nt(dy_b, split_pair(xdt.astype(BF16)))
            gea = grad[:, :128] * jnp.exp2(jnp.minimum(ga, 0.0))
            geb = grad[:, 128:] * jnp.exp2(jnp.minimum(gb, 0.0))
            dq = dq + gea + geb
            pp = jnp.concatenate([(gea * qs).astype(BF16), (geb * qs).astype(BF16)], axis=1)
            rsum = rsum + dot(pp, pick[j, :, :])
            csum = dot(jnp.ones((8, T), BF16), pp)
            cs_rows[2 * j : 2 * j + 1, :] = csum[0:1, :128]
            cs_rows[2 * j + 1 : 2 * j + 2, :] = csum[0:1, 128:]
            eta = (jnp.exp2(jnp.minimum(-ga, 0.0)) * qt).astype(BF16)
            etb = (jnp.exp2(jnp.minimum(-gb, 0.0)) * qt).astype(BF16)
            dxdt = dot(jnp.concatenate([eta, etb], axis=1), split_pair(dy_b))
            dx_state = to_end * dot(bm, dstate_b[:, cols])
            dxdt = dxdt + dx_state
            y_in = into * dot(cm, st_ref[c, :, cols])
            dyec_p = (dy * into).astype(BF16)
            dyec[:, cols] = dyec_p
            xte[:, cols] = (xdt * to_end).astype(BF16)
            ddt = ddt + dot((xc * dxdt).astype(BF16), fold[j, :, :])
            rsum = rsum + dot((dy * y_in).astype(BF16), fold[j, :, :])
            xsum = xsum + dot((xdt * dx_state).astype(BF16), fold[j, :, :])
            old = dstate[:, cols]
            kpart = row_sums(old * st_ref[c, :, cols].astype(F32)) * decay
            khigh = kpart.astype(BF16)
            klow = (kpart - khigh.astype(F32)).astype(BF16)
            ksum = ksum + dot(jnp.concatenate([khigh, klow], axis=0), fold[j, :, :])
            dstate[:, cols] = old * decay + dot(ct, dyec_p)
            dxcv = (dxdt * dt_e + chp_ref[5:6, cols] * dy) * dsx
            dbuf[0:T, cols] = dxcv
            xs = xs_ref[rows, cols].astype(F32)
            dxs = dxcv * chp_ref[3:4, cols]
            accc_out[4, :, cols] += row_sums(dxcv)
            accc_out[3, :, cols] += row_sums(dxcv * xs)
            for d in (1, 2, 3):
                moved = dbuf[d : d + T, cols] * ahead[d - 1]
                dxs = dxs + moved * chp_ref[3 - d : 4 - d, cols]
                accc_out[3 - d, :, cols] += row_sums(moved * xs)
            dproj_out[rows, channels + j * 128 : channels + j * 128 + 128] = dxs.astype(BF16)
        dbuf[T : T + 8, :] = dbuf[0:8, :]
        dqm = jnp.where(same & below, dq, 0.0)
        dc = dot(dqm.astype(BF16), bm) + dot_nt(dyec[...], st_ref[c, :, :])
        db_rows = dot(dqm.T.astype(BF16), cm) + dot_nt(xte[...], dstate_b[...])
        for half, grad_half in enumerate((db_rows, dc)):
            cols = slice(half * 128, half * 128 + 128)
            raw = bcv_ref[rows, cols].astype(F32)
            sb = 0.5 + 0.5 * jnp.tanh(0.5 * raw)
            dcv = grad_half * (sb + raw * sb * (1.0 - sb))
            dbcbuf[0:T, cols] = dcv
            xs = bcr_ref[rows, cols].astype(F32)
            dxs = dcv * bcp_ref[3:4, cols]
            accb_out[4, :, cols] += row_sums(dcv)
            accb_out[3, :, cols] += row_sums(dcv * xs)
            for d in (1, 2, 3):
                moved = dbcbuf[d : d + T, cols] * ahead[d - 1]
                dxs = dxs + moved * bcp_ref[3 - d : 4 - d, cols]
                accb_out[3 - d, :, cols] += row_sums(moved * xs)
            dproj_out[rows, 2 * channels + half * 128 : 2 * channels + half * 128 + 128] = dxs.astype(BF16)
        dbcbuf[T : T + 8, :] = dbcbuf[0:8, :]
        after = (iota((T, T), 0) <= iota((T, T), 1)).astype(F32)
        before = (iota((T, T), 0) > iota((T, T), 1)).astype(F32)
        dla = dot(after, rsum - cs_rows[...].T, HIGHEST) + dot(before, xsum, HIGHEST)
        dla = dla + jnp.sum(ksum, axis=0, keepdims=True)
        ddtr = (ddt + dla * hp_ref[1:2, :]) * (0.5 + 0.5 * jnp.tanh(0.5 * shifted))
        acch_out[0, :, :] += row_sums(ddtr)
        acch_out[1, :, :] += row_sums(dla * la)
        dproj_out[rows, 2 * channels + 256 : 2 * channels + 384] = ddtr.astype(BF16)


MESH_ID = pl.DeviceIdType.MESH


def meet(n, axis):
    me = lax.axis_index(axis)
    barrier = pltpu.get_barrier_semaphore()
    for peer in range(n):

        @pl.when(me != peer)
        def _():
            pl.semaphore_signal(barrier, inc=1, device_id={axis: peer}, device_id_type=MESH_ID)

    pl.semaphore_wait(barrier, n - 1)
    return me


def to_peer(source, target, send_sem, recv_sem, axis, peer):
    return pltpu.make_async_remote_copy(
        src_ref=source, dst_ref=target, send_sem=send_sem, recv_sem=recv_sem,
        device_id={axis: peer}, device_id_type=MESH_ID,
    )


def finish_kernel(
    dp, tp, ac_ref, ah_ref, ab_ref, gp_ref, lost_ref, gc_ref,
    mine_out, both_out, cols_out, got, got_both, cols, got_cols, sems,
):
    me_dp, me_tp = lax.axis_index("dp"), lax.axis_index("tp")
    barrier = pltpu.get_barrier_semaphore()
    for peer in range(dp):

        @pl.when(me_dp != peer)
        def _():
            pl.semaphore_signal(barrier, inc=1, device_id={"dp": peer}, device_id_type=MESH_ID)

    for peer in range(tp):

        @pl.when(me_tp != peer)
        def _():
            pl.semaphore_signal(barrier, inc=1, device_id={"tp": peer}, device_id_type=MESH_ID)

    channels = ac_ref.shape[2]
    per = channels // 128
    first = mine_out.shape[0]
    top = gp_ref.shape[1] // 128
    got[me_dp] = jnp.zeros_like(got[0])

    def put(line, value):
        got[pl.ds(me_dp, 1), line : line + 1, :] = value[None]

    for k in range(7):
        sums = jnp.sum(ac_ref[k], axis=0, keepdims=True)
        for c in range(per):
            put(k * per + c, sums[:, c * 128 : c * 128 + 128])
    for k in range(2):
        put(7 * per + k, jnp.sum(ah_ref[k], axis=0, keepdims=True))
    sums = jnp.sum(gp_ref[...], axis=0, keepdims=True)
    for c in range(top):
        put(first + c, sums[:, c * 128 : c * 128 + 128])
    for k in range(5):
        sums = jnp.sum(ab_ref[k], axis=0, keepdims=True)
        for c in range(2):
            put(first + top + 2 * k + c, sums[:, c * 128 : c * 128 + 128])
    put(first + top + 10, jnp.sum(lost_ref[0:8, :], axis=0, keepdims=True))
    put(first + top + 11, lost_ref[8:9, :])
    turned = gc_ref[:, 2 * channels : 2 * channels + 256].astype(F32).T
    cols[...] = turned.reshape(cols.shape)
    pl.semaphore_wait(barrier, dp - 1 + tp - 1)

    def over_dp(peer, slot):
        return to_peer(got.at[me_dp], got.at[slot], sems.at[0, peer], sems.at[1, slot], "dp", peer)

    def over_tp(peer, slot):
        return to_peer(got_both.at[me_tp], got_both.at[slot], sems.at[2, peer], sems.at[3, slot], "tp", peer)

    def over_cols(peer, slot):
        return to_peer(cols.at[peer], got_cols.at[slot], sems.at[4, peer], sems.at[5, slot], "tp", peer)

    for peer in range(dp):

        @pl.when(me_dp != peer)
        def _():
            over_dp(peer, me_dp).start()

    for peer in range(tp):

        @pl.when(me_tp != peer)
        def _():
            over_cols(peer, me_tp).start()

    got_cols[pl.ds(me_tp, 1)] = cols[pl.ds(me_tp, 1)]
    for peer in range(dp):

        @pl.when(me_dp != peer)
        def _():
            over_dp(peer, peer).wait_recv()

    total = got[0]
    for peer in range(1, dp):
        total = total + got[peer]
    mine_out[...] = total[:first]
    got_both[pl.ds(me_tp, 1)] = total[first:][None]
    for peer in range(tp):

        @pl.when(me_tp != peer)
        def _():
            over_tp(peer, me_tp).start()

    for peer in range(tp):

        @pl.when(me_tp != peer)
        def _():
            over_cols(peer, peer).wait_recv()
            over_tp(peer, peer).wait_recv()

    total, columns = got_both[0], got_cols[0]
    for peer in range(1, tp):
        total, columns = total + got_both[peer], columns + got_cols[peer]
    both_out[...] = total
    cols_out[...] = columns
    for peer in range(dp):

        @pl.when(me_dp != peer)
        def _():
            over_dp(peer, me_dp).wait_send()

    for peer in range(tp):

        @pl.when(me_tp != peer)
        def _():
            over_cols(peer, me_tp).wait_send()
            over_tp(peer, me_tp).wait_send()


def finish(accc, acch, accb, gain_part, lost, g_cat, dp, tp, collective_id):
    vmem = pl.BlockSpec(memory_space=pltpu.VMEM)
    first = -(-(7 * accc.shape[2] // 128 + 2) // 8) * 8
    second = -(-(gain_part.shape[1] // 128 + 12) // 8) * 8
    cols = (tp, 256 // tp, g_cat.shape[0])
    shape = jax.ShapeDtypeStruct
    return pl.pallas_call(
        partial(finish_kernel, dp, tp),
        out_shape=[shape((first, 128), F32), shape((second, 128), F32), shape(cols[1:], F32)],
        in_specs=[vmem] * 6,
        out_specs=[vmem] * 3,
        scratch_shapes=[
            pltpu.VMEM((dp, first + second, 128), F32),
            pltpu.VMEM((tp, second, 128), F32),
            pltpu.VMEM(cols, F32),
            pltpu.VMEM(cols, F32),
            pltpu.SemaphoreType.DMA((6, max(dp, tp))),
        ],
        compiler_params=pltpu.CompilerParams(collective_id=collective_id, has_side_effects=True),
        name="finish",
    )(accc, acch, accb, gain_part, lost, g_cat)


def back_kernel(
    n, db_ref, rk_ref, seg_ref, chp_ref, bcp_ref, hp_ref, wo_any,
    z_any, xs_any, xcv_any, y_any, bcr_any, bcv_any, dtr_any, bcc_any, st_any,
    dproj_any, yn_any, dball_any, accc_out, accb_out, acch_out,
    dball, rk_all, wo, zb, xsb, xcvb, yb, bcrb, bcvb, dtrb, bccb, stb, dprojb, ynb,
    dyn, dbuf, dbcbuf, dstate, dstate_b, dyec, xte, cs_rows, fold, pick, segc, segf,
    keep_sem, load_sem, save_sem, ag_send, ag_recv, r_send, r_recv,
):
    rows = db_ref.shape[0]
    pieces = rows // T
    gps = rows // TB
    subs = TB // T
    blocks = n * gps
    pairs = wo.shape[0] // 128
    sources = (z_any, xs_any, xcv_any, y_any, bcr_any, bcv_any, dtr_any, bcc_any, st_any)
    held = (zb, xsb, xcvb, yb, bcrb, bcvb, dtrb, bccb, stb)

    def load(i, t):
        block = blocks - 1 - t
        step = subs if i == len(held) - 1 else TB
        there = sources[i].at[pl.ds(pl.multiple_of(block * step, step), step)]
        return pltpu.make_async_copy(there, held[i].at[t % 2], load_sem.at[i, t % 2])

    fetch = pltpu.make_async_copy(wo_any, wo, keep_sem.at[0])
    fetch.start()
    own_rows = pl.ds(pl.multiple_of(lax.axis_index("tp") * rows, rows), rows)
    keep = pltpu.make_async_copy(db_ref, dball.at[own_rows], keep_sem.at[1])
    keep.start()
    for i in range(len(held)):
        load(i, 0).start()
    me = meet(n, "tp")

    def rk_to(peer, owner):
        return to_peer(rk_ref, rk_all.at[pl.ds(owner * pieces, pieces)], r_send.at[peer], r_recv.at[owner], "tp", peer)

    for peer in range(n):

        @pl.when(me != peer)
        def _():
            rk_to(peer, me).start()

    rk_all[pl.ds(me * pieces, pieces)] = rk_ref[...]

    def ag(way, index):
        here = dball.at[pl.ds(pl.multiple_of(index * T, T), T)]
        peer = me + 1 if way == 0 else me - 1
        return to_peer(here, here, ag_send.at[way, index], ag_recv.at[way, index], "tp", peer)

    keep.wait()
    mirror = n - 1 - me
    for p in range(pieces):
        index = ((me + 1) * gps - 1 - p // subs) * subs + p % subs

        @pl.when(me < n - 1)
        def _():
            ag(0, index).start()

        @pl.when((me > 0) & ((mirror == 0) | (mirror > p)))
        def _():
            ag(1, index).start()

    def low(k):
        for sub in range(subs):
            index = (me * gps - 1 - k) * subs + sub

            @pl.when((me * gps - 1 - k >= 0) & (k >= 0))
            def _():
                ag(0, index).wait_recv()

                @pl.when(me < n - 1)
                def _():
                    ag(0, index).start()

    def relay(k):
        for sub in range(subs):
            index = (blocks - 1 - k) * subs + sub

            @pl.when(k < mirror * gps)
            def _():
                ag(1, index).wait_recv()

                @pl.when(me > 0)
                def _():
                    ag(1, index).start()

        @pl.when(me < n - 1)
        def _():
            low(k)

        @pl.when((k == mirror * gps - 1) & (me > 0))
        def _():
            for p in range(pieces):

                @pl.when(mirror <= p)
                def _():
                    ag(1, ((me + 1) * gps - 1 - p // subs) * subs + p % subs).start()

    document_columns(seg_ref, segc, segf)
    dstate[...] = jnp.zeros_like(dstate)
    dbuf[...] = jnp.zeros_like(dbuf)
    dbcbuf[...] = jnp.zeros_like(dbcbuf)
    accc_out[...] = jnp.zeros_like(accc_out)
    accb_out[...] = jnp.zeros_like(accb_out)
    acch_out[...] = jnp.zeros_like(acch_out)
    cs_rows[...] = jnp.zeros_like(cs_rows)
    for j in range(pairs):
        half = (iota((128, 128), 0) >= 64).astype(jnp.int32)
        fold[j, :, :] = (iota((128, 128), 1) == 2 * j + half).astype(F32).astype(BF16)
        part = (iota((256, 128), 0) >= 128).astype(jnp.int32)
        pick[j, :, :] = (iota((256, 128), 1) == 2 * j + part).astype(F32).astype(BF16)
    for peer in range(n):

        @pl.when(me != peer)
        def _():
            rk_to(peer, peer).wait_recv()

    fetch.wait()
    relay(0)

    def save(i, t):
        block = blocks - 1 - t
        source, target = ((dprojb, dproj_any), (ynb, yn_any))[i]
        return pltpu.make_async_copy(source, target.at[pl.ds(pl.multiple_of(block * TB, TB), TB)], save_sem.at[i])

    def turn(t, carry):
        @pl.when(t + 1 < blocks)
        def _():
            for i in range(len(held)):
                load(i, t + 1).start()

        for i in range(len(held)):
            load(i, t).wait()

        @pl.when(t > 0)
        def _():
            for i in range(2):
                save(i, t - 1).wait()

        @pl.when((me == n - 1) & (t >= gps))
        def _():
            low(t - gps)

        slot = t % 2
        backward_block(
            t, blocks - 1 - t, dball, wo, rk_all, segc, segf, chp_ref, bcp_ref, hp_ref,
            zb.at[slot], xsb.at[slot], xcvb.at[slot], yb.at[slot], bcrb.at[slot], bcvb.at[slot],
            dtrb.at[slot], bccb.at[slot], stb.at[slot],
            dprojb, ynb, accc_out, accb_out, acch_out,
            dyn, dbuf, dbcbuf, dstate, dstate_b, dyec, xte, cs_rows, fold, pick,
        )
        for i in range(2):
            save(i, t).start()

        @pl.when(t + 1 < blocks - gps)
        def _():
            relay(t + 1)

        return carry

    lax.fori_loop(0, blocks, turn, 0)
    keep_all = pltpu.make_async_copy(dball, dball_any, keep_sem.at[2])
    keep_all.start()
    for i in range(2):
        save(i, blocks - 1).wait()

    def drain(index, carry):
        block = index // subs

        @pl.when((me < n - 1) & (block < (me + 1) * gps))
        def _():
            ag(0, index).wait_send()

        @pl.when((me > 0) & (block >= me * gps))
        def _():
            ag(1, index).wait_send()

        return carry

    lax.fori_loop(0, n * pieces, drain, 0)
    for peer in range(n):

        @pl.when(me != peer)
        def _():
            rk_to(peer, me).wait_send()

    keep_all.wait()


def back_stage(db, rk, seg, chp, bcp, hp, wo, saved, n, collective_id):
    rows, width = db.shape
    length = n * rows
    channels = wo.shape[0]
    pairs = channels // 128
    total = 2 * channels + 384
    shape = jax.ShapeDtypeStruct
    vmem = pl.BlockSpec(memory_space=pltpu.VMEM)
    anywhere = pl.BlockSpec(memory_space=pl.ANY)
    dma = pltpu.SemaphoreType.DMA
    held = [pltpu.VMEM((2, TB) + item.shape[1:], item.dtype) for item in saved[:-1]]
    held.append(pltpu.VMEM((2, TB // T, 128, channels), BF16))
    return pl.pallas_call(
        partial(back_kernel, n),
        out_shape=[
            shape((length, total), BF16), shape((length, channels), BF16), shape((length, width), BF16),
            shape((7, 8, channels), F32), shape((5, 8, 256), F32), shape((2, 8, 128), F32),
        ],
        in_specs=[anywhere] + [vmem] * 5 + [anywhere] * 10,
        out_specs=[anywhere] * 3 + [vmem] * 3,
        scratch_shapes=[
            pltpu.VMEM((length, width), BF16),
            pltpu.VMEM((length // T, 8, 128), F32),
            pltpu.VMEM(wo.shape, BF16),
        ] + held + [
            pltpu.VMEM((TB, total), BF16),
            pltpu.VMEM((TB, channels), BF16),
            pltpu.VMEM((TB, channels), F32),
            pltpu.VMEM((T + 8, channels), F32),
            pltpu.VMEM((T + 8, 256), F32),
            pltpu.VMEM((128, channels), F32),
            pltpu.VMEM((128, channels), BF16),
            pltpu.VMEM((T, channels), BF16),
            pltpu.VMEM((T, channels), BF16),
            pltpu.VMEM((128, 128), F32),
            pltpu.VMEM((pairs, 128, 128), BF16),
            pltpu.VMEM((pairs, 256, 128), BF16),
            pltpu.VMEM((length + 16, 128), F32),
            pltpu.VMEM((length // T, 128), F32),
            dma((3,)), dma((9, 2)), dma((2,)),
            dma((2, length // T)), dma((2, length // T)), dma((n,)), dma((n,)),
        ],
        compiler_params=pltpu.CompilerParams(
            collective_id=collective_id, has_side_effects=True, vmem_limit_bytes=60 << 20
        ),
        name="back_stage",
    )(db, rk, seg, chp, bcp, hp, wo, *saved)


def scatter_body(n, me, a_ref, right_refs, acc, part, slots, send_sem, recv_sem):
    rows, width = acc.shape
    group = part.shape[0]
    piece = slots.shape[2]
    pieces = rows // piece
    groups = rows // group
    subs = group // piece

    def link(way, index):
        peer = me + 1 if way == 0 else me - 1
        return to_peer(
            slots.at[way, index], slots.at[way, index], send_sem.at[way, index], recv_sem.at[way, index], "tp", peer
        )

    def own(start, target, base):
        def tile(i, carry):
            cols = pl.ds(pl.multiple_of(i * 256, 256), 256)
            total, at = None, 0
            for w_ref in right_refs:
                depth = w_ref.shape[1]
                term = dot_nt(a_ref[pl.ds(start, group), at : at + depth], w_ref[cols, :])
                total = term if total is None else total + term
                at += depth
            target[pl.ds(base, group), cols] = total
            return carry

        lax.fori_loop(0, width // 256, tile, 0)

    def pass_on(way, q, at_end):
        shard = n - 1 - q // groups if way == 0 else q // groups
        start = pl.multiple_of(shard * rows + (q % groups) * group, group)
        own(start, part, 0)
        for sub in range(subs):
            index = shard * pieces + (q % groups) * subs + sub
            here = slice(sub * piece, (sub + 1) * piece)

            @pl.when(at_end)
            def _():
                slots[way, index] = part[here, :].astype(BF16)

            @pl.when(jnp.logical_not(at_end))
            def _():
                link(way, index).wait_recv()
                slots[way, index] = (part[here, :] + slots[way, index].astype(F32)).astype(BF16)

            link(way, index).start()

    def turn(t, carry):
        for way in (0, 1):
            hops = me if way == 0 else n - 1 - me
            q = t - hops

            @pl.when((q >= 0) & (q < (n - 1 - hops) * groups))
            def _():
                pass_on(way, q, hops == 0)

        late = t - (n - 1)

        @pl.when((late >= 0) & (late < groups))
        def _():
            base = pl.multiple_of(late * group, group)
            own(pl.multiple_of(me * rows + late * group, group), acc, base)

        return carry

    lax.fori_loop(0, (n - 1) * groups + n - 1, turn, 0)

    def arrived(p):
        for way in (0, 1):

            @pl.when((me > 0) if way == 0 else (me < n - 1))
            def _():
                link(way, me * pieces + p).wait_recv()
                here = pl.ds(pl.multiple_of(p * piece, piece), piece)
                acc[here, :] += slots[way, me * pieces + p].astype(F32)

    def drain():
        def done(index, carry):
            shard = index // pieces
            for way in (0, 1):

                @pl.when((me < shard) if way == 0 else (me > shard))
                def _():
                    link(way, index).wait_send()

            return carry

        lax.fori_loop(0, n * pieces, done, 0)

    return arrived, drain


def forward_block(
    t, nb, wc, segc, segf, chp_ref, bcp_ref, hp_ref,
    zbuf, xs_out, xcv_out, y_out, u_all, bcr_out, bcv_out, dtr_out, bcc_out, st_out, sq_all,
    xbuf, bcbuf, state,
):
    channels = zbuf.shape[1]
    pairs = channels // 128
    start = pl.multiple_of(t * TB, TB)
    nb_rows = pl.ds(start, TB)
    for n in range(channels // 256):
        cols = slice(n * 256, n * 256 + 256)
        zbuf[:, cols] = dot(nb[nb_rows, :], wc[:, cols])
        xbuf[8 : 8 + TB, cols] = dot(nb[nb_rows, :], wc[:, channels + n * 256 : channels + n * 256 + 256])
    bd = dot(nb[nb_rows, :], wc[:, 2 * channels :])
    bcbuf[8 : 8 + TB, :] = bd[:, :256]
    dtr_out[...] = bd[:, 256:]
    bcr_out[...] = bd[:, :256].astype(BF16)
    first = iota((T, 128), 1) < 64
    for c in range(TB // T):
        r0 = c * T
        rows = slice(r0, r0 + T)
        chunk = t * (TB // T) + c
        at = pl.ds(pl.multiple_of(start + r0, T), T)
        near = segc[pl.ds(pl.multiple_of(start + r0, T), T + 8), :]
        seg_col = near[8:, :]
        masks = [(near[8 - d : 8 - d + T, :] == seg_col).astype(F32) for d in (1, 2, 3)]
        start_b = (seg_col == near[7:8, :]).astype(F32)
        end_b = (seg_col == near[T + 7 : T + 8, :]).astype(F32)
        parts = []
        for half in range(2):
            cols = slice(half * 128, half * 128 + 128)
            acc = bcbuf[8 + r0 : 8 + r0 + T, cols] * bcp_ref[3:4, cols] + bcp_ref[4:5, cols]
            for d in (1, 2, 3):
                acc = acc + bcbuf[8 + r0 - d : 8 + r0 - d + T, cols] * bcp_ref[3 - d : 4 - d, cols] * masks[d - 1]
            bcv_out[rows, cols] = acc.astype(BF16)
            hv = 0.5 * acc
            parts.append((hv + hv * jnp.tanh(hv)).astype(BF16))
            bcc_out[rows, cols] = parts[-1]
        bm, cm = parts
        bt = bm.T
        _, dt, la, cum = step_sizes(dtr_out[rows, :], hp_ref)
        cum_t = cum.T
        scores = dot_nt(cm, bm)
        keep = (seg_col == segf[pl.ds(chunk, 1), :]) & (iota((T, T), 0) >= iota((T, T), 1))
        qm = jnp.where(keep, scores, 0.0)
        sq = jnp.zeros((T, 128), F32)
        st_out[c, :, :] = state[...].astype(BF16)
        for j in range(pairs):
            cols = slice(j * 128, j * 128 + 128)
            acc = xbuf[8 + r0 : 8 + r0 + T, cols] * chp_ref[3:4, cols] + chp_ref[4:5, cols]
            xs_out[rows, cols] = xbuf[8 + r0 : 8 + r0 + T, cols].astype(BF16)
            for d in (1, 2, 3):
                acc = acc + xbuf[8 + r0 - d : 8 + r0 - d + T, cols] * chp_ref[3 - d : 4 - d, cols] * masks[d - 1]
            xcv_out[rows, cols] = acc.astype(BF16)
            hv = 0.5 * acc
            xc = hv + hv * jnp.tanh(hv)
            dt_e = jnp.where(first, lanes(dt, 2 * j), lanes(dt, 2 * j + 1))
            ca, cb = lanes(cum, 2 * j), lanes(cum, 2 * j + 1)
            cum_e = jnp.where(first, ca, cb)
            xdt = xc * dt_e
            ea = jnp.exp2(jnp.minimum(ca - cum_t[2 * j : 2 * j + 1, :], 0.0))
            eb = jnp.exp2(jnp.minimum(cb - cum_t[2 * j + 1 : 2 * j + 2, :], 0.0))
            mix = jnp.concatenate([(ea * qm).astype(BF16), (eb * qm).astype(BF16)], axis=1)
            y = dot(mix, split_pair(xdt.astype(BF16)))
            into = jnp.exp2(cum_e) * start_b
            last = cum_e[T - 1 : T, :]
            to_end = jnp.exp2(last - cum_e) * end_b
            y = y + into * dot(cm, st_out[c, :, cols])
            state[:, cols] = state[:, cols] * into[T - 1 : T, :] + dot(bt, (xdt * to_end).astype(BF16))
            y = y + chp_ref[5:6, cols] * xc
            y_out[rows, cols] = y
            hz = 0.5 * zbuf[rows, cols]
            g = y * (hz + hz * jnp.tanh(hz))
            sq = sq + g * g
            u_all[at, cols] = (g * chp_ref[6:7, cols]).astype(BF16)
        sq_all[chunk, :, :] = lax.dot_general(
            jnp.ones((8, 128), F32), sq, (((1,), (1,)), ((), ())), preferred_element_type=F32, precision=HIGHEST
        )
    xbuf[0:8, :] = xbuf[TB : TB + 8, :]
    bcbuf[0:8, :] = bcbuf[TB : TB + 8, :]


def front_kernel(
    n, dp, inner,
    x_ref, t_ref, wz_ref, wx_ref, wos_ref, bct_ref, dtt_ref, bp_ref, pg_ref, seg_ref, cw_ref, cb_ref, gain_ref, hp_ref, v_ref,
    z_out, xs_out, xcv_out, y_out, bcr_out, bcv_out, dtr_out, bcc_out, st_out,
    nb_out, wc_out, wo_out, er_out, db_out, rk_out, loss_out, chp_out, bcp_out, hp_out,
    nb, wc, wo, u_all, slots, acc, part,
    zbuf, xsb, xcvb, yb, bcrb, bcvb, dtrb, bccb, stb,
    xbuf, bcbuf, state, sq_all, sqs, xst, tst, erb, dbb,
    segc, segf, bc_all, bp_all, wbd,
    load_sem, keep_sem, save_sem, s_send, s_recv, w_send, w_hop, w_pass, w_recv, ag_send, ag_recv, rs_send, rs_recv, q_send, q_recv,
):
    me, me_dp = lax.axis_index("tp"), lax.axis_index("dp")
    rows, width = acc.shape
    pieces = rows // T
    tiles = width // 128
    gps = rows // TB
    subs = TB // T
    blocks = n * gps
    share_rows = wz_ref.shape[0]
    channels = wz_ref.shape[1]
    pairs = channels // 128
    barrier = pltpu.get_barrier_semaphore()
    for peer in range(dp):

        @pl.when(me_dp != peer)
        def _():
            pl.semaphore_signal(barrier, inc=1, device_id={"dp": peer}, device_id_type=MESH_ID)

    for peer in range(n):

        @pl.when(me != peer)
        def _():
            pl.semaphore_signal(barrier, inc=1, device_id={"tp": peer}, device_id_type=MESH_ID)

    def load(source, target, slot, p):
        view = source.at[pl.ds(pl.multiple_of(p * (T * tiles), T * tiles), T * tiles)]
        return pltpu.make_async_copy(view, target.at[slot], load_sem.at[0 if target is xst else 1, slot])

    load(x_ref, xst, 0, 0).start()

    def place(i, owner):
        at = pl.ds(pl.multiple_of(owner * share_rows, share_rows), share_rows)
        if i == 0:
            return wc.at[at, 0:channels]
        if i == 1:
            return wc.at[at, channels : 2 * channels]
        if i == 2:
            return wc.at[at, 2 * channels : 2 * channels + 384]
        return wo.at[:, at]

    local = (wz_ref, wx_ref, wbd, wos_ref)

    def keep_own(i):
        return pltpu.make_async_copy(local[i], place(i, me_dp), keep_sem.at[3 + i])

    for i in (0, 1, 3):
        keep_own(i).start()
    state[...] = jnp.zeros_like(state)
    xbuf[0:8, :] = jnp.zeros((8, xbuf.shape[1]), F32)
    bcbuf[0:8, :] = jnp.zeros((8, 256), F32)
    pl.semaphore_wait(barrier, dp - 1 + n - 1)

    core = me_dp % 2
    chip = me_dp // 2
    sibling = me_dp + 1 - 2 * core

    def give(i, peer):
        return to_peer(local[i], place(i, me_dp), w_send.at[i, peer], w_recv.at[i, me_dp], "dp", peer)

    def passed(i, owner):
        there = place(i, owner)
        return to_peer(there, there, w_pass.at[i, owner], w_recv.at[i, owner], "dp", sibling)

    square = dp == 8
    across = chip + 1 - 2 * (chip % 2)
    along = (chip + 2) % 4
    corner = 3 - chip

    def hop(i, owner, peer):
        there = place(i, owner)
        return to_peer(there, there, w_hop.at[i], w_recv.at[i, owner], "dp", peer)

    def onward(i):
        source, target = ((across, along), (along, across))[i]
        return hop(i, 2 * source + core, 2 * target + core)

    def give_all(i):
        if square and i < 2:
            give(i, 2 * across + core).start()
            give(i, 2 * along + core).start()
        else:
            for k in range(dp // 2):

                @pl.when(chip != k)
                def _():
                    give(i, 2 * k + core).start()

        give(i, sibling).start()

    def turn_corner(i):
        if square:
            owner = 2 * (across, along)[i] + core
            passed(i, owner).wait_recv()
            onward(i).start()
            passed(i, owner).start()

    def pass_all(i):
        if square and i < 2:
            for owner in (2 * (along, across)[i] + core, 2 * corner + core):
                passed(i, owner).wait_recv()
                passed(i, owner).start()
        else:
            for k in range(dp // 2):

                @pl.when(chip != k)
                def _():
                    passed(i, 2 * k + core).wait_recv()
                    passed(i, 2 * k + core).start()

    def wait_all(i):
        keep_own(i).wait()
        passed(i, sibling).wait_recv()
        for k in range(dp // 2):

            @pl.when(chip != k)
            def _():
                passed(i, 2 * k + 1 - core).wait_recv()

    def swap(i, peer, slot):
        source, target = ((bct_ref, bc_all), (bp_ref, bp_all))[i]
        return to_peer(source, target.at[slot], s_send.at[i, peer], s_recv.at[i, slot], "tp", peer)

    for peer in range(n):

        @pl.when(me != peer)
        def _():
            swap(0, peer, me).start()
            swap(1, peer, me).start()

    bc_all[pl.ds(me, 1)] = bct_ref[...][None]
    bp_all[pl.ds(me, 1)] = bp_ref[...][None]
    give_all(1)
    give_all(0)

    def ag(way, index):
        here = nb.at[pl.ds(pl.multiple_of(index * T, T), T)]
        peer = me + 1 if way == 0 else me - 1
        return to_peer(here, here, ag_send.at[way, index], ag_recv.at[way, index], "tp", peer)

    for p in range(pieces):
        load(x_ref, xst, p % 2, p).wait()
        if p + 1 < pieces:
            load(x_ref, xst, (p + 1) % 2, p + 1).start()
        squares = jnp.zeros((T, 128), F32)
        for c in range(tiles):
            xt = xst[p % 2, pl.ds(c, T, stride=tiles), :]
            squares = squares + xt * xt
        inv = lax.rsqrt(jnp.sum(squares, axis=1, keepdims=True) / width + EPS)
        inv_b = jnp.broadcast_to(inv, (T, 128))
        index = me * pieces + p
        here = pl.ds(pl.multiple_of(index * T, T), T)
        for c in range(tiles):
            cols = slice(c * 128, c * 128 + 128)
            xt = xst[p % 2, pl.ds(c, T, stride=tiles), :]
            nb[here, cols] = (xt * inv_b * pg_ref[0:1, cols]).astype(BF16)
        @pl.when((me < n - 1) & ((me == 0) | (me > p)))
        def _():
            ag(0, index).start()

        @pl.when(me > 0)
        def _():
            ag(1, index).start()

    for peer in range(n):

        @pl.when(me != peer)
        def _():
            swap(0, peer, peer).wait_recv()
            swap(1, peer, peer).wait_recv()

    columns = bc_all.shape[0] * bc_all.shape[1]
    wbd[:, 0:256] = bc_all[...].reshape(columns, share_rows).T
    wbd[:, 256:384] = dtt_ref[...].T
    keep_own(2).start()
    give_all(2)
    bcp_out[...] = bp_all[...].reshape(columns, 128).T[0:8, :]
    hp_out[...] = hp_ref[...]
    hp_out[1:2, :] = -jnp.exp(hp_ref[1:2, :])
    chp_out[0:4, :] = cw_ref[...]
    chp_out[4:5, :] = cb_ref[...]
    chp_out[6:7, :] = gain_ref[...]
    chp_out[7:8, :] = gain_ref[...]
    half = iota((1, 128), 1) < 64
    for j in range(pairs):
        low, high = hp_ref[2:3, 2 * j : 2 * j + 1], hp_ref[2:3, 2 * j + 1 : 2 * j + 2]
        chp_out[5:6, j * 128 : j * 128 + 128] = jnp.where(
            half, jnp.broadcast_to(low, (1, 128)), jnp.broadcast_to(high, (1, 128))
        )
    document_columns(seg_ref, segc, segf)

    def low(k):
        for sub in range(subs):
            index = k * subs + sub

            @pl.when(k < me * gps)
            def _():
                ag(0, index).wait_recv()

                @pl.when(me < n - 1)
                def _():
                    ag(0, index).start()

        @pl.when((k == me * gps - 1) & (me < n - 1))
        def _():
            for p in range(pieces):

                @pl.when(me <= p)
                def _():
                    ag(0, me * pieces + p).start()

    def high(k):
        for sub in range(subs):
            index = ((me + 1) * gps + k) * subs + sub

            @pl.when((me + 1) * gps + k < blocks)
            def _():
                ag(1, index).wait_recv()

                @pl.when(me > 0)
                def _():
                    ag(1, index).start()

    middle = (me > 0) & (me < n - 1)
    turn_corner(1)
    turn_corner(0)
    early = min(2, blocks - gps)

    @pl.when(middle)
    def _():
        for k in range(early):
            low(k)
            high(k)

    for i in (1, 0, 2):
        pass_all(i)
    give_all(3)
    for i in range(3):
        wait_all(i)

    saves = (
        (zbuf, z_out), (xsb, xs_out), (xcvb, xcv_out), (yb, y_out),
        (bcrb, bcr_out), (bcvb, bcv_out), (dtrb, dtr_out), (bccb, bcc_out),
    )

    def save(i, t):
        if i == len(saves):
            there = st_out.at[pl.ds(pl.multiple_of(t * subs, subs), subs)]
            return pltpu.make_async_copy(stb, there, save_sem.at[i])
        there = saves[i][1].at[pl.ds(pl.multiple_of(t * TB, TB), TB)]
        return pltpu.make_async_copy(saves[i][0], there, save_sem.at[i])

    def link(way, shard, p):
        source = shard * pieces + p
        if way == 0:
            target, peer = source, me + 1
        else:
            gap = jnp.minimum(me - 1 - shard, 1)
            target, peer = (shard + (n - shard) * (1 - gap)) * pieces + p, me - 1
        return to_peer(slots.at[source], slots.at[target], rs_send.at[way, source], rs_recv.at[way, target], "tp", peer)

    def landed(way, slot):
        peer = me - 1 if way == 0 else me + 1
        return to_peer(slots.at[slot], slots.at[slot], rs_send.at[way, slot], rs_recv.at[way, slot], "tp", peer)

    def own(block, target, base):
        def tile(i, carry):
            cols = pl.ds(pl.multiple_of(i * 256, 256), 256)
            target[pl.ds(base, TB), cols] = dot(u_all[pl.ds(pl.multiple_of(block * TB, TB), TB), :], wo[:, cols])
            return carry

        lax.fori_loop(0, width // 256, tile, 0)

    def pass_on(way, block, at_end):
        shard = block // gps
        own(block, part, 0)
        for sub in range(subs):
            p = (block % gps) * subs + sub
            slot = shard * pieces + p
            here = slice(sub * T, sub * T + T)

            @pl.when(at_end)
            def _():
                slots[slot] = part[here, :].astype(BF16)

            @pl.when(jnp.logical_not(at_end))
            def _():
                landed(way, slot).wait_recv()
                slots[slot] = (part[here, :] + slots[slot].astype(F32)).astype(BF16)

            link(way, shard, p).start()

    def squares_to(peer, slot):
        return to_peer(sq_all.at[pl.ds(peer * pieces, pieces)], sqs.at[slot], q_send.at[peer], q_recv.at[slot], "tp", peer)

    kept = (
        pltpu.make_async_copy(nb, nb_out, keep_sem.at[0]),
        pltpu.make_async_copy(wc, wc_out, keep_sem.at[1]),
        pltpu.make_async_copy(wo, wo_out, keep_sem.at[2]),
    )

    left_lag = LEFT_LAG

    def turn(t, carry):
        @pl.when(t < blocks)
        def _():
            @pl.when(t > 0)
            def _():
                for i in range(len(saves) + 1):
                    save(i, t - 1).wait()

            @pl.when((me == 0) & (t >= gps))
            def _():
                high(t - gps)

            @pl.when(me == n - 1)
            def _():
                low(t)

            forward_block(
                t, nb, wc, segc, segf, chp_out, bcp_out, hp_out,
                zbuf, xsb, xcvb, yb, u_all, bcrb, bcvb, dtrb, bccb, stb, sq_all,
                xbuf, bcbuf, state,
            )
            for i in range(len(saves) + 1):
                save(i, t).start()

            @pl.when(middle & (t + 1 >= early) & (t + 1 < blocks - gps))
            def _():
                low(t + 1)
                high(t + 1)

        @pl.when(t == jnp.minimum(n - 1 - me, gps))
        def _():
            pass_all(3)
            wait_all(3)
            for copy in kept[1:]:
                copy.start()

        @pl.when(t == blocks - 1)
        def _():
            kept[0].start()
            for peer in range(n):

                @pl.when(me != peer)
                def _():
                    squares_to(peer, me).start()

        left = t - left_lag * (n - 1 - me)

        @pl.when((left >= 0) & (left < me * gps))
        def _():
            pass_on(1, left, me == n - 1)

        right = t - me

        @pl.when((right >= (me + 1) * gps) & (right < blocks))
        def _():
            pass_on(0, right, me == 0)

        mine = t - gps - me * gps

        @pl.when((mine >= 0) & (mine < gps))
        def _():
            own(t - gps, acc, pl.multiple_of(mine * TB, TB))

        return carry

    turns = max(blocks + n - 1, max(m * gps + left_lag * (n - 1 - m) for m in range(n)))
    lax.fori_loop(0, turns, turn, 0)
    load(x_ref, xst, 0, 0).start()
    load(t_ref, tst, 0, 0).start()
    sqs[pl.ds(me, 1)] = sq_all[pl.ds(me * pieces, pieces)][None]
    for peer in range(n):

        @pl.when(me != peer)
        def _():
            squares_to(peer, peer).wait_recv()

    loss_out[...] = jnp.zeros_like(loss_out)

    def store(i, p):
        source, target = ((erb, er_out), (dbb, db_out))[i]
        return pltpu.make_async_copy(source, target.at[pl.ds(pl.multiple_of(p * T, T), T)], save_sem.at[i])

    for i in range(len(saves) + 1):
        save(i, blocks - 1).wait()
    for p in range(pieces):
        load(x_ref, xst, p % 2, p).wait()
        load(t_ref, tst, p % 2, p).wait()
        if p + 1 < pieces:
            load(x_ref, xst, (p + 1) % 2, p + 1).start()
            load(t_ref, tst, (p + 1) % 2, p + 1).start()
        here = slice(p * T, p * T + T)

        @pl.when(me > 0)
        def _():
            landed(0, me * pieces + p).wait_recv()
            acc[here, :] += slots[me * pieces + p].astype(F32)

        @pl.when(me < n - 1)
        def _():
            landed(1, n * pieces + p).wait_recv()
            acc[here, :] += slots[n * pieces + p].astype(F32)

        if p > 0:
            for i in range(2):
                store(i, p - 1).wait()
        total = sqs[0, p]
        for peer in range(1, n):
            total = total + sqs[peer, p]
        rg_row = lax.rsqrt(total / inner + EPS)
        rg_b = jnp.broadcast_to(column(rg_row[0:1, :]), (T, 128))
        valid_row = v_ref[p : p + 1, :].astype(F32)
        mask_b = jnp.broadcast_to(column(valid_row), (T, 128))
        dots = jnp.zeros((T, 128), F32)
        lost = jnp.zeros((T, 128), F32)
        for c in range(tiles):
            cols = slice(c * 128, c * 128 + 128)
            view = pl.ds(c, T, stride=tiles)
            branch = acc[here, cols] * rg_b
            error = xst[p % 2, view, :] + branch - tst[p % 2, view, :]
            d_out = error * mask_b
            erb[:, cols] = error
            d_branch = d_out.astype(BF16)
            dbb[:, cols] = d_branch
            lost = lost + d_out * error
            dots = dots + d_branch.astype(F32) * branch
        loss_out[0:8, :] += row_sums(lost)
        loss_out[8:9, :] += valid_row
        coefficient = jnp.sum(dots, axis=1, keepdims=True)
        rk_out[p, 0:1, :] = rg_row[0:1, :]
        rk_out[p, 1:2, :] = row(coefficient) * rg_row[0:1, :] * rg_row[0:1, :] / inner
        rk_out[p, 2:8, :] = jnp.zeros((6, 128), F32)
        for i in range(2):
            store(i, p).start()

    for i in range(2):
        store(i, pieces - 1).wait()
    for copy in kept:
        copy.wait()

    def drain(index, carry):
        block = index // subs
        shard = index // pieces

        @pl.when((me < n - 1) & (block < (me + 1) * gps))
        def _():
            ag(0, index).wait_send()

        @pl.when((me > 0) & (block >= me * gps))
        def _():
            ag(1, index).wait_send()

        @pl.when(me < shard)
        def _():
            link(0, shard, index % pieces).wait_send()

        @pl.when(me > shard)
        def _():
            link(1, shard, index % pieces).wait_send()

        return carry

    lax.fori_loop(0, n * pieces, drain, 0)
    for i in range(4):
        give(i, sibling).wait_send()
        if square and i < 2:
            onward(i).wait_send()
            give(i, 2 * across + core).wait_send()
            give(i, 2 * along + core).wait_send()
            for owner in (2 * across + core, 2 * along + core, 2 * corner + core):
                passed(i, owner).wait_send()
        else:
            for k in range(dp // 2):

                @pl.when(chip != k)
                def _():
                    give(i, 2 * k + core).wait_send()
                    passed(i, 2 * k + core).wait_send()

    for peer in range(n):

        @pl.when(me != peer)
        def _():
            swap(0, peer, me).wait_send()
            swap(1, peer, me).wait_send()
            squares_to(peer, me).wait_send()


def front_stage(x_view, t_view, wz, wx, wos, bct, dtt, bp, pg, seg, cw, cb, gain, hp, v_rows, n, dp, inner, collective_id):
    width = pg.shape[1]
    rows = x_view.shape[0] * 128 // width
    length = n * rows
    share_rows, channels = wz.shape
    total = 2 * channels + 384
    vmem = pl.BlockSpec(memory_space=pltpu.VMEM)
    anywhere = pl.BlockSpec(memory_space=pl.ANY)
    tile_rows = T * width // 128
    shape = jax.ShapeDtypeStruct
    saved = [
        shape((length, channels), F32), shape((length, channels), BF16), shape((length, channels), BF16),
        shape((length, channels), F32), shape((length, 256), BF16), shape((length, 256), BF16),
        shape((length, 128), F32), shape((length, 256), BF16),
        shape((length // T, 128, channels), BF16),
    ]
    buffers = [pltpu.VMEM((TB,) + item.shape[1:], item.dtype) for item in saved[:-1]]
    buffers.append(pltpu.VMEM((TB // T, 128, channels), BF16))
    dma = pltpu.SemaphoreType.DMA
    return pl.pallas_call(
        partial(front_kernel, n, dp, inner),
        out_shape=saved + [
            shape((length, width), BF16), shape((width, total), BF16), shape((channels, width), BF16),
            shape((rows, width), F32), shape((rows, width), BF16),
            shape((rows // T, 8, 128), F32), shape((16, 128), F32),
            shape((8, channels), F32), shape((8, 256), F32), shape((8, 128), F32),
        ],
        in_specs=[anywhere] * 5 + [vmem] * 10,
        out_specs=[anywhere] * 14 + [vmem] * 5,
        scratch_shapes=[
            pltpu.VMEM((length, width), BF16),
            pltpu.VMEM((width, total), BF16),
            pltpu.VMEM((channels, width), BF16),
            pltpu.VMEM((length, channels), BF16),
            pltpu.VMEM(((n + 1) * rows // T, T, width), BF16),
            pltpu.VMEM((rows, width), F32),
            pltpu.VMEM((TB, width), F32),
        ] + buffers + [
            pltpu.VMEM((TB + 8, channels), F32),
            pltpu.VMEM((TB + 8, 256), F32),
            pltpu.VMEM((128, channels), F32),
            pltpu.VMEM((length // T, 8, 128), F32),
            pltpu.VMEM((n, rows // T, 8, 128), F32),
            pltpu.VMEM((2, tile_rows, 128), F32),
            pltpu.VMEM((2, tile_rows, 128), F32),
            pltpu.VMEM((T, width), F32),
            pltpu.VMEM((T, width), BF16),
            pltpu.VMEM((length + 16, 128), F32),
            pltpu.VMEM((length // T, 128), F32),
            pltpu.VMEM((n,) + bct.shape, BF16),
            pltpu.VMEM((n,) + bp.shape, F32),
            pltpu.VMEM((share_rows, 384), BF16),
            dma((2, 2)), dma((7,)), dma((9,)), dma((2, n)), dma((2, n)),
            dma((4, dp)), dma((2,)), dma((4, dp)), dma((4, dp)),
            dma((2, length // T)), dma((2, length // T)),
            dma((2, (n + 1) * rows // T)), dma((2, (n + 1) * rows // T)),
            dma((n,)), dma((n,)),
        ],
        compiler_params=pltpu.CompilerParams(
            collective_id=collective_id, has_side_effects=True, vmem_limit_bytes=63 << 20
        ),
        name="front_stage",
    )(x_view, t_view, wz, wx, wos, bct, dtt, bp, pg, seg, cw, cb, gain, hp, v_rows)


def scatter_scratch(length, rows, width):
    return [
        pltpu.VMEM((rows, width), F32),
        pltpu.VMEM((min(rows, 256), width), F32),
        pltpu.VMEM((2, length // T, T, width), BF16),
    ], [
        pltpu.SemaphoreType.DMA((2, length // T)),
        pltpu.SemaphoreType.DMA((2, length // T)),
    ]


def input_kernel(n, a_any, w_any, acc, a_ref, w_ref, part, slots, load_sem, send_sem, recv_sem):
    loads = [
        pltpu.make_async_copy(source, target, load_sem.at[i])
        for i, (source, target) in enumerate(((w_any, w_ref), (a_any, a_ref)))
    ]
    for copy in loads:
        copy.start()
    me = meet(n, "tp")
    for copy in loads:
        copy.wait()
    arrived, drain = scatter_body(n, me, a_ref, (w_ref,), acc, part, slots, send_sem, recv_sem)

    def last(p, carry):
        arrived(p)
        return carry

    lax.fori_loop(0, acc.shape[0] // T, last, 0)
    drain()


def input_stage(dproj, weight, n, collective_id):
    length, width = dproj.shape[0], weight.shape[0]
    rows = length // n
    vmem = pl.BlockSpec(memory_space=pltpu.VMEM)
    anywhere = pl.BlockSpec(memory_space=pl.ANY)
    buffers, sems = scatter_scratch(length, rows, width)
    return pl.pallas_call(
        partial(input_kernel, n),
        out_shape=jax.ShapeDtypeStruct((rows, width), F32),
        in_specs=[anywhere] * 2,
        out_specs=vmem,
        scratch_shapes=[pltpu.VMEM(dproj.shape, BF16), pltpu.VMEM(weight.shape, BF16)]
        + buffers[1:] + [pltpu.SemaphoreType.DMA((2,))] + sems,
        compiler_params=pltpu.CompilerParams(
            collective_id=collective_id, has_side_effects=True, vmem_limit_bytes=60 << 20
        ),
        cost_estimate=pl.CostEstimate(
            flops=2 * length * width * dproj.shape[1], bytes_accessed=400 << 20, transcendentals=0
        ),
        name="input_stage",
    )(dproj, weight)


def output_kernel(dn_ref, er_ref, x_ref, t_ref, v_ref, pg_ref, lo_out, gx_out, gp_out):
    width = dn_ref.shape[1]
    tiles = width // 128

    @pl.when(pl.program_id(0) == 0)
    def _():
        gp_out[...] = jnp.zeros_like(gp_out)

    squares = jnp.zeros((T, 128), F32)
    dots = jnp.zeros((T, 128), F32)
    for c in range(tiles):
        cols = slice(c * 128, c * 128 + 128)
        xt = x_ref[pl.ds(c, T, stride=tiles), :]
        squares = squares + xt * xt
        dots = dots + dn_ref[:, cols] * pg_ref[0:1, cols] * xt
    inv = lax.rsqrt(jnp.sum(squares, axis=1, keepdims=True) / width + EPS)
    inv_b = jnp.broadcast_to(inv, (T, 128))
    mean = jnp.sum(dots, axis=1, keepdims=True) / width
    back_b = jnp.broadcast_to(inv * inv * inv * mean, (T, 128))
    mask_b = jnp.broadcast_to(column(v_ref[pl.ds(pl.program_id(0), 1), :].astype(F32)), (T, 128))
    for c in range(tiles):
        cols = slice(c * 128, c * 128 + 128)
        view = pl.ds(c, T, stride=tiles)
        xt = x_ref[view, :]
        scaled = dn_ref[:, cols] * inv_b
        error = er_ref[:, cols]
        lo_out[view, :] = error + t_ref[view, :]
        gx_out[view, :] = error * mask_b + scaled * pg_ref[0:1, cols] - xt * back_b
        gp_out[:, cols] += row_sums(scaled * xt)


def output_stage(dn, error, x_view, t_view, valid_rows, pg):
    rows, width = dn.shape
    block = pl.BlockSpec((T, width), lambda i: (i, 0))
    view = pl.BlockSpec((T * width // 128, 128), lambda i: (i, 0))
    whole = lambda shape: pl.BlockSpec(shape, lambda i: (0, 0))
    shape = jax.ShapeDtypeStruct
    return pl.pallas_call(
        output_kernel,
        grid=(rows // T,),
        in_specs=[block, block, view, view, whole(valid_rows.shape), whole(pg.shape)],
        out_specs=[view, view, whole((8, width))],
        out_shape=[shape(x_view.shape, F32), shape(x_view.shape, F32), shape((8, width), F32)],
        compiler_params=pltpu.CompilerParams(vmem_limit_bytes=62 << 20),
        name="output_stage",
    )(dn, error, x_view, t_view, valid_rows, pg)


def last_kernel(
    tp, mine, both, cols, gc_ref, go_ref,
    wz_out, wx_out, wdt_out, wbc_out, wo_out, cw_out, cb_out, gain_out, skip_out, dtb_out, alog_out,
    gp_out, bw_out, bb_out, loss_out,
):
    channels = wz_out.shape[1]
    heads = wdt_out.shape[0]
    width = gp_out.shape[1]
    wz_out[...] = gc_ref[:, 0:channels].astype(F32)
    wx_out[...] = gc_ref[:, channels : 2 * channels].astype(F32)
    wdt_out[...] = gc_ref[:, 2 * channels + 256 : 2 * channels + 384].astype(F32).T[0:heads, :]
    wbc_out[...] = cols[...]
    for c in range(channels // 128):
        here = slice(c * 128, c * 128 + 128)
        wo_out[here, :] = go_ref[:, here].astype(F32).T
    per = channels // 128
    for k in range(7):
        for c in range(per):
            here = slice(c * 128, c * 128 + 128)
            line = mine[k * per + c : k * per + c + 1, :]
            if k < 4:
                cw_out[k : k + 1, here] = line
            elif k == 4:
                cb_out[:, here] = line
            elif k == 5:
                gain_out[:, here] = line
    lane = iota((1, 128), 1)
    skip = jnp.zeros((1, 128), F32)
    for c in range(per):
        line = mine[6 * per + c : 6 * per + c + 1, :]
        low = jnp.sum(jnp.where(lane < 64, line, 0.0), axis=1, keepdims=True)
        high = jnp.sum(jnp.where(lane < 64, 0.0, line), axis=1, keepdims=True)
        skip = skip + jnp.where(lane == 2 * c, low, 0.0) + jnp.where(lane == 2 * c + 1, high, 0.0)
    skip_out[...] = skip[:, 0:heads]
    dtb_out[...] = mine[7 * per : 7 * per + 1, 0:heads]
    alog_out[...] = mine[7 * per + 1 : 7 * per + 2, 0:heads]
    top = width // 128
    for c in range(top):
        gp_out[:, c * 128 : c * 128 + 128] = both[c : c + 1, :]
    me = lax.axis_index("tp")
    local = bb_out.shape[1]
    for k in range(5):
        for peer in range(tp):
            at = peer * local
            line = both[top + 2 * k + at // 128 : top + 2 * k + at // 128 + 1, at % 128 : at % 128 + local]

            @pl.when(me == peer)
            def _():
                if k < 4:
                    bw_out[k : k + 1, :] = line
                else:
                    bb_out[...] = line

    lost = jnp.sum(both[top + 10 : top + 11, :], axis=1, keepdims=True)
    count = jnp.sum(both[top + 11 : top + 12, :], axis=1, keepdims=True)
    loss_out[...] = lost / (jnp.maximum(count, 1.0) * width)


def last_stage(mine, both, cols, g_cat, g_out, heads, width, tp):
    rows = g_cat.shape[0]
    channels = g_out.shape[1]
    local = cols.shape[0]
    vmem = pl.BlockSpec(memory_space=pltpu.VMEM)
    shapes = [
        (rows, channels), (rows, channels), (heads, rows), cols.shape, (channels, rows),
        (4, channels), (1, channels), (1, channels), (1, heads), (1, heads), (1, heads),
        (1, width), (4, local), (1, local), (1, 1),
    ]
    return pl.pallas_call(
        partial(last_kernel, tp),
        in_specs=[vmem] * 5,
        out_specs=[vmem] * len(shapes),
        out_shape=[jax.ShapeDtypeStruct(shape, F32) for shape in shapes],
        compiler_params=pltpu.CompilerParams(vmem_limit_bytes=40 << 20),
        name="last_stage",
    )(mine, both, cols, g_cat, g_out)


def local(
    x_in, target, seg_ids, valid, pre_gain, w_z, w_x, w_bc, w_dt, conv_x_w, conv_x_b,
    conv_bc_w, conv_bc_b, dt_bias, a_log, d_skip, norm_gain, w_out,
):
    rows, _, width = x_in.shape
    channels = w_z.shape[1]
    heads = w_dt.shape[1]
    tp = lax.axis_size("tp")
    inner = channels * tp
    bc_local = w_bc.shape[1]
    dp = lax.axis_size("dp")
    x_view = x_in.reshape(rows * width // 128, 128)
    t_view = target.reshape(rows * width // 128, 128)
    seg = seg_ids.reshape(-1, 128)
    bp = jnp.pad(jnp.concatenate([conv_bc_w, conv_bc_b[:, None]], axis=1), ((0, 0), (0, 123)))
    dtt = jnp.pad(w_dt.T, ((0, 128 - heads), (0, 0)))
    hp = jnp.pad(jnp.stack([dt_bias, a_log, d_skip]), ((0, 5), (0, 128 - heads)), constant_values=-100.0)
    (
        z, xs, xcv, y, bcr, bcv, dtr, bcc, st,
        normed_all, wc, wo, error, d_branch, rk_own, lost, chp, bcp, hp,
    ) = front_stage(
        x_view, t_view, w_z, w_x, w_out, w_bc.T, dtt, bp, pre_gain[None], seg, conv_x_w.T, conv_x_b[None],
        norm_gain[None], hp, valid.reshape(-1, 128), tp, dp, inner, 1,
    )
    saved = (z, xs, xcv, y, bcr, bcv, dtr, bcc, st)
    dproj, yn, db_all, accc, accb, acch = back_stage(d_branch, rk_own, seg, chp, bcp, hp, wo, saved, tp, 2)

    def dot_tn(a, b):
        return lax.dot_general(a, b, (((0,), (0,)), ((), ())), preferred_element_type=F32)

    g_out = dot_tn(db_all, yn).astype(BF16)
    g_cat = dot_tn(normed_all, dproj).astype(BF16)
    g_out, g_cat, dproj = lax.optimization_barrier((g_out, g_cat, dproj))
    g_out = lax.psum_scatter(g_out, "dp", scatter_dimension=0, tiled=True)
    g_cat = lax.psum_scatter(g_cat, "dp", scatter_dimension=0, tiled=True)
    d_normed = input_stage(dproj, wc, tp, 3)
    lo_view, gx_view, gain_part = output_stage(
        d_normed, error, x_view, t_view, valid.reshape(-1, 128), pre_gain[None]
    )
    mine, both, cols = finish(accc, acch, accb, gain_part, lost, g_cat, dp, tp, 5)
    (
        grad_wz, grad_wx, grad_wdt, grad_wbc, grad_wo, grad_cw, grad_cb, grad_gain, grad_skip, grad_dtb, grad_alog,
        grad_pre, grad_bw, grad_bb, loss,
    ) = last_stage(mine, both, cols, g_cat, g_out, heads, width, tp)
    return (
        lo_view.reshape(x_in.shape),
        loss.reshape(()),
        gx_view.reshape(x_in.shape),
        grad_pre.reshape(-1),
        grad_wz,
        grad_wx,
        grad_wbc.T,
        grad_wdt.T,
        grad_cw.T,
        grad_cb.reshape(-1),
        grad_bw.T,
        grad_bb.reshape(-1),
        grad_dtb.reshape(-1),
        grad_alog.reshape(-1),
        grad_skip.reshape(-1),
        grad_gain.reshape(-1),
        grad_wo,
    )


def solution(mesh):
    tok, col, head = P("tp", "dp", None), P("dp", "tp"), P("tp")
    in_specs = (
        tok, tok, P("dp", None), col, P(), col, col, col, col,
        P("tp", None), head, P("tp", None), head, head, head, head, head, P("tp", "dp"),
    )
    out_specs = (
        tok, P(), tok, P(), col, col, col, col,
        P("tp", None), head, P("tp", None), head, head, head, head, head, P("tp", "dp"),
    )
    return jax.shard_map(local, mesh=mesh, in_specs=in_specs, out_specs=out_specs, check_vma=False)
```

```python
from functools import partial

import jax
import jax.numpy as jnp
from jax import lax
from jax.experimental import pallas as pl
from jax.experimental.pallas import tpu as pltpu
from jax.sharding import PartitionSpec as P

T = 128
TB = 256
EPS = 1e-05
LEFT_LAG = 3
LOG2E = 1.4426950408889634
F32 = jnp.float32
BF16 = jnp.bfloat16
ZT = YT = F32
XT = CT = BF16
HIGHEST = lax.Precision.HIGHEST


def dot(a, b, precision=None):
    return jnp.dot(a, b, preferred_element_type=F32, precision=precision)


def dot_nt(a, b):
    return lax.dot_general(a, b, (((1,), (1,)), ((), ())), preferred_element_type=F32)


def lanes(column_of, index, rows=T):
    return jnp.broadcast_to(column_of[:, index : index + 1], (rows, 128))


def iota(shape, axis):
    return lax.broadcasted_iota(jnp.int32, shape, axis)


def step_sizes(raw, hp_ref):
    shifted = raw + hp_ref[0:1, :]
    dt = jnp.maximum(shifted, 0.0) + jnp.log1p(jnp.exp(-jnp.abs(shifted)))
    la = dt * hp_ref[1:2, :]
    inclusive = (iota((T, T), 0) >= iota((T, T), 1)).astype(F32)
    cum = dot(inclusive, la * LOG2E, HIGHEST)
    return shifted, dt, la, cum


def split_pair(value):
    first = iota((T, 128), 1) < 64
    zero = jnp.zeros_like(value)
    return jnp.concatenate([jnp.where(first, value, zero), jnp.where(first, zero, value)], axis=0)


def eye():
    return iota((T, T), 0) == iota((T, T), 1)


def column(row):
    return jnp.sum(jnp.where(eye(), jnp.broadcast_to(row, (T, T)), 0.0), axis=1, keepdims=True)


def row(col):
    return jnp.sum(jnp.where(eye(), jnp.broadcast_to(col, (T, T)), 0.0), axis=0, keepdims=True)


def document_columns(seg_ref, segc, segf):
    length = segc.shape[0] - 16
    segf[...] = seg_ref[...].astype(F32)
    segc[0:8, :] = jnp.full((8, 128), -1.0, F32)
    segc[length + 8 : length + 16, :] = jnp.full((8, 128), -1.0, F32)

    def chunk(i, carry):
        here = pl.ds(pl.multiple_of(i * T + 8, 8), T)
        segc[here, :] = jnp.broadcast_to(column(segf[pl.ds(i, 1), :]), (T, 128))
        return carry

    lax.fori_loop(0, length // T, chunk, 0)


def row_sums(value):
    return jnp.sum(value.reshape(value.shape[0] // 8, 8, value.shape[1]), axis=0)


def backward_block(
    t, block, dball, wo_ref, rk_all, segc, segf, chp_ref, bcp_ref, hp_ref,
    z_ref, xs_ref, xcv_ref, y_ref, bcr_ref, bcv_ref, dtr_ref, bcc_ref, st_ref,
    dproj_out, yn_out, accc_out, accb_out, acch_out,
    dyn, dbuf, dbcbuf, dstate, dstate_b, dyec, xte, cs_rows, fold, pick, leaving, entering, prod, decays,
):
    channels = wo_ref.shape[0]
    pairs = channels // 128
    start = pl.multiple_of(block * TB, TB)
    for n in range(channels // 256):
        cols = slice(n * 256, n * 256 + 256)
        dyn[:, cols] = dot_nt(dball[pl.ds(start, TB), :], wo_ref[cols, :])
    first = iota((T, 128), 1) < 64
    for c in reversed(range(TB // T)):
        r0 = c * T
        rows = slice(r0, r0 + T)
        chunk = block * (TB // T) + c
        near = segc[pl.ds(pl.multiple_of(start + r0, T), T + 16), :]
        seg_col = near[8 : T + 8, :]
        ahead = [(near[8 + d : 8 + d + T, :] == seg_col).astype(F32) for d in (1, 2, 3)]
        start_b = (seg_col == near[7:8, :]).astype(F32)
        end_b = (seg_col == near[T + 7 : T + 8, :]).astype(F32)
        rg_b = jnp.broadcast_to(column(rk_all[chunk, 0:1, :]), (T, 128))
        kc_b = jnp.broadcast_to(column(rk_all[chunk, 1:2, :]), (T, 128))
        bm, cm = bcc_ref[rows, 0:128], bcc_ref[rows, 128:256]
        ct = cm.T
        shifted, dt, la, cum = step_sizes(dtr_ref[rows, :], hp_ref)
        cum_t = cum.T
        scores, scores_t = dot_nt(cm, bm), dot_nt(bm, cm)
        same = seg_col == segf[pl.ds(chunk, 1), :]
        below = iota((T, T), 0) >= iota((T, T), 1)
        strict = iota((T, T), 0) > iota((T, T), 1)
        above = iota((T, T), 0) <= iota((T, T), 1)
        qs = jnp.where(same & strict, scores, 0.0)
        qt = jnp.where(same & above, scores_t, 0.0)
        dstate_b[...] = dstate[...].astype(BF16)
        leaving[...] = dot(bm, dstate_b[...])
        entering[...] = dot(cm, st_ref[c, :, :])
        dq = jnp.zeros((T, T), F32)
        rsum = jnp.zeros((T, 128), F32)
        for j in range(pairs):
            cols = slice(j * 128, j * 128 + 128)
            zz = z_ref[rows, cols].astype(F32)
            y = y_ref[rows, cols].astype(F32)
            sz = 0.5 + 0.5 * jnp.tanh(0.5 * zz)
            silu_z = zz * sz
            dsz = sz + silu_z * (1.0 - sz)
            g = y * silu_z
            gr = g * rg_b
            gain = chp_ref[6:7, cols]
            dynp = dyn[rows, cols]
            yn_out[rows, cols] = (gr * gain).astype(BF16)
            accc_out[5, :, cols] += row_sums(dynp * gr)
            dg = rg_b * dynp * gain - g * kc_b
            dy = dg * silu_z
            dproj_out[rows, cols] = (dg * y * dsz).astype(BF16)
            xcv = xcv_ref[rows, cols].astype(F32)
            sx = 0.5 + 0.5 * jnp.tanh(0.5 * xcv)
            xc = xcv * sx
            dsx = sx + xc * (1.0 - sx)
            accc_out[6, :, cols] += row_sums(dy * xc)
            dt_e = jnp.where(first, lanes(dt, 2 * j), lanes(dt, 2 * j + 1))
            ca, cb = lanes(cum, 2 * j), lanes(cum, 2 * j + 1)
            cum_e = jnp.where(first, ca, cb)
            into = jnp.exp2(cum_e) * start_b
            to_end = jnp.exp2(cum_e[T - 1 : T, :] - cum_e) * end_b
            decay = into[T - 1 : T, :]
            decays[0:1, cols] = decay
            xdt = xc * dt_e
            dy_b = dy.astype(BF16)
            ga = ca - cum_t[2 * j : 2 * j + 1, :]
            gb = cb - cum_t[2 * j + 1 : 2 * j + 2, :]
            grad = dot_nt(dy_b, split_pair(xdt.astype(BF16)))
            gea = grad[:, :128] * jnp.exp2(jnp.minimum(ga, 0.0))
            geb = grad[:, 128:] * jnp.exp2(jnp.minimum(gb, 0.0))
            dq = dq + gea + geb
            pp = jnp.concatenate([(gea * qs).astype(BF16), (geb * qs).astype(BF16)], axis=1)
            rsum = rsum + dot(pp, pick[j, :, :])
            csum = jnp.sum(pp.astype(F32), axis=0, keepdims=True)
            cs_rows[2 * j : 2 * j + 1, :] = csum[:, :128]
            cs_rows[2 * j + 1 : 2 * j + 2, :] = csum[:, 128:]
            eta = (jnp.exp2(jnp.minimum(-ga, 0.0)) * qt).astype(BF16)
            etb = (jnp.exp2(jnp.minimum(-gb, 0.0)) * qt).astype(BF16)
            dxdt = dot(jnp.concatenate([eta, etb], axis=1), split_pair(dy_b))
            dx_state = to_end * leaving[:, cols]
            dxdt = dxdt + dx_state
            y_in = into * entering[:, cols]
            dyec_p = (dy * into).astype(BF16)
            dyec[:, cols] = dyec_p
            xte[:, cols] = (xdt * to_end).astype(BF16)
            prod[0:T, cols] = (xc * dxdt).astype(BF16)
            prod[T : 2 * T, cols] = (dy * y_in).astype(BF16)
            prod[2 * T : 3 * T, cols] = (xdt * dx_state).astype(BF16)
            kpart = row_sums(dstate[:, cols] * st_ref[c, :, cols].astype(F32)) * decay
            khigh = kpart.astype(BF16)
            klow = (kpart - khigh.astype(F32)).astype(BF16)
            prod[3 * T : 3 * T + 16, cols] = jnp.concatenate([khigh, klow], axis=0)
            dxcv = (dxdt * dt_e + chp_ref[5:6, cols] * dy) * dsx
            dbuf[0:T, cols] = dxcv
            xs = xs_ref[rows, cols].astype(F32)
            dxs = dxcv * chp_ref[3:4, cols]
            accc_out[4, :, cols] += row_sums(dxcv)
            accc_out[3, :, cols] += row_sums(dxcv * xs)
            for d in (1, 2, 3):
                moved = dbuf[d : d + T, cols] * ahead[d - 1]
                dxs = dxs + moved * chp_ref[3 - d : 4 - d, cols]
                accc_out[3 - d, :, cols] += row_sums(moved * xs)
            dproj_out[rows, channels + j * 128 : channels + j * 128 + 128] = dxs.astype(BF16)
        dstate[...] = dstate[...] * decays[0:1, :] + dot(ct, dyec[...])
        sums = dot(prod[...], fold[...])
        ddt, xsum, ksum = sums[0:T], sums[2 * T : 3 * T], sums[3 * T : 3 * T + 16]
        rsum = rsum + sums[T : 2 * T]
        dbuf[T : T + 8, :] = dbuf[0:8, :]
        dqm = jnp.where(same & below, dq, 0.0)
        dc = dot(dqm.astype(BF16), bm) + dot_nt(dyec[...], st_ref[c, :, :])
        db_rows = dot(dqm.T.astype(BF16), cm) + dot_nt(xte[...], dstate_b[...])
        for half, grad_half in enumerate((db_rows, dc)):
            cols = slice(half * 128, half * 128 + 128)
            raw = bcv_ref[rows, cols].astype(F32)
            sb = 0.5 + 0.5 * jnp.tanh(0.5 * raw)
            dcv = grad_half * (sb + raw * sb * (1.0 - sb))
            dbcbuf[0:T, cols] = dcv
            xs = bcr_ref[rows, cols].astype(F32)
            dxs = dcv * bcp_ref[3:4, cols]
            accb_out[4, :, cols] += row_sums(dcv)
            accb_out[3, :, cols] += row_sums(dcv * xs)
            for d in (1, 2, 3):
                moved = dbcbuf[d : d + T, cols] * ahead[d - 1]
                dxs = dxs + moved * bcp_ref[3 - d : 4 - d, cols]
                accb_out[3 - d, :, cols] += row_sums(moved * xs)
            dproj_out[rows, 2 * channels + half * 128 : 2 * channels + half * 128 + 128] = dxs.astype(BF16)
        dbcbuf[T : T + 8, :] = dbcbuf[0:8, :]
        after = (iota((T, T), 0) <= iota((T, T), 1)).astype(F32)
        before = (iota((T, T), 0) > iota((T, T), 1)).astype(F32)
        dla = dot(after, rsum - cs_rows[...].T, HIGHEST) + dot(before, xsum, HIGHEST)
        dla = dla + jnp.sum(ksum, axis=0, keepdims=True)
        ddtr = (ddt + dla * hp_ref[1:2, :]) * (0.5 + 0.5 * jnp.tanh(0.5 * shifted))
        acch_out[0, :, :] += row_sums(ddtr)
        acch_out[1, :, :] += row_sums(dla * la)
        dproj_out[rows, 2 * channels + 256 : 2 * channels + 384] = ddtr.astype(BF16)


MESH_ID = pl.DeviceIdType.MESH


def meet(n, axis):
    me = lax.axis_index(axis)
    barrier = pltpu.get_barrier_semaphore()
    for peer in range(n):

        @pl.when(me != peer)
        def _():
            pl.semaphore_signal(barrier, inc=1, device_id={axis: peer}, device_id_type=MESH_ID)

    pl.semaphore_wait(barrier, n - 1)
    return me


def to_peer(source, target, send_sem, recv_sem, axis, peer):
    return pltpu.make_async_remote_copy(
        src_ref=source, dst_ref=target, send_sem=send_sem, recv_sem=recv_sem,
        device_id={axis: peer}, device_id_type=MESH_ID,
    )


def finish_kernel(
    dp, tp, ac_ref, ah_ref, ab_ref, gp_ref, lost_ref, gc_ref,
    mine_out, both_out, cols_out, got, got_both, cols, got_cols, sems,
):
    me_dp, me_tp = lax.axis_index("dp"), lax.axis_index("tp")
    barrier = pltpu.get_barrier_semaphore()
    for peer in range(dp):

        @pl.when(me_dp != peer)
        def _():
            pl.semaphore_signal(barrier, inc=1, device_id={"dp": peer}, device_id_type=MESH_ID)

    for peer in range(tp):

        @pl.when(me_tp != peer)
        def _():
            pl.semaphore_signal(barrier, inc=1, device_id={"tp": peer}, device_id_type=MESH_ID)

    channels = ac_ref.shape[2]
    per = channels // 128
    first = mine_out.shape[0]
    top = gp_ref.shape[1] // 128
    got[me_dp] = jnp.zeros_like(got[0])

    def put(line, value):
        got[pl.ds(me_dp, 1), line : line + 1, :] = value[None]

    for k in range(7):
        sums = jnp.sum(ac_ref[k], axis=0, keepdims=True)
        for c in range(per):
            put(k * per + c, sums[:, c * 128 : c * 128 + 128])
    for k in range(2):
        put(7 * per + k, jnp.sum(ah_ref[k], axis=0, keepdims=True))
    sums = jnp.sum(gp_ref[...], axis=0, keepdims=True)
    for c in range(top):
        put(first + c, sums[:, c * 128 : c * 128 + 128])
    for k in range(5):
        sums = jnp.sum(ab_ref[k], axis=0, keepdims=True)
        for c in range(2):
            put(first + top + 2 * k + c, sums[:, c * 128 : c * 128 + 128])
    put(first + top + 10, jnp.sum(lost_ref[0:8, :], axis=0, keepdims=True))
    put(first + top + 11, lost_ref[8:9, :])
    turned = gc_ref[:, 2 * channels : 2 * channels + 256].astype(F32).T
    cols[...] = turned.reshape(cols.shape)
    pl.semaphore_wait(barrier, dp - 1 + tp - 1)

    def over_dp(peer, slot):
        return to_peer(got.at[me_dp], got.at[slot], sems.at[0, peer], sems.at[1, slot], "dp", peer)

    def over_tp(peer, slot):
        return to_peer(got_both.at[me_tp], got_both.at[slot], sems.at[2, peer], sems.at[3, slot], "tp", peer)

    def over_cols(peer, slot):
        return to_peer(cols.at[peer], got_cols.at[slot], sems.at[4, peer], sems.at[5, slot], "tp", peer)

    for peer in range(dp):

        @pl.when(me_dp != peer)
        def _():
            over_dp(peer, me_dp).start()

    for peer in range(tp):

        @pl.when(me_tp != peer)
        def _():
            over_cols(peer, me_tp).start()

    got_cols[pl.ds(me_tp, 1)] = cols[pl.ds(me_tp, 1)]
    for peer in range(dp):

        @pl.when(me_dp != peer)
        def _():
            over_dp(peer, peer).wait_recv()

    total = got[0]
    for peer in range(1, dp):
        total = total + got[peer]
    mine_out[...] = total[:first]
    got_both[pl.ds(me_tp, 1)] = total[first:][None]
    for peer in range(tp):

        @pl.when(me_tp != peer)
        def _():
            over_tp(peer, me_tp).start()

    for peer in range(tp):

        @pl.when(me_tp != peer)
        def _():
            over_cols(peer, peer).wait_recv()
            over_tp(peer, peer).wait_recv()

    total, columns = got_both[0], got_cols[0]
    for peer in range(1, tp):
        total, columns = total + got_both[peer], columns + got_cols[peer]
    both_out[...] = total
    cols_out[...] = columns
    for peer in range(dp):

        @pl.when(me_dp != peer)
        def _():
            over_dp(peer, me_dp).wait_send()

    for peer in range(tp):

        @pl.when(me_tp != peer)
        def _():
            over_cols(peer, me_tp).wait_send()
            over_tp(peer, me_tp).wait_send()


def finish(accc, acch, accb, gain_part, lost, g_cat, dp, tp, collective_id):
    vmem = pl.BlockSpec(memory_space=pltpu.VMEM)
    first = -(-(7 * accc.shape[2] // 128 + 2) // 8) * 8
    second = -(-(gain_part.shape[1] // 128 + 12) // 8) * 8
    cols = (tp, 256 // tp, g_cat.shape[0])
    shape = jax.ShapeDtypeStruct
    return pl.pallas_call(
        partial(finish_kernel, dp, tp),
        out_shape=[shape((first, 128), F32), shape((second, 128), F32), shape(cols[1:], F32)],
        in_specs=[vmem] * 6,
        out_specs=[vmem] * 3,
        scratch_shapes=[
            pltpu.VMEM((dp, first + second, 128), F32),
            pltpu.VMEM((tp, second, 128), F32),
            pltpu.VMEM(cols, F32),
            pltpu.VMEM(cols, F32),
            pltpu.SemaphoreType.DMA((6, max(dp, tp))),
        ],
        compiler_params=pltpu.CompilerParams(collective_id=collective_id, has_side_effects=True),
        name="finish",
    )(accc, acch, accb, gain_part, lost, g_cat)


def back_kernel(
    n, db_ref, rk_ref, seg_ref, chp_ref, bcp_ref, hp_ref, wo_any,
    z_any, xs_any, xcv_any, y_any, bcr_any, bcv_any, dtr_any, bcc_any, st_any,
    dproj_any, yn_any, dball_any, accc_out, accb_out, acch_out,
    dball, rk_all, wo, zb, xsb, xcvb, yb, bcrb, bcvb, dtrb, bccb, stb, dprojb, ynb,
    dyn, dbuf, dbcbuf, dstate, dstate_b, dyec, xte, cs_rows, fold, pick, leaving, entering, prod, decays, segc, segf,
    keep_sem, load_sem, save_sem, ag_send, ag_recv, r_send, r_recv,
):
    rows = db_ref.shape[0]
    pieces = rows // T
    gps = rows // TB
    subs = TB // T
    blocks = n * gps
    pairs = wo.shape[0] // 128
    sources = (z_any, xs_any, xcv_any, y_any, bcr_any, bcv_any, dtr_any, bcc_any, st_any)
    held = (zb, xsb, xcvb, yb, bcrb, bcvb, dtrb, bccb, stb)

    def load(i, t):
        block = blocks - 1 - t
        step = subs if i == len(held) - 1 else TB
        there = sources[i].at[pl.ds(pl.multiple_of(block * step, step), step)]
        return pltpu.make_async_copy(there, held[i].at[t % 2], load_sem.at[i, t % 2])

    fetch = pltpu.make_async_copy(wo_any, wo, keep_sem.at[0])
    fetch.start()
    own_rows = pl.ds(pl.multiple_of(lax.axis_index("tp") * rows, rows), rows)
    keep = pltpu.make_async_copy(db_ref, dball.at[own_rows], keep_sem.at[1])
    keep.start()
    for i in range(len(held)):
        load(i, 0).start()
    me = meet(n, "tp")

    def rk_to(peer, owner):
        return to_peer(rk_ref, rk_all.at[pl.ds(owner * pieces, pieces)], r_send.at[peer], r_recv.at[owner], "tp", peer)

    for peer in range(n):

        @pl.when(me != peer)
        def _():
            rk_to(peer, me).start()

    rk_all[pl.ds(me * pieces, pieces)] = rk_ref[...]

    def ag(way, index):
        here = dball.at[pl.ds(pl.multiple_of(index * T, T), T)]
        peer = me + 1 if way == 0 else me - 1
        return to_peer(here, here, ag_send.at[way, index], ag_recv.at[way, index], "tp", peer)

    keep.wait()
    mirror = n - 1 - me
    for p in range(pieces):
        index = ((me + 1) * gps - 1 - p // subs) * subs + p % subs

        @pl.when(me < n - 1)
        def _():
            ag(0, index).start()

        @pl.when((me > 0) & ((mirror == 0) | (mirror > p)))
        def _():
            ag(1, index).start()

    def low(k):
        for sub in range(subs):
            index = (me * gps - 1 - k) * subs + sub

            @pl.when((me * gps - 1 - k >= 0) & (k >= 0))
            def _():
                ag(0, index).wait_recv()

                @pl.when(me < n - 1)
                def _():
                    ag(0, index).start()

    def relay(k):
        for sub in range(subs):
            index = (blocks - 1 - k) * subs + sub

            @pl.when(k < mirror * gps)
            def _():
                ag(1, index).wait_recv()

                @pl.when(me > 0)
                def _():
                    ag(1, index).start()

        @pl.when(me < n - 1)
        def _():
            low(k)

        @pl.when((k == mirror * gps - 1) & (me > 0))
        def _():
            for p in range(pieces):

                @pl.when(mirror <= p)
                def _():
                    ag(1, ((me + 1) * gps - 1 - p // subs) * subs + p % subs).start()

    document_columns(seg_ref, segc, segf)
    dstate[...] = jnp.zeros_like(dstate)
    dbuf[...] = jnp.zeros_like(dbuf)
    dbcbuf[...] = jnp.zeros_like(dbcbuf)
    accc_out[...] = jnp.zeros_like(accc_out)
    accb_out[...] = jnp.zeros_like(accb_out)
    acch_out[...] = jnp.zeros_like(acch_out)
    cs_rows[...] = jnp.zeros_like(cs_rows)
    for j in range(pairs):
        half = (iota((128, 128), 0) >= 64).astype(jnp.int32)
        fold[j * 128 : j * 128 + 128, :] = (iota((128, 128), 1) == 2 * j + half).astype(F32).astype(BF16)
        part = (iota((256, 128), 0) >= 128).astype(jnp.int32)
        pick[j, :, :] = (iota((256, 128), 1) == 2 * j + part).astype(F32).astype(BF16)
    for peer in range(n):

        @pl.when(me != peer)
        def _():
            rk_to(peer, peer).wait_recv()

    fetch.wait()
    relay(0)

    def save(i, t):
        block = blocks - 1 - t
        source, target = ((dprojb, dproj_any), (ynb, yn_any))[i]
        return pltpu.make_async_copy(source, target.at[pl.ds(pl.multiple_of(block * TB, TB), TB)], save_sem.at[i])

    def turn(t, carry):
        @pl.when(t + 1 < blocks)
        def _():
            for i in range(len(held)):
                load(i, t + 1).start()

        for i in range(len(held)):
            load(i, t).wait()

        @pl.when(t > 0)
        def _():
            for i in range(2):
                save(i, t - 1).wait()

        @pl.when((me == n - 1) & (t >= gps))
        def _():
            low(t - gps)

        slot = t % 2
        backward_block(
            t, blocks - 1 - t, dball, wo, rk_all, segc, segf, chp_ref, bcp_ref, hp_ref,
            zb.at[slot], xsb.at[slot], xcvb.at[slot], yb.at[slot], bcrb.at[slot], bcvb.at[slot],
            dtrb.at[slot], bccb.at[slot], stb.at[slot],
            dprojb, ynb, accc_out, accb_out, acch_out,
            dyn, dbuf, dbcbuf, dstate, dstate_b, dyec, xte, cs_rows, fold, pick, leaving, entering, prod, decays,
        )
        for i in range(2):
            save(i, t).start()

        @pl.when(t + 1 < blocks - gps)
        def _():
            relay(t + 1)

        return carry

    lax.fori_loop(0, blocks, turn, 0)
    keep_all = pltpu.make_async_copy(dball, dball_any, keep_sem.at[2])
    keep_all.start()
    for i in range(2):
        save(i, blocks - 1).wait()

    def drain(index, carry):
        block = index // subs

        @pl.when((me < n - 1) & (block < (me + 1) * gps))
        def _():
            ag(0, index).wait_send()

        @pl.when((me > 0) & (block >= me * gps))
        def _():
            ag(1, index).wait_send()

        return carry

    lax.fori_loop(0, n * pieces, drain, 0)
    for peer in range(n):

        @pl.when(me != peer)
        def _():
            rk_to(peer, me).wait_send()

    keep_all.wait()


def back_stage(db, rk, seg, chp, bcp, hp, wo, saved, n, collective_id):
    rows, width = db.shape
    length = n * rows
    channels = wo.shape[0]
    pairs = channels // 128
    total = 2 * channels + 384
    shape = jax.ShapeDtypeStruct
    vmem = pl.BlockSpec(memory_space=pltpu.VMEM)
    anywhere = pl.BlockSpec(memory_space=pl.ANY)
    dma = pltpu.SemaphoreType.DMA
    held = [pltpu.VMEM((2, TB) + item.shape[1:], item.dtype) for item in saved[:-1]]
    held.append(pltpu.VMEM((2, TB // T, 128, channels), BF16))
    return pl.pallas_call(
        partial(back_kernel, n),
        out_shape=[
            shape((length, total), BF16), shape((length, channels), BF16), shape((length, width), BF16),
            shape((7, 8, channels), F32), shape((5, 8, 256), F32), shape((2, 8, 128), F32),
        ],
        in_specs=[anywhere] + [vmem] * 5 + [anywhere] * 10,
        out_specs=[anywhere] * 3 + [vmem] * 3,
        scratch_shapes=[
            pltpu.VMEM((length, width), BF16),
            pltpu.VMEM((length // T, 8, 128), F32),
            pltpu.VMEM(wo.shape, BF16),
        ] + held + [
            pltpu.VMEM((TB, total), BF16),
            pltpu.VMEM((TB, channels), BF16),
            pltpu.VMEM((TB, channels), F32),
            pltpu.VMEM((T + 8, channels), F32),
            pltpu.VMEM((T + 8, 256), F32),
            pltpu.VMEM((128, channels), F32),
            pltpu.VMEM((128, channels), BF16),
            pltpu.VMEM((T, channels), BF16),
            pltpu.VMEM((T, channels), BF16),
            pltpu.VMEM((128, 128), F32),
            pltpu.VMEM((channels, 128), BF16),
            pltpu.VMEM((pairs, 256, 128), BF16),
            pltpu.VMEM((T, channels), F32),
            pltpu.VMEM((T, channels), F32),
            pltpu.VMEM((3 * T + 16, channels), BF16),
            pltpu.VMEM((8, channels), F32),
            pltpu.VMEM((length + 16, 128), F32),
            pltpu.VMEM((length // T, 128), F32),
            dma((3,)), dma((9, 2)), dma((2,)),
            dma((2, length // T)), dma((2, length // T)), dma((n,)), dma((n,)),
        ],
        compiler_params=pltpu.CompilerParams(
            collective_id=collective_id, has_side_effects=True, vmem_limit_bytes=60 << 20
        ),
        name="back_stage",
    )(db, rk, seg, chp, bcp, hp, wo, *saved)


def scatter_body(n, me, a_ref, right_refs, acc, part, slots, send_sem, recv_sem):
    rows, width = acc.shape
    group = part.shape[0]
    piece = slots.shape[2]
    pieces = rows // piece
    groups = rows // group
    subs = group // piece

    def link(way, index):
        peer = me + 1 if way == 0 else me - 1
        return to_peer(
            slots.at[way, index], slots.at[way, index], send_sem.at[way, index], recv_sem.at[way, index], "tp", peer
        )

    def own(start, target, base):
        def tile(i, carry):
            cols = pl.ds(pl.multiple_of(i * 256, 256), 256)
            total, at = None, 0
            for w_ref in right_refs:
                depth = w_ref.shape[1]
                term = dot_nt(a_ref[pl.ds(start, group), at : at + depth], w_ref[cols, :])
                total = term if total is None else total + term
                at += depth
            target[pl.ds(base, group), cols] = total
            return carry

        lax.fori_loop(0, width // 256, tile, 0)

    def pass_on(way, q, at_end):
        shard = n - 1 - q // groups if way == 0 else q // groups
        start = pl.multiple_of(shard * rows + (q % groups) * group, group)
        own(start, part, 0)
        for sub in range(subs):
            index = shard * pieces + (q % groups) * subs + sub
            here = slice(sub * piece, (sub + 1) * piece)

            @pl.when(at_end)
            def _():
                slots[way, index] = part[here, :].astype(BF16)

            @pl.when(jnp.logical_not(at_end))
            def _():
                link(way, index).wait_recv()
                slots[way, index] = (part[here, :] + slots[way, index].astype(F32)).astype(BF16)

            link(way, index).start()

    def turn(t, carry):
        for way in (0, 1):
            hops = me if way == 0 else n - 1 - me
            q = t - hops

            @pl.when((q >= 0) & (q < (n - 1 - hops) * groups))
            def _():
                pass_on(way, q, hops == 0)

        late = t - (n - 1)

        @pl.when((late >= 0) & (late < groups))
        def _():
            base = pl.multiple_of(late * group, group)
            own(pl.multiple_of(me * rows + late * group, group), acc, base)

        return carry

    lax.fori_loop(0, (n - 1) * groups + n - 1, turn, 0)

    def arrived(p):
        for way in (0, 1):

            @pl.when((me > 0) if way == 0 else (me < n - 1))
            def _():
                link(way, me * pieces + p).wait_recv()
                here = pl.ds(pl.multiple_of(p * piece, piece), piece)
                acc[here, :] += slots[way, me * pieces + p].astype(F32)

    def drain():
        def done(index, carry):
            shard = index // pieces
            for way in (0, 1):

                @pl.when((me < shard) if way == 0 else (me > shard))
                def _():
                    link(way, index).wait_send()

            return carry

        lax.fori_loop(0, n * pieces, done, 0)

    return arrived, drain


def forward_block(
    t, nb, wc, segc, segf, chp_ref, bcp_ref, hp_ref,
    zbuf, xs_out, xcv_out, y_out, u_all, bcr_out, bcv_out, dtr_out, bcc_out, st_out, sq_all,
    xbuf, bcbuf, state, entering, weighted, decays,
):
    channels = zbuf.shape[1]
    pairs = channels // 128
    start = pl.multiple_of(t * TB, TB)
    nb_rows = pl.ds(start, TB)
    for n in range(channels // 256):
        cols = slice(n * 256, n * 256 + 256)
        zbuf[:, cols] = dot(nb[nb_rows, :], wc[:, cols])
        xbuf[8 : 8 + TB, cols] = dot(nb[nb_rows, :], wc[:, channels + n * 256 : channels + n * 256 + 256])
    bd = dot(nb[nb_rows, :], wc[:, 2 * channels :])
    bcbuf[8 : 8 + TB, :] = bd[:, :256]
    dtr_out[...] = bd[:, 256:]
    bcr_out[...] = bd[:, :256].astype(BF16)
    first = iota((T, 128), 1) < 64
    for c in range(TB // T):
        r0 = c * T
        rows = slice(r0, r0 + T)
        chunk = t * (TB // T) + c
        at = pl.ds(pl.multiple_of(start + r0, T), T)
        near = segc[pl.ds(pl.multiple_of(start + r0, T), T + 8), :]
        seg_col = near[8:, :]
        masks = [(near[8 - d : 8 - d + T, :] == seg_col).astype(F32) for d in (1, 2, 3)]
        start_b = (seg_col == near[7:8, :]).astype(F32)
        end_b = (seg_col == near[T + 7 : T + 8, :]).astype(F32)
        parts = []
        for half in range(2):
            cols = slice(half * 128, half * 128 + 128)
            acc = bcbuf[8 + r0 : 8 + r0 + T, cols] * bcp_ref[3:4, cols] + bcp_ref[4:5, cols]
            for d in (1, 2, 3):
                acc = acc + bcbuf[8 + r0 - d : 8 + r0 - d + T, cols] * bcp_ref[3 - d : 4 - d, cols] * masks[d - 1]
            bcv_out[rows, cols] = acc.astype(BF16)
            hv = 0.5 * acc
            parts.append((hv + hv * jnp.tanh(hv)).astype(BF16))
            bcc_out[rows, cols] = parts[-1]
        bm, cm = parts
        bt = bm.T
        _, dt, la, cum = step_sizes(dtr_out[rows, :], hp_ref)
        cum_t = cum.T
        scores = dot_nt(cm, bm)
        keep = (seg_col == segf[pl.ds(chunk, 1), :]) & (iota((T, T), 0) >= iota((T, T), 1))
        qm = jnp.where(keep, scores, 0.0)
        sq = jnp.zeros((T, 128), F32)
        st_out[c, :, :] = state[...].astype(BF16)
        entering[...] = dot(cm, st_out[c, :, :])
        for j in range(pairs):
            cols = slice(j * 128, j * 128 + 128)
            acc = xbuf[8 + r0 : 8 + r0 + T, cols] * chp_ref[3:4, cols] + chp_ref[4:5, cols]
            xs_out[rows, cols] = xbuf[8 + r0 : 8 + r0 + T, cols].astype(BF16)
            for d in (1, 2, 3):
                acc = acc + xbuf[8 + r0 - d : 8 + r0 - d + T, cols] * chp_ref[3 - d : 4 - d, cols] * masks[d - 1]
            xcv_out[rows, cols] = acc.astype(BF16)
            hv = 0.5 * acc
            xc = hv + hv * jnp.tanh(hv)
            dt_e = jnp.where(first, lanes(dt, 2 * j), lanes(dt, 2 * j + 1))
            ca, cb = lanes(cum, 2 * j), lanes(cum, 2 * j + 1)
            cum_e = jnp.where(first, ca, cb)
            xdt = xc * dt_e
            ea = jnp.exp2(jnp.minimum(ca - cum_t[2 * j : 2 * j + 1, :], 0.0))
            eb = jnp.exp2(jnp.minimum(cb - cum_t[2 * j + 1 : 2 * j + 2, :], 0.0))
            mix = jnp.concatenate([(ea * qm).astype(BF16), (eb * qm).astype(BF16)], axis=1)
            y = dot(mix, split_pair(xdt.astype(BF16)))
            into = jnp.exp2(cum_e) * start_b
            last = cum_e[T - 1 : T, :]
            to_end = jnp.exp2(last - cum_e) * end_b
            y = y + into * entering[:, cols]
            weighted[:, cols] = (xdt * to_end).astype(BF16)
            decays[0:1, cols] = into[T - 1 : T, :]
            y = y + chp_ref[5:6, cols] * xc
            y_out[rows, cols] = y
            hz = 0.5 * zbuf[rows, cols]
            g = y * (hz + hz * jnp.tanh(hz))
            sq = sq + g * g
            u_all[at, cols] = (g * chp_ref[6:7, cols]).astype(BF16)
        state[...] = state[...] * decays[0:1, :] + dot(bt, weighted[...])
        sq_all[chunk, :, :] = lax.dot_general(
            jnp.ones((8, 128), F32), sq, (((1,), (1,)), ((), ())), preferred_element_type=F32, precision=HIGHEST
        )
    xbuf[0:8, :] = xbuf[TB : TB + 8, :]
    bcbuf[0:8, :] = bcbuf[TB : TB + 8, :]


def front_kernel(
    n, dp, inner,
    x_ref, t_ref, wz_ref, wx_ref, wos_ref, bct_ref, dtt_ref, bp_ref, pg_ref, seg_ref, cw_ref, cb_ref, gain_ref, hp_ref, v_ref,
    z_out, xs_out, xcv_out, y_out, bcr_out, bcv_out, dtr_out, bcc_out, st_out,
    nb_out, wc_out, wo_out, er_out, db_out, rk_out, loss_out, chp_out, bcp_out, hp_out,
    nb, wc, wo, u_all, slots, acc, part,
    zbuf, xsb, xcvb, yb, bcrb, bcvb, dtrb, bccb, stb,
    xbuf, bcbuf, state, sq_all, sqs, xst, tst, erb, dbb,
    segc, segf, bc_all, bp_all, wbd, entering, weighted, decays,
    load_sem, keep_sem, save_sem, s_send, s_recv, w_send, w_hop, w_pass, w_recv, ag_send, ag_recv, rs_send, rs_recv, q_send, q_recv,
):
    me, me_dp = lax.axis_index("tp"), lax.axis_index("dp")
    rows, width = acc.shape
    pieces = rows // T
    tiles = width // 128
    gps = rows // TB
    subs = TB // T
    blocks = n * gps
    share_rows = wz_ref.shape[0]
    channels = wz_ref.shape[1]
    pairs = channels // 128
    barrier = pltpu.get_barrier_semaphore()
    for peer in range(dp):

        @pl.when(me_dp != peer)
        def _():
            pl.semaphore_signal(barrier, inc=1, device_id={"dp": peer}, device_id_type=MESH_ID)

    for peer in range(n):

        @pl.when(me != peer)
        def _():
            pl.semaphore_signal(barrier, inc=1, device_id={"tp": peer}, device_id_type=MESH_ID)

    def load(source, target, slot, p):
        view = source.at[pl.ds(pl.multiple_of(p * (T * tiles), T * tiles), T * tiles)]
        return pltpu.make_async_copy(view, target.at[slot], load_sem.at[0 if target is xst else 1, slot])

    load(x_ref, xst, 0, 0).start()

    def place(i, owner):
        at = pl.ds(pl.multiple_of(owner * share_rows, share_rows), share_rows)
        if i == 0:
            return wc.at[at, 0:channels]
        if i == 1:
            return wc.at[at, channels : 2 * channels]
        if i == 2:
            return wc.at[at, 2 * channels : 2 * channels + 384]
        return wo.at[:, at]

    local = (wz_ref, wx_ref, wbd, wos_ref)

    def keep_own(i):
        return pltpu.make_async_copy(local[i], place(i, me_dp), keep_sem.at[3 + i])

    for i in (0, 1, 3):
        keep_own(i).start()
    state[...] = jnp.zeros_like(state)
    xbuf[0:8, :] = jnp.zeros((8, xbuf.shape[1]), F32)
    bcbuf[0:8, :] = jnp.zeros((8, 256), F32)
    pl.semaphore_wait(barrier, dp - 1 + n - 1)

    core = me_dp % 2
    chip = me_dp // 2
    sibling = me_dp + 1 - 2 * core

    def give(i, peer):
        return to_peer(local[i], place(i, me_dp), w_send.at[i, peer], w_recv.at[i, me_dp], "dp", peer)

    def passed(i, owner):
        there = place(i, owner)
        return to_peer(there, there, w_pass.at[i, owner], w_recv.at[i, owner], "dp", sibling)

    square = dp == 8
    across = chip + 1 - 2 * (chip % 2)
    along = (chip + 2) % 4
    corner = 3 - chip

    def hop(i, owner, peer):
        there = place(i, owner)
        return to_peer(there, there, w_hop.at[i], w_recv.at[i, owner], "dp", peer)

    def onward(i):
        source, target = ((across, along), (along, across))[i]
        return hop(i, 2 * source + core, 2 * target + core)

    def give_all(i):
        if square and i < 2:
            give(i, 2 * across + core).start()
            give(i, 2 * along + core).start()
        else:
            for k in range(dp // 2):

                @pl.when(chip != k)
                def _():
                    give(i, 2 * k + core).start()

        give(i, sibling).start()

    def turn_corner(i):
        if square:
            owner = 2 * (across, along)[i] + core
            passed(i, owner).wait_recv()
            onward(i).start()
            passed(i, owner).start()

    def pass_all(i):
        if square and i < 2:
            for owner in (2 * (along, across)[i] + core, 2 * corner + core):
                passed(i, owner).wait_recv()
                passed(i, owner).start()
        else:
            for k in range(dp // 2):

                @pl.when(chip != k)
                def _():
                    passed(i, 2 * k + core).wait_recv()
                    passed(i, 2 * k + core).start()

    def wait_all(i):
        keep_own(i).wait()
        passed(i, sibling).wait_recv()
        for k in range(dp // 2):

            @pl.when(chip != k)
            def _():
                passed(i, 2 * k + 1 - core).wait_recv()

    def swap(i, peer, slot):
        source, target = ((bct_ref, bc_all), (bp_ref, bp_all))[i]
        return to_peer(source, target.at[slot], s_send.at[i, peer], s_recv.at[i, slot], "tp", peer)

    for peer in range(n):

        @pl.when(me != peer)
        def _():
            swap(0, peer, me).start()
            swap(1, peer, me).start()

    bc_all[pl.ds(me, 1)] = bct_ref[...][None]
    bp_all[pl.ds(me, 1)] = bp_ref[...][None]
    give_all(1)
    give_all(0)

    def ag(way, index):
        here = nb.at[pl.ds(pl.multiple_of(index * T, T), T)]
        peer = me + 1 if way == 0 else me - 1
        return to_peer(here, here, ag_send.at[way, index], ag_recv.at[way, index], "tp", peer)

    def normalize(p, carry):
        load(x_ref, xst, p % 2, p).wait()

        @pl.when(p + 1 < pieces)
        def _():
            load(x_ref, xst, (p + 1) % 2, p + 1).start()

        squares = jnp.zeros((T, 128), F32)
        for c in range(tiles):
            xt = xst[p % 2, pl.ds(c, T, stride=tiles), :]
            squares = squares + xt * xt
        inv = lax.rsqrt(jnp.sum(squares, axis=1, keepdims=True) / width + EPS)
        inv_b = jnp.broadcast_to(inv, (T, 128))
        index = me * pieces + p
        here = pl.ds(pl.multiple_of(index * T, T), T)
        for c in range(tiles):
            cols = slice(c * 128, c * 128 + 128)
            xt = xst[p % 2, pl.ds(c, T, stride=tiles), :]
            nb[here, cols] = (xt * inv_b * pg_ref[0:1, cols]).astype(BF16)
        @pl.when((me < n - 1) & ((me == 0) | (me > p)))
        def _():
            ag(0, index).start()

        @pl.when(me > 0)
        def _():
            ag(1, index).start()

        return carry

    lax.fori_loop(0, pieces, normalize, 0)
    for peer in range(n):

        @pl.when(me != peer)
        def _():
            swap(0, peer, peer).wait_recv()
            swap(1, peer, peer).wait_recv()

    columns = bc_all.shape[0] * bc_all.shape[1]
    wbd[:, 0:256] = bc_all[...].reshape(columns, share_rows).T
    wbd[:, 256:384] = dtt_ref[...].T
    keep_own(2).start()
    give_all(2)
    bcp_out[...] = bp_all[...].reshape(columns, 128).T[0:8, :]
    hp_out[...] = hp_ref[...]
    hp_out[1:2, :] = -jnp.exp(hp_ref[1:2, :])
    chp_out[0:4, :] = cw_ref[...]
    chp_out[4:5, :] = cb_ref[...]
    chp_out[6:7, :] = gain_ref[...]
    chp_out[7:8, :] = gain_ref[...]
    half = iota((1, 128), 1) < 64
    for j in range(pairs):
        low, high = hp_ref[2:3, 2 * j : 2 * j + 1], hp_ref[2:3, 2 * j + 1 : 2 * j + 2]
        chp_out[5:6, j * 128 : j * 128 + 128] = jnp.where(
            half, jnp.broadcast_to(low, (1, 128)), jnp.broadcast_to(high, (1, 128))
        )
    document_columns(seg_ref, segc, segf)

    def low(k):
        for sub in range(subs):
            index = k * subs + sub

            @pl.when(k < me * gps)
            def _():
                ag(0, index).wait_recv()

                @pl.when(me < n - 1)
                def _():
                    ag(0, index).start()

        @pl.when((k == me * gps - 1) & (me < n - 1))
        def _():
            for p in range(pieces):

                @pl.when(me <= p)
                def _():
                    ag(0, me * pieces + p).start()

    def high(k):
        for sub in range(subs):
            index = ((me + 1) * gps + k) * subs + sub

            @pl.when((me + 1) * gps + k < blocks)
            def _():
                ag(1, index).wait_recv()

                @pl.when(me > 0)
                def _():
                    ag(1, index).start()

    middle = (me > 0) & (me < n - 1)
    turn_corner(1)
    turn_corner(0)
    early = min(2, blocks - gps)

    @pl.when(middle)
    def _():
        for k in range(early):
            low(k)
            high(k)

    for i in (1, 0, 2):
        pass_all(i)
    give_all(3)
    for i in range(3):
        wait_all(i)

    saves = (
        (zbuf, z_out), (xsb, xs_out), (xcvb, xcv_out), (yb, y_out),
        (bcrb, bcr_out), (bcvb, bcv_out), (dtrb, dtr_out), (bccb, bcc_out),
    )

    def save(i, t):
        if i == len(saves):
            there = st_out.at[pl.ds(pl.multiple_of(t * subs, subs), subs)]
            return pltpu.make_async_copy(stb, there, save_sem.at[i])
        there = saves[i][1].at[pl.ds(pl.multiple_of(t * TB, TB), TB)]
        return pltpu.make_async_copy(saves[i][0], there, save_sem.at[i])

    def link(way, shard, p):
        source = shard * pieces + p
        if way == 0:
            target, peer = source, me + 1
        else:
            gap = jnp.minimum(me - 1 - shard, 1)
            target, peer = (shard + (n - shard) * (1 - gap)) * pieces + p, me - 1
        return to_peer(slots.at[source], slots.at[target], rs_send.at[way, source], rs_recv.at[way, target], "tp", peer)

    def landed(way, slot):
        peer = me - 1 if way == 0 else me + 1
        return to_peer(slots.at[slot], slots.at[slot], rs_send.at[way, slot], rs_recv.at[way, slot], "tp", peer)

    def own(block, target, base):
        def tile(i, carry):
            cols = pl.ds(pl.multiple_of(i * 256, 256), 256)
            target[pl.ds(base, TB), cols] = dot(u_all[pl.ds(pl.multiple_of(block * TB, TB), TB), :], wo[:, cols])
            return carry

        lax.fori_loop(0, width // 256, tile, 0)

    def pass_on(way, block, at_end):
        shard = block // gps
        own(block, part, 0)
        for sub in range(subs):
            p = (block % gps) * subs + sub
            slot = shard * pieces + p
            here = slice(sub * T, sub * T + T)

            @pl.when(at_end)
            def _():
                slots[slot] = part[here, :].astype(BF16)

            @pl.when(jnp.logical_not(at_end))
            def _():
                landed(way, slot).wait_recv()
                slots[slot] = (part[here, :] + slots[slot].astype(F32)).astype(BF16)

            link(way, shard, p).start()

    def squares_to(peer, slot):
        return to_peer(sq_all.at[pl.ds(peer * pieces, pieces)], sqs.at[slot], q_send.at[peer], q_recv.at[slot], "tp", peer)

    kept = (
        pltpu.make_async_copy(nb, nb_out, keep_sem.at[0]),
        pltpu.make_async_copy(wc, wc_out, keep_sem.at[1]),
        pltpu.make_async_copy(wo, wo_out, keep_sem.at[2]),
    )

    left_lag = LEFT_LAG

    def turn(t, carry):
        @pl.when(t < blocks)
        def _():
            @pl.when(t > 0)
            def _():
                for i in range(len(saves) + 1):
                    save(i, t - 1).wait()

            @pl.when((me == 0) & (t >= gps))
            def _():
                high(t - gps)

            @pl.when(me == n - 1)
            def _():
                low(t)

            forward_block(
                t, nb, wc, segc, segf, chp_out, bcp_out, hp_out,
                zbuf, xsb, xcvb, yb, u_all, bcrb, bcvb, dtrb, bccb, stb, sq_all,
                xbuf, bcbuf, state, entering, weighted, decays,
            )
            for i in range(len(saves) + 1):
                save(i, t).start()

            @pl.when(middle & (t + 1 >= early) & (t + 1 < blocks - gps))
            def _():
                low(t + 1)
                high(t + 1)

        @pl.when(t == jnp.minimum(n - 1 - me, gps))
        def _():
            pass_all(3)
            wait_all(3)
            for copy in kept[1:]:
                copy.start()

        @pl.when(t == blocks - 1)
        def _():
            kept[0].start()
            for peer in range(n):

                @pl.when(me != peer)
                def _():
                    squares_to(peer, me).start()

        left = t - left_lag * (n - 1 - me)

        @pl.when((left >= 0) & (left < me * gps))
        def _():
            pass_on(1, left, me == n - 1)

        right = t - me

        @pl.when((right >= (me + 1) * gps) & (right < blocks))
        def _():
            pass_on(0, right, me == 0)

        mine = t - gps - me * gps

        @pl.when((mine >= 0) & (mine < gps))
        def _():
            own(t - gps, acc, pl.multiple_of(mine * TB, TB))

        return carry

    turns = max(blocks + n - 1, max(m * gps + left_lag * (n - 1 - m) for m in range(n)))
    lax.fori_loop(0, turns, turn, 0)
    load(x_ref, xst, 0, 0).start()
    load(t_ref, tst, 0, 0).start()
    sqs[pl.ds(me, 1)] = sq_all[pl.ds(me * pieces, pieces)][None]
    for peer in range(n):

        @pl.when(me != peer)
        def _():
            squares_to(peer, peer).wait_recv()

    loss_out[...] = jnp.zeros_like(loss_out)

    def store(i, p):
        source, target = ((erb, er_out), (dbb, db_out))[i]
        return pltpu.make_async_copy(source, target.at[pl.ds(pl.multiple_of(p * T, T), T)], save_sem.at[i])

    for i in range(len(saves) + 1):
        save(i, blocks - 1).wait()
    def judge(p, carry):
        load(x_ref, xst, p % 2, p).wait()
        load(t_ref, tst, p % 2, p).wait()

        @pl.when(p + 1 < pieces)
        def _():
            load(x_ref, xst, (p + 1) % 2, p + 1).start()
            load(t_ref, tst, (p + 1) % 2, p + 1).start()

        here = pl.ds(pl.multiple_of(p * T, T), T)

        @pl.when(me > 0)
        def _():
            landed(0, me * pieces + p).wait_recv()
            acc[here, :] += slots[me * pieces + p].astype(F32)

        @pl.when(me < n - 1)
        def _():
            landed(1, n * pieces + p).wait_recv()
            acc[here, :] += slots[n * pieces + p].astype(F32)

        @pl.when(p > 0)
        def _():
            for i in range(2):
                store(i, p - 1).wait()

        total = sqs[0, p]
        for peer in range(1, n):
            total = total + sqs[peer, p]
        rg_row = lax.rsqrt(total / inner + EPS)
        rg_b = jnp.broadcast_to(column(rg_row[0:1, :]), (T, 128))
        valid_row = v_ref[pl.ds(p, 1), :].astype(F32)
        mask_b = jnp.broadcast_to(column(valid_row), (T, 128))
        dots = jnp.zeros((T, 128), F32)
        lost = jnp.zeros((T, 128), F32)
        for c in range(tiles):
            cols = slice(c * 128, c * 128 + 128)
            view = pl.ds(c, T, stride=tiles)
            branch = acc[here, cols] * rg_b
            error = xst[p % 2, view, :] + branch - tst[p % 2, view, :]
            d_out = error * mask_b
            erb[:, cols] = error
            d_branch = d_out.astype(BF16)
            dbb[:, cols] = d_branch
            lost = lost + d_out * error
            dots = dots + d_branch.astype(F32) * branch
        loss_out[0:8, :] += row_sums(lost)
        loss_out[8:9, :] += valid_row
        coefficient = jnp.sum(dots, axis=1, keepdims=True)
        rk_out[p, 0:1, :] = rg_row[0:1, :]
        rk_out[p, 1:2, :] = row(coefficient) * rg_row[0:1, :] * rg_row[0:1, :] / inner
        rk_out[p, 2:8, :] = jnp.zeros((6, 128), F32)
        for i in range(2):
            store(i, p).start()

        return carry

    lax.fori_loop(0, pieces, judge, 0)
    for i in range(2):
        store(i, pieces - 1).wait()
    for copy in kept:
        copy.wait()

    def drain(index, carry):
        block = index // subs
        shard = index // pieces

        @pl.when((me < n - 1) & (block < (me + 1) * gps))
        def _():
            ag(0, index).wait_send()

        @pl.when((me > 0) & (block >= me * gps))
        def _():
            ag(1, index).wait_send()

        @pl.when(me < shard)
        def _():
            link(0, shard, index % pieces).wait_send()

        @pl.when(me > shard)
        def _():
            link(1, shard, index % pieces).wait_send()

        return carry

    lax.fori_loop(0, n * pieces, drain, 0)
    for i in range(4):
        give(i, sibling).wait_send()
        if square and i < 2:
            onward(i).wait_send()
            give(i, 2 * across + core).wait_send()
            give(i, 2 * along + core).wait_send()
            for owner in (2 * across + core, 2 * along + core, 2 * corner + core):
                passed(i, owner).wait_send()
        else:
            for k in range(dp // 2):

                @pl.when(chip != k)
                def _():
                    give(i, 2 * k + core).wait_send()
                    passed(i, 2 * k + core).wait_send()

    for peer in range(n):

        @pl.when(me != peer)
        def _():
            swap(0, peer, me).wait_send()
            swap(1, peer, me).wait_send()
            squares_to(peer, me).wait_send()


def front_stage(x_view, t_view, wz, wx, wos, bct, dtt, bp, pg, seg, cw, cb, gain, hp, v_rows, n, dp, inner, collective_id):
    width = pg.shape[1]
    rows = x_view.shape[0] * 128 // width
    length = n * rows
    share_rows, channels = wz.shape
    total = 2 * channels + 384
    vmem = pl.BlockSpec(memory_space=pltpu.VMEM)
    anywhere = pl.BlockSpec(memory_space=pl.ANY)
    tile_rows = T * width // 128
    shape = jax.ShapeDtypeStruct
    saved = [
        shape((length, channels), F32), shape((length, channels), BF16), shape((length, channels), BF16),
        shape((length, channels), F32), shape((length, 256), BF16), shape((length, 256), BF16),
        shape((length, 128), F32), shape((length, 256), BF16),
        shape((length // T, 128, channels), BF16),
    ]
    buffers = [pltpu.VMEM((TB,) + item.shape[1:], item.dtype) for item in saved[:-1]]
    buffers.append(pltpu.VMEM((TB // T, 128, channels), BF16))
    dma = pltpu.SemaphoreType.DMA
    return pl.pallas_call(
        partial(front_kernel, n, dp, inner),
        out_shape=saved + [
            shape((length, width), BF16), shape((width, total), BF16), shape((channels, width), BF16),
            shape((rows, width), F32), shape((rows, width), BF16),
            shape((rows // T, 8, 128), F32), shape((16, 128), F32),
            shape((8, channels), F32), shape((8, 256), F32), shape((8, 128), F32),
        ],
        in_specs=[anywhere] * 5 + [vmem] * 10,
        out_specs=[anywhere] * 14 + [vmem] * 5,
        scratch_shapes=[
            pltpu.VMEM((length, width), BF16),
            pltpu.VMEM((width, total), BF16),
            pltpu.VMEM((channels, width), BF16),
            pltpu.VMEM((length, channels), BF16),
            pltpu.VMEM(((n + 1) * rows // T, T, width), BF16),
            pltpu.VMEM((rows, width), F32),
            pltpu.VMEM((TB, width), F32),
        ] + buffers + [
            pltpu.VMEM((TB + 8, channels), F32),
            pltpu.VMEM((TB + 8, 256), F32),
            pltpu.VMEM((128, channels), F32),
            pltpu.VMEM((length // T, 8, 128), F32),
            pltpu.VMEM((n, rows // T, 8, 128), F32),
            pltpu.VMEM((2, tile_rows, 128), F32),
            pltpu.VMEM((2, tile_rows, 128), F32),
            pltpu.VMEM((T, width), F32),
            pltpu.VMEM((T, width), BF16),
            pltpu.VMEM((length + 16, 128), F32),
            pltpu.VMEM((length // T, 128), F32),
            pltpu.VMEM((n,) + bct.shape, BF16),
            pltpu.VMEM((n,) + bp.shape, F32),
            pltpu.VMEM((share_rows, 384), BF16),
            pltpu.VMEM((T, channels), F32),
            pltpu.VMEM((T, channels), BF16),
            pltpu.VMEM((8, channels), F32),
            dma((2, 2)), dma((7,)), dma((9,)), dma((2, n)), dma((2, n)),
            dma((4, dp)), dma((2,)), dma((4, dp)), dma((4, dp)),
            dma((2, length // T)), dma((2, length // T)),
            dma((2, (n + 1) * rows // T)), dma((2, (n + 1) * rows // T)),
            dma((n,)), dma((n,)),
        ],
        compiler_params=pltpu.CompilerParams(
            collective_id=collective_id, has_side_effects=True, vmem_limit_bytes=63 << 20
        ),
        name="front_stage",
    )(x_view, t_view, wz, wx, wos, bct, dtt, bp, pg, seg, cw, cb, gain, hp, v_rows)


def scatter_scratch(length, rows, width):
    return [
        pltpu.VMEM((rows, width), F32),
        pltpu.VMEM((min(rows, 256), width), F32),
        pltpu.VMEM((2, length // T, T, width), BF16),
    ], [
        pltpu.SemaphoreType.DMA((2, length // T)),
        pltpu.SemaphoreType.DMA((2, length // T)),
    ]


def input_kernel(n, a_any, w_any, acc, a_ref, w_ref, part, slots, load_sem, send_sem, recv_sem):
    loads = [
        pltpu.make_async_copy(source, target, load_sem.at[i])
        for i, (source, target) in enumerate(((w_any, w_ref), (a_any, a_ref)))
    ]
    for copy in loads:
        copy.start()
    me = meet(n, "tp")
    for copy in loads:
        copy.wait()
    arrived, drain = scatter_body(n, me, a_ref, (w_ref,), acc, part, slots, send_sem, recv_sem)

    def last(p, carry):
        arrived(p)
        return carry

    lax.fori_loop(0, acc.shape[0] // T, last, 0)
    drain()


def input_stage(dproj, weight, n, collective_id):
    length, width = dproj.shape[0], weight.shape[0]
    rows = length // n
    vmem = pl.BlockSpec(memory_space=pltpu.VMEM)
    anywhere = pl.BlockSpec(memory_space=pl.ANY)
    buffers, sems = scatter_scratch(length, rows, width)
    return pl.pallas_call(
        partial(input_kernel, n),
        out_shape=jax.ShapeDtypeStruct((rows, width), F32),
        in_specs=[anywhere] * 2,
        out_specs=vmem,
        scratch_shapes=[pltpu.VMEM(dproj.shape, BF16), pltpu.VMEM(weight.shape, BF16)]
        + buffers[1:] + [pltpu.SemaphoreType.DMA((2,))] + sems,
        compiler_params=pltpu.CompilerParams(
            collective_id=collective_id, has_side_effects=True, vmem_limit_bytes=60 << 20
        ),
        cost_estimate=pl.CostEstimate(
            flops=2 * length * width * dproj.shape[1], bytes_accessed=400 << 20, transcendentals=0
        ),
        name="input_stage",
    )(dproj, weight)


def output_kernel(dn_ref, er_ref, x_ref, t_ref, v_ref, pg_ref, lo_out, gx_out, gp_out):
    width = dn_ref.shape[1]
    tiles = width // 128

    @pl.when(pl.program_id(0) == 0)
    def _():
        gp_out[...] = jnp.zeros_like(gp_out)

    squares = jnp.zeros((T, 128), F32)
    dots = jnp.zeros((T, 128), F32)
    for c in range(tiles):
        cols = slice(c * 128, c * 128 + 128)
        xt = x_ref[pl.ds(c, T, stride=tiles), :]
        squares = squares + xt * xt
        dots = dots + dn_ref[:, cols] * pg_ref[0:1, cols] * xt
    inv = lax.rsqrt(jnp.sum(squares, axis=1, keepdims=True) / width + EPS)
    inv_b = jnp.broadcast_to(inv, (T, 128))
    mean = jnp.sum(dots, axis=1, keepdims=True) / width
    back_b = jnp.broadcast_to(inv * inv * inv * mean, (T, 128))
    mask_b = jnp.broadcast_to(column(v_ref[pl.ds(pl.program_id(0), 1), :].astype(F32)), (T, 128))
    for c in range(tiles):
        cols = slice(c * 128, c * 128 + 128)
        view = pl.ds(c, T, stride=tiles)
        xt = x_ref[view, :]
        scaled = dn_ref[:, cols] * inv_b
        error = er_ref[:, cols]
        lo_out[view, :] = error + t_ref[view, :]
        gx_out[view, :] = error * mask_b + scaled * pg_ref[0:1, cols] - xt * back_b
        gp_out[:, cols] += row_sums(scaled * xt)


def output_stage(dn, error, x_view, t_view, valid_rows, pg):
    rows, width = dn.shape
    block = pl.BlockSpec((T, width), lambda i: (i, 0))
    view = pl.BlockSpec((T * width // 128, 128), lambda i: (i, 0))
    whole = lambda shape: pl.BlockSpec(shape, lambda i: (0, 0))
    shape = jax.ShapeDtypeStruct
    return pl.pallas_call(
        output_kernel,
        grid=(rows // T,),
        in_specs=[block, block, view, view, whole(valid_rows.shape), whole(pg.shape)],
        out_specs=[view, view, whole((8, width))],
        out_shape=[shape(x_view.shape, F32), shape(x_view.shape, F32), shape((8, width), F32)],
        compiler_params=pltpu.CompilerParams(vmem_limit_bytes=62 << 20),
        name="output_stage",
    )(dn, error, x_view, t_view, valid_rows, pg)


def last_kernel(
    tp, mine, both, cols, gc_ref, go_ref,
    wz_out, wx_out, wdt_out, wbc_out, wo_out, cw_out, cb_out, gain_out, skip_out, dtb_out, alog_out,
    gp_out, bw_out, bb_out, loss_out,
):
    channels = wz_out.shape[1]
    heads = wdt_out.shape[0]
    width = gp_out.shape[1]
    wz_out[...] = gc_ref[:, 0:channels].astype(F32)
    wx_out[...] = gc_ref[:, channels : 2 * channels].astype(F32)
    wdt_out[...] = gc_ref[:, 2 * channels + 256 : 2 * channels + 384].astype(F32).T[0:heads, :]
    wbc_out[...] = cols[...]
    for c in range(channels // 128):
        here = slice(c * 128, c * 128 + 128)
        wo_out[here, :] = go_ref[:, here].astype(F32).T
    per = channels // 128
    for k in range(7):
        for c in range(per):
            here = slice(c * 128, c * 128 + 128)
            line = mine[k * per + c : k * per + c + 1, :]
            if k < 4:
                cw_out[k : k + 1, here] = line
            elif k == 4:
                cb_out[:, here] = line
            elif k == 5:
                gain_out[:, here] = line
    lane = iota((1, 128), 1)
    skip = jnp.zeros((1, 128), F32)
    for c in range(per):
        line = mine[6 * per + c : 6 * per + c + 1, :]
        low = jnp.sum(jnp.where(lane < 64, line, 0.0), axis=1, keepdims=True)
        high = jnp.sum(jnp.where(lane < 64, 0.0, line), axis=1, keepdims=True)
        skip = skip + jnp.where(lane == 2 * c, low, 0.0) + jnp.where(lane == 2 * c + 1, high, 0.0)
    skip_out[...] = skip[:, 0:heads]
    dtb_out[...] = mine[7 * per : 7 * per + 1, 0:heads]
    alog_out[...] = mine[7 * per + 1 : 7 * per + 2, 0:heads]
    top = width // 128
    for c in range(top):
        gp_out[:, c * 128 : c * 128 + 128] = both[c : c + 1, :]
    me = lax.axis_index("tp")
    local = bb_out.shape[1]
    for k in range(5):
        for peer in range(tp):
            at = peer * local
            line = both[top + 2 * k + at // 128 : top + 2 * k + at // 128 + 1, at % 128 : at % 128 + local]

            @pl.when(me == peer)
            def _():
                if k < 4:
                    bw_out[k : k + 1, :] = line
                else:
                    bb_out[...] = line

    lost = jnp.sum(both[top + 10 : top + 11, :], axis=1, keepdims=True)
    count = jnp.sum(both[top + 11 : top + 12, :], axis=1, keepdims=True)
    loss_out[...] = lost / (jnp.maximum(count, 1.0) * width)


def last_stage(mine, both, cols, g_cat, g_out, heads, width, tp):
    rows = g_cat.shape[0]
    channels = g_out.shape[1]
    local = cols.shape[0]
    vmem = pl.BlockSpec(memory_space=pltpu.VMEM)
    shapes = [
        (rows, channels), (rows, channels), (heads, rows), cols.shape, (channels, rows),
        (4, channels), (1, channels), (1, channels), (1, heads), (1, heads), (1, heads),
        (1, width), (4, local), (1, local), (1, 1),
    ]
    return pl.pallas_call(
        partial(last_kernel, tp),
        in_specs=[vmem] * 5,
        out_specs=[vmem] * len(shapes),
        out_shape=[jax.ShapeDtypeStruct(shape, F32) for shape in shapes],
        compiler_params=pltpu.CompilerParams(vmem_limit_bytes=40 << 20),
        name="last_stage",
    )(mine, both, cols, g_cat, g_out)


def local(
    x_in, target, seg_ids, valid, pre_gain, w_z, w_x, w_bc, w_dt, conv_x_w, conv_x_b,
    conv_bc_w, conv_bc_b, dt_bias, a_log, d_skip, norm_gain, w_out,
):
    rows, _, width = x_in.shape
    channels = w_z.shape[1]
    heads = w_dt.shape[1]
    tp = lax.axis_size("tp")
    inner = channels * tp
    bc_local = w_bc.shape[1]
    dp = lax.axis_size("dp")
    x_view = x_in.reshape(rows * width // 128, 128)
    t_view = target.reshape(rows * width // 128, 128)
    seg = seg_ids.reshape(-1, 128)
    bp = jnp.pad(jnp.concatenate([conv_bc_w, conv_bc_b[:, None]], axis=1), ((0, 0), (0, 123)))
    dtt = jnp.pad(w_dt.T, ((0, 128 - heads), (0, 0)))
    hp = jnp.pad(jnp.stack([dt_bias, a_log, d_skip]), ((0, 5), (0, 128 - heads)), constant_values=-100.0)
    (
        z, xs, xcv, y, bcr, bcv, dtr, bcc, st,
        normed_all, wc, wo, error, d_branch, rk_own, lost, chp, bcp, hp,
    ) = front_stage(
        x_view, t_view, w_z, w_x, w_out, w_bc.T, dtt, bp, pre_gain[None], seg, conv_x_w.T, conv_x_b[None],
        norm_gain[None], hp, valid.reshape(-1, 128), tp, dp, inner, 1,
    )
    saved = (z, xs, xcv, y, bcr, bcv, dtr, bcc, st)
    dproj, yn, db_all, accc, accb, acch = back_stage(d_branch, rk_own, seg, chp, bcp, hp, wo, saved, tp, 2)

    def dot_tn(a, b):
        return lax.dot_general(a, b, (((0,), (0,)), ((), ())), preferred_element_type=F32)

    g_out = dot_tn(db_all, yn).astype(BF16)
    g_cat = dot_tn(normed_all, dproj).astype(BF16)
    g_out, g_cat, dproj = lax.optimization_barrier((g_out, g_cat, dproj))
    g_out = lax.psum_scatter(g_out, "dp", scatter_dimension=0, tiled=True)
    g_cat = lax.psum_scatter(g_cat, "dp", scatter_dimension=0, tiled=True)
    d_normed = input_stage(dproj, wc, tp, 3)
    lo_view, gx_view, gain_part = output_stage(
        d_normed, error, x_view, t_view, valid.reshape(-1, 128), pre_gain[None]
    )
    mine, both, cols = finish(accc, acch, accb, gain_part, lost, g_cat, dp, tp, 5)
    (
        grad_wz, grad_wx, grad_wdt, grad_wbc, grad_wo, grad_cw, grad_cb, grad_gain, grad_skip, grad_dtb, grad_alog,
        grad_pre, grad_bw, grad_bb, loss,
    ) = last_stage(mine, both, cols, g_cat, g_out, heads, width, tp)
    return (
        lo_view.reshape(x_in.shape),
        loss.reshape(()),
        gx_view.reshape(x_in.shape),
        grad_pre.reshape(-1),
        grad_wz,
        grad_wx,
        grad_wbc.T,
        grad_wdt.T,
        grad_cw.T,
        grad_cb.reshape(-1),
        grad_bw.T,
        grad_bb.reshape(-1),
        grad_dtb.reshape(-1),
        grad_alog.reshape(-1),
        grad_skip.reshape(-1),
        grad_gain.reshape(-1),
        grad_wo,
    )


def solution(mesh):
    tok, col, head = P("tp", "dp", None), P("dp", "tp"), P("tp")
    in_specs = (
        tok, tok, P("dp", None), col, P(), col, col, col, col,
        P("tp", None), head, P("tp", None), head, head, head, head, head, P("tp", "dp"),
    )
    out_specs = (
        tok, P(), tok, P(), col, col, col, col,
        P("tp", None), head, P("tp", None), head, head, head, head, head, P("tp", "dp"),
    )
    return jax.shard_map(local, mesh=mesh, in_specs=in_specs, out_specs=out_specs, check_vma=False)
```
